32 devices in a mesh: dp: 16 (over z, y, x), tensor: 2 (over core).
Axes of the slice: x: 2, y: 2, z: 4, core: 2. Of those that a mesh axis runs over, the one named last changes fastest.
Arguments:
- tokens: bfloat16 [32, 2, 512, 1024], P('dp', None, None, 'tensor'), may hold values from -6 to 6
- memory: bfloat16 [10, 1024], P(None, 'tensor'), may hold values from -6 to 6
- w_qkv: bfloat16 [1024, 3, 1024], P('dp', None, 'tensor'), may hold values from -0.1875 to 0.1875
- b_qv: bfloat16 [2, 1024], P(None, 'tensor'), may hold values from -3 to 3
- w_out: bfloat16 [1024, 1024], P('tensor', 'dp'), may hold values from -0.75 to 0.75
- out_biases: bfloat16 [2, 1024], P(None, 'tensor'), may hold values from -3 to 3
- norm_gains: bfloat16 [2, 1024], P(None, 'tensor'), may hold values from 0.099609375 to 1.8984375
- norm_shifts: bfloat16 [2, 1024], P(None, 'tensor'), may hold values from -3 to 3
- w_in: bfloat16 [1024, 4096], P('dp', 'tensor'), may hold values from -0.1875 to 0.1875
- b_in: bfloat16 [4096], P('tensor'), may hold values from -3 to 3
- w_down: bfloat16 [4096, 1024], P('tensor', 'dp'), may hold values from -0.09375 to 0.09375
- cotangent: bfloat16 [32, 2, 512, 1024], P('dp', None, None, 'tensor'), may hold values from -6 to 6
- mlm_mask: int32 [32, 2, 512], P('dp'), may hold values from 0 to 1, as said below
Outputs:
- outputs: bfloat16 [32, 2, 512, 1024], P('dp', None, None, 'tensor')
- input_grad: float32 [32, 2, 512, 1024], P('dp', None, None, 'tensor')
- memory_grad: float32 [10, 1024], P(None, 'tensor')
- grad_qkv: float32 [1024, 3, 1024], P('dp', None, 'tensor')
- grad_qv_bias: float32 [2, 1024], P(None, 'tensor')
- grad_out: float32 [1024, 1024], P('tensor', 'dp')
- grad_out_biases: float32 [2, 1024], P(None, 'tensor')
- grad_gains: float32 [2, 1024], P(None, 'tensor')
- grad_shifts: float32 [2, 1024], P(None, 'tensor')
- grad_in: float32 [1024, 4096], P('dp', 'tensor')
- grad_in_bias: float32 [4096], P('tensor')
- grad_down: float32 [4096, 1024], P('tensor', 'dp')
The draws below stay inside these ranges and needn't reach their ends.
Inputs may be any that keep to these rules, and one draw needn't show every extreme that they name: mlm_mask holds 0 or 1; each segment of an item has at most 153 ones, some item has exactly 153 in every segment, and the share of ones differs from item to item.
All inputs are finite; a program needn't handle non-finite values.
Results may differ from the reference program's by a relative error of at most 0.022.
Values may be sent and summed in bfloat16 or wider, within the bound.
A program may use at most 320 MiB of HBM per device.

```python
import jax
import jax.numpy as jnp
from jax import lax

D = 1024
HEADS = 16
FF = 4096
DH = 64
MEM = 10
TOK = 512
MASKED = 153
SEGS = 2
ITEMS = 32


def draw_mlm_mask(key, part):
    count_key = jax.random.fold_in(key, 11)
    full_key = jax.random.fold_in(key, 17)
    order_key = jax.random.fold_in(key, 23)
    counts = jax.random.randint(count_key, (ITEMS, SEGS), TOK // 20, MASKED + 1)
    full_item = jax.random.randint(full_key, (), 0, ITEMS)
    item_ids = jnp.arange(ITEMS, dtype=jnp.int32)[:, None]
    counts = jnp.where(item_ids == full_item, MASKED, counts)
    row_keys = jax.random.split(order_key, ITEMS * SEGS)
    ranks = jax.vmap(lambda single: jax.random.permutation(single, TOK))(row_keys).reshape(ITEMS, SEGS, TOK)
    return (ranks < counts[..., None]).astype(jnp.int32)


def block_scale(stream_key, shape, shards, low, high):
    def one(position, shards_of):
        heights = jax.random.uniform(jax.random.fold_in(jax.random.fold_in(stream_key, 6), position), (shards_of,), jnp.float32, low / len(shards), high / len(shards))
        return jnp.repeat(jnp.exp(heights), shape[position] // shards_of).reshape((-1,) + (1,) * (len(shape) - position - 1))

    factor_of = one(*shards[0])
    for cut in shards[1:]:
        factor_of = factor_of * one(*cut)
    return factor_of


def centred(rng, extent, deviation, limit, cuts=(), kind=jnp.bfloat16):
    values = jax.random.normal(rng, extent, jnp.float32) * deviation
    if len(cuts) > 0:
        values = block_scale(rng, extent, cuts, -0.22, 0.18) * values
    return jnp.clip(values, min=-limit, max=limit).astype(kind)


def setup_inputs(seed: int = 0) -> dict:
    arg_keys = jax.random.split(jax.random.key(seed), 14)
    tokens = centred(arg_keys[0], (ITEMS, SEGS, TOK, D), 1.0, 6.0, ((0, 16), (3, 2)))
    memory = centred(arg_keys[1], (MEM, D), 1.0, 6.0, ((1, 2),))
    w_qkv = centred(arg_keys[2], (D, 3, D), D ** -0.5, 0.1875, ((0, 16), (2, 2)))
    b_qv = centred(arg_keys[3], (2, D), 0.5, 3.0, ((1, 2),))
    w_out = centred(arg_keys[4], (D, D), (D // 16) ** -0.5, 0.75, ((0, 2), (1, 16)))
    out_biases = centred(arg_keys[5], (2, D), 0.5, 3.0, ((1, 2),))
    norm_gains = jnp.clip(1.0 + 0.18 * jax.random.normal(arg_keys[6], (2, D), jnp.float32), 0.099609375, 1.8984375).astype(jnp.bfloat16)
    norm_shifts = centred(arg_keys[7], (2, D), 0.5, 3.0, ((1, 2),))
    w_in = centred(arg_keys[8], (D, FF), D ** -0.5, 0.1875, ((0, 16), (1, 2)))
    b_in = centred(arg_keys[9], (FF,), 0.5, 3.0, ((0, 2),))
    w_down = centred(arg_keys[10], (FF, D), FF ** -0.5, 0.09375, ((0, 2), (1, 16)))
    cotangent = centred(arg_keys[11], (ITEMS, SEGS, TOK, D), 1.0, 6.0, ((0, 16), (3, 2)))
    mlm_mask = draw_mlm_mask(jax.random.fold_in(arg_keys[13], 71), 0)
    return dict(tokens=tokens, memory=memory, w_qkv=w_qkv, b_qv=b_qv, w_out=w_out, out_biases=out_biases, norm_gains=norm_gains, norm_shifts=norm_shifts, w_in=w_in, b_in=b_in, w_down=w_down, cotangent=cotangent, mlm_mask=mlm_mask)


eps_norm = 1e-05
exact_mode = lax.Precision.HIGHEST

@jax.custom_vjp
def low(v):
    return lax.optimization_barrier(v.astype(jnp.bfloat16)).astype(jnp.float32)

@jax.custom_vjp
def low_back(v):
    return v

def low_keep(v):
    return (low(v), None)

def low_pass(kept, grad):
    return (grad,)

def back_keep(v):
    return (v, None)

def back_low(kept, grad):
    return (low(grad),)
low.defvjp(low_keep, low_pass)
low_back.defvjp(back_keep, back_low)

def layer_norm(resid, gain, shift):
    center = lax.optimization_barrier(jnp.mean(resid, axis=-1, keepdims=True))
    spread = lax.optimization_barrier(jnp.mean(resid * resid, axis=-1, keepdims=True)) - center * center
    return (resid - center) * lax.rsqrt(spread + eps_norm) * gain + shift

def segment(params, memory_rows, token_rows):
    qkv_weight, qv_bias, out_weight, out_bias, gains, shifts, in_weight, in_bias, down_weight = params
    stacked = jnp.concatenate([memory_rows, token_rows], axis=0)
    length = stacked.shape[0]
    bias_three = jnp.stack([qv_bias[0], jnp.zeros_like(qv_bias[0]), qv_bias[1]])
    projected = jnp.einsum('ld,dcf->lcf', stacked, qkv_weight, precision=exact_mode) + bias_three
    projected = low(low_back(projected)).reshape(length, 3, HEADS, DH)
    scores = jnp.einsum('qhe,khe->hqk', projected[:, 0], projected[:, 1], precision=exact_mode) * DH ** (-0.5)
    scores = low_back(scores)
    probs = jax.nn.softmax(scores, axis=-1)
    context = jnp.einsum('hqk,khe->qhe', low(probs), projected[:, 2], precision=exact_mode).reshape(length, D)
    context = low(low_back(context))
    attended = low_back(jnp.dot(context, out_weight, precision=exact_mode))
    middle = layer_norm(stacked + attended + out_bias[0], gains[0], shifts[0])
    before = low_back(jnp.dot(low(middle), in_weight, precision=exact_mode) + in_bias)
    hidden = low(jax.nn.gelu(before, approximate=False))
    branch = low_back(jnp.dot(hidden, down_weight, precision=exact_mode))
    return layer_norm(middle + branch + out_bias[1], gains[1], shifts[1])

def forward(params, start_memory, rows):

    def one_item(item_rows):

        def advance(carry, seg_rows):
            result = segment(params, carry, seg_rows)
            return (low(result[:MEM]), result[MEM:])
        final_memory, token_outs = lax.scan(jax.checkpoint(advance), start_memory, item_rows)
        return token_outs
    return lax.map(one_item, rows)

def reference(tokens, memory, w_qkv, b_qv, w_out, out_biases, norm_gains, norm_shifts, w_in, b_in, w_down, cotangent, mlm_mask):
    params = (w_qkv.astype(jnp.float32), b_qv.astype(jnp.float32), w_out.astype(jnp.float32), out_biases.astype(jnp.float32), norm_gains.astype(jnp.float32), norm_shifts.astype(jnp.float32), w_in.astype(jnp.float32), b_in.astype(jnp.float32), w_down.astype(jnp.float32))
    start_memory = memory.astype(jnp.float32)
    rows = tokens.astype(jnp.float32)
    results, pullback = jax.vjp(forward, params, start_memory, rows)
    weighted = cotangent.astype(jnp.float32) * mlm_mask.astype(jnp.float32)[..., None]
    param_grads, memory_grad, input_grad = pullback(weighted)
    return (results.astype(jnp.bfloat16), input_grad, memory_grad, param_grads[0], param_grads[1], param_grads[2], param_grads[3], param_grads[4], param_grads[5], param_grads[6], param_grads[7], param_grads[8])
```

```python
import functools

import jax
import jax.numpy as jnp
from jax import lax
from jax.experimental import pallas as pl
from jax.experimental.pallas import tpu as pltpu
from jax.sharding import PartitionSpec as P

D = 1024
DH = 64
MICRO = 2


eps_norm = 1e-05
root_half = 0.7071067811865476
inv_root_two_pi = 0.3989422804014327


def gelu_value(before):
    return 0.5 * before * (1.0 + lax.erf(before * root_half))


def gelu_slope(before):
    return 0.5 * (1.0 + lax.erf(before * root_half)) + before * inv_root_two_pi * jnp.exp(
        -0.5 * before * before
    )


def fetch_weights(w_qkv, w_in, w_out, w_down):
    return (
        lax.all_gather(w_qkv, "dp", axis=0, tiled=True),
        lax.all_gather(w_in, "dp", axis=0, tiled=True),
        lax.all_gather(w_out, "dp", axis=1, tiled=True),
        lax.all_gather(w_down, "dp", axis=1, tiled=True),
    )


def reduce_weights(grad_proj, grad_inner, grad_outer, grad_lower):
    return (
        lax.psum_scatter(
            grad_proj.astype(jnp.bfloat16), "dp", scatter_dimension=0, tiled=True
        ).astype(jnp.float32),
        lax.psum_scatter(
            grad_inner.astype(jnp.bfloat16), "dp", scatter_dimension=0, tiled=True
        ).astype(jnp.float32),
        lax.psum_scatter(
            grad_outer.astype(jnp.bfloat16), "dp", scatter_dimension=1, tiled=True
        ).astype(jnp.float32),
        lax.psum_scatter(
            grad_lower.astype(jnp.bfloat16), "dp", scatter_dimension=1, tiled=True
        ).astype(jnp.float32),
    )


def gather_rows(block):
    return lax.all_gather(block, "tensor", axis=2, tiled=True)


def branch_sum(partial_value):
    return lax.psum_scatter(partial_value, "tensor", scatter_dimension=2, tiled=True)


def gather_grads(block):
    return lax.all_gather(block, "tensor", axis=2, tiled=True)


def input_sum(partial_value):
    return lax.psum_scatter(
        partial_value.astype(jnp.bfloat16), "tensor", scatter_dimension=2, tiled=True
    ).astype(jnp.float32)


def norm_forward(resid, gain, shift):
    totals = jnp.sum(resid, axis=-1)
    squares = jnp.sum(resid * resid, axis=-1)
    totals, squares = lax.psum((totals, squares), "tensor")
    center = totals / D
    spread = squares / D - center * center
    rstd = lax.rsqrt(spread + eps_norm)
    normed = (resid - center[..., None]) * rstd[..., None]
    return (normed * gain + shift, normed, rstd)


def norm_backward(upstream, normed, rstd, gain):
    scaled = upstream * gain
    first = jnp.sum(scaled, axis=-1)
    second = jnp.sum(scaled * normed, axis=-1)
    first, second = lax.psum((first, second), "tensor")
    result = rstd[..., None] * (scaled - first[..., None] / D - normed * (second[..., None] / D))
    return (result, jnp.sum(upstream * normed, axis=(0, 1)), jnp.sum(upstream, axis=(0, 1)))


def attention_scores(query, key_rows):
    return jnp.einsum(
        "bqhe,bkhe->bhqk", query, key_rows, preferred_element_type=jnp.float32
    ) * DH ** (-0.5)


def segment_forward(weights, smalls, memory_rows, token_rows):
    proj_weight, inner_weight, outer_weight, lower_weight = weights
    qv_bias, out_bias, gains, shifts, inner_bias = smalls
    batch = token_rows.shape[0]
    stacked = jnp.concatenate([memory_rows, token_rows], axis=1)
    length = stacked.shape[1]
    local = proj_weight.shape[2]
    heads = local // DH
    wide_rows = gather_rows(stacked)
    bias_three = jnp.stack([qv_bias[0], jnp.zeros_like(qv_bias[0]), qv_bias[1]])
    projected = (
        jnp.einsum("bld,dcf->blcf", wide_rows, proj_weight, preferred_element_type=jnp.float32)
        + bias_three
    ).astype(jnp.bfloat16)
    split = projected.reshape(batch, length, 3, heads, DH)
    scores = attention_scores(split[:, :, 0], split[:, :, 1])
    peak = jnp.max(scores, axis=-1, keepdims=True)
    expo = jnp.exp(scores - peak)
    totals = jnp.sum(expo, axis=-1, keepdims=True)
    probs = expo / totals
    logsum = peak[..., 0] + jnp.log(totals[..., 0])
    context = jnp.einsum(
        "bhqk,bkhe->bqhe",
        probs.astype(jnp.bfloat16),
        split[:, :, 2],
        preferred_element_type=jnp.float32,
    )
    context = context.astype(jnp.bfloat16).reshape(batch, length, local)
    attended = branch_sum(
        jnp.einsum("bld,df->blf", context, outer_weight, preferred_element_type=jnp.float32)
    )
    middle, normed_one, rstd_one = norm_forward(
        stacked.astype(jnp.float32) + attended + out_bias[0], gains[0], shifts[0]
    )
    middle_wide = gather_rows(middle.astype(jnp.bfloat16))
    before = (
        jnp.einsum("bld,df->blf", middle_wide, inner_weight, preferred_element_type=jnp.float32)
        + inner_bias
    )
    hidden = gelu_value(before).astype(jnp.bfloat16)
    branch = branch_sum(
        jnp.einsum("blf,fd->bld", hidden, lower_weight, preferred_element_type=jnp.float32)
    )
    layer_out, normed_two, rstd_two = norm_forward(
        middle + branch + out_bias[1], gains[1], shifts[1]
    )
    stored = (
        wide_rows,
        projected,
        logsum,
        context,
        normed_one,
        rstd_one,
        middle_wide,
        before,
        hidden,
        normed_two,
        rstd_two,
    )
    return (layer_out, stored)


def segment_backward(weights, smalls, upstream, stored):
    proj_weight, inner_weight, outer_weight, lower_weight = weights
    qv_bias, out_bias, gains, shifts, inner_bias = smalls
    (
        wide_rows,
        projected,
        logsum,
        context,
        normed_one,
        rstd_one,
        middle_wide,
        before,
        hidden,
        normed_two,
        rstd_two,
    ) = stored
    batch, length, local = context.shape
    heads = local // DH
    grad_two, gain_two, shift_two = norm_backward(upstream, normed_two, rstd_two, gains[1])
    grad_branch = gather_grads(grad_two.astype(jnp.bfloat16))
    grad_lower = jnp.einsum("blf,bld->fd", hidden, grad_branch, preferred_element_type=jnp.float32)
    grad_hidden = jnp.einsum(
        "bld,fd->blf", grad_branch, lower_weight, preferred_element_type=jnp.float32
    )
    grad_before = (grad_hidden * gelu_slope(before)).astype(jnp.bfloat16)
    grad_inner = jnp.einsum(
        "bld,blf->df", middle_wide, grad_before, preferred_element_type=jnp.float32
    )
    grad_inner_bias = jnp.sum(grad_before.astype(jnp.float32), axis=(0, 1))
    grad_middle = grad_two + lax.psum_scatter(
        jnp.einsum(
            "blf,df->bld", grad_before, inner_weight, preferred_element_type=jnp.float32
        ).astype(jnp.bfloat16),
        "tensor",
        scatter_dimension=2,
        tiled=True,
    ).astype(jnp.float32)
    grad_one, gain_one, shift_one = norm_backward(grad_middle, normed_one, rstd_one, gains[0])
    grad_attended = gather_grads(grad_one.astype(jnp.bfloat16))
    grad_outer = jnp.einsum(
        "bld,blf->df", context, grad_attended, preferred_element_type=jnp.float32
    )
    grad_context = jnp.einsum(
        "blf,df->bld", grad_attended, outer_weight, preferred_element_type=jnp.float32
    )
    grad_context = grad_context.astype(jnp.bfloat16)
    grad_context = grad_context.reshape(batch, length, heads, DH)
    split = projected.reshape(batch, length, 3, heads, DH)
    query, key_rows, value_rows = (split[:, :, 0], split[:, :, 1], split[:, :, 2])
    probs = jnp.exp(attention_scores(query, key_rows) - logsum[..., None])
    grad_probs = jnp.einsum(
        "bqhe,bkhe->bhqk", grad_context, value_rows, preferred_element_type=jnp.float32
    )
    weighted_sum = jnp.sum(probs * grad_probs, axis=-1, keepdims=True)
    grad_scores = (probs * (grad_probs - weighted_sum)).astype(jnp.bfloat16)
    grad_query = jnp.einsum(
        "bhqk,bkhe->bqhe", grad_scores, key_rows, preferred_element_type=jnp.float32
    ) * DH ** (-0.5)
    grad_key = jnp.einsum(
        "bhqk,bqhe->bkhe", grad_scores, query, preferred_element_type=jnp.float32
    ) * DH ** (-0.5)
    grad_value = jnp.einsum(
        "bhqk,bqhe->bkhe",
        probs.astype(jnp.bfloat16),
        grad_context,
        preferred_element_type=jnp.float32,
    )
    grad_projected = (
        jnp.stack([grad_query, grad_key, grad_value], axis=2)
        .reshape(batch, length, 3, local)
        .astype(jnp.bfloat16)
    )
    grad_proj = jnp.einsum(
        "bld,blcf->dcf", wide_rows, grad_projected, preferred_element_type=jnp.float32
    )
    column_sums = jnp.sum(grad_projected.astype(jnp.float32), axis=(0, 1))
    grad_qv = jnp.stack([column_sums[0], column_sums[2]])
    grad_stacked = grad_one + input_sum(
        jnp.einsum("blcf,dcf->bld", grad_projected, proj_weight, preferred_element_type=jnp.float32)
    )
    grad_biases = jnp.stack([jnp.sum(grad_one, axis=(0, 1)), jnp.sum(grad_two, axis=(0, 1))])
    large_grads = (grad_proj, grad_inner, grad_outer, grad_lower)
    small_grads = (
        grad_qv,
        grad_biases,
        jnp.stack([gain_one, gain_two]),
        jnp.stack([shift_one, shift_two]),
        grad_inner_bias,
    )
    return (grad_stacked, large_grads, small_grads)


def add_tuples(first, second):
    return tuple((left + right for left, right in zip(first, second)))


def shards(
    tokens,
    memory,
    w_qkv,
    b_qv,
    w_out,
    out_biases,
    norm_gains,
    norm_shifts,
    w_in,
    b_in,
    w_down,
    cotangent,
    mlm_mask,
):
    smalls = (
        b_qv.astype(jnp.float32),
        out_biases.astype(jnp.float32),
        norm_gains.astype(jnp.float32),
        norm_shifts.astype(jnp.float32),
        b_in.astype(jnp.float32),
    )
    per_batch = tokens.shape[0] // MICRO
    segments = tokens.shape[1]
    mem_rows = memory.shape[0]
    local = w_qkv.shape[2]
    inner_local = w_in.shape[1]
    empty_large = (
        jnp.zeros((D, 3, local), jnp.float32),
        jnp.zeros((D, inner_local), jnp.float32),
        jnp.zeros((local, D), jnp.float32),
        jnp.zeros((inner_local, D), jnp.float32),
    )
    full_grads = empty_large
    shard_grads = (
        jnp.zeros(w_qkv.shape, jnp.float32),
        jnp.zeros(w_in.shape, jnp.float32),
        jnp.zeros(w_out.shape, jnp.float32),
        jnp.zeros(w_down.shape, jnp.float32),
    )
    small_total = (
        jnp.zeros((2, local), jnp.float32),
        jnp.zeros((2, local), jnp.float32),
        jnp.zeros((2, local), jnp.float32),
        jnp.zeros((2, local), jnp.float32),
        jnp.zeros((inner_local,), jnp.float32),
    )
    memory_total = jnp.zeros((mem_rows, local), jnp.float32)
    out_blocks = []
    grad_blocks = []
    for batch_index in range(MICRO):
        offset = batch_index * per_batch
        batch_tokens = tokens[offset : offset + per_batch]
        batch_mask = mlm_mask[offset : offset + per_batch]
        batch_cot = cotangent[offset : offset + per_batch].astype(jnp.float32) * batch_mask[
            ..., None
        ].astype(jnp.float32)
        weights = fetch_weights(w_qkv, w_in, w_out, w_down)
        carried = memory[None]
        stored_all = []
        token_outs = []
        for seg_index in range(segments):
            layer_out, stored = segment_forward(
                weights, smalls, carried, batch_tokens[:, seg_index]
            )
            carried = layer_out[:, :mem_rows].astype(jnp.bfloat16)
            token_outs.append(layer_out[:, mem_rows:].astype(jnp.bfloat16))
            stored_all.append(stored)
        returning = jnp.zeros((per_batch, mem_rows, local), jnp.float32)
        token_grads = [None] * segments
        for seg_index in reversed(range(segments)):
            upstream = jnp.concatenate([returning, batch_cot[:, seg_index]], axis=1)
            grad_stacked, large_grads, small_grads = segment_backward(
                weights, smalls, upstream, stored_all[seg_index]
            )
            returning = grad_stacked[:, :mem_rows]
            token_grads[seg_index] = grad_stacked[:, mem_rows:]
            full_grads = add_tuples(full_grads, large_grads)
            small_total = add_tuples(small_total, small_grads)
        memory_total = memory_total + jnp.sum(returning, axis=0)
        reduced = reduce_weights(full_grads[0], full_grads[1], full_grads[2], full_grads[3])
        shard_grads = add_tuples(shard_grads, reduced)
        full_grads = empty_large
        out_blocks.append(jnp.stack(token_outs, axis=1))
        grad_blocks.append(jnp.stack(token_grads, axis=1))
    grad_qv, grad_biases, grad_gains, grad_shifts, grad_inner_bias, memory_grad = lax.psum(
        (
            small_total[0],
            small_total[1],
            small_total[2],
            small_total[3],
            small_total[4],
            memory_total,
        ),
        "dp",
    )
    outputs = jnp.concatenate(out_blocks, axis=0)
    input_grad = jnp.concatenate(grad_blocks, axis=0)
    return (
        outputs,
        input_grad,
        memory_grad,
        shard_grads[0],
        grad_qv,
        shard_grads[2],
        grad_biases,
        grad_gains,
        grad_shifts,
        shard_grads[1],
        grad_inner_bias,
        shard_grads[3],
    )


ROWS = 528
LIVE = 176


def dot_nn(left, right):
    return jnp.dot(left, right, preferred_element_type=jnp.float32)


def dot_nt(left, right):
    return lax.dot_general(
        left, right, (((1,), (1,)), ((), ())), preferred_element_type=jnp.float32
    )


def dot_tn(left, right):
    return lax.dot_general(
        left, right, (((0,), (0,)), ((), ())), preferred_element_type=jnp.float32
    )


def norm_rows(resid, gain, shift):
    center = jnp.mean(resid, axis=-1, keepdims=True)
    spread = jnp.mean(resid * resid, axis=-1, keepdims=True) - center * center
    rstd = lax.rsqrt(spread + eps_norm)
    normed = (resid - center) * rstd
    return (normed * gain + shift, normed, rstd)


def norm_rows_back(upstream, normed, rstd, gain):
    scaled = upstream * gain
    first = jnp.mean(scaled, axis=-1, keepdims=True)
    second = jnp.mean(scaled * normed, axis=-1, keepdims=True)
    result = rstd * (scaled - first - normed * second)
    return (result, jnp.sum(upstream * normed, axis=0), jnp.sum(upstream, axis=0))


MESH = pl.DeviceIdType.MESH
HBM = pl.BlockSpec(memory_space=pl.ANY)
VMEM = pl.BlockSpec(memory_space=pltpu.VMEM)
GATHER_PIECES = ((0, 0), (1, 0), (2, 0), (3, 0), (4, 0), (4, 1), (4, 2), (4, 3), (5, 0), (5, 1), (5, 2), (5, 3))
SCATTER_PIECES = ((5, 0), (5, 1), (5, 2), (5, 3), (4, 0), (4, 1), (4, 2), (4, 3), (0, 0), (1, 0), (2, 0), (3, 0))
GATHER_HOPS = (
    (3, 0, 1, 2), (2, 3, 0, 1), (3, 2, 1, 0), (3, 0, 1, 2), (3, 2, 0, 1), (2, 3, 0, 1),
    (2, 3, 0, 1), (3, 1, 2, 0), (3, 2, 1, 0), (2, 3, 1, 0), (1, 0, 3, 2), (2, 0, 1, 3),
)
SCATTER_HOPS = (
    (0, 1, 3, 2), (3, 1, 0, 2), (1, 0, 2, 3), (2, 0, 1, 3), (1, 0, 2, 3), (0, 1, 2, 3),
    (0, 1, 2, 3), (1, 3, 0, 2), (3, 0, 1, 2), (0, 1, 2, 3), (0, 1, 2, 3), (2, 1, 3, 0),
)
GATHER_STEPS = (
    0, 8, 16, 1, 9, 24, 32, 17, 40, 2, 48, 56, 64, 10, 72, 18, 80, 3, 25, 41, 88, 49, 33, 11,
    19, 57, 73, 26, 81, 65, 4, 12, 20, 58, 82, 89, 42, 90, 27, 34, 50, 43, 91, 66, 74, 35,
    59, 51, 44, 67, 83, 60, 75, 28, 68, 36, 76, 52, 84, 92,
)
SCATTER_STEPS = (
    0, 8, 16, 24, 1, 9, 17, 32, 25, 40, 48, 33, 56, 41, 49, 2, 57, 64, 18, 72, 65, 80, 73, 42,
    10, 26, 81, 34, 88, 3, 89, 50, 19, 58, 66, 43, 90, 74, 4, 20, 11, 27, 51, 44, 5, 59, 91,
    21, 52, 82, 45, 75, 28, 35, 92, 76, 53, 83, 36, 67, 29, 12, 77, 84, 68, 60, 13, 37, 93,
    69, 85, 61,
)
SLOTS = 3


def here():
    me = lax.axis_index("dp")
    core = lax.axis_index("tensor")
    bits = tuple((me // (1 << b)) % 2 for b in range(4))
    peers = tuple({"dp": me + (1 - 2 * bits[b]) * (1 << b)} for b in range(4))
    return core, bits, peers + ({"tensor": 1 - core},)


def greet(peers):
    barrier = pltpu.get_barrier_semaphore()
    for peer in peers:
        pl.semaphore_signal(barrier, inc=1, device_id=peer, device_id_type=MESH)
    pl.semaphore_wait(barrier, len(peers))


def block_index(bits, free, flip=None):
    index = []
    for b in (3, 2, 1, 0):
        if b == flip:
            index.append(1 - bits[b])
        elif b in free:
            index.append(slice(None))
        else:
            index.append(bits[b])
    return tuple(index)


def columns(array, part, core, width):
    blocks = 4 if array > 3 else 1
    return pl.ds(pl.multiple_of((core * blocks + part) * width, width), width)


def shard_columns(array, part, width):
    return pl.ds((array if array < 3 else part) * width, width)


def gather_kernel(toks, cots, pack, sq, so, si, sl, x_full, c_full, packs, fq, fk, fv, fo, fi, fl,
                  tok_v, cot_v, send, recv, local, extra):
    core, bits, peers = here()
    width = pack.shape[1]
    shards = (sq, sq, sq, so, si, sl)
    fulls = (fq, fk, fv, fo, fi, fl)
    mine = pl.ds(pl.multiple_of(core * width, width), width)
    stage_in = [
        pltpu.make_async_copy(toks.at[core], tok_v, extra.at[0]),
        pltpu.make_async_copy(cots.at[core], cot_v, extra.at[1]),
    ]
    for copy in stage_in:
        copy.start()
    own = []
    for p, (array, part) in enumerate(GATHER_PIECES):
        own.append(pltpu.make_async_copy(
            shards[array].at[:, shard_columns(array, part, width)],
            fulls[array].at[block_index(bits, ()) + (slice(None), columns(array, part, core, width))],
            local.at[p],
        ))
        own[-1].start()
    greet(peers)

    def remote(src, dst, slot, peer):
        return pltpu.make_async_remote_copy(
            src_ref=src, dst_ref=dst, send_sem=send.at[slot], recv_sem=recv.at[slot],
            device_id=peer, device_id_type=MESH)

    def stage(p, s):
        array, part = GATHER_PIECES[p]
        order = GATHER_HOPS[p]
        cols = columns(array, part, core, width)
        dst = fulls[array].at[block_index(bits, order[:s]) + (slice(None), cols)]
        if s == 0:
            src = shards[array].at[:, shard_columns(array, part, width)]
        else:
            src = dst
        peer = peers[order[s]] if s < 4 else peers[4]
        return remote(src, dst, p * 5 + s, peer)

    swaps = [
        remote(toks.at[1 - core], x_full.at[:, :, mine], 60, peers[4]),
        remote(cots.at[1 - core], c_full.at[:, :, mine], 61, peers[4]),
        remote(pack, packs.at[core], 62, peers[4]),
    ]
    pack_own = pltpu.make_async_copy(pack, packs.at[core], extra.at[4])
    pack_own.start()
    started = {}
    for tick, step in enumerate(GATHER_STEPS):
        p, s = step // 8, step % 8
        if s > 0:
            started[p, s - 1].wait_recv()
        if s == 1:
            own[p].wait()
        started[p, s] = stage(p, s)
        started[p, s].start()
        if tick == 2:
            for swap in swaps:
                swap.start()
            for copy in stage_in:
                copy.wait()
            stage_out = [
                pltpu.make_async_copy(tok_v, x_full.at[:, :, mine], extra.at[2]),
                pltpu.make_async_copy(cot_v, c_full.at[:, :, mine], extra.at[3]),
            ]
            for copy in stage_out:
                copy.start()
    for p in range(len(GATHER_PIECES)):
        started[p, 4].wait_recv()
        for s in range(5):
            started[p, s].wait_send()
    for swap in swaps:
        swap.wait()
    for copy in stage_out:
        copy.wait()
    pack_own.wait()


def gather_all(toks, cots, pack, sq, so, si, sl):
    width = pack.shape[1]
    rows = sq.shape[0]
    low = jnp.bfloat16
    out = [jax.ShapeDtypeStruct(toks.shape[1:3] + (2 * width,), low)] * 2
    out.append(jax.ShapeDtypeStruct((2,) + pack.shape, low))
    for size in [2 * width] * 4 + [2 * si.shape[1], 2 * sl.shape[1]]:
        out.append(jax.ShapeDtypeStruct((2, 2, 2, 2, rows, size), low))
    got = pl.pallas_call(
        gather_kernel,
        out_shape=out,
        in_specs=[HBM, HBM] + [VMEM] * 5,
        out_specs=[HBM] * len(out),
        scratch_shapes=[
            pltpu.VMEM(toks.shape[1:], low),
            pltpu.VMEM(toks.shape[1:], low),
            pltpu.SemaphoreType.DMA((63,)),
            pltpu.SemaphoreType.DMA((63,)),
            pltpu.SemaphoreType.DMA((12,)),
            pltpu.SemaphoreType.DMA((5,)),
        ],
        compiler_params=pltpu.CompilerParams(collective_id=0, has_side_effects=True, vmem_limit_bytes=32 << 20),
        name="gather_all",
    )(toks, cots, pack, sq, so, si, sl)
    wide = [array.reshape(16 * rows, array.shape[-1]) for array in got[3:]]
    return got[0], got[1], got[2], wide


def scatter_kernel(*refs):
    first_rows, second_rows = refs[0:10], refs[10:20]
    small, outs_a, outs_b, grads_a, grads_b = refs[20:25]
    oq, oo, oi, ol, osmall, out_item, grad_item = refs[25:32]
    (acc, first, second, third, fourth, slots, wide_x, wide_s,
     small_in, small_recv, out_v, grad_v, send, recv, extra) = refs[32:]
    core, bits, peers = here()
    width = osmall.shape[1]
    live = second_rows[1].shape[0]
    bufs = (first, second, third, fourth)
    lefts = (0, 0, 0, 4, 6, 8)
    rights = (1, 2, 3, 5, 7, 9)
    turned = set()
    mine = pl.ds(pl.multiple_of(core * width, width), width)
    other = pl.ds(pl.multiple_of((1 - core) * width, width), width)
    small_own = pltpu.make_async_copy(small.at[:, mine], small_in.at[0], extra.at[0])
    small_own.start()
    stage_in = [
        pltpu.make_async_copy(outs_a.at[:, mine], out_v.at[0], extra.at[1]),
        pltpu.make_async_copy(outs_b.at[:, mine], out_v.at[1], extra.at[2]),
        pltpu.make_async_copy(grads_a.at[:, mine], grad_v.at[0], extra.at[3]),
        pltpu.make_async_copy(grads_b.at[:, mine], grad_v.at[1], extra.at[4]),
    ]
    for copy in stage_in:
        copy.start()
    greet(peers)

    def remote(src, dst, slot, peer):
        return pltpu.make_async_remote_copy(
            src_ref=src, dst_ref=dst, send_sem=send.at[slot], recv_sem=recv.at[slot],
            device_id=peer, device_id_type=MESH)

    def turn(array):
        left = lefts[array]
        if left in turned:
            return
        turned.add(left)
        for n, rows in enumerate((first_rows, second_rows)):
            if left == 0:
                wide_x[n] = rows[0][...].T
            else:
                wide_s[left // 2 - 2, n] = rows[left][...].T

    def multiply(array, offset, size):
        total = None
        for n, rows in enumerate((first_rows, second_rows)):
            right = rows[rights[array]][:, pl.ds(offset, size)]
            if array in (1, 2):
                left = wide_x[n]
            elif array == 0:
                left = wide_x[n, :, :live]
            else:
                left = wide_s[lefts[array] // 2 - 2, n]
            term = jnp.dot(left, right, preferred_element_type=jnp.float32)
            total = term if total is None else total + term
        return total

    tile = width // 2

    def produce(p, slot):
        array, part = SCATTER_PIECES[p]
        turn(array)
        blocks = 4 if array > 3 else 1
        base = ((1 - core) * blocks + part) * width

        def body(n, carry):
            offset = pl.multiple_of(base + n * tile, tile)
            got = multiply(array, offset, tile).astype(jnp.bfloat16)
            slots[slot, :, :, :, :, :, pl.ds(pl.multiple_of(n * tile, tile), tile)] = got.reshape(
                slots.shape[1:6] + (tile,)
            )
            return carry

        lax.fori_loop(0, 2, body, 0)

    def combine(p):
        array, part = SCATTER_PIECES[p]
        blocks = 4 if array > 3 else 1
        base = (core * blocks + part) * width

        def body(n, carry):
            offset = pl.multiple_of(base + n * tile, tile)
            cols = pl.ds(pl.multiple_of(n * tile, tile), tile)
            got = multiply(array, offset, tile).reshape(slots.shape[1:6] + (tile,))
            acc[p, :, :, :, :, :, cols] = (
                got + acc[p, :, :, :, :, :, cols].astype(jnp.float32)
            ).astype(jnp.bfloat16)
            return carry

        lax.fori_loop(0, 2, body, 0)

    def stage(p, s):
        if s == 0:
            return remote(slots.at[p % SLOTS], acc.at[p], p * 5, peers[4])
        order = SCATTER_HOPS[p]
        src = acc.at[(p,) + block_index(bits, order[s:], flip=order[s - 1])]
        return remote(src, bufs[s - 1].at[p], p * 5 + s, peers[order[s - 1]])

    def fold(p, s):
        array, part = SCATTER_PIECES[p]
        order = SCATTER_HOPS[p]
        free = [b for b in (3, 2, 1, 0) if b in order[s:]]
        for n in range(1 << len(free)):
            at = {b: (n >> i) % 2 for i, b in enumerate(reversed(free))}
            where = tuple(at.get(b, bits[b]) for b in (3, 2, 1, 0))
            got = bufs[s - 1][(p,) + tuple(at[b] for b in free)]
            if s < 4:
                acc[(p,) + where] = acc[(p,) + where] + got
            else:
                total = acc[(p,) + where].astype(jnp.float32) + got.astype(jnp.float32)
                if array < 3:
                    oq[:, array] = total
                elif array == 4:
                    oi[:, pl.ds(part * width, width)] = total
                elif array == 3:
                    oo[...] = total.T
                else:
                    ol[pl.ds(part * width, width), :] = total.T

    small_started = {}

    def small_stage(s):
        peer = peers[4] if s == 0 else peers[s - 1]
        src = small.at[:, other] if s == 0 else small_in.at[s]
        return remote(src, small_recv.at[s], 60 + s, peer)

    swaps = [
        remote(outs_a.at[:, other], out_item.at[core, 0], 65, peers[4]),
        remote(outs_b.at[:, other], out_item.at[core, 1], 66, peers[4]),
        remote(grads_a.at[:, other], grad_item.at[core, 0], 67, peers[4]),
        remote(grads_b.at[:, other], grad_item.at[core, 1], 68, peers[4]),
    ]
    started = {}
    for tick, step in enumerate(SCATTER_STEPS):
        p, s = step // 8, step % 8
        if s == 0:
            if p >= SLOTS:
                started[p - SLOTS, 0].wait_send()
            produce(p, p % SLOTS)
        else:
            started[p, s - 1].wait_recv()
            if s == 1:
                combine(p)
            else:
                fold(p, s - 1)
        if s < 5:
            started[p, s] = stage(p, s)
            started[p, s].start()
        if tick % 6 == 5 and tick < 36:
            n = tick // 6
            if n == 0:
                small_own.wait()
            else:
                small_started[n - 1].wait_recv()
                total = small_in[n - 1] + small_recv[n - 1]
                if n < 5:
                    small_in[n] = total
                else:
                    osmall[...] = total
            if n < 5:
                small_started[n] = small_stage(n)
                small_started[n].start()
        if tick == 30:
            for swap in swaps:
                swap.start()
            for copy in stage_in:
                copy.wait()
            stage_out = [
                pltpu.make_async_copy(out_v, out_item.at[core], extra.at[5]),
                pltpu.make_async_copy(grad_v, grad_item.at[core], extra.at[6]),
            ]
            for copy in stage_out:
                copy.start()
    for (p, s), copy in started.items():
        if s > 0 or p >= len(SCATTER_PIECES) - SLOTS:
            copy.wait_send()
    for s in range(5):
        small_started[s].wait_send()
    for swap in swaps:
        swap.wait()
    for copy in stage_out:
        copy.wait()


def scatter_all(first_rows, second_rows, small, outs, grads):
    width = small.shape[1] // 2
    rows = 2 * width // 16
    low, full = jnp.bfloat16, jnp.float32
    count = len(SCATTER_PIECES)
    item = (2, 2) + outs[0].shape[:1] + (width,)
    long, live = first_rows[0].shape[0], first_rows[1].shape[0]
    return pl.pallas_call(
        scatter_kernel,
        out_shape=[
            jax.ShapeDtypeStruct((rows, 3, width), full),
            jax.ShapeDtypeStruct((width, rows), full),
            jax.ShapeDtypeStruct((rows, 4 * width), full),
            jax.ShapeDtypeStruct((4 * width, rows), full),
            jax.ShapeDtypeStruct((small.shape[0], width), full),
            jax.ShapeDtypeStruct(item, low),
            jax.ShapeDtypeStruct(item, low),
        ],
        in_specs=[VMEM] * 20 + [HBM] * 5,
        out_specs=[VMEM] * 5 + [HBM] * 2,
        scratch_shapes=[
            pltpu.VMEM((count, 2, 2, 2, 2, rows, width), low),
            pltpu.VMEM((count, 2, 2, 2, rows, width), low),
            pltpu.VMEM((count, 2, 2, rows, width), low),
            pltpu.VMEM((count, 2, rows, width), low),
            pltpu.VMEM((count, rows, width), low),
            pltpu.VMEM((SLOTS, 2, 2, 2, 2, rows, width), low),
            pltpu.VMEM((2, 2 * width, long), low),
            pltpu.VMEM((3, 2, 2 * width, live), low),
            pltpu.VMEM((5, small.shape[0], width), full),
            pltpu.VMEM((5, small.shape[0], width), full),
            pltpu.VMEM(item[1:], low),
            pltpu.VMEM(item[1:], low),
            pltpu.SemaphoreType.DMA((69,)),
            pltpu.SemaphoreType.DMA((69,)),
            pltpu.SemaphoreType.DMA((7,)),
        ],
        compiler_params=pltpu.CompilerParams(collective_id=1, has_side_effects=True, vmem_limit_bytes=63 << 20),
        name="scatter_all",
    )(*first_rows, *second_rows, small, *outs, *grads)


def attend_kernel(valid, q_ref, k_ref, v_ref, out_ref):
    query, key_rows, value_rows = q_ref[...], k_ref[...], v_ref[...]
    group = lax.broadcasted_iota(jnp.int32, query.shape, 1) // DH
    zero = jnp.zeros_like(query)
    result = None
    for head in range(query.shape[1] // DH):
        picked = jnp.where(group == head, query * DH ** (-0.5), zero)
        scores = dot_nt(picked, key_rows)
        scores = jnp.where(lax.broadcasted_iota(jnp.int32, scores.shape, 1) < valid, scores, -1e30)
        expo = jnp.exp(scores - jnp.max(scores, axis=1, keepdims=True))
        total = jnp.sum(expo, axis=1, keepdims=True)
        context = dot_nn(expo.astype(jnp.bfloat16), value_rows) / total
        result = context if result is None else jnp.where(group == head, context, result)
    out_ref[...] = result.astype(jnp.bfloat16)


def attend(query, key_rows, value_rows, valid):
    block = pl.BlockSpec((query.shape[0], 2 * DH), lambda i: (0, i))
    return pl.pallas_call(
        functools.partial(attend_kernel, valid),
        grid=(D // (2 * DH),),
        out_shape=jax.ShapeDtypeStruct(query.shape, jnp.bfloat16),
        in_specs=[block] * 3,
        out_specs=block,
        compiler_params=pltpu.CompilerParams(vmem_limit_bytes=32 << 20),
        name="attend",
    )(query, key_rows, value_rows)


def attend_back_kernel(valid, q_ref, k_ref, v_ref, g_ref, dq_ref, dk_ref, dv_ref):
    query, key_rows, value_rows, grads = q_ref[...], k_ref[...], v_ref[...], g_ref[...]
    group = lax.broadcasted_iota(jnp.int32, query.shape, 1) // DH
    zero = jnp.zeros_like(query)
    grad_query = grad_key = grad_value = None
    for head in range(query.shape[1] // DH):
        picked = jnp.where(group == head, query * DH ** (-0.5), zero)
        up = jnp.where(group == head, grads, zero)
        scores = dot_nt(key_rows, picked)
        scores = jnp.where(lax.broadcasted_iota(jnp.int32, scores.shape, 0) < valid, scores, -1e30)
        expo = jnp.exp(scores - jnp.max(scores, axis=0, keepdims=True))
        probs = expo / jnp.sum(expo, axis=0, keepdims=True)
        grad_probs = dot_nt(value_rows, up)
        weighted = jnp.sum(probs * grad_probs, axis=0, keepdims=True)
        grad_scores = (probs * (grad_probs - weighted)).astype(jnp.bfloat16)
        dq = dot_tn(grad_scores, key_rows)
        dk = dot_nn(grad_scores, picked)
        dv = dot_nn(probs.astype(jnp.bfloat16), up)
        if head == 0:
            grad_query, grad_key, grad_value = dq, dk, dv
        else:
            grad_query = jnp.where(group == head, dq, grad_query)
            grad_key = grad_key + dk
            grad_value = grad_value + dv
    dq_ref[...] = (grad_query * DH ** (-0.5)).astype(jnp.bfloat16)
    dk_ref[...] = grad_key.astype(jnp.bfloat16)
    dv_ref[...] = grad_value.astype(jnp.bfloat16)


def attend_back(query, key_rows, value_rows, grad_context, valid):
    live = grad_context.shape[0]
    short = pl.BlockSpec((live, 2 * DH), lambda i: (0, i))
    tall = pl.BlockSpec((key_rows.shape[0], 2 * DH), lambda i: (0, i))
    low = jnp.bfloat16
    return pl.pallas_call(
        functools.partial(attend_back_kernel, valid),
        grid=(D // (2 * DH),),
        out_shape=[jax.ShapeDtypeStruct((live, D), low)] + [jax.ShapeDtypeStruct(key_rows.shape, low)] * 2,
        in_specs=[short, tall, tall, short],
        out_specs=[short, tall, tall],
        compiler_params=pltpu.CompilerParams(vmem_limit_bytes=32 << 20),
        name="attend_back",
    )(query, key_rows, value_rows, grad_context)


def item_shards(
    tokens,
    memory,
    w_qkv,
    b_qv,
    w_out,
    out_biases,
    norm_gains,
    norm_shifts,
    w_in,
    b_in,
    w_down,
    cotangent,
    mlm_mask,
):
    core = lax.axis_index("tensor")
    segments, count = tokens.shape[1], tokens.shape[2]
    mem_rows = memory.shape[0]
    valid = mem_rows + count
    half = memory.shape[1]

    mask = lax.dynamic_index_in_dim(mlm_mask, core, 0, keepdims=False)
    packed = jnp.concatenate(
        [b_qv, out_biases, norm_gains, norm_shifts, b_in.reshape(-1, half), memory], axis=0
    )
    packed = jnp.pad(packed, ((0, -packed.shape[0] % 16), (0, 0)))
    rows_in, cots_in, both, (wq, wk, wv, outer, inner, lower) = gather_all(
        tokens, cotangent, packed, w_qkv.reshape(w_qkv.shape[0], -1), w_out.T, w_in, w_down.T
    )
    wide = jnp.concatenate([both[0], both[1]], axis=1)
    qv_bias, out_bias, gains, shifts = (wide[2 * i : 2 * i + 2].astype(jnp.float32) for i in range(4))
    inner_rows = b_in.shape[0] // half
    inner_bias = both[:, 8 : 8 + inner_rows].reshape(-1).astype(jnp.float32)
    start_memory = wide[8 + inner_rows : 8 + inner_rows + mem_rows]

    lower_tri = (
        lax.broadcasted_iota(jnp.int32, (count, count), 0)
        <= lax.broadcasted_iota(jnp.int32, (count, count), 1)
    ).astype(jnp.bfloat16)
    ones = mask.astype(jnp.bfloat16)
    upto = dot_nn(ones, lower_tri).astype(jnp.int32)
    total = upto[:, -1:]
    index = lax.broadcasted_iota(jnp.int32, mask.shape, 1)
    place = mem_rows + jnp.where(mask > 0, upto - 1, total + index - upto)
    move = (
        lax.broadcasted_iota(jnp.int32, (segments, ROWS, count), 1) == place[:, None, :]
    ).astype(jnp.bfloat16)
    live_move = move[:, :LIVE] * ones[:, None, :]

    carried = start_memory
    stored = []
    outs = []
    for seg in range(segments):
        moved = dot_nn(move[seg], rows_in[seg]).astype(jnp.bfloat16)
        stacked = jnp.concatenate([carried, moved[mem_rows:]], axis=0)
        query = (dot_nn(stacked, wq) + qv_bias[0]).astype(jnp.bfloat16)
        key_rows = dot_nn(stacked, wk).astype(jnp.bfloat16)
        value_rows = (dot_nn(stacked, wv) + qv_bias[1]).astype(jnp.bfloat16)
        context = attend(query, key_rows, value_rows, valid)
        attended = dot_nt(context, outer)
        middle, normed_one, rstd_one = norm_rows(
            stacked.astype(jnp.float32) + attended + out_bias[0], gains[0], shifts[0]
        )
        middle_low = middle.astype(jnp.bfloat16)
        before = dot_nn(middle_low, inner) + inner_bias
        hidden = gelu_value(before).astype(jnp.bfloat16)
        branch = dot_nt(hidden, lower)
        layer_out, normed_two, rstd_two = norm_rows(
            middle + branch + out_bias[1], gains[1], shifts[1]
        )
        low_out = layer_out.astype(jnp.bfloat16)
        carried = low_out[:mem_rows]
        outs.append(dot_tn(move[seg], low_out).astype(jnp.bfloat16))
        stored.append(
            (
                stacked,
                query,
                key_rows,
                value_rows,
                context[:LIVE],
                normed_one[:LIVE],
                rstd_one[:LIVE],
                middle_low[:LIVE],
                before[:LIVE],
                hidden[:LIVE],
                normed_two[:LIVE],
                rstd_two[:LIVE],
            )
        )

    returning = jnp.zeros((mem_rows, D), jnp.float32)
    token_grads = [None] * segments
    pieces = [None] * segments
    smalls = None
    for seg in reversed(range(segments)):
        (
            stacked,
            query,
            key_rows,
            value_rows,
            context,
            normed_one,
            rstd_one,
            middle_low,
            before,
            hidden,
            normed_two,
            rstd_two,
        ) = stored[seg]
        upstream = dot_nn(live_move[seg], cots_in[seg])
        upstream = upstream + jnp.pad(returning, ((0, LIVE - mem_rows), (0, 0)))
        grad_two, gain_two, shift_two = norm_rows_back(upstream, normed_two, rstd_two, gains[1])
        grad_branch = grad_two.astype(jnp.bfloat16)
        grad_hidden = dot_nn(grad_branch, lower)
        grad_before = (grad_hidden * gelu_slope(before)).astype(jnp.bfloat16)
        grad_middle = grad_two + dot_nt(grad_before, inner)
        grad_one, gain_one, shift_one = norm_rows_back(
            grad_middle, normed_one, rstd_one, gains[0]
        )
        grad_attended = grad_one.astype(jnp.bfloat16)
        grad_context = dot_nn(grad_attended, outer).astype(jnp.bfloat16)
        grad_query, grad_key, grad_value = attend_back(
            query, key_rows, value_rows, grad_context, valid
        )
        grad_stacked = dot_nt(grad_key, wk) + dot_nt(grad_value, wv)
        live_part = grad_one + dot_nt(grad_query, wq)
        grad_stacked = grad_stacked + jnp.pad(live_part, ((0, ROWS - LIVE), (0, 0)))
        returning = grad_stacked[:mem_rows]
        token_grads[seg] = dot_tn(move[seg], grad_stacked.astype(jnp.bfloat16)).astype(
            jnp.bfloat16
        )
        pieces[seg] = (
            stacked,
            grad_query,
            grad_key,
            grad_value,
            grad_attended,
            context,
            middle_low,
            grad_before,
            grad_branch,
            hidden,
        )
        sums = jnp.concatenate(
            [
                jnp.stack(
                    [
                        jnp.sum(grad_query.astype(jnp.float32), axis=0),
                        jnp.sum(grad_value.astype(jnp.float32), axis=0),
                        jnp.sum(grad_one, axis=0),
                        jnp.sum(grad_two, axis=0),
                        gain_one,
                        gain_two,
                        shift_one,
                        shift_two,
                    ]
                ),
                jnp.sum(grad_before.astype(jnp.float32), axis=0).reshape(-1, D),
            ],
            axis=0,
        )
        smalls = sums if smalls is None else smalls + sums

    inner_sums = smalls[8:].reshape(2, inner_rows, half).transpose(1, 0, 2).reshape(inner_rows, D)
    small = jnp.concatenate([smalls[:8], inner_sums, returning], axis=0)
    small = jnp.pad(small, ((0, -small.shape[0] % 8), (0, 0)))
    grad_proj, grad_outer, grad_inner, grad_lower, mine, outputs, input_grad = scatter_all(
        pieces[0], pieces[1], small, outs, token_grads
    )
    inner_sum = mine[8 : 8 + inner_rows].reshape(-1)
    return (
        outputs,
        input_grad.astype(jnp.float32),
        mine[8 + inner_rows : 8 + inner_rows + mem_rows],
        grad_proj,
        mine[0:2],
        grad_outer,
        mine[2:4],
        mine[4:6],
        mine[6:8],
        grad_inner,
        inner_sum,
        grad_lower,
    )


def solution(mesh):
    def body(*arrays):
        if mesh.shape["dp"] == 16 and mesh.shape["tensor"] == arrays[0].shape[0] == 2:
            return item_shards(*arrays)
        return shards(*arrays)

    placed = (
        P("dp", None, None, "tensor"),
        P(None, "tensor"),
        P("dp", None, "tensor"),
        P(None, "tensor"),
        P("tensor", "dp"),
        P(None, "tensor"),
        P(None, "tensor"),
        P(None, "tensor"),
        P("dp", "tensor"),
        P("tensor"),
        P("tensor", "dp"),
        P("dp", None, None, "tensor"),
        P("dp", None, None),
    )
    return jax.shard_map(
        body,
        mesh=mesh,
        in_specs=placed,
        out_specs=(
            P("dp", None, None, "tensor"),
            P("dp", None, None, "tensor"),
            P(None, "tensor"),
            P("dp", None, "tensor"),
            P(None, "tensor"),
            P("tensor", "dp"),
            P(None, "tensor"),
            P(None, "tensor"),
            P(None, "tensor"),
            P("dp", "tensor"),
            P("tensor"),
            P("tensor", "dp"),
        ),
        check_vma=False,
    )
```

```python
import functools

import jax
import jax.numpy as jnp
from jax import lax
from jax.experimental import pallas as pl
from jax.experimental.pallas import tpu as pltpu
from jax.sharding import PartitionSpec as P

D = 1024
DH = 64
MICRO = 2


eps_norm = 1e-05
root_half = 0.7071067811865476
inv_root_two_pi = 0.3989422804014327


def gelu_value(before):
    return 0.5 * before * (1.0 + lax.erf(before * root_half))


def gelu_slope(before):
    return 0.5 * (1.0 + lax.erf(before * root_half)) + before * inv_root_two_pi * jnp.exp(
        -0.5 * before * before
    )


def fetch_weights(w_qkv, w_in, w_out, w_down):
    return (
        lax.all_gather(w_qkv, "dp", axis=0, tiled=True),
        lax.all_gather(w_in, "dp", axis=0, tiled=True),
        lax.all_gather(w_out, "dp", axis=1, tiled=True),
        lax.all_gather(w_down, "dp", axis=1, tiled=True),
    )


def reduce_weights(grad_proj, grad_inner, grad_outer, grad_lower):
    return (
        lax.psum_scatter(
            grad_proj.astype(jnp.bfloat16), "dp", scatter_dimension=0, tiled=True
        ).astype(jnp.float32),
        lax.psum_scatter(
            grad_inner.astype(jnp.bfloat16), "dp", scatter_dimension=0, tiled=True
        ).astype(jnp.float32),
        lax.psum_scatter(
            grad_outer.astype(jnp.bfloat16), "dp", scatter_dimension=1, tiled=True
        ).astype(jnp.float32),
        lax.psum_scatter(
            grad_lower.astype(jnp.bfloat16), "dp", scatter_dimension=1, tiled=True
        ).astype(jnp.float32),
    )


def gather_rows(block):
    return lax.all_gather(block, "tensor", axis=2, tiled=True)


def branch_sum(partial_value):
    return lax.psum_scatter(partial_value, "tensor", scatter_dimension=2, tiled=True)


def gather_grads(block):
    return lax.all_gather(block, "tensor", axis=2, tiled=True)


def input_sum(partial_value):
    return lax.psum_scatter(
        partial_value.astype(jnp.bfloat16), "tensor", scatter_dimension=2, tiled=True
    ).astype(jnp.float32)


def norm_forward(resid, gain, shift):
    totals = jnp.sum(resid, axis=-1)
    squares = jnp.sum(resid * resid, axis=-1)
    totals, squares = lax.psum((totals, squares), "tensor")
    center = totals / D
    spread = squares / D - center * center
    rstd = lax.rsqrt(spread + eps_norm)
    normed = (resid - center[..., None]) * rstd[..., None]
    return (normed * gain + shift, normed, rstd)


def norm_backward(upstream, normed, rstd, gain):
    scaled = upstream * gain
    first = jnp.sum(scaled, axis=-1)
    second = jnp.sum(scaled * normed, axis=-1)
    first, second = lax.psum((first, second), "tensor")
    result = rstd[..., None] * (scaled - first[..., None] / D - normed * (second[..., None] / D))
    return (result, jnp.sum(upstream * normed, axis=(0, 1)), jnp.sum(upstream, axis=(0, 1)))


def attention_scores(query, key_rows):
    return jnp.einsum(
        "bqhe,bkhe->bhqk", query, key_rows, preferred_element_type=jnp.float32
    ) * DH ** (-0.5)


def segment_forward(weights, smalls, memory_rows, token_rows):
    proj_weight, inner_weight, outer_weight, lower_weight = weights
    qv_bias, out_bias, gains, shifts, inner_bias = smalls
    batch = token_rows.shape[0]
    stacked = jnp.concatenate([memory_rows, token_rows], axis=1)
    length = stacked.shape[1]
    local = proj_weight.shape[2]
    heads = local // DH
    wide_rows = gather_rows(stacked)
    bias_three = jnp.stack([qv_bias[0], jnp.zeros_like(qv_bias[0]), qv_bias[1]])
    projected = (
        jnp.einsum("bld,dcf->blcf", wide_rows, proj_weight, preferred_element_type=jnp.float32)
        + bias_three
    ).astype(jnp.bfloat16)
    split = projected.reshape(batch, length, 3, heads, DH)
    scores = attention_scores(split[:, :, 0], split[:, :, 1])
    peak = jnp.max(scores, axis=-1, keepdims=True)
    expo = jnp.exp(scores - peak)
    totals = jnp.sum(expo, axis=-1, keepdims=True)
    probs = expo / totals
    logsum = peak[..., 0] + jnp.log(totals[..., 0])
    context = jnp.einsum(
        "bhqk,bkhe->bqhe",
        probs.astype(jnp.bfloat16),
        split[:, :, 2],
        preferred_element_type=jnp.float32,
    )
    context = context.astype(jnp.bfloat16).reshape(batch, length, local)
    attended = branch_sum(
        jnp.einsum("bld,df->blf", context, outer_weight, preferred_element_type=jnp.float32)
    )
    middle, normed_one, rstd_one = norm_forward(
        stacked.astype(jnp.float32) + attended + out_bias[0], gains[0], shifts[0]
    )
    middle_wide = gather_rows(middle.astype(jnp.bfloat16))
    before = (
        jnp.einsum("bld,df->blf", middle_wide, inner_weight, preferred_element_type=jnp.float32)
        + inner_bias
    )
    hidden = gelu_value(before).astype(jnp.bfloat16)
    branch = branch_sum(
        jnp.einsum("blf,fd->bld", hidden, lower_weight, preferred_element_type=jnp.float32)
    )
    layer_out, normed_two, rstd_two = norm_forward(
        middle + branch + out_bias[1], gains[1], shifts[1]
    )
    stored = (
        wide_rows,
        projected,
        logsum,
        context,
        normed_one,
        rstd_one,
        middle_wide,
        before,
        hidden,
        normed_two,
        rstd_two,
    )
    return (layer_out, stored)


def segment_backward(weights, smalls, upstream, stored):
    proj_weight, inner_weight, outer_weight, lower_weight = weights
    qv_bias, out_bias, gains, shifts, inner_bias = smalls
    (
        wide_rows,
        projected,
        logsum,
        context,
        normed_one,
        rstd_one,
        middle_wide,
        before,
        hidden,
        normed_two,
        rstd_two,
    ) = stored
    batch, length, local = context.shape
    heads = local // DH
    grad_two, gain_two, shift_two = norm_backward(upstream, normed_two, rstd_two, gains[1])
    grad_branch = gather_grads(grad_two.astype(jnp.bfloat16))
    grad_lower = jnp.einsum("blf,bld->fd", hidden, grad_branch, preferred_element_type=jnp.float32)
    grad_hidden = jnp.einsum(
        "bld,fd->blf", grad_branch, lower_weight, preferred_element_type=jnp.float32
    )
    grad_before = (grad_hidden * gelu_slope(before)).astype(jnp.bfloat16)
    grad_inner = jnp.einsum(
        "bld,blf->df", middle_wide, grad_before, preferred_element_type=jnp.float32
    )
    grad_inner_bias = jnp.sum(grad_before.astype(jnp.float32), axis=(0, 1))
    grad_middle = grad_two + lax.psum_scatter(
        jnp.einsum(
            "blf,df->bld", grad_before, inner_weight, preferred_element_type=jnp.float32
        ).astype(jnp.bfloat16),
        "tensor",
        scatter_dimension=2,
        tiled=True,
    ).astype(jnp.float32)
    grad_one, gain_one, shift_one = norm_backward(grad_middle, normed_one, rstd_one, gains[0])
    grad_attended = gather_grads(grad_one.astype(jnp.bfloat16))
    grad_outer = jnp.einsum(
        "bld,blf->df", context, grad_attended, preferred_element_type=jnp.float32
    )
    grad_context = jnp.einsum(
        "blf,df->bld", grad_attended, outer_weight, preferred_element_type=jnp.float32
    )
    grad_context = grad_context.astype(jnp.bfloat16)
    grad_context = grad_context.reshape(batch, length, heads, DH)
    split = projected.reshape(batch, length, 3, heads, DH)
    query, key_rows, value_rows = (split[:, :, 0], split[:, :, 1], split[:, :, 2])
    probs = jnp.exp(attention_scores(query, key_rows) - logsum[..., None])
    grad_probs = jnp.einsum(
        "bqhe,bkhe->bhqk", grad_context, value_rows, preferred_element_type=jnp.float32
    )
    weighted_sum = jnp.sum(probs * grad_probs, axis=-1, keepdims=True)
    grad_scores = (probs * (grad_probs - weighted_sum)).astype(jnp.bfloat16)
    grad_query = jnp.einsum(
        "bhqk,bkhe->bqhe", grad_scores, key_rows, preferred_element_type=jnp.float32
    ) * DH ** (-0.5)
    grad_key = jnp.einsum(
        "bhqk,bqhe->bkhe", grad_scores, query, preferred_element_type=jnp.float32
    ) * DH ** (-0.5)
    grad_value = jnp.einsum(
        "bhqk,bqhe->bkhe",
        probs.astype(jnp.bfloat16),
        grad_context,
        preferred_element_type=jnp.float32,
    )
    grad_projected = (
        jnp.stack([grad_query, grad_key, grad_value], axis=2)
        .reshape(batch, length, 3, local)
        .astype(jnp.bfloat16)
    )
    grad_proj = jnp.einsum(
        "bld,blcf->dcf", wide_rows, grad_projected, preferred_element_type=jnp.float32
    )
    column_sums = jnp.sum(grad_projected.astype(jnp.float32), axis=(0, 1))
    grad_qv = jnp.stack([column_sums[0], column_sums[2]])
    grad_stacked = grad_one + input_sum(
        jnp.einsum("blcf,dcf->bld", grad_projected, proj_weight, preferred_element_type=jnp.float32)
    )
    grad_biases = jnp.stack([jnp.sum(grad_one, axis=(0, 1)), jnp.sum(grad_two, axis=(0, 1))])
    large_grads = (grad_proj, grad_inner, grad_outer, grad_lower)
    small_grads = (
        grad_qv,
        grad_biases,
        jnp.stack([gain_one, gain_two]),
        jnp.stack([shift_one, shift_two]),
        grad_inner_bias,
    )
    return (grad_stacked, large_grads, small_grads)


def add_tuples(first, second):
    return tuple((left + right for left, right in zip(first, second)))


def shards(
    tokens,
    memory,
    w_qkv,
    b_qv,
    w_out,
    out_biases,
    norm_gains,
    norm_shifts,
    w_in,
    b_in,
    w_down,
    cotangent,
    mlm_mask,
):
    smalls = (
        b_qv.astype(jnp.float32),
        out_biases.astype(jnp.float32),
        norm_gains.astype(jnp.float32),
        norm_shifts.astype(jnp.float32),
        b_in.astype(jnp.float32),
    )
    per_batch = tokens.shape[0] // MICRO
    segments = tokens.shape[1]
    mem_rows = memory.shape[0]
    local = w_qkv.shape[2]
    inner_local = w_in.shape[1]
    empty_large = (
        jnp.zeros((D, 3, local), jnp.float32),
        jnp.zeros((D, inner_local), jnp.float32),
        jnp.zeros((local, D), jnp.float32),
        jnp.zeros((inner_local, D), jnp.float32),
    )
    full_grads = empty_large
    shard_grads = (
        jnp.zeros(w_qkv.shape, jnp.float32),
        jnp.zeros(w_in.shape, jnp.float32),
        jnp.zeros(w_out.shape, jnp.float32),
        jnp.zeros(w_down.shape, jnp.float32),
    )
    small_total = (
        jnp.zeros((2, local), jnp.float32),
        jnp.zeros((2, local), jnp.float32),
        jnp.zeros((2, local), jnp.float32),
        jnp.zeros((2, local), jnp.float32),
        jnp.zeros((inner_local,), jnp.float32),
    )
    memory_total = jnp.zeros((mem_rows, local), jnp.float32)
    out_blocks = []
    grad_blocks = []
    for batch_index in range(MICRO):
        offset = batch_index * per_batch
        batch_tokens = tokens[offset : offset + per_batch]
        batch_mask = mlm_mask[offset : offset + per_batch]
        batch_cot = cotangent[offset : offset + per_batch].astype(jnp.float32) * batch_mask[
            ..., None
        ].astype(jnp.float32)
        weights = fetch_weights(w_qkv, w_in, w_out, w_down)
        carried = memory[None]
        stored_all = []
        token_outs = []
        for seg_index in range(segments):
            layer_out, stored = segment_forward(
                weights, smalls, carried, batch_tokens[:, seg_index]
            )
            carried = layer_out[:, :mem_rows].astype(jnp.bfloat16)
            token_outs.append(layer_out[:, mem_rows:].astype(jnp.bfloat16))
            stored_all.append(stored)
        returning = jnp.zeros((per_batch, mem_rows, local), jnp.float32)
        token_grads = [None] * segments
        for seg_index in reversed(range(segments)):
            upstream = jnp.concatenate([returning, batch_cot[:, seg_index]], axis=1)
            grad_stacked, large_grads, small_grads = segment_backward(
                weights, smalls, upstream, stored_all[seg_index]
            )
            returning = grad_stacked[:, :mem_rows]
            token_grads[seg_index] = grad_stacked[:, mem_rows:]
            full_grads = add_tuples(full_grads, large_grads)
            small_total = add_tuples(small_total, small_grads)
        memory_total = memory_total + jnp.sum(returning, axis=0)
        reduced = reduce_weights(full_grads[0], full_grads[1], full_grads[2], full_grads[3])
        shard_grads = add_tuples(shard_grads, reduced)
        full_grads = empty_large
        out_blocks.append(jnp.stack(token_outs, axis=1))
        grad_blocks.append(jnp.stack(token_grads, axis=1))
    grad_qv, grad_biases, grad_gains, grad_shifts, grad_inner_bias, memory_grad = lax.psum(
        (
            small_total[0],
            small_total[1],
            small_total[2],
            small_total[3],
            small_total[4],
            memory_total,
        ),
        "dp",
    )
    outputs = jnp.concatenate(out_blocks, axis=0)
    input_grad = jnp.concatenate(grad_blocks, axis=0)
    return (
        outputs,
        input_grad,
        memory_grad,
        shard_grads[0],
        grad_qv,
        shard_grads[2],
        grad_biases,
        grad_gains,
        grad_shifts,
        shard_grads[1],
        grad_inner_bias,
        shard_grads[3],
    )


ROWS = 528
LIVE = 176


def dot_nn(left, right):
    return jnp.dot(left, right, preferred_element_type=jnp.float32)


def dot_nt(left, right):
    return lax.dot_general(
        left, right, (((1,), (1,)), ((), ())), preferred_element_type=jnp.float32
    )


def dot_tn(left, right):
    return lax.dot_general(
        left, right, (((0,), (0,)), ((), ())), preferred_element_type=jnp.float32
    )


def norm_rows(resid, gain, shift):
    center = jnp.mean(resid, axis=-1, keepdims=True)
    spread = jnp.mean(resid * resid, axis=-1, keepdims=True) - center * center
    rstd = lax.rsqrt(spread + eps_norm)
    normed = (resid - center) * rstd
    return (normed * gain + shift, normed, rstd)


def norm_rows_back(upstream, normed, rstd, gain):
    scaled = upstream * gain
    first = jnp.mean(scaled, axis=-1, keepdims=True)
    second = jnp.mean(scaled * normed, axis=-1, keepdims=True)
    result = rstd * (scaled - first - normed * second)
    return (result, jnp.sum(upstream * normed, axis=0), jnp.sum(upstream, axis=0))


MESH = pl.DeviceIdType.MESH
HBM = pl.BlockSpec(memory_space=pl.ANY)
VMEM = pl.BlockSpec(memory_space=pltpu.VMEM)
GATHER_PIECES = ((0, 0), (1, 0), (2, 0), (3, 0), (4, 0), (5, 0), (4, 1), (5, 1), (4, 2), (5, 2), (4, 3), (5, 3))
SCATTER_PIECES = ((5, 0), (5, 1), (5, 2), (5, 3), (4, 0), (4, 1), (4, 2), (4, 3), (0, 0), (1, 0), (2, 0), (3, 0))
GATHER_HOPS = (
    (3, 2, 1, 0), (3, 0, 2, 1), (3, 2, 0, 1), (0, 3, 1, 2), (2, 3, 1, 0), (2, 1, 3, 0),
    (2, 3, 0, 1), (1, 3, 2, 0), (3, 0, 1, 2), (3, 0, 2, 1), (2, 1, 3, 0), (3, 0, 1, 2),
)
SCATTER_HOPS = (
    (0, 1, 3, 2), (3, 1, 0, 2), (1, 0, 2, 3), (2, 0, 1, 3), (1, 0, 2, 3), (0, 1, 2, 3),
    (0, 1, 2, 3), (1, 3, 0, 2), (3, 0, 1, 2), (0, 1, 2, 3), (0, 1, 2, 3), (2, 1, 3, 0),
)
GATHER_STEPS = (
    0, 8, 16, 24, 1, 100, 32, 40, 25, 9, 48, 2, 56, 17, 33, 64, 41, 10, 72, 80,
    88, 3, 49, 57, 26, 18, 42, 34, 27, 65, 4, 11, 5, 35, 81, 73, 101, 19, 89, 66,
    50, 12, 13, 82, 58, 102, 36, 74, 37, 90, 28, 20, 43, 29, 51, 21, 103, 67, 104, 105,
    59, 106, 91, 83, 107, 44, 75, 108, 45, 109, 52, 60, 68, 53, 61, 110, 69, 76, 84, 77,
    92, 111, 85, 93, 112, 113,
)
SCATTER_STEPS = (
    0, 8, 16, 24, 1, 9, 17, 32, 25, 40, 48, 33, 56, 41, 49, 2, 57, 64, 18, 72, 65, 80, 73, 42,
    10, 26, 81, 34, 88, 3, 89, 50, 19, 58, 66, 43, 90, 74, 4, 20, 11, 27, 51, 44, 5, 59, 91,
    21, 52, 82, 45, 75, 28, 35, 92, 76, 53, 83, 36, 67, 29, 12, 77, 84, 68, 60, 13, 37, 93,
    69, 85, 61,
)
SLOTS = 3


def here():
    me = lax.axis_index("dp")
    core = lax.axis_index("tensor")
    bits = tuple((me // (1 << b)) % 2 for b in range(4))
    peers = tuple({"dp": me + (1 - 2 * bits[b]) * (1 << b)} for b in range(4))
    return core, bits, peers + ({"tensor": 1 - core},)


def greet(peers):
    barrier = pltpu.get_barrier_semaphore()
    for peer in peers:
        pl.semaphore_signal(barrier, inc=1, device_id=peer, device_id_type=MESH)
    pl.semaphore_wait(barrier, len(peers))


def block_index(bits, free, flip=None):
    index = []
    for b in (3, 2, 1, 0):
        if b == flip:
            index.append(1 - bits[b])
        elif b in free:
            index.append(slice(None))
        else:
            index.append(bits[b])
    return tuple(index)


def columns(array, part, core, width):
    blocks = 4 if array > 3 else 1
    return pl.ds(pl.multiple_of((core * blocks + part) * width, width), width)


def shard_columns(array, part, width):
    return pl.ds((array if array < 3 else part) * width, width)


def attend_pair(query, key_rows, value_rows, valid):
    main = key_rows.shape[0] - 16
    lane = lax.broadcasted_iota(jnp.int32, (1, 2 * DH), 1)
    left = lane < DH
    query = query * DH ** (-0.5)
    zero = jnp.zeros_like(query)
    tail_lane = lax.broadcasted_iota(jnp.int32, (1, 32), 1)
    tail_zero = jnp.zeros((16, 2 * DH), query.dtype)
    key_tail, value_tail = key_rows[main:], value_rows[main:]
    keys_both = jnp.concatenate(
        [jnp.where(left, key_tail, tail_zero), jnp.where(left, tail_zero, key_tail)], axis=0
    )
    values_both = jnp.concatenate(
        [jnp.where(left, value_tail, tail_zero), jnp.where(left, tail_zero, value_tail)], axis=0
    )
    ones_both = jnp.concatenate(
        [jnp.where(left, tail_zero, tail_zero + 1), jnp.where(left, tail_zero + 1, tail_zero)], axis=0
    )
    tail = dot_nt(query, keys_both)
    tail = jnp.where(tail_lane % 16 < valid - main, tail, -1e30)
    peaks, parts = [], []
    for head in range(2):
        picked = jnp.where(left if head == 0 else ~left, query, zero)
        scores = dot_nt(picked, key_rows[:main])
        side = (tail_lane < 16) if head == 0 else (tail_lane >= 16)
        peak = jnp.maximum(
            jnp.max(scores, axis=1, keepdims=True),
            jnp.max(jnp.where(side, tail, -1e30), axis=1, keepdims=True),
        )
        expo = jnp.exp(scores - peak).astype(jnp.bfloat16)
        one = jnp.ones_like(value_rows[:main])
        values = jnp.where(left if head == 0 else ~left, value_rows[:main], one)
        parts.append(dot_nn(expo, values))
        peaks.append(peak)
    tail = jnp.exp(tail - jnp.where(tail_lane < 16, peaks[0], peaks[1])).astype(jnp.bfloat16)
    both = dot_nn(tail, jnp.concatenate([values_both, ones_both], axis=1))
    value_sum = jnp.where(left, parts[0], parts[1]) + both[:, : 2 * DH]
    total = jnp.where(left, parts[1], parts[0]) + both[:, 2 * DH :]
    return (value_sum / pltpu.roll(total, DH, 1)).astype(jnp.bfloat16)


def attend_kernel(valid, q_ref, k_ref, v_ref, out_ref):
    out_ref[...] = attend_pair(q_ref[...], k_ref[...], v_ref[...], valid)


def attend(query, key_rows, value_rows, valid):
    block = pl.BlockSpec((query.shape[0], 2 * DH), lambda i: (0, i))
    return pl.pallas_call(
        functools.partial(attend_kernel, valid),
        grid=(D // (2 * DH),),
        out_shape=jax.ShapeDtypeStruct(query.shape, jnp.bfloat16),
        in_specs=[block] * 3,
        out_specs=block,
        compiler_params=pltpu.CompilerParams(vmem_limit_bytes=32 << 20),
        name="attend",
    )(query, key_rows, value_rows)


def attend_back_kernel(valid, q_ref, k_ref, v_ref, g_ref, dq_ref, dk_ref, dv_ref):
    query, key_rows, value_rows, grads = q_ref[...], k_ref[...], v_ref[...], g_ref[...]
    live = query.shape[0]
    left = lax.broadcasted_iota(jnp.int32, (1, 2 * DH), 1) < DH
    zero = jnp.zeros_like(query)
    query = query * DH ** (-0.5)
    picked = jnp.concatenate([jnp.where(left, query, zero), jnp.where(left, zero, query)], axis=0)
    up = jnp.concatenate([jnp.where(left, grads, zero), jnp.where(left, zero, grads)], axis=0)
    scores = dot_nt(key_rows, picked)
    scores = jnp.where(lax.broadcasted_iota(jnp.int32, scores.shape, 0) < valid, scores, -1e30)
    expo = jnp.exp(scores - jnp.max(scores, axis=0, keepdims=True))
    probs = expo * (1.0 / jnp.sum(expo, axis=0, keepdims=True))
    grad_probs = dot_nt(value_rows, up)
    weighted = jnp.sum(probs * grad_probs, axis=0, keepdims=True)
    grad_scores = (probs * (grad_probs - weighted)).astype(jnp.bfloat16)
    grad_query = dot_tn(grad_scores, key_rows)
    grad_query = jnp.where(left, grad_query[:live], grad_query[live:])
    dq_ref[...] = (grad_query * DH ** (-0.5)).astype(jnp.bfloat16)
    dk_ref[...] = dot_nn(grad_scores, picked).astype(jnp.bfloat16)
    dv_ref[...] = dot_nn(probs.astype(jnp.bfloat16), up).astype(jnp.bfloat16)


def attend_back(query, key_rows, value_rows, grad_context, valid):
    live = grad_context.shape[0]
    short = pl.BlockSpec((live, 2 * DH), lambda i: (0, i))
    tall = pl.BlockSpec((key_rows.shape[0], 2 * DH), lambda i: (0, i))
    low = jnp.bfloat16
    return pl.pallas_call(
        functools.partial(attend_back_kernel, valid),
        grid=(D // (2 * DH),),
        out_shape=[jax.ShapeDtypeStruct((live, D), low)] + [jax.ShapeDtypeStruct(key_rows.shape, low)] * 2,
        in_specs=[short, tall, tall, short],
        out_specs=[short, tall, tall],
        compiler_params=pltpu.CompilerParams(vmem_limit_bytes=32 << 20),
        name="attend_back",
    )(query, key_rows, value_rows, grad_context)


PACK_BIASES, PACK_OUT, PACK_GAINS, PACK_SHIFTS, PACK_INNER = 16, 18, 20, 22, 24


def gather_kernel(
    mem_rows, valid, toks, cots, pack, sq, so, si, sl, move, live_move,
    packs, fq, fk, fv, fo, fi, fl, stacked_a, moved_b, ups, query, key_rows, value_rows,
    context_live, normed_one, rstd_one, middle_live, before_live, hidden_live, normed_two, rstd_two, low_out,
    x_v, c_v, vq, vo, vi, vl, held, context, middle, middle_low, branch,
    send, recv, local, loads, extra,
):
    core, bits, peers = here()
    width = pack.shape[1]
    live = ups.shape[1]
    shards = (vq, vq, vq, vo, vi, vl)
    fulls = (fq, fk, fv, fo, fi, fl)
    mine = pl.ds(pl.multiple_of(core * width, width), width)
    shard_in = [
        pltpu.make_async_copy(src, dst, extra.at[n])
        for n, (src, dst) in enumerate(((sq, vq), (so, vo), (si, vi), (sl, vl)))
    ]
    rows_own = [
        pltpu.make_async_copy(toks.at[core], x_v.at[:, :, mine], extra.at[4]),
        pltpu.make_async_copy(cots.at[core], c_v.at[:, :, mine], extra.at[5]),
        pltpu.make_async_copy(pack, packs.at[core], extra.at[6]),
    ]
    for copy in shard_in + rows_own:
        copy.start()
    own = []
    for p, (array, part) in enumerate(GATHER_PIECES):
        own.append(pltpu.make_async_copy(
            shards[array].at[:, shard_columns(array, part, width)],
            fulls[array].at[block_index(bits, ()) + (slice(None), columns(array, part, core, width))],
            local.at[p],
        ))
    greet(peers)
    for copy in shard_in:
        copy.wait()
    for copy in own:
        copy.start()

    def remote(src, dst, slot, peer):
        return pltpu.make_async_remote_copy(
            src_ref=src, dst_ref=dst, send_sem=send.at[slot], recv_sem=recv.at[slot],
            device_id=peer, device_id_type=MESH)

    def stage(p, s):
        array, part = GATHER_PIECES[p]
        order = GATHER_HOPS[p]
        cols = columns(array, part, core, width)
        dst = fulls[array].at[block_index(bits, order[:s]) + (slice(None), cols)]
        if s == 0:
            src = shards[array].at[:, shard_columns(array, part, width)]
        else:
            src = dst
        peer = peers[order[s]] if s < 4 else peers[4]
        return remote(src, dst, p * 5 + s, peer)

    swaps = [
        remote(toks.at[1 - core], x_v.at[:, :, mine], 60, peers[4]),
        remote(cots.at[1 - core], c_v.at[:, :, mine], 61, peers[4]),
        remote(pack, packs.at[core], 62, peers[4]),
    ]
    started, loading = {}, {}

    def load(p):
        array, part = GATHER_PIECES[p]
        blocks = 4 if array > 3 else 1
        every = (slice(None),) * 5
        loading[p] = [
            pltpu.make_async_copy(
                fulls[array].at[every + (pl.ds((half * blocks + part) * width, width),)],
                held.at[(p % 6,) + every + (pl.ds(half * width, width),)],
                loads.at[2 * p + half],
            )
            for half in range(2)
        ]
        for copy in loading[p]:
            copy.start()

    def loaded(p):
        for copy in loading.pop(p):
            copy.wait()

    def weight(p, cols):
        block = held[p % 6, :, :, :, :, :, cols]
        return block.reshape(2 * width, block.shape[-1])

    def wide(row):
        return jnp.concatenate([packs[0, row : row + 1], packs[1, row : row + 1]], axis=1).astype(jnp.float32)

    def norm(resid, gain, shift):
        center = jnp.mean(resid, axis=1, keepdims=True)
        spread = jnp.mean(resid * resid, axis=1, keepdims=True) - center * center
        rstd = lax.rsqrt(spread + eps_norm)
        normed = (resid - center) * rstd
        return normed * gain + shift, normed, rstd

    def compute(task):
        if task == 0:
            for copy in rows_own:
                copy.wait()
            for swap in swaps:
                swap.wait_recv()
            memory = jnp.concatenate([packs[0, :16], packs[1, :16]], axis=1)
            is_memory = lax.broadcasted_iota(jnp.int32, memory.shape, 0) < mem_rows
            stacked_a[...] = dot_nn(move[0], x_v[0]).astype(jnp.bfloat16)
            stacked_a[:16] = jnp.where(is_memory, memory, stacked_a[:16])
            moved_b[...] = dot_nn(move[1], x_v[1]).astype(jnp.bfloat16)
            for n in range(2):
                ups[n] = dot_nn(live_move[n], c_v[n]).astype(jnp.bfloat16)
        elif task < 4:
            n = task - 1
            loaded(n)
            target = (query, key_rows, value_rows)[n]
            for half in range(2):
                cols = pl.ds(half * width, width)
                got = dot_nn(stacked_a[...], weight(n, cols))
                if n != 1:
                    row = PACK_BIASES + n // 2
                    got = got + packs[half, row : row + 1].astype(jnp.float32)
                target[:, cols] = got.astype(jnp.bfloat16)
        elif task < 8:

            def pair(n, carry):
                cols = pl.ds(pl.multiple_of((2 * (task - 4) + n) * 2 * DH, 2 * DH), 2 * DH)
                context[:, cols] = attend_pair(query[:, cols], key_rows[:, cols], value_rows[:, cols], valid)
                return carry

            lax.fori_loop(0, 2, pair, 0)
        elif task == 8:
            loaded(3)
            attended = dot_nt(context[...], weight(3, slice(None)))
            resid = stacked_a[...].astype(jnp.float32) + attended + wide(PACK_OUT)
            value, normed, rstd = norm(resid, wide(PACK_GAINS), wide(PACK_SHIFTS))
            middle[...] = value
            middle_low[...] = value.astype(jnp.bfloat16)
            middle_live[...] = value[:live].astype(jnp.bfloat16)
            context_live[...] = context[:live]
            normed_one[...] = normed[:live]
            rstd_one[...] = rstd[:live]
        elif task < 13:
            j = task - 9
            loaded(4 + 2 * j)
            loaded(5 + 2 * j)

            def hidden_block(half, carry):
                cols = pl.ds(pl.multiple_of(half * width, width), width)
                place = pl.ds(pl.multiple_of((half * 4 + j) * width, width), width)
                bias = packs[half, PACK_INNER + j : PACK_INNER + j + 1].astype(jnp.float32)
                before = dot_nn(middle_low[...], weight(4 + 2 * j, cols)) + bias
                before_live[:, place] = before[:live]
                hidden = gelu_value(before).astype(jnp.bfloat16)
                hidden_live[:, place] = hidden[:live]
                branch[...] = branch[...] + dot_nt(hidden, weight(5 + 2 * j, cols))
                return carry

            if j == 0:
                branch[...] = middle[...] + wide(PACK_OUT + 1)
            lax.fori_loop(0, 2, hidden_block, 0)
        else:
            value, normed, rstd = norm(branch[...], wide(PACK_GAINS + 1), wide(PACK_SHIFTS + 1))
            low_out[...] = value.astype(jnp.bfloat16)
            normed_two[...] = normed[:live]
            rstd_two[...] = rstd[:live]

    for tick, step in enumerate(GATHER_STEPS):
        if step >= 100:
            compute(step - 100)
            continue
        p, s = step // 8, step % 8
        if s > 0:
            started[p, s - 1].wait_recv()
        if s == 1:
            own[p].wait()
        if s == 5:
            load(p)
        else:
            started[p, s] = stage(p, s)
            started[p, s].start()
        if tick == 2:
            for swap in swaps:
                swap.start()
    for copy in started.values():
        copy.wait_send()
    for swap in swaps:
        swap.wait_send()


def gather_all(mem_rows, valid, toks, cots, pack, sq, so, si, sl, move, live_move):
    width = pack.shape[1]
    rows = sq.shape[0]
    low, full = jnp.bfloat16, jnp.float32
    total, live = move.shape[1], live_move.shape[1]
    hidden = 2 * si.shape[1]
    out = [((2,) + pack.shape, low)]
    for size in (2 * width, 2 * width, 2 * width, 2 * width, hidden, hidden):
        out.append(((2, 2, 2, 2, rows, size), low))
    out += [((total, 2 * width), low)] * 2 + [((2, live, 2 * width), low)]
    out += [((total, 2 * width), low)] * 3 + [((live, 2 * width), low)]
    out += [((live, 2 * width), full), ((live, 1), full), ((live, 2 * width), low)]
    out += [((live, hidden), full), ((live, hidden), low)]
    out += [((live, 2 * width), full), ((live, 1), full), ((total, 2 * width), low)]
    block = (2, 2, 2, 2, rows, 2 * width)
    got = pl.pallas_call(
        functools.partial(gather_kernel, mem_rows, valid),
        out_shape=[jax.ShapeDtypeStruct(*one) for one in out],
        in_specs=[HBM, HBM, VMEM] + [HBM] * 4 + [VMEM] * 2,
        out_specs=[VMEM] + [HBM] * 6 + [VMEM] * (len(out) - 7),
        scratch_shapes=[
            pltpu.VMEM(toks.shape[1:3] + (2 * width,), low),
            pltpu.VMEM(toks.shape[1:3] + (2 * width,), low),
            pltpu.VMEM(sq.shape, low),
            pltpu.VMEM(so.shape, low),
            pltpu.VMEM(si.shape, low),
            pltpu.VMEM(sl.shape, low),
            pltpu.VMEM((6,) + block, low),
            pltpu.VMEM((total, 2 * width), low),
            pltpu.VMEM((total, 2 * width), full),
            pltpu.VMEM((total, 2 * width), low),
            pltpu.VMEM((total, 2 * width), full),
            pltpu.SemaphoreType.DMA((63,)),
            pltpu.SemaphoreType.DMA((63,)),
            pltpu.SemaphoreType.DMA((12,)),
            pltpu.SemaphoreType.DMA((24,)),
            pltpu.SemaphoreType.DMA((7,)),
        ],
        compiler_params=pltpu.CompilerParams(collective_id=0, has_side_effects=True, vmem_limit_bytes=62 << 20),
        name="gather_all",
    )(toks, cots, pack, sq, so, si, sl, move, live_move)
    wide = [array.reshape(16 * rows, array.shape[-1]) for array in got[1:7]]
    return got[0], wide, got[7:]


def scatter_kernel(*refs):
    first_rows, second_rows = refs[0:10], refs[10:20]
    small, outs_a, outs_b, grads_a, grads_b = refs[20:25]
    oq, oo, oi, ol, osmall, out_item, grad_item = refs[25:32]
    (acc, first, second, third, fourth, slots, wide_x, wide_s,
     small_in, small_recv, out_v, grad_v, send, recv, extra) = refs[32:]
    core, bits, peers = here()
    width = osmall.shape[1]
    live = second_rows[1].shape[0]
    bufs = (first, second, third, fourth)
    lefts = (0, 0, 0, 4, 6, 8)
    rights = (1, 2, 3, 5, 7, 9)
    turned = set()
    mine = pl.ds(pl.multiple_of(core * width, width), width)
    other = pl.ds(pl.multiple_of((1 - core) * width, width), width)
    small_own = pltpu.make_async_copy(small.at[:, mine], small_in.at[0], extra.at[0])
    small_own.start()
    stage_in = [
        pltpu.make_async_copy(outs_a.at[:, mine], out_v.at[0], extra.at[1]),
        pltpu.make_async_copy(outs_b.at[:, mine], out_v.at[1], extra.at[2]),
        pltpu.make_async_copy(grads_a.at[:, mine], grad_v.at[0], extra.at[3]),
        pltpu.make_async_copy(grads_b.at[:, mine], grad_v.at[1], extra.at[4]),
    ]
    for copy in stage_in:
        copy.start()
    greet(peers)

    def remote(src, dst, slot, peer):
        return pltpu.make_async_remote_copy(
            src_ref=src, dst_ref=dst, send_sem=send.at[slot], recv_sem=recv.at[slot],
            device_id=peer, device_id_type=MESH)

    def turn(array):
        left = lefts[array]
        if left in turned:
            return
        turned.add(left)
        for n, rows in enumerate((first_rows, second_rows)):
            if left == 0:
                wide_x[n] = rows[0][...].T
            else:
                wide_s[left // 2 - 2, n] = rows[left][...].T

    def multiply(array, offset, size):
        total = None
        for n, rows in enumerate((first_rows, second_rows)):
            right = rows[rights[array]][:, pl.ds(offset, size)]
            if array in (1, 2):
                left = wide_x[n]
            elif array == 0:
                left = wide_x[n, :, :live]
            else:
                left = wide_s[lefts[array] // 2 - 2, n]
            term = jnp.dot(left, right, preferred_element_type=jnp.float32)
            total = term if total is None else total + term
        return total

    tile = width // 2

    def produce(p, slot):
        array, part = SCATTER_PIECES[p]
        turn(array)
        blocks = 4 if array > 3 else 1
        base = ((1 - core) * blocks + part) * width

        def body(n, carry):
            offset = pl.multiple_of(base + n * tile, tile)
            got = multiply(array, offset, tile).astype(jnp.bfloat16)
            slots[slot, :, :, :, :, :, pl.ds(pl.multiple_of(n * tile, tile), tile)] = got.reshape(
                slots.shape[1:6] + (tile,)
            )
            return carry

        lax.fori_loop(0, 2, body, 0)

    def combine(p):
        array, part = SCATTER_PIECES[p]
        blocks = 4 if array > 3 else 1
        base = (core * blocks + part) * width

        def body(n, carry):
            offset = pl.multiple_of(base + n * tile, tile)
            cols = pl.ds(pl.multiple_of(n * tile, tile), tile)
            got = multiply(array, offset, tile).reshape(slots.shape[1:6] + (tile,))
            acc[p, :, :, :, :, :, cols] = (
                got + acc[p, :, :, :, :, :, cols].astype(jnp.float32)
            ).astype(jnp.bfloat16)
            return carry

        lax.fori_loop(0, 2, body, 0)

    def stage(p, s):
        if s == 0:
            return remote(slots.at[p % SLOTS], acc.at[p], p * 5, peers[4])
        order = SCATTER_HOPS[p]
        src = acc.at[(p,) + block_index(bits, order[s:], flip=order[s - 1])]
        return remote(src, bufs[s - 1].at[p], p * 5 + s, peers[order[s - 1]])

    def fold(p, s):
        array, part = SCATTER_PIECES[p]
        order = SCATTER_HOPS[p]
        free = [b for b in (3, 2, 1, 0) if b in order[s:]]
        for n in range(1 << len(free)):
            at = {b: (n >> i) % 2 for i, b in enumerate(reversed(free))}
            where = tuple(at.get(b, bits[b]) for b in (3, 2, 1, 0))
            got = bufs[s - 1][(p,) + tuple(at[b] for b in free)]
            if s < 4:
                acc[(p,) + where] = acc[(p,) + where] + got
            else:
                total = acc[(p,) + where].astype(jnp.float32) + got.astype(jnp.float32)
                if array < 3:
                    oq[:, array] = total
                elif array == 4:
                    oi[:, pl.ds(part * width, width)] = total
                elif array == 3:
                    oo[...] = total.T
                else:
                    ol[pl.ds(part * width, width), :] = total.T

    small_started = {}

    def small_stage(s):
        peer = peers[4] if s == 0 else peers[s - 1]
        src = small.at[:, other] if s == 0 else small_in.at[s]
        return remote(src, small_recv.at[s], 60 + s, peer)

    swaps = [
        remote(outs_a.at[:, other], out_item.at[core, 0], 65, peers[4]),
        remote(outs_b.at[:, other], out_item.at[core, 1], 66, peers[4]),
        remote(grads_a.at[:, other], grad_item.at[core, 0], 67, peers[4]),
        remote(grads_b.at[:, other], grad_item.at[core, 1], 68, peers[4]),
    ]
    started = {}
    for tick, step in enumerate(SCATTER_STEPS):
        p, s = step // 8, step % 8
        if s == 0:
            if p >= SLOTS:
                started[p - SLOTS, 0].wait_send()
            produce(p, p % SLOTS)
        else:
            started[p, s - 1].wait_recv()
            if s == 1:
                combine(p)
            else:
                fold(p, s - 1)
        if s < 5:
            started[p, s] = stage(p, s)
            started[p, s].start()
        if tick % 6 == 5 and tick < 36:
            n = tick // 6
            if n == 0:
                small_own.wait()
            else:
                small_started[n - 1].wait_recv()
                total = small_in[n - 1] + small_recv[n - 1]
                if n < 5:
                    small_in[n] = total
                else:
                    osmall[...] = total
            if n < 5:
                small_started[n] = small_stage(n)
                small_started[n].start()
        if tick == 30:
            for swap in swaps:
                swap.start()
            for copy in stage_in:
                copy.wait()
            stage_out = [
                pltpu.make_async_copy(out_v, out_item.at[core], extra.at[5]),
                pltpu.make_async_copy(grad_v, grad_item.at[core], extra.at[6]),
            ]
            for copy in stage_out:
                copy.start()
    for (p, s), copy in started.items():
        if s > 0 or p >= len(SCATTER_PIECES) - SLOTS:
            copy.wait_send()
    for s in range(5):
        small_started[s].wait_send()
    for swap in swaps:
        swap.wait()
    for copy in stage_out:
        copy.wait()


def scatter_all(first_rows, second_rows, small, outs, grads):
    width = small.shape[1] // 2
    rows = 2 * width // 16
    low, full = jnp.bfloat16, jnp.float32
    count = len(SCATTER_PIECES)
    item = (2, 2) + outs[0].shape[:1] + (width,)
    long, live = first_rows[0].shape[0], first_rows[1].shape[0]
    return pl.pallas_call(
        scatter_kernel,
        out_shape=[
            jax.ShapeDtypeStruct((rows, 3, width), full),
            jax.ShapeDtypeStruct((width, rows), full),
            jax.ShapeDtypeStruct((rows, 4 * width), full),
            jax.ShapeDtypeStruct((4 * width, rows), full),
            jax.ShapeDtypeStruct((small.shape[0], width), full),
            jax.ShapeDtypeStruct(item, low),
            jax.ShapeDtypeStruct(item, low),
        ],
        in_specs=[VMEM] * 20 + [HBM] * 5,
        out_specs=[VMEM] * 5 + [HBM] * 2,
        scratch_shapes=[
            pltpu.VMEM((count, 2, 2, 2, 2, rows, width), low),
            pltpu.VMEM((count, 2, 2, 2, rows, width), low),
            pltpu.VMEM((count, 2, 2, rows, width), low),
            pltpu.VMEM((count, 2, rows, width), low),
            pltpu.VMEM((count, rows, width), low),
            pltpu.VMEM((SLOTS, 2, 2, 2, 2, rows, width), low),
            pltpu.VMEM((2, 2 * width, long), low),
            pltpu.VMEM((3, 2, 2 * width, live), low),
            pltpu.VMEM((5, small.shape[0], width), full),
            pltpu.VMEM((5, small.shape[0], width), full),
            pltpu.VMEM(item[1:], low),
            pltpu.VMEM(item[1:], low),
            pltpu.SemaphoreType.DMA((69,)),
            pltpu.SemaphoreType.DMA((69,)),
            pltpu.SemaphoreType.DMA((7,)),
        ],
        compiler_params=pltpu.CompilerParams(collective_id=1, has_side_effects=True, vmem_limit_bytes=63 << 20),
        name="scatter_all",
    )(*first_rows, *second_rows, small, *outs, *grads)


def item_shards(
    tokens,
    memory,
    w_qkv,
    b_qv,
    w_out,
    out_biases,
    norm_gains,
    norm_shifts,
    w_in,
    b_in,
    w_down,
    cotangent,
    mlm_mask,
):
    core = lax.axis_index("tensor")
    segments, count = tokens.shape[1], tokens.shape[2]
    mem_rows = memory.shape[0]
    valid = mem_rows + count
    half = memory.shape[1]

    mask = lax.dynamic_index_in_dim(mlm_mask, core, 0, keepdims=False)
    lower_tri = (
        lax.broadcasted_iota(jnp.int32, (count, count), 0)
        <= lax.broadcasted_iota(jnp.int32, (count, count), 1)
    ).astype(jnp.bfloat16)
    ones = mask.astype(jnp.bfloat16)
    upto = dot_nn(ones, lower_tri).astype(jnp.int32)
    total = upto[:, -1:]
    index = lax.broadcasted_iota(jnp.int32, mask.shape, 1)
    place = mem_rows + jnp.where(mask > 0, upto - 1, total + index - upto)
    move = (
        lax.broadcasted_iota(jnp.int32, (segments, ROWS, count), 1) == place[:, None, :]
    ).astype(jnp.bfloat16)
    live_move = move[:, :LIVE] * ones[:, None, :]

    packed = jnp.concatenate(
        [
            jnp.pad(memory, ((0, PACK_BIASES - mem_rows), (0, 0))),
            b_qv,
            out_biases,
            norm_gains,
            norm_shifts,
            b_in.reshape(-1, half),
        ],
        axis=0,
    )
    packed = jnp.pad(packed, ((0, -packed.shape[0] % 16), (0, 0)))
    both, (wq, wk, wv, outer, inner, lower), first = gather_all(
        mem_rows,
        valid,
        tokens,
        cotangent,
        packed,
        w_qkv.reshape(w_qkv.shape[0], -1),
        w_out.T,
        w_in,
        w_down.T,
        move,
        live_move,
    )
    (
        stacked,
        moved,
        ups,
        query,
        key_rows,
        value_rows,
        context,
        normed_one,
        rstd_one,
        middle_low,
        before,
        hidden,
        normed_two,
        rstd_two,
        low_out,
    ) = first
    wide = jnp.concatenate([both[0], both[1]], axis=1).astype(jnp.float32)
    qv_bias, out_bias, gains, shifts = (
        wide[n : n + 2] for n in (PACK_BIASES, PACK_OUT, PACK_GAINS, PACK_SHIFTS)
    )
    inner_rows = b_in.shape[0] // half
    inner_bias = both[:, PACK_INNER : PACK_INNER + inner_rows].reshape(-1).astype(jnp.float32)
    stored = [
        (
            stacked,
            query,
            key_rows,
            value_rows,
            context,
            normed_one,
            rstd_one,
            middle_low,
            before,
            hidden,
            normed_two,
            rstd_two,
        )
    ]
    outs = [dot_tn(move[0], low_out).astype(jnp.bfloat16)]
    stacked = jnp.concatenate([low_out[:mem_rows], moved[mem_rows:]], axis=0)
    query = (dot_nn(stacked, wq) + qv_bias[0]).astype(jnp.bfloat16)
    key_rows = dot_nn(stacked, wk).astype(jnp.bfloat16)
    value_rows = (dot_nn(stacked, wv) + qv_bias[1]).astype(jnp.bfloat16)
    context = attend(query, key_rows, value_rows, valid)
    attended = dot_nt(context, outer)
    middle, normed_one, rstd_one = norm_rows(
        stacked.astype(jnp.float32) + attended + out_bias[0], gains[0], shifts[0]
    )
    middle_low = middle.astype(jnp.bfloat16)
    before = dot_nn(middle_low, inner) + inner_bias
    hidden = gelu_value(before).astype(jnp.bfloat16)
    branch = dot_nt(hidden, lower)
    layer_out, normed_two, rstd_two = norm_rows(
        middle + branch + out_bias[1], gains[1], shifts[1]
    )
    low_out = layer_out.astype(jnp.bfloat16)
    outs.append(dot_tn(move[1], low_out).astype(jnp.bfloat16))
    stored.append(
        (
            stacked,
            query,
            key_rows,
            value_rows,
            context[:LIVE],
            normed_one[:LIVE],
            rstd_one[:LIVE],
            middle_low[:LIVE],
            before[:LIVE],
            hidden[:LIVE],
            normed_two[:LIVE],
            rstd_two[:LIVE],
        )
    )

    returning = jnp.zeros((mem_rows, D), jnp.float32)
    token_grads = [None] * segments
    pieces = [None] * segments
    smalls = None
    for seg in reversed(range(segments)):
        (
            stacked,
            query,
            key_rows,
            value_rows,
            context,
            normed_one,
            rstd_one,
            middle_low,
            before,
            hidden,
            normed_two,
            rstd_two,
        ) = stored[seg]
        upstream = ups[seg].astype(jnp.float32)
        upstream = upstream + jnp.pad(returning, ((0, LIVE - mem_rows), (0, 0)))
        grad_two, gain_two, shift_two = norm_rows_back(upstream, normed_two, rstd_two, gains[1])
        grad_branch = grad_two.astype(jnp.bfloat16)
        grad_hidden = dot_nn(grad_branch, lower)
        grad_before = (grad_hidden * gelu_slope(before)).astype(jnp.bfloat16)
        grad_middle = grad_two + dot_nt(grad_before, inner)
        grad_one, gain_one, shift_one = norm_rows_back(
            grad_middle, normed_one, rstd_one, gains[0]
        )
        grad_attended = grad_one.astype(jnp.bfloat16)
        grad_context = dot_nn(grad_attended, outer).astype(jnp.bfloat16)
        grad_query, grad_key, grad_value = attend_back(
            query, key_rows, value_rows, grad_context, valid
        )
        grad_stacked = dot_nt(grad_key, wk) + dot_nt(grad_value, wv)
        live_part = grad_one + dot_nt(grad_query, wq)
        grad_stacked = grad_stacked + jnp.pad(live_part, ((0, ROWS - LIVE), (0, 0)))
        returning = grad_stacked[:mem_rows]
        token_grads[seg] = dot_tn(move[seg], grad_stacked.astype(jnp.bfloat16)).astype(
            jnp.bfloat16
        )
        pieces[seg] = (
            stacked,
            grad_query,
            grad_key,
            grad_value,
            grad_attended,
            context,
            middle_low,
            grad_before,
            grad_branch,
            hidden,
        )
        sums = jnp.concatenate(
            [
                jnp.stack(
                    [
                        jnp.sum(grad_query.astype(jnp.float32), axis=0),
                        jnp.sum(grad_value.astype(jnp.float32), axis=0),
                        jnp.sum(grad_one, axis=0),
                        jnp.sum(grad_two, axis=0),
                        gain_one,
                        gain_two,
                        shift_one,
                        shift_two,
                    ]
                ),
                jnp.sum(grad_before.astype(jnp.float32), axis=0).reshape(-1, D),
            ],
            axis=0,
        )
        smalls = sums if smalls is None else smalls + sums

    inner_sums = smalls[8:].reshape(2, inner_rows, half).transpose(1, 0, 2).reshape(inner_rows, D)
    small = jnp.concatenate([smalls[:8], inner_sums, returning], axis=0)
    small = jnp.pad(small, ((0, -small.shape[0] % 8), (0, 0)))
    grad_proj, grad_outer, grad_inner, grad_lower, mine, outputs, input_grad = scatter_all(
        pieces[0], pieces[1], small, outs, token_grads
    )
    inner_sum = mine[8 : 8 + inner_rows].reshape(-1)
    return (
        outputs,
        input_grad.astype(jnp.float32),
        mine[8 + inner_rows : 8 + inner_rows + mem_rows],
        grad_proj,
        mine[0:2],
        grad_outer,
        mine[2:4],
        mine[4:6],
        mine[6:8],
        grad_inner,
        inner_sum,
        grad_lower,
    )


def solution(mesh):
    def body(*arrays):
        if mesh.shape["dp"] == 16 and mesh.shape["tensor"] == arrays[0].shape[0] == arrays[0].shape[1] == 2:
            return item_shards(*arrays)
        return shards(*arrays)

    placed = (
        P("dp", None, None, "tensor"),
        P(None, "tensor"),
        P("dp", None, "tensor"),
        P(None, "tensor"),
        P("tensor", "dp"),
        P(None, "tensor"),
        P(None, "tensor"),
        P(None, "tensor"),
        P("dp", "tensor"),
        P("tensor"),
        P("tensor", "dp"),
        P("dp", None, None, "tensor"),
        P("dp", None, None),
    )
    return jax.shard_map(
        body,
        mesh=mesh,
        in_specs=placed,
        out_specs=(
            P("dp", None, None, "tensor"),
            P("dp", None, None, "tensor"),
            P(None, "tensor"),
            P("dp", None, "tensor"),
            P(None, "tensor"),
            P("tensor", "dp"),
            P(None, "tensor"),
            P(None, "tensor"),
            P(None, "tensor"),
            P("dp", "tensor"),
            P("tensor"),
            P("tensor", "dp"),
        ),
        check_vma=False,
    )
```

```python
import functools

import jax
import jax.numpy as jnp
from jax import lax
from jax.experimental import pallas as pl
from jax.experimental.pallas import tpu as pltpu
from jax.sharding import PartitionSpec as P

D = 1024
DH = 64
MICRO = 2


eps_norm = 1e-05
root_half = 0.7071067811865476
inv_root_two_pi = 0.3989422804014327


def gelu_value(before):
    return 0.5 * before * (1.0 + lax.erf(before * root_half))


def gelu_slope(before):
    return 0.5 * (1.0 + lax.erf(before * root_half)) + before * inv_root_two_pi * jnp.exp(
        -0.5 * before * before
    )


def fetch_weights(w_qkv, w_in, w_out, w_down):
    return (
        lax.all_gather(w_qkv, "dp", axis=0, tiled=True),
        lax.all_gather(w_in, "dp", axis=0, tiled=True),
        lax.all_gather(w_out, "dp", axis=1, tiled=True),
        lax.all_gather(w_down, "dp", axis=1, tiled=True),
    )


def reduce_weights(grad_proj, grad_inner, grad_outer, grad_lower):
    return (
        lax.psum_scatter(
            grad_proj.astype(jnp.bfloat16), "dp", scatter_dimension=0, tiled=True
        ).astype(jnp.float32),
        lax.psum_scatter(
            grad_inner.astype(jnp.bfloat16), "dp", scatter_dimension=0, tiled=True
        ).astype(jnp.float32),
        lax.psum_scatter(
            grad_outer.astype(jnp.bfloat16), "dp", scatter_dimension=1, tiled=True
        ).astype(jnp.float32),
        lax.psum_scatter(
            grad_lower.astype(jnp.bfloat16), "dp", scatter_dimension=1, tiled=True
        ).astype(jnp.float32),
    )


def gather_rows(block):
    return lax.all_gather(block, "tensor", axis=2, tiled=True)


def branch_sum(partial_value):
    return lax.psum_scatter(partial_value, "tensor", scatter_dimension=2, tiled=True)


def gather_grads(block):
    return lax.all_gather(block, "tensor", axis=2, tiled=True)


def input_sum(partial_value):
    return lax.psum_scatter(
        partial_value.astype(jnp.bfloat16), "tensor", scatter_dimension=2, tiled=True
    ).astype(jnp.float32)


def norm_forward(resid, gain, shift):
    totals = jnp.sum(resid, axis=-1)
    squares = jnp.sum(resid * resid, axis=-1)
    totals, squares = lax.psum((totals, squares), "tensor")
    center = totals / D
    spread = squares / D - center * center
    rstd = lax.rsqrt(spread + eps_norm)
    normed = (resid - center[..., None]) * rstd[..., None]
    return (normed * gain + shift, normed, rstd)


def norm_backward(upstream, normed, rstd, gain):
    scaled = upstream * gain
    first = jnp.sum(scaled, axis=-1)
    second = jnp.sum(scaled * normed, axis=-1)
    first, second = lax.psum((first, second), "tensor")
    result = rstd[..., None] * (scaled - first[..., None] / D - normed * (second[..., None] / D))
    return (result, jnp.sum(upstream * normed, axis=(0, 1)), jnp.sum(upstream, axis=(0, 1)))


def attention_scores(query, key_rows):
    return jnp.einsum(
        "bqhe,bkhe->bhqk", query, key_rows, preferred_element_type=jnp.float32
    ) * DH ** (-0.5)


def segment_forward(weights, smalls, memory_rows, token_rows):
    proj_weight, inner_weight, outer_weight, lower_weight = weights
    qv_bias, out_bias, gains, shifts, inner_bias = smalls
    batch = token_rows.shape[0]
    stacked = jnp.concatenate([memory_rows, token_rows], axis=1)
    length = stacked.shape[1]
    local = proj_weight.shape[2]
    heads = local // DH
    wide_rows = gather_rows(stacked)
    bias_three = jnp.stack([qv_bias[0], jnp.zeros_like(qv_bias[0]), qv_bias[1]])
    projected = (
        jnp.einsum("bld,dcf->blcf", wide_rows, proj_weight, preferred_element_type=jnp.float32)
        + bias_three
    ).astype(jnp.bfloat16)
    split = projected.reshape(batch, length, 3, heads, DH)
    scores = attention_scores(split[:, :, 0], split[:, :, 1])
    peak = jnp.max(scores, axis=-1, keepdims=True)
    expo = jnp.exp(scores - peak)
    totals = jnp.sum(expo, axis=-1, keepdims=True)
    probs = expo / totals
    logsum = peak[..., 0] + jnp.log(totals[..., 0])
    context = jnp.einsum(
        "bhqk,bkhe->bqhe",
        probs.astype(jnp.bfloat16),
        split[:, :, 2],
        preferred_element_type=jnp.float32,
    )
    context = context.astype(jnp.bfloat16).reshape(batch, length, local)
    attended = branch_sum(
        jnp.einsum("bld,df->blf", context, outer_weight, preferred_element_type=jnp.float32)
    )
    middle, normed_one, rstd_one = norm_forward(
        stacked.astype(jnp.float32) + attended + out_bias[0], gains[0], shifts[0]
    )
    middle_wide = gather_rows(middle.astype(jnp.bfloat16))
    before = (
        jnp.einsum("bld,df->blf", middle_wide, inner_weight, preferred_element_type=jnp.float32)
        + inner_bias
    )
    hidden = gelu_value(before).astype(jnp.bfloat16)
    branch = branch_sum(
        jnp.einsum("blf,fd->bld", hidden, lower_weight, preferred_element_type=jnp.float32)
    )
    layer_out, normed_two, rstd_two = norm_forward(
        middle + branch + out_bias[1], gains[1], shifts[1]
    )
    stored = (
        wide_rows,
        projected,
        logsum,
        context,
        normed_one,
        rstd_one,
        middle_wide,
        before,
        hidden,
        normed_two,
        rstd_two,
    )
    return (layer_out, stored)


def segment_backward(weights, smalls, upstream, stored):
    proj_weight, inner_weight, outer_weight, lower_weight = weights
    qv_bias, out_bias, gains, shifts, inner_bias = smalls
    (
        wide_rows,
        projected,
        logsum,
        context,
        normed_one,
        rstd_one,
        middle_wide,
        before,
        hidden,
        normed_two,
        rstd_two,
    ) = stored
    batch, length, local = context.shape
    heads = local // DH
    grad_two, gain_two, shift_two = norm_backward(upstream, normed_two, rstd_two, gains[1])
    grad_branch = gather_grads(grad_two.astype(jnp.bfloat16))
    grad_lower = jnp.einsum("blf,bld->fd", hidden, grad_branch, preferred_element_type=jnp.float32)
    grad_hidden = jnp.einsum(
        "bld,fd->blf", grad_branch, lower_weight, preferred_element_type=jnp.float32
    )
    grad_before = (grad_hidden * gelu_slope(before)).astype(jnp.bfloat16)
    grad_inner = jnp.einsum(
        "bld,blf->df", middle_wide, grad_before, preferred_element_type=jnp.float32
    )
    grad_inner_bias = jnp.sum(grad_before.astype(jnp.float32), axis=(0, 1))
    grad_middle = grad_two + lax.psum_scatter(
        jnp.einsum(
            "blf,df->bld", grad_before, inner_weight, preferred_element_type=jnp.float32
        ).astype(jnp.bfloat16),
        "tensor",
        scatter_dimension=2,
        tiled=True,
    ).astype(jnp.float32)
    grad_one, gain_one, shift_one = norm_backward(grad_middle, normed_one, rstd_one, gains[0])
    grad_attended = gather_grads(grad_one.astype(jnp.bfloat16))
    grad_outer = jnp.einsum(
        "bld,blf->df", context, grad_attended, preferred_element_type=jnp.float32
    )
    grad_context = jnp.einsum(
        "blf,df->bld", grad_attended, outer_weight, preferred_element_type=jnp.float32
    )
    grad_context = grad_context.astype(jnp.bfloat16)
    grad_context = grad_context.reshape(batch, length, heads, DH)
    split = projected.reshape(batch, length, 3, heads, DH)
    query, key_rows, value_rows = (split[:, :, 0], split[:, :, 1], split[:, :, 2])
    probs = jnp.exp(attention_scores(query, key_rows) - logsum[..., None])
    grad_probs = jnp.einsum(
        "bqhe,bkhe->bhqk", grad_context, value_rows, preferred_element_type=jnp.float32
    )
    weighted_sum = jnp.sum(probs * grad_probs, axis=-1, keepdims=True)
    grad_scores = (probs * (grad_probs - weighted_sum)).astype(jnp.bfloat16)
    grad_query = jnp.einsum(
        "bhqk,bkhe->bqhe", grad_scores, key_rows, preferred_element_type=jnp.float32
    ) * DH ** (-0.5)
    grad_key = jnp.einsum(
        "bhqk,bqhe->bkhe", grad_scores, query, preferred_element_type=jnp.float32
    ) * DH ** (-0.5)
    grad_value = jnp.einsum(
        "bhqk,bqhe->bkhe",
        probs.astype(jnp.bfloat16),
        grad_context,
        preferred_element_type=jnp.float32,
    )
    grad_projected = (
        jnp.stack([grad_query, grad_key, grad_value], axis=2)
        .reshape(batch, length, 3, local)
        .astype(jnp.bfloat16)
    )
    grad_proj = jnp.einsum(
        "bld,blcf->dcf", wide_rows, grad_projected, preferred_element_type=jnp.float32
    )
    column_sums = jnp.sum(grad_projected.astype(jnp.float32), axis=(0, 1))
    grad_qv = jnp.stack([column_sums[0], column_sums[2]])
    grad_stacked = grad_one + input_sum(
        jnp.einsum("blcf,dcf->bld", grad_projected, proj_weight, preferred_element_type=jnp.float32)
    )
    grad_biases = jnp.stack([jnp.sum(grad_one, axis=(0, 1)), jnp.sum(grad_two, axis=(0, 1))])
    large_grads = (grad_proj, grad_inner, grad_outer, grad_lower)
    small_grads = (
        grad_qv,
        grad_biases,
        jnp.stack([gain_one, gain_two]),
        jnp.stack([shift_one, shift_two]),
        grad_inner_bias,
    )
    return (grad_stacked, large_grads, small_grads)


def add_tuples(first, second):
    return tuple((left + right for left, right in zip(first, second)))


def shards(
    tokens,
    memory,
    w_qkv,
    b_qv,
    w_out,
    out_biases,
    norm_gains,
    norm_shifts,
    w_in,
    b_in,
    w_down,
    cotangent,
    mlm_mask,
):
    smalls = (
        b_qv.astype(jnp.float32),
        out_biases.astype(jnp.float32),
        norm_gains.astype(jnp.float32),
        norm_shifts.astype(jnp.float32),
        b_in.astype(jnp.float32),
    )
    per_batch = tokens.shape[0] // MICRO
    segments = tokens.shape[1]
    mem_rows = memory.shape[0]
    local = w_qkv.shape[2]
    inner_local = w_in.shape[1]
    empty_large = (
        jnp.zeros((D, 3, local), jnp.float32),
        jnp.zeros((D, inner_local), jnp.float32),
        jnp.zeros((local, D), jnp.float32),
        jnp.zeros((inner_local, D), jnp.float32),
    )
    full_grads = empty_large
    shard_grads = (
        jnp.zeros(w_qkv.shape, jnp.float32),
        jnp.zeros(w_in.shape, jnp.float32),
        jnp.zeros(w_out.shape, jnp.float32),
        jnp.zeros(w_down.shape, jnp.float32),
    )
    small_total = (
        jnp.zeros((2, local), jnp.float32),
        jnp.zeros((2, local), jnp.float32),
        jnp.zeros((2, local), jnp.float32),
        jnp.zeros((2, local), jnp.float32),
        jnp.zeros((inner_local,), jnp.float32),
    )
    memory_total = jnp.zeros((mem_rows, local), jnp.float32)
    out_blocks = []
    grad_blocks = []
    for batch_index in range(MICRO):
        offset = batch_index * per_batch
        batch_tokens = tokens[offset : offset + per_batch]
        batch_mask = mlm_mask[offset : offset + per_batch]
        batch_cot = cotangent[offset : offset + per_batch].astype(jnp.float32) * batch_mask[
            ..., None
        ].astype(jnp.float32)
        weights = fetch_weights(w_qkv, w_in, w_out, w_down)
        carried = memory[None]
        stored_all = []
        token_outs = []
        for seg_index in range(segments):
            layer_out, stored = segment_forward(
                weights, smalls, carried, batch_tokens[:, seg_index]
            )
            carried = layer_out[:, :mem_rows].astype(jnp.bfloat16)
            token_outs.append(layer_out[:, mem_rows:].astype(jnp.bfloat16))
            stored_all.append(stored)
        returning = jnp.zeros((per_batch, mem_rows, local), jnp.float32)
        token_grads = [None] * segments
        for seg_index in reversed(range(segments)):
            upstream = jnp.concatenate([returning, batch_cot[:, seg_index]], axis=1)
            grad_stacked, large_grads, small_grads = segment_backward(
                weights, smalls, upstream, stored_all[seg_index]
            )
            returning = grad_stacked[:, :mem_rows]
            token_grads[seg_index] = grad_stacked[:, mem_rows:]
            full_grads = add_tuples(full_grads, large_grads)
            small_total = add_tuples(small_total, small_grads)
        memory_total = memory_total + jnp.sum(returning, axis=0)
        reduced = reduce_weights(full_grads[0], full_grads[1], full_grads[2], full_grads[3])
        shard_grads = add_tuples(shard_grads, reduced)
        full_grads = empty_large
        out_blocks.append(jnp.stack(token_outs, axis=1))
        grad_blocks.append(jnp.stack(token_grads, axis=1))
    grad_qv, grad_biases, grad_gains, grad_shifts, grad_inner_bias, memory_grad = lax.psum(
        (
            small_total[0],
            small_total[1],
            small_total[2],
            small_total[3],
            small_total[4],
            memory_total,
        ),
        "dp",
    )
    outputs = jnp.concatenate(out_blocks, axis=0)
    input_grad = jnp.concatenate(grad_blocks, axis=0)
    return (
        outputs,
        input_grad,
        memory_grad,
        shard_grads[0],
        grad_qv,
        shard_grads[2],
        grad_biases,
        grad_gains,
        grad_shifts,
        shard_grads[1],
        grad_inner_bias,
        shard_grads[3],
    )


ROWS = 528
LIVE = 176


def dot_nn(left, right):
    return jnp.dot(left, right, preferred_element_type=jnp.float32)


def dot_nt(left, right):
    return lax.dot_general(
        left, right, (((1,), (1,)), ((), ())), preferred_element_type=jnp.float32
    )


def dot_tn(left, right):
    return lax.dot_general(
        left, right, (((0,), (0,)), ((), ())), preferred_element_type=jnp.float32
    )


def norm_rows(resid, gain, shift):
    center = jnp.mean(resid, axis=-1, keepdims=True)
    spread = jnp.mean(resid * resid, axis=-1, keepdims=True) - center * center
    rstd = lax.rsqrt(spread + eps_norm)
    normed = (resid - center) * rstd
    return (normed * gain + shift, normed, rstd)


def norm_rows_back(upstream, normed, rstd, gain):
    scaled = upstream * gain
    first = jnp.mean(scaled, axis=-1, keepdims=True)
    second = jnp.mean(scaled * normed, axis=-1, keepdims=True)
    result = rstd * (scaled - first - normed * second)
    return (result, jnp.sum(upstream * normed, axis=0), jnp.sum(upstream, axis=0))


MESH = pl.DeviceIdType.MESH
HBM = pl.BlockSpec(memory_space=pl.ANY)
VMEM = pl.BlockSpec(memory_space=pltpu.VMEM)
GATHER_PIECES = ((0, 0), (1, 0), (2, 0), (3, 0), (4, 0), (5, 0), (4, 1), (5, 1), (4, 2), (5, 2), (4, 3), (5, 3))
SCATTER_PIECES = ((5, 0), (5, 1), (5, 2), (5, 3), (4, 0), (4, 1), (4, 2), (4, 3), (3, 0), (0, 0), (1, 0), (2, 0))
GATHER_HOPS = (
    (3, 2, 1, 0), (3, 0, 2, 1), (3, 2, 0, 1), (0, 3, 1, 2), (2, 3, 1, 0), (2, 1, 3, 0),
    (2, 3, 0, 1), (1, 3, 2, 0), (3, 0, 1, 2), (3, 0, 2, 1), (2, 1, 3, 0), (3, 0, 1, 2),
)
SCATTER_HOPS = (
    (0, 1, 2, 3), (3, 2, 1, 0), (1, 0, 3, 2), (0, 1, 3, 2), (3, 0, 1, 2), (1, 2, 0, 3),
    (1, 0, 2, 3), (1, 2, 0, 3), (0, 3, 1, 2), (2, 1, 0, 3), (0, 1, 2, 3), (0, 1, 2, 3),
)
GATHER_STEPS = (
    0, 8, 16, 24, 1, 100, 32, 40, 25, 9, 48, 2, 56, 17, 33, 64, 41, 10, 72, 80,
    88, 3, 49, 57, 26, 18, 42, 34, 27, 65, 4, 11, 5, 35, 81, 73, 101, 19, 89, 66,
    50, 12, 13, 82, 58, 102, 36, 74, 37, 90, 28, 20, 43, 29, 51, 21, 103, 67, 104, 105,
    59, 106, 91, 83, 107, 44, 75, 108, 45, 109, 52, 60, 68, 53, 61, 110, 69, 76, 84, 77,
    92, 111, 85, 93, 112, 113,
)
SCATTER_STEPS = (
    0, 8, 16, 1, 9, 17, 24, 32, 100, 25, 33, 40, 48, 2, 101, 18, 41, 49, 56, 64,
    3, 102, 57, 26, 10, 65, 103, 4, 19, 72, 80, 42, 11, 73, 88, 81, 104, 66, 89, 43,
    50, 105, 106, 34, 107, 108, 5, 109, 82, 110, 58, 74, 20, 27, 12, 90, 59, 44, 21, 67,
    83, 51, 28, 75, 84, 45, 52, 35, 29, 13, 91, 85, 60, 68, 53, 92, 76, 36, 61, 69,
    93, 37, 77,
)
SLOTS = 2


def here():
    me = lax.axis_index("dp")
    core = lax.axis_index("tensor")
    bits = tuple((me // (1 << b)) % 2 for b in range(4))
    peers = tuple({"dp": me + (1 - 2 * bits[b]) * (1 << b)} for b in range(4))
    return core, bits, peers + ({"tensor": 1 - core},)


def greet(peers):
    barrier = pltpu.get_barrier_semaphore()
    for peer in peers:
        pl.semaphore_signal(barrier, inc=1, device_id=peer, device_id_type=MESH)
    pl.semaphore_wait(barrier, len(peers))


def block_index(bits, free, flip=None):
    index = []
    for b in (3, 2, 1, 0):
        if b == flip:
            index.append(1 - bits[b])
        elif b in free:
            index.append(slice(None))
        else:
            index.append(bits[b])
    return tuple(index)


def columns(array, part, core, width):
    blocks = 4 if array > 3 else 1
    return pl.ds(pl.multiple_of((core * blocks + part) * width, width), width)


def shard_block(shards, piece, width):
    array, part = piece
    if array < 3:
        return shards[array].at[array]
    return shards[array].at[:, pl.ds(part * width, width)]


def attend_pair(query, key_rows, value_rows, valid):
    main = key_rows.shape[0] - 16
    lane = lax.broadcasted_iota(jnp.int32, (1, 2 * DH), 1)
    left = lane < DH
    query = query * DH ** (-0.5)
    zero = jnp.zeros_like(query)
    tail_lane = lax.broadcasted_iota(jnp.int32, (1, 32), 1)
    tail_zero = jnp.zeros((16, 2 * DH), query.dtype)
    key_tail, value_tail = key_rows[main:], value_rows[main:]
    keys_both = jnp.concatenate(
        [jnp.where(left, key_tail, tail_zero), jnp.where(left, tail_zero, key_tail)], axis=0
    )
    values_both = jnp.concatenate(
        [jnp.where(left, value_tail, tail_zero), jnp.where(left, tail_zero, value_tail)], axis=0
    )
    ones_both = jnp.concatenate(
        [jnp.where(left, tail_zero, tail_zero + 1), jnp.where(left, tail_zero + 1, tail_zero)], axis=0
    )
    tail = dot_nt(query, keys_both)
    tail = jnp.where(tail_lane % 16 < valid - main, tail, -1e30)
    peaks, parts = [], []
    for head in range(2):
        picked = jnp.where(left if head == 0 else ~left, query, zero)
        scores = dot_nt(picked, key_rows[:main])
        side = (tail_lane < 16) if head == 0 else (tail_lane >= 16)
        peak = jnp.maximum(
            jnp.max(scores, axis=1, keepdims=True),
            jnp.max(jnp.where(side, tail, -1e30), axis=1, keepdims=True),
        )
        expo = jnp.exp(scores - peak).astype(jnp.bfloat16)
        one = jnp.ones_like(value_rows[:main])
        values = jnp.where(left if head == 0 else ~left, value_rows[:main], one)
        parts.append(dot_nn(expo, values))
        peaks.append(peak)
    tail = jnp.exp(tail - jnp.where(tail_lane < 16, peaks[0], peaks[1])).astype(jnp.bfloat16)
    both = dot_nn(tail, jnp.concatenate([values_both, ones_both], axis=1))
    value_sum = jnp.where(left, parts[0], parts[1]) + both[:, : 2 * DH]
    total = jnp.where(left, parts[1], parts[0]) + both[:, 2 * DH :]
    return (value_sum / pltpu.roll(total, DH, 1)).astype(jnp.bfloat16)


def attend_kernel(valid, q_ref, k_ref, v_ref, out_ref):
    out_ref[...] = attend_pair(q_ref[...], k_ref[...], v_ref[...], valid)


def attend(query, key_rows, value_rows, valid):
    block = pl.BlockSpec((query.shape[0], 2 * DH), lambda i: (0, i))
    return pl.pallas_call(
        functools.partial(attend_kernel, valid),
        grid=(D // (2 * DH),),
        out_shape=jax.ShapeDtypeStruct(query.shape, jnp.bfloat16),
        in_specs=[block] * 3,
        out_specs=block,
        compiler_params=pltpu.CompilerParams(vmem_limit_bytes=32 << 20),
        name="attend",
    )(query, key_rows, value_rows)


def attend_back_pair(query, key_rows, value_rows, grads, valid):
    live = query.shape[0]
    left = lax.broadcasted_iota(jnp.int32, (1, 2 * DH), 1) < DH
    zero = jnp.zeros_like(query)
    query = query * DH ** (-0.5)
    picked = jnp.concatenate([jnp.where(left, query, zero), jnp.where(left, zero, query)], axis=0)
    up = jnp.concatenate([jnp.where(left, grads, zero), jnp.where(left, zero, grads)], axis=0)
    scores = dot_nt(key_rows, picked)
    scores = jnp.where(lax.broadcasted_iota(jnp.int32, scores.shape, 0) < valid, scores, -1e30)
    expo = jnp.exp(scores - jnp.max(scores, axis=0, keepdims=True))
    probs = expo * (1.0 / jnp.sum(expo, axis=0, keepdims=True))
    grad_probs = dot_nt(value_rows, up)
    weighted = jnp.sum(probs * grad_probs, axis=0, keepdims=True)
    grad_scores = (probs * (grad_probs - weighted)).astype(jnp.bfloat16)
    grad_query = dot_tn(grad_scores, key_rows)
    grad_query = jnp.where(left, grad_query[:live], grad_query[live:]) * DH ** (-0.5)
    grad_key = dot_nn(grad_scores, picked)
    grad_value = dot_nn(probs.astype(jnp.bfloat16), up)
    return tuple(grad.astype(jnp.bfloat16) for grad in (grad_query, grad_key, grad_value))


def attend_back_kernel(valid, q_ref, k_ref, v_ref, g_ref, dq_ref, dk_ref, dv_ref):
    dq_ref[...], dk_ref[...], dv_ref[...] = attend_back_pair(
        q_ref[...], k_ref[...], v_ref[...], g_ref[...], valid
    )


def attend_back(query, key_rows, value_rows, grad_context, valid):
    live = grad_context.shape[0]
    short = pl.BlockSpec((live, 2 * DH), lambda i: (0, i))
    tall = pl.BlockSpec((key_rows.shape[0], 2 * DH), lambda i: (0, i))
    low = jnp.bfloat16
    return pl.pallas_call(
        functools.partial(attend_back_kernel, valid),
        grid=(D // (2 * DH),),
        out_shape=[jax.ShapeDtypeStruct((live, D), low)] + [jax.ShapeDtypeStruct(key_rows.shape, low)] * 2,
        in_specs=[short, tall, tall, short],
        out_specs=[short, tall, tall],
        compiler_params=pltpu.CompilerParams(vmem_limit_bytes=32 << 20),
        name="attend_back",
    )(query, key_rows, value_rows, grad_context)


PACK_BIASES, PACK_OUT, PACK_GAINS, PACK_SHIFTS, PACK_INNER = 16, 18, 20, 22, 24


def gather_kernel(
    mem_rows, valid, toks, cots, pack, sq, so, si, sl, move, live_move,
    packs, fq, fk, fv, fo, fi, fl, stacked_a, moved_b, ups, query, key_rows, value_rows,
    context_live, normed_one, rstd_one, middle_live, before_live, hidden_live, normed_two, rstd_two, low_out,
    x_v, c_v, vq, vo, vi, vl, held, context, middle, middle_low, branch,
    send, recv, local, loads, extra,
):
    core, bits, peers = here()
    width = pack.shape[1]
    live = ups.shape[1]
    shards = (vq, vq, vq, vo, vi, vl)
    fulls = (fq, fk, fv, fo, fi, fl)
    mine = pl.ds(pl.multiple_of(core * width, width), width)
    shard_in = [
        pltpu.make_async_copy(src, dst, extra.at[n])
        for n, (src, dst) in enumerate(((sq, vq), (so, vo), (si, vi), (sl, vl)))
    ]
    rows_own = [
        pltpu.make_async_copy(toks.at[core], x_v.at[:, :, mine], extra.at[4]),
        pltpu.make_async_copy(cots.at[core], c_v.at[:, :, mine], extra.at[5]),
        pltpu.make_async_copy(pack, packs.at[core], extra.at[6]),
    ]
    for copy in shard_in + rows_own:
        copy.start()
    own = []
    for p, (array, part) in enumerate(GATHER_PIECES):
        own.append(pltpu.make_async_copy(
            shard_block(shards, (array, part), width),
            fulls[array].at[block_index(bits, ()) + (slice(None), columns(array, part, core, width))],
            local.at[p],
        ))
    greet(peers)
    for copy in shard_in:
        copy.wait()
    for copy in own:
        copy.start()

    def remote(src, dst, slot, peer):
        return pltpu.make_async_remote_copy(
            src_ref=src, dst_ref=dst, send_sem=send.at[slot], recv_sem=recv.at[slot],
            device_id=peer, device_id_type=MESH)

    def stage(p, s):
        array, part = GATHER_PIECES[p]
        order = GATHER_HOPS[p]
        cols = columns(array, part, core, width)
        dst = fulls[array].at[block_index(bits, order[:s]) + (slice(None), cols)]
        if s == 0:
            src = shard_block(shards, (array, part), width)
        else:
            src = dst
        peer = peers[order[s]] if s < 4 else peers[4]
        return remote(src, dst, p * 5 + s, peer)

    swaps = [
        remote(toks.at[1 - core], x_v.at[:, :, mine], 60, peers[4]),
        remote(cots.at[1 - core], c_v.at[:, :, mine], 61, peers[4]),
        remote(pack, packs.at[core], 62, peers[4]),
    ]
    started, loading = {}, {}

    def load(p):
        array, part = GATHER_PIECES[p]
        blocks = 4 if array > 3 else 1
        every = (slice(None),) * 5
        loading[p] = [
            pltpu.make_async_copy(
                fulls[array].at[every + (pl.ds((half * blocks + part) * width, width),)],
                held.at[(p % 6,) + every + (pl.ds(half * width, width),)],
                loads.at[2 * p + half],
            )
            for half in range(2)
        ]
        for copy in loading[p]:
            copy.start()

    def loaded(p):
        for copy in loading.pop(p):
            copy.wait()

    def weight(p, cols):
        block = held[p % 6, :, :, :, :, :, cols]
        return block.reshape(2 * width, block.shape[-1])

    def wide(row):
        return jnp.concatenate([packs[0, row : row + 1], packs[1, row : row + 1]], axis=1).astype(jnp.float32)

    def norm(resid, gain, shift):
        center = jnp.mean(resid, axis=1, keepdims=True)
        spread = jnp.mean(resid * resid, axis=1, keepdims=True) - center * center
        rstd = lax.rsqrt(spread + eps_norm)
        normed = (resid - center) * rstd
        return normed * gain + shift, normed, rstd

    def compute(task):
        if task == 0:
            for copy in rows_own:
                copy.wait()
            for swap in swaps:
                swap.wait_recv()
            memory = jnp.concatenate([packs[0, :16], packs[1, :16]], axis=1)
            is_memory = lax.broadcasted_iota(jnp.int32, memory.shape, 0) < mem_rows
            stacked_a[...] = dot_nn(move[0], x_v[0]).astype(jnp.bfloat16)
            stacked_a[:16] = jnp.where(is_memory, memory, stacked_a[:16])
            moved_b[...] = dot_nn(move[1], x_v[1]).astype(jnp.bfloat16)
            for n in range(2):
                ups[n] = dot_nn(live_move[n], c_v[n]).astype(jnp.bfloat16)
        elif task < 4:
            n = task - 1
            loaded(n)
            target = (query, key_rows, value_rows)[n]
            for half in range(2):
                cols = pl.ds(half * width, width)
                got = dot_nn(stacked_a[...], weight(n, cols))
                if n != 1:
                    row = PACK_BIASES + n // 2
                    got = got + packs[half, row : row + 1].astype(jnp.float32)
                target[:, cols] = got.astype(jnp.bfloat16)
        elif task < 8:

            def pair(n, carry):
                cols = pl.ds(pl.multiple_of((2 * (task - 4) + n) * 2 * DH, 2 * DH), 2 * DH)
                context[:, cols] = attend_pair(query[:, cols], key_rows[:, cols], value_rows[:, cols], valid)
                return carry

            lax.fori_loop(0, 2, pair, 0)
        elif task == 8:
            loaded(3)
            attended = dot_nt(context[...], weight(3, slice(None)))
            resid = stacked_a[...].astype(jnp.float32) + attended + wide(PACK_OUT)
            value, normed, rstd = norm(resid, wide(PACK_GAINS), wide(PACK_SHIFTS))
            middle[...] = value
            middle_low[...] = value.astype(jnp.bfloat16)
            middle_live[...] = value[:live].astype(jnp.bfloat16)
            context_live[...] = context[:live]
            normed_one[...] = normed[:live]
            rstd_one[...] = jnp.broadcast_to(rstd[:live], rstd_one.shape)
        elif task < 13:
            j = task - 9
            loaded(4 + 2 * j)
            loaded(5 + 2 * j)

            def hidden_block(half, carry):
                cols = pl.ds(pl.multiple_of(half * width, width), width)
                place = pl.ds(pl.multiple_of((half * 4 + j) * width, width), width)
                bias = packs[half, PACK_INNER + j : PACK_INNER + j + 1].astype(jnp.float32)
                before = dot_nn(middle_low[...], weight(4 + 2 * j, cols)) + bias
                before_live[:, place] = before[:live]
                hidden = gelu_value(before).astype(jnp.bfloat16)
                hidden_live[:, place] = hidden[:live]
                branch[...] = branch[...] + dot_nt(hidden, weight(5 + 2 * j, cols))
                return carry

            if j == 0:
                branch[...] = middle[...] + wide(PACK_OUT + 1)
            lax.fori_loop(0, 2, hidden_block, 0)
        else:
            value, normed, rstd = norm(branch[...], wide(PACK_GAINS + 1), wide(PACK_SHIFTS + 1))
            low_out[...] = value.astype(jnp.bfloat16)
            normed_two[...] = normed[:live]
            rstd_two[...] = jnp.broadcast_to(rstd[:live], rstd_two.shape)

    for tick, step in enumerate(GATHER_STEPS):
        if step >= 100:
            compute(step - 100)
            continue
        p, s = step // 8, step % 8
        if s > 0:
            started[p, s - 1].wait_recv()
        if s == 1:
            own[p].wait()
        if s == 5:
            load(p)
        else:
            started[p, s] = stage(p, s)
            started[p, s].start()
        if tick == 2:
            for swap in swaps:
                swap.start()
    for copy in started.values():
        copy.wait_send()
    for swap in swaps:
        swap.wait_send()


def gather_all(mem_rows, valid, toks, cots, pack, sq, so, si, sl, move, live_move):
    width = pack.shape[1]
    rows = sq.shape[1]
    low, full = jnp.bfloat16, jnp.float32
    total, live = move.shape[1], live_move.shape[1]
    hidden = 2 * si.shape[1]
    out = [((2,) + pack.shape, low)]
    for size in (2 * width, 2 * width, 2 * width, 2 * width, hidden, hidden):
        out.append(((2, 2, 2, 2, rows, size), low))
    out += [((total, 2 * width), low)] * 2 + [((2, live, 2 * width), low)]
    out += [((total, 2 * width), low)] * 3 + [((live, 2 * width), low)]
    out += [((live, 2 * width), full), ((live, 2 * width), full), ((live, 2 * width), low)]
    out += [((live, hidden), full), ((live, hidden), low)]
    out += [((live, 2 * width), full), ((live, 2 * width), full), ((total, 2 * width), low)]
    block = (2, 2, 2, 2, rows, 2 * width)
    got = pl.pallas_call(
        functools.partial(gather_kernel, mem_rows, valid),
        out_shape=[jax.ShapeDtypeStruct(*one) for one in out],
        in_specs=[HBM, HBM, VMEM] + [HBM] * 4 + [VMEM] * 2,
        out_specs=[VMEM] + [HBM] * 6 + [VMEM] * (len(out) - 7),
        scratch_shapes=[
            pltpu.VMEM(toks.shape[1:3] + (2 * width,), low),
            pltpu.VMEM(toks.shape[1:3] + (2 * width,), low),
            pltpu.VMEM(sq.shape, low),
            pltpu.VMEM(so.shape, low),
            pltpu.VMEM(si.shape, low),
            pltpu.VMEM(sl.shape, low),
            pltpu.VMEM((6,) + block, low),
            pltpu.VMEM((total, 2 * width), low),
            pltpu.VMEM((total, 2 * width), full),
            pltpu.VMEM((total, 2 * width), low),
            pltpu.VMEM((total, 2 * width), full),
            pltpu.SemaphoreType.DMA((63,)),
            pltpu.SemaphoreType.DMA((63,)),
            pltpu.SemaphoreType.DMA((12,)),
            pltpu.SemaphoreType.DMA((24,)),
            pltpu.SemaphoreType.DMA((7,)),
        ],
        compiler_params=pltpu.CompilerParams(collective_id=0, has_side_effects=True, vmem_limit_bytes=62 << 20),
        name="gather_all",
    )(toks, cots, pack, sq, so, si, sl, move, live_move)
    wide = [array.reshape(16 * rows, array.shape[-1]) for array in got[1:7]]
    return got[0], wide, got[7:]


def scatter_kernel(mem_rows, valid, *refs):
    (rows_a, out_a, context_a, middle_a, before_a, branch_a, hidden_a) = refs[0:7]
    second_rows = refs[7:17]
    query, keys_in, values_in, up, grad_one, wq, wk, wv, move, small, outs_a, outs_b, grads_b = refs[17:30]
    oq, oo, oi, ol, osmall, out_item, grad_item = refs[30:37]
    (acc, first, second, third, fourth, slots, wide_x, wide_s, held, grad_query, key_rows, value_rows,
     source, result, total_rows, small_v, small_in, small_recv, send, recv, extra, sent) = refs[37:]
    first_rows = (rows_a, grad_query, key_rows, value_rows, out_a, context_a, middle_a, before_a, branch_a, hidden_a)
    core, bits, peers = here()
    width = osmall.shape[1]
    live = grad_query.shape[0]
    bufs = (first, second, third, fourth)
    lefts = (0, 0, 0, 4, 6, 8)
    rights = (1, 2, 3, 5, 7, 9)
    turned = set()
    mine = pl.ds(pl.multiple_of(core * width, width), width)
    other = pl.ds(pl.multiple_of((1 - core) * width, width), width)
    stage_in = [
        pltpu.make_async_copy(keys_in, key_rows, extra.at[0]),
        pltpu.make_async_copy(values_in, value_rows, extra.at[1]),
    ]
    for copy in stage_in:
        copy.start()
    greet(peers)

    def bring(src, dst, sem):
        copy = pltpu.make_async_copy(src, dst, extra.at[sem])
        copy.start()
        return copy

    def remote(src, dst, slot, peer):
        return pltpu.make_async_remote_copy(
            src_ref=src, dst_ref=dst, send_sem=send.at[slot], recv_sem=recv.at[slot],
            device_id=peer, device_id_type=MESH)

    def turn(array):
        left = lefts[array]
        if left in turned:
            return
        turned.add(left)
        for n, rows in enumerate((first_rows, second_rows)):
            if left == 0:
                bring(rows[0], source, 2).wait()
                wide_x[n] = source[...].T
            else:
                wide_s[left // 2 - 2, n] = rows[left][...].T

    def multiply(array, offset, size):
        total = None
        for n, rows in enumerate((first_rows, second_rows)):
            right = rows[rights[array]][:, pl.ds(offset, size)]
            if array in (1, 2):
                left = wide_x[n]
            elif array == 0:
                left = wide_x[n, :, :live]
            else:
                left = wide_s[lefts[array] // 2 - 2, n]
            term = jnp.dot(left, right, preferred_element_type=jnp.float32)
            total = term if total is None else total + term
        return total

    tile = width // 2

    def produce(p, slot):
        array, part = SCATTER_PIECES[p]
        turn(array)
        blocks = 4 if array > 3 else 1
        base = ((1 - core) * blocks + part) * width

        def body(n, carry):
            offset = pl.multiple_of(base + n * tile, tile)
            got = multiply(array, offset, tile).astype(jnp.bfloat16)
            slots[slot, :, :, :, :, :, pl.ds(pl.multiple_of(n * tile, tile), tile)] = got.reshape(
                slots.shape[1:6] + (tile,)
            )
            return carry

        lax.fori_loop(0, 2, body, 0)

    def combine(p):
        array, part = SCATTER_PIECES[p]
        blocks = 4 if array > 3 else 1
        base = (core * blocks + part) * width

        def body(n, carry):
            offset = pl.multiple_of(base + n * tile, tile)
            cols = pl.ds(pl.multiple_of(n * tile, tile), tile)
            got = multiply(array, offset, tile).reshape(slots.shape[1:6] + (tile,))
            acc[p, :, :, :, :, :, cols] = (
                got + acc[p, :, :, :, :, :, cols].astype(jnp.float32)
            ).astype(jnp.bfloat16)
            return carry

        lax.fori_loop(0, 2, body, 0)

    def stage(p, s):
        if s == 0:
            return remote(slots.at[p % SLOTS], acc.at[p], p * 5, peers[4])
        order = SCATTER_HOPS[p]
        src = acc.at[(p,) + block_index(bits, order[s:], flip=order[s - 1])]
        return remote(src, bufs[s - 1].at[p], p * 5 + s, peers[order[s - 1]])

    def fold(p, s):
        array, part = SCATTER_PIECES[p]
        order = SCATTER_HOPS[p]
        free = [b for b in (3, 2, 1, 0) if b in order[s:]]
        for n in range(1 << len(free)):
            at = {b: (n >> i) % 2 for i, b in enumerate(reversed(free))}
            where = tuple(at.get(b, bits[b]) for b in (3, 2, 1, 0))
            got = bufs[s - 1][(p,) + tuple(at[b] for b in free)]
            if s < 4:
                acc[(p,) + where] = acc[(p,) + where] + got
            else:
                total = acc[(p,) + where].astype(jnp.float32) + got.astype(jnp.float32)
                if array < 3:
                    oq[array] = total
                elif array == 4:
                    oi[:, pl.ds(part * width, width)] = total
                elif array == 3:
                    oo[...] = total
                else:
                    ol[:, pl.ds(part * width, width)] = total

    small_started = {}

    def small_stage(s):
        peer = peers[4] if s == 0 else peers[s - 1]
        src = small_v.at[:, other] if s == 0 else small_in.at[s]
        return remote(src, small_recv.at[s], 60 + s, peer)

    def small_step(n):
        if n == 0:
            small_in[0] = small_v[:, mine]
        else:
            small_started[n - 1].wait_recv()
            total = small_in[n - 1] + small_recv[n - 1]
            if n < 5:
                small_in[n] = total
            else:
                osmall[...] = total
        if n < 5:
            small_started[n] = small_stage(n)
            small_started[n].start()

    swaps, places = [], []

    def unpermute(n, values, target, segment):
        if n > 1:
            swaps[n - 2].wait_send()
            places[n - 2].wait()
        result[n % 2] = dot_tn(move[segment], values).astype(jnp.bfloat16)
        places.append(
            pltpu.make_async_copy(result.at[n % 2, :, mine], target.at[core, segment], sent.at[n])
        )
        swaps.append(remote(result.at[n % 2, :, other], target.at[core, segment], 65 + n, peers[4]))
        places[n].start()
        swaps[n].start()

    weights = (wk, wv, wq)
    fetched = {}

    def compute(task):
        if task < 4:
            if task == 0:
                for copy in stage_in:
                    copy.wait()
                fetched[0] = bring(weights[0], held, 3)

            def pair(n, carry):
                cols = pl.ds(pl.multiple_of((2 * task + n) * 2 * DH, 2 * DH), 2 * DH)
                grad_query[:, cols], key_rows[:, cols], value_rows[:, cols] = attend_back_pair(
                    query[:, cols], key_rows[:, cols], value_rows[:, cols], up[:, cols], valid
                )
                return carry

            lax.fori_loop(0, 2, pair, 0)
        elif task < 7:
            n = task - 4
            fetched[n].wait()
            if n == 0:
                total_rows[...] = dot_nt(key_rows[...], held[...])
            elif n == 1:
                total_rows[...] = total_rows[...] + dot_nt(value_rows[...], held[...])
            else:
                total_rows[:live] = total_rows[:live] + grad_one[...] + dot_nt(grad_query[...], held[...])
                row = lax.broadcasted_iota(jnp.int32, (16, 2 * width), 0)
                small_v[...] = small[...]
                small_v[:16] = jnp.where(row < mem_rows, total_rows[:16], 0.0)
                query_sum = jnp.sum(grad_query[...].astype(jnp.float32), axis=0, keepdims=True)
                value_sum = jnp.sum(value_rows[...].astype(jnp.float32), axis=0, keepdims=True)
                small_v[16:24] = small[16:24] + jnp.where(
                    row[:8] == 0, query_sum, jnp.where(row[:8] == 1, value_sum, 0.0)
                )
            if n < 2:
                fetched[n + 1] = bring(weights[n + 1], held, 3)
        elif task == 7:
            unpermute(0, total_rows[...].astype(jnp.bfloat16), grad_item, 0)
        else:
            values, target, segment = (
                (outs_a, out_item, 0),
                (outs_b, out_item, 1),
                (grads_b, grad_item, 1),
            )[task - 8]
            bring(values, source, 2).wait()
            unpermute(task - 7, source[...], target, segment)

    started = {}
    ready = None
    for step in SCATTER_STEPS:
        if step >= 100:
            compute(step - 100)
            if step == 106:
                ready = 0
            continue
        p, s = step // 8, step % 8
        if s == 0:
            if p >= SLOTS:
                started[p - SLOTS, 0].wait_send()
            produce(p, p % SLOTS)
        else:
            started[p, s - 1].wait_recv()
            if s == 1:
                combine(p)
            else:
                fold(p, s - 1)
        if s < 5:
            started[p, s] = stage(p, s)
            started[p, s].start()
        if ready is not None:
            ready += 1
            if ready % 4 == 0 and ready < 28:
                small_step(ready // 4 - 1)
    for (p, s), copy in started.items():
        if s > 0 or p >= len(SCATTER_PIECES) - SLOTS:
            copy.wait_send()
    for s in range(5):
        small_started[s].wait_send()
    for n in range(4):
        if n > 1:
            swaps[n].wait_send()
            places[n].wait()
        swaps[n].wait_recv()


def scatter_all(mem_rows, valid, first_rows, second_rows, tail, small, outs, grads):
    width = small.shape[1] // 2
    rows = 2 * width // 16
    low, full = jnp.bfloat16, jnp.float32
    count = len(SCATTER_PIECES)
    long, live = second_rows[0].shape[0], second_rows[1].shape[0]
    move = tail[-1]
    tokens = move.shape[2]
    item = (2, 2, tokens, width)
    return pl.pallas_call(
        functools.partial(scatter_kernel, mem_rows, valid),
        out_shape=[
            jax.ShapeDtypeStruct((3, rows, width), full),
            jax.ShapeDtypeStruct((rows, width), full),
            jax.ShapeDtypeStruct((rows, 4 * width), full),
            jax.ShapeDtypeStruct((rows, 4 * width), full),
            jax.ShapeDtypeStruct((small.shape[0], width), full),
            jax.ShapeDtypeStruct(item, low),
            jax.ShapeDtypeStruct(item, low),
        ],
        in_specs=[HBM] + [VMEM] * 6 + [HBM] + [VMEM] * 9
        + [VMEM, HBM, HBM, VMEM, VMEM, HBM, HBM, HBM, VMEM, VMEM, HBM, HBM, HBM],
        out_specs=[VMEM] * 5 + [HBM] * 2,
        scratch_shapes=[
            pltpu.VMEM((count, 2, 2, 2, 2, rows, width), low),
            pltpu.VMEM((count, 2, 2, 2, rows, width), low),
            pltpu.VMEM((count, 2, 2, rows, width), low),
            pltpu.VMEM((count, 2, rows, width), low),
            pltpu.VMEM((count, rows, width), low),
            pltpu.VMEM((SLOTS, 2, 2, 2, 2, rows, width), low),
            pltpu.VMEM((2, 2 * width, long), low),
            pltpu.VMEM((3, 2, 2 * width, live), low),
            pltpu.VMEM((2 * width, 2 * width), low),
            pltpu.VMEM((live, 2 * width), low),
            pltpu.VMEM((long, 2 * width), low),
            pltpu.VMEM((long, 2 * width), low),
            pltpu.VMEM((long, 2 * width), low),
            pltpu.VMEM((2, tokens, 2 * width), low),
            pltpu.VMEM((long, 2 * width), full),
            pltpu.VMEM(small.shape, full),
            pltpu.VMEM((5, small.shape[0], width), full),
            pltpu.VMEM((5, small.shape[0], width), full),
            pltpu.SemaphoreType.DMA((69,)),
            pltpu.SemaphoreType.DMA((69,)),
            pltpu.SemaphoreType.DMA((4,)),
            pltpu.SemaphoreType.DMA((4,)),
        ],
        compiler_params=pltpu.CompilerParams(collective_id=1, has_side_effects=True, vmem_limit_bytes=67_000_000),
        name="scatter_all",
    )(*first_rows, *second_rows, *tail[:-1], move, small, *outs, *grads)


def item_shards(
    tokens,
    memory,
    w_qkv,
    b_qv,
    w_out,
    out_biases,
    norm_gains,
    norm_shifts,
    w_in,
    b_in,
    w_down,
    cotangent,
    mlm_mask,
):
    core = lax.axis_index("tensor")
    segments, count = tokens.shape[1], tokens.shape[2]
    mem_rows = memory.shape[0]
    valid = mem_rows + count
    half = memory.shape[1]

    mask = lax.dynamic_index_in_dim(mlm_mask, core, 0, keepdims=False)
    lower_tri = (
        lax.broadcasted_iota(jnp.int32, (count, count), 0)
        <= lax.broadcasted_iota(jnp.int32, (count, count), 1)
    ).astype(jnp.bfloat16)
    ones = mask.astype(jnp.bfloat16)
    upto = dot_nn(ones, lower_tri).astype(jnp.int32)
    total = upto[:, -1:]
    index = lax.broadcasted_iota(jnp.int32, mask.shape, 1)
    place = mem_rows + jnp.where(mask > 0, upto - 1, total + index - upto)
    move = (
        lax.broadcasted_iota(jnp.int32, (segments, ROWS, count), 1) == place[:, None, :]
    ).astype(jnp.bfloat16)
    live_move = move[:, :LIVE] * ones[:, None, :]

    packed = jnp.concatenate(
        [
            jnp.pad(memory, ((0, PACK_BIASES - mem_rows), (0, 0))),
            b_qv,
            out_biases,
            norm_gains,
            norm_shifts,
            b_in.reshape(-1, half),
        ],
        axis=0,
    )
    packed = jnp.pad(packed, ((0, -packed.shape[0] % 16), (0, 0)))
    both, (wq, wk, wv, outer, inner, lower), first = gather_all(
        mem_rows,
        valid,
        tokens,
        cotangent,
        packed,
        w_qkv.transpose(1, 0, 2),
        w_out.T,
        w_in,
        w_down.T,
        move,
        live_move,
    )
    (
        stacked,
        moved,
        ups,
        query,
        key_rows,
        value_rows,
        context,
        normed_one,
        rstd_one,
        middle_low,
        before,
        hidden,
        normed_two,
        rstd_two,
        low_out,
    ) = first
    wide = jnp.concatenate([both[0], both[1]], axis=1).astype(jnp.float32)
    qv_bias, out_bias, gains, shifts = (
        wide[n : n + 2] for n in (PACK_BIASES, PACK_OUT, PACK_GAINS, PACK_SHIFTS)
    )
    inner_rows = b_in.shape[0] // half
    inner_bias = both[:, PACK_INNER : PACK_INNER + inner_rows].reshape(-1).astype(jnp.float32)
    stored = [
        (
            stacked,
            query,
            key_rows,
            value_rows,
            context,
            normed_one,
            rstd_one,
            middle_low,
            before,
            hidden,
            normed_two,
            rstd_two,
        )
    ]
    outs = [low_out]
    stacked = jnp.concatenate([low_out[:mem_rows], moved[mem_rows:]], axis=0)
    query = (dot_nn(stacked, wq) + qv_bias[0]).astype(jnp.bfloat16)
    key_rows = dot_nn(stacked, wk).astype(jnp.bfloat16)
    value_rows = (dot_nn(stacked, wv) + qv_bias[1]).astype(jnp.bfloat16)
    context = attend(query, key_rows, value_rows, valid)
    attended = dot_nt(context, outer)
    middle, normed_one, rstd_one = norm_rows(
        stacked.astype(jnp.float32) + attended + out_bias[0], gains[0], shifts[0]
    )
    middle_low = middle.astype(jnp.bfloat16)
    before = dot_nn(middle_low, inner) + inner_bias
    hidden = gelu_value(before).astype(jnp.bfloat16)
    branch = dot_nt(hidden, lower)
    layer_out, normed_two, rstd_two = norm_rows(
        middle + branch + out_bias[1], gains[1], shifts[1]
    )
    low_out = layer_out.astype(jnp.bfloat16)
    outs.append(low_out)
    stored.append(
        (
            stacked,
            query,
            key_rows,
            value_rows,
            context[:LIVE],
            normed_one[:LIVE],
            rstd_one[:LIVE],
            middle_low[:LIVE],
            before[:LIVE],
            hidden[:LIVE],
            normed_two[:LIVE],
            rstd_two[:LIVE],
        )
    )

    returning = jnp.zeros((mem_rows, D), jnp.float32)
    token_grads = []
    pieces = [None] * segments
    smalls = None
    for seg in reversed(range(segments)):
        (
            stacked,
            query,
            key_rows,
            value_rows,
            context,
            normed_one,
            rstd_one,
            middle_low,
            before,
            hidden,
            normed_two,
            rstd_two,
        ) = stored[seg]
        upstream = ups[seg].astype(jnp.float32)
        upstream = upstream + jnp.pad(returning, ((0, LIVE - mem_rows), (0, 0)))
        grad_two, gain_two, shift_two = norm_rows_back(upstream, normed_two, rstd_two, gains[1])
        grad_branch = grad_two.astype(jnp.bfloat16)
        grad_hidden = dot_nn(grad_branch, lower)
        grad_before = (grad_hidden * gelu_slope(before)).astype(jnp.bfloat16)
        grad_middle = grad_two + dot_nt(grad_before, inner)
        grad_one, gain_one, shift_one = norm_rows_back(
            grad_middle, normed_one, rstd_one, gains[0]
        )
        grad_attended = grad_one.astype(jnp.bfloat16)
        grad_context = dot_nn(grad_attended, outer).astype(jnp.bfloat16)
        sums = [jnp.zeros((D,), jnp.float32)] * 2
        if seg > 0:
            grad_query, grad_key, grad_value = attend_back(
                query, key_rows, value_rows, grad_context, valid
            )
            grad_stacked = dot_nt(grad_key, wk) + dot_nt(grad_value, wv)
            live_part = grad_one + dot_nt(grad_query, wq)
            grad_stacked = grad_stacked + jnp.pad(live_part, ((0, ROWS - LIVE), (0, 0)))
            returning = grad_stacked[:mem_rows]
            token_grads.append(grad_stacked.astype(jnp.bfloat16))
            attention_grads = [grad_query, grad_key, grad_value]
            sums = [jnp.sum(grad.astype(jnp.float32), axis=0) for grad in (grad_query, grad_value)]
        else:
            attention_grads = []
            tail = [query[:LIVE], key_rows, value_rows, grad_context, grad_one, wq, wk, wv, move]
        pieces[seg] = (
            stacked,
            *attention_grads,
            grad_attended,
            context,
            middle_low,
            grad_before,
            grad_branch,
            hidden,
        )
        sums = jnp.concatenate(
            [
                jnp.stack(
                    [
                        *sums,
                        jnp.sum(grad_one, axis=0),
                        jnp.sum(grad_two, axis=0),
                        gain_one,
                        gain_two,
                        shift_one,
                        shift_two,
                    ]
                ),
                jnp.sum(grad_before.astype(jnp.float32), axis=0).reshape(-1, D),
            ],
            axis=0,
        )
        smalls = sums if smalls is None else smalls + sums

    inner_sums = smalls[8:].reshape(2, inner_rows, half).transpose(1, 0, 2).reshape(inner_rows, D)
    small = jnp.concatenate([jnp.zeros((16, D), jnp.float32), smalls[:8], inner_sums], axis=0)
    small = jnp.pad(small, ((0, -small.shape[0] % 8), (0, 0)))
    grad_proj, grad_outer, grad_inner, grad_lower, mine, outputs, input_grad = scatter_all(
        mem_rows, valid, pieces[0], pieces[1], tail, small, outs, token_grads
    )
    return (
        outputs,
        input_grad.astype(jnp.float32),
        mine[:mem_rows],
        grad_proj.transpose(1, 0, 2),
        mine[16:18],
        grad_outer.T,
        mine[18:20],
        mine[20:22],
        mine[22:24],
        grad_inner,
        mine[24 : 24 + inner_rows].reshape(-1),
        grad_lower.T,
    )


def solution(mesh):
    def body(*arrays):
        if mesh.shape["dp"] == 16 and mesh.shape["tensor"] == arrays[0].shape[0] == arrays[0].shape[1] == 2:
            return item_shards(*arrays)
        return shards(*arrays)

    placed = (
        P("dp", None, None, "tensor"),
        P(None, "tensor"),
        P("dp", None, "tensor"),
        P(None, "tensor"),
        P("tensor", "dp"),
        P(None, "tensor"),
        P(None, "tensor"),
        P(None, "tensor"),
        P("dp", "tensor"),
        P("tensor"),
        P("tensor", "dp"),
        P("dp", None, None, "tensor"),
        P("dp", None, None),
    )
    return jax.shard_map(
        body,
        mesh=mesh,
        in_specs=placed,
        out_specs=(
            P("dp", None, None, "tensor"),
            P("dp", None, None, "tensor"),
            P(None, "tensor"),
            P("dp", None, "tensor"),
            P(None, "tensor"),
            P("tensor", "dp"),
            P(None, "tensor"),
            P(None, "tensor"),
            P(None, "tensor"),
            P("dp", "tensor"),
            P("tensor"),
            P("tensor", "dp"),
        ),
        check_vma=False,
    )
```

```python
import functools

import jax
import jax.numpy as jnp
from jax import lax
from jax.experimental import pallas as pl
from jax.experimental.pallas import tpu as pltpu
from jax.sharding import PartitionSpec as P

D = 1024
DH = 64
MICRO = 2


eps_norm = 1e-05
root_half = 0.7071067811865476
inv_root_two_pi = 0.3989422804014327


def gelu_value(before):
    return 0.5 * before * (1.0 + lax.erf(before * root_half))


def gelu_slope(before):
    return 0.5 * (1.0 + lax.erf(before * root_half)) + before * inv_root_two_pi * jnp.exp(
        -0.5 * before * before
    )


def fetch_weights(w_qkv, w_in, w_out, w_down):
    return (
        lax.all_gather(w_qkv, "dp", axis=0, tiled=True),
        lax.all_gather(w_in, "dp", axis=0, tiled=True),
        lax.all_gather(w_out, "dp", axis=1, tiled=True),
        lax.all_gather(w_down, "dp", axis=1, tiled=True),
    )


def reduce_weights(grad_proj, grad_inner, grad_outer, grad_lower):
    return (
        lax.psum_scatter(
            grad_proj.astype(jnp.bfloat16), "dp", scatter_dimension=0, tiled=True
        ).astype(jnp.float32),
        lax.psum_scatter(
            grad_inner.astype(jnp.bfloat16), "dp", scatter_dimension=0, tiled=True
        ).astype(jnp.float32),
        lax.psum_scatter(
            grad_outer.astype(jnp.bfloat16), "dp", scatter_dimension=1, tiled=True
        ).astype(jnp.float32),
        lax.psum_scatter(
            grad_lower.astype(jnp.bfloat16), "dp", scatter_dimension=1, tiled=True
        ).astype(jnp.float32),
    )


def gather_rows(block):
    return lax.all_gather(block, "tensor", axis=2, tiled=True)


def branch_sum(partial_value):
    return lax.psum_scatter(partial_value, "tensor", scatter_dimension=2, tiled=True)


def gather_grads(block):
    return lax.all_gather(block, "tensor", axis=2, tiled=True)


def input_sum(partial_value):
    return lax.psum_scatter(
        partial_value.astype(jnp.bfloat16), "tensor", scatter_dimension=2, tiled=True
    ).astype(jnp.float32)


def norm_forward(resid, gain, shift):
    totals = jnp.sum(resid, axis=-1)
    squares = jnp.sum(resid * resid, axis=-1)
    totals, squares = lax.psum((totals, squares), "tensor")
    center = totals / D
    spread = squares / D - center * center
    rstd = lax.rsqrt(spread + eps_norm)
    normed = (resid - center[..., None]) * rstd[..., None]
    return (normed * gain + shift, normed, rstd)


def norm_backward(upstream, normed, rstd, gain):
    scaled = upstream * gain
    first = jnp.sum(scaled, axis=-1)
    second = jnp.sum(scaled * normed, axis=-1)
    first, second = lax.psum((first, second), "tensor")
    result = rstd[..., None] * (scaled - first[..., None] / D - normed * (second[..., None] / D))
    return (result, jnp.sum(upstream * normed, axis=(0, 1)), jnp.sum(upstream, axis=(0, 1)))


def attention_scores(query, key_rows):
    return jnp.einsum(
        "bqhe,bkhe->bhqk", query, key_rows, preferred_element_type=jnp.float32
    ) * DH ** (-0.5)


def segment_forward(weights, smalls, memory_rows, token_rows):
    proj_weight, inner_weight, outer_weight, lower_weight = weights
    qv_bias, out_bias, gains, shifts, inner_bias = smalls
    batch = token_rows.shape[0]
    stacked = jnp.concatenate([memory_rows, token_rows], axis=1)
    length = stacked.shape[1]
    local = proj_weight.shape[2]
    heads = local // DH
    wide_rows = gather_rows(stacked)
    bias_three = jnp.stack([qv_bias[0], jnp.zeros_like(qv_bias[0]), qv_bias[1]])
    projected = (
        jnp.einsum("bld,dcf->blcf", wide_rows, proj_weight, preferred_element_type=jnp.float32)
        + bias_three
    ).astype(jnp.bfloat16)
    split = projected.reshape(batch, length, 3, heads, DH)
    scores = attention_scores(split[:, :, 0], split[:, :, 1])
    peak = jnp.max(scores, axis=-1, keepdims=True)
    expo = jnp.exp(scores - peak)
    totals = jnp.sum(expo, axis=-1, keepdims=True)
    probs = expo / totals
    logsum = peak[..., 0] + jnp.log(totals[..., 0])
    context = jnp.einsum(
        "bhqk,bkhe->bqhe",
        probs.astype(jnp.bfloat16),
        split[:, :, 2],
        preferred_element_type=jnp.float32,
    )
    context = context.astype(jnp.bfloat16).reshape(batch, length, local)
    attended = branch_sum(
        jnp.einsum("bld,df->blf", context, outer_weight, preferred_element_type=jnp.float32)
    )
    middle, normed_one, rstd_one = norm_forward(
        stacked.astype(jnp.float32) + attended + out_bias[0], gains[0], shifts[0]
    )
    middle_wide = gather_rows(middle.astype(jnp.bfloat16))
    before = (
        jnp.einsum("bld,df->blf", middle_wide, inner_weight, preferred_element_type=jnp.float32)
        + inner_bias
    )
    hidden = gelu_value(before).astype(jnp.bfloat16)
    branch = branch_sum(
        jnp.einsum("blf,fd->bld", hidden, lower_weight, preferred_element_type=jnp.float32)
    )
    layer_out, normed_two, rstd_two = norm_forward(
        middle + branch + out_bias[1], gains[1], shifts[1]
    )
    stored = (
        wide_rows,
        projected,
        logsum,
        context,
        normed_one,
        rstd_one,
        middle_wide,
        before,
        hidden,
        normed_two,
        rstd_two,
    )
    return (layer_out, stored)


def segment_backward(weights, smalls, upstream, stored):
    proj_weight, inner_weight, outer_weight, lower_weight = weights
    qv_bias, out_bias, gains, shifts, inner_bias = smalls
    (
        wide_rows,
        projected,
        logsum,
        context,
        normed_one,
        rstd_one,
        middle_wide,
        before,
        hidden,
        normed_two,
        rstd_two,
    ) = stored
    batch, length, local = context.shape
    heads = local // DH
    grad_two, gain_two, shift_two = norm_backward(upstream, normed_two, rstd_two, gains[1])
    grad_branch = gather_grads(grad_two.astype(jnp.bfloat16))
    grad_lower = jnp.einsum("blf,bld->fd", hidden, grad_branch, preferred_element_type=jnp.float32)
    grad_hidden = jnp.einsum(
        "bld,fd->blf", grad_branch, lower_weight, preferred_element_type=jnp.float32
    )
    grad_before = (grad_hidden * gelu_slope(before)).astype(jnp.bfloat16)
    grad_inner = jnp.einsum(
        "bld,blf->df", middle_wide, grad_before, preferred_element_type=jnp.float32
    )
    grad_inner_bias = jnp.sum(grad_before.astype(jnp.float32), axis=(0, 1))
    grad_middle = grad_two + lax.psum_scatter(
        jnp.einsum(
            "blf,df->bld", grad_before, inner_weight, preferred_element_type=jnp.float32
        ).astype(jnp.bfloat16),
        "tensor",
        scatter_dimension=2,
        tiled=True,
    ).astype(jnp.float32)
    grad_one, gain_one, shift_one = norm_backward(grad_middle, normed_one, rstd_one, gains[0])
    grad_attended = gather_grads(grad_one.astype(jnp.bfloat16))
    grad_outer = jnp.einsum(
        "bld,blf->df", context, grad_attended, preferred_element_type=jnp.float32
    )
    grad_context = jnp.einsum(
        "blf,df->bld", grad_attended, outer_weight, preferred_element_type=jnp.float32
    )
    grad_context = grad_context.astype(jnp.bfloat16)
    grad_context = grad_context.reshape(batch, length, heads, DH)
    split = projected.reshape(batch, length, 3, heads, DH)
    query, key_rows, value_rows = (split[:, :, 0], split[:, :, 1], split[:, :, 2])
    probs = jnp.exp(attention_scores(query, key_rows) - logsum[..., None])
    grad_probs = jnp.einsum(
        "bqhe,bkhe->bhqk", grad_context, value_rows, preferred_element_type=jnp.float32
    )
    weighted_sum = jnp.sum(probs * grad_probs, axis=-1, keepdims=True)
    grad_scores = (probs * (grad_probs - weighted_sum)).astype(jnp.bfloat16)
    grad_query = jnp.einsum(
        "bhqk,bkhe->bqhe", grad_scores, key_rows, preferred_element_type=jnp.float32
    ) * DH ** (-0.5)
    grad_key = jnp.einsum(
        "bhqk,bqhe->bkhe", grad_scores, query, preferred_element_type=jnp.float32
    ) * DH ** (-0.5)
    grad_value = jnp.einsum(
        "bhqk,bqhe->bkhe",
        probs.astype(jnp.bfloat16),
        grad_context,
        preferred_element_type=jnp.float32,
    )
    grad_projected = (
        jnp.stack([grad_query, grad_key, grad_value], axis=2)
        .reshape(batch, length, 3, local)
        .astype(jnp.bfloat16)
    )
    grad_proj = jnp.einsum(
        "bld,blcf->dcf", wide_rows, grad_projected, preferred_element_type=jnp.float32
    )
    column_sums = jnp.sum(grad_projected.astype(jnp.float32), axis=(0, 1))
    grad_qv = jnp.stack([column_sums[0], column_sums[2]])
    grad_stacked = grad_one + input_sum(
        jnp.einsum("blcf,dcf->bld", grad_projected, proj_weight, preferred_element_type=jnp.float32)
    )
    grad_biases = jnp.stack([jnp.sum(grad_one, axis=(0, 1)), jnp.sum(grad_two, axis=(0, 1))])
    large_grads = (grad_proj, grad_inner, grad_outer, grad_lower)
    small_grads = (
        grad_qv,
        grad_biases,
        jnp.stack([gain_one, gain_two]),
        jnp.stack([shift_one, shift_two]),
        grad_inner_bias,
    )
    return (grad_stacked, large_grads, small_grads)


def add_tuples(first, second):
    return tuple((left + right for left, right in zip(first, second)))


def shards(
    tokens,
    memory,
    w_qkv,
    b_qv,
    w_out,
    out_biases,
    norm_gains,
    norm_shifts,
    w_in,
    b_in,
    w_down,
    cotangent,
    mlm_mask,
):
    smalls = (
        b_qv.astype(jnp.float32),
        out_biases.astype(jnp.float32),
        norm_gains.astype(jnp.float32),
        norm_shifts.astype(jnp.float32),
        b_in.astype(jnp.float32),
    )
    per_batch = tokens.shape[0] // MICRO
    segments = tokens.shape[1]
    mem_rows = memory.shape[0]
    local = w_qkv.shape[2]
    inner_local = w_in.shape[1]
    empty_large = (
        jnp.zeros((D, 3, local), jnp.float32),
        jnp.zeros((D, inner_local), jnp.float32),
        jnp.zeros((local, D), jnp.float32),
        jnp.zeros((inner_local, D), jnp.float32),
    )
    full_grads = empty_large
    shard_grads = (
        jnp.zeros(w_qkv.shape, jnp.float32),
        jnp.zeros(w_in.shape, jnp.float32),
        jnp.zeros(w_out.shape, jnp.float32),
        jnp.zeros(w_down.shape, jnp.float32),
    )
    small_total = (
        jnp.zeros((2, local), jnp.float32),
        jnp.zeros((2, local), jnp.float32),
        jnp.zeros((2, local), jnp.float32),
        jnp.zeros((2, local), jnp.float32),
        jnp.zeros((inner_local,), jnp.float32),
    )
    memory_total = jnp.zeros((mem_rows, local), jnp.float32)
    out_blocks = []
    grad_blocks = []
    for batch_index in range(MICRO):
        offset = batch_index * per_batch
        batch_tokens = tokens[offset : offset + per_batch]
        batch_mask = mlm_mask[offset : offset + per_batch]
        batch_cot = cotangent[offset : offset + per_batch].astype(jnp.float32) * batch_mask[
            ..., None
        ].astype(jnp.float32)
        weights = fetch_weights(w_qkv, w_in, w_out, w_down)
        carried = memory[None]
        stored_all = []
        token_outs = []
        for seg_index in range(segments):
            layer_out, stored = segment_forward(
                weights, smalls, carried, batch_tokens[:, seg_index]
            )
            carried = layer_out[:, :mem_rows].astype(jnp.bfloat16)
            token_outs.append(layer_out[:, mem_rows:].astype(jnp.bfloat16))
            stored_all.append(stored)
        returning = jnp.zeros((per_batch, mem_rows, local), jnp.float32)
        token_grads = [None] * segments
        for seg_index in reversed(range(segments)):
            upstream = jnp.concatenate([returning, batch_cot[:, seg_index]], axis=1)
            grad_stacked, large_grads, small_grads = segment_backward(
                weights, smalls, upstream, stored_all[seg_index]
            )
            returning = grad_stacked[:, :mem_rows]
            token_grads[seg_index] = grad_stacked[:, mem_rows:]
            full_grads = add_tuples(full_grads, large_grads)
            small_total = add_tuples(small_total, small_grads)
        memory_total = memory_total + jnp.sum(returning, axis=0)
        reduced = reduce_weights(full_grads[0], full_grads[1], full_grads[2], full_grads[3])
        shard_grads = add_tuples(shard_grads, reduced)
        full_grads = empty_large
        out_blocks.append(jnp.stack(token_outs, axis=1))
        grad_blocks.append(jnp.stack(token_grads, axis=1))
    grad_qv, grad_biases, grad_gains, grad_shifts, grad_inner_bias, memory_grad = lax.psum(
        (
            small_total[0],
            small_total[1],
            small_total[2],
            small_total[3],
            small_total[4],
            memory_total,
        ),
        "dp",
    )
    outputs = jnp.concatenate(out_blocks, axis=0)
    input_grad = jnp.concatenate(grad_blocks, axis=0)
    return (
        outputs,
        input_grad,
        memory_grad,
        shard_grads[0],
        grad_qv,
        shard_grads[2],
        grad_biases,
        grad_gains,
        grad_shifts,
        shard_grads[1],
        grad_inner_bias,
        shard_grads[3],
    )


ROWS = 528
LIVE = 176


def dot_nn(left, right):
    return jnp.dot(left, right, preferred_element_type=jnp.float32)


def dot_nt(left, right):
    return lax.dot_general(
        left, right, (((1,), (1,)), ((), ())), preferred_element_type=jnp.float32
    )


def dot_tn(left, right):
    return lax.dot_general(
        left, right, (((0,), (0,)), ((), ())), preferred_element_type=jnp.float32
    )


def norm_rows(resid, gain, shift):
    center = jnp.mean(resid, axis=-1, keepdims=True)
    spread = jnp.mean(resid * resid, axis=-1, keepdims=True) - center * center
    rstd = lax.rsqrt(spread + eps_norm)
    normed = (resid - center) * rstd
    return (normed * gain + shift, normed, rstd)


def norm_rows_back(upstream, normed, rstd, gain):
    scaled = upstream * gain
    first = jnp.mean(scaled, axis=-1, keepdims=True)
    second = jnp.mean(scaled * normed, axis=-1, keepdims=True)
    result = rstd * (scaled - first - normed * second)
    return (result, jnp.sum(upstream * normed, axis=0), jnp.sum(upstream, axis=0))


MESH = pl.DeviceIdType.MESH
HBM = pl.BlockSpec(memory_space=pl.ANY)
VMEM = pl.BlockSpec(memory_space=pltpu.VMEM)
GATHER_PIECES = ((0, 0), (1, 0), (2, 0), (3, 0), (4, 0), (5, 0), (4, 1), (5, 1), (4, 2), (5, 2), (4, 3), (5, 3))
SCATTER_PIECES = ((5, 0), (5, 1), (5, 2), (5, 3), (4, 0), (4, 1), (4, 2), (4, 3), (3, 0), (0, 0), (1, 0), (2, 0))
GATHER_HOPS = (
    (3, 2, 1, 0), (3, 2, 0, 1), (3, 2, 1, 0), (3, 0, 1, 2), (3, 2, 1, 0), (3, 1, 0, 2),
    (3, 2, 0, 1), (3, 2, 1, 0), (3, 0, 1, 2), (3, 2, 0, 1), (3, 2, 1, 0), (3, 0, 1, 2),
)
SCATTER_HOPS = (
    (2, 1, 0, 3), (0, 1, 2, 3), (1, 0, 2, 3), (2, 1, 0, 3), (0, 1, 2, 3), (2, 0, 3, 1),
    (0, 1, 2, 3), (1, 2, 0, 3), (0, 2, 1, 3), (0, 1, 2, 3), (1, 0, 2, 3), (1, 0, 2, 3),
)
GATHER_STEPS = (
    0, 8, 1, 100, 16, 9, 24, 2, 17, 32, 10, 40, 3, 25, 48, 18, 11, 56, 33, 64,
    41, 19, 49, 72, 57, 80, 4, 34, 26, 88, 5, 65, 101, 12, 50, 42, 73, 13, 102, 58,
    35, 20, 81, 66, 21, 89, 103, 27, 74, 104, 51, 82, 105, 59, 106, 43, 107, 67, 28, 29,
    36, 108, 52, 90, 37, 44, 53, 75, 83, 45, 109, 91, 68, 60, 69, 61, 76, 110, 77, 92,
    84, 111, 93, 85, 112, 113,
)
SCATTER_STEPS = (
    0, 8, 16, 1, 9, 17, 24, 32, 100, 25, 33, 2, 40, 10, 48, 18, 101, 41, 3, 49,
    26, 56, 34, 64, 11, 102, 19, 57, 27, 65, 4, 42, 103, 12, 35, 72, 20, 80, 5, 73,
    50, 88, 13, 28, 36, 81, 21, 58, 89, 29, 51, 104, 37, 105, 66, 106, 59, 107, 43, 108,
    52, 82, 109, 110, 67, 74, 44, 90, 60, 53, 68, 61, 83, 69, 75, 45, 84, 91, 76, 85,
    92, 77, 93,
)
SLOTS = 2


def here():
    me = lax.axis_index("dp")
    core = lax.axis_index("tensor")
    bits = tuple((me // (1 << b)) % 2 for b in range(4))
    peers = tuple({"dp": me + (1 - 2 * bits[b]) * (1 << b)} for b in range(4))
    return core, bits, peers + ({"tensor": 1 - core},)


def greet(peers):
    barrier = pltpu.get_barrier_semaphore()
    for peer in peers:
        pl.semaphore_signal(barrier, inc=1, device_id=peer, device_id_type=MESH)
    pl.semaphore_wait(barrier, len(peers))


def block_index(bits, free, flip=None):
    index = []
    for b in (3, 2, 1, 0):
        if b == flip:
            index.append(1 - bits[b])
        elif b in free:
            index.append(slice(None))
        else:
            index.append(bits[b])
    return tuple(index)


def columns(array, part, core, width):
    blocks = 4 if array > 3 else 1
    return pl.ds(pl.multiple_of((core * blocks + part) * width, width), width)


def shard_block(shards, piece, width):
    array, part = piece
    if array < 3:
        return shards[array].at[array]
    return shards[array].at[:, pl.ds(part * width, width)]


def attend_pair(query, key_rows, value_rows, valid):
    main = key_rows.shape[0] - 16
    lane = lax.broadcasted_iota(jnp.int32, (1, 2 * DH), 1)
    left = lane < DH
    query = query * DH ** (-0.5)
    zero = jnp.zeros_like(query)
    tail_lane = lax.broadcasted_iota(jnp.int32, (1, 32), 1)
    tail_zero = jnp.zeros((16, 2 * DH), query.dtype)
    key_tail, value_tail = key_rows[main:], value_rows[main:]
    keys_both = jnp.concatenate(
        [jnp.where(left, key_tail, tail_zero), jnp.where(left, tail_zero, key_tail)], axis=0
    )
    values_both = jnp.concatenate(
        [jnp.where(left, value_tail, tail_zero), jnp.where(left, tail_zero, value_tail)], axis=0
    )
    ones_both = jnp.concatenate(
        [jnp.where(left, tail_zero, tail_zero + 1), jnp.where(left, tail_zero + 1, tail_zero)], axis=0
    )
    tail = dot_nt(query, keys_both)
    tail = jnp.where(tail_lane % 16 < valid - main, tail, -1e30)
    peaks, parts = [], []
    for head in range(2):
        picked = jnp.where(left if head == 0 else ~left, query, zero)
        scores = dot_nt(picked, key_rows[:main])
        side = (tail_lane < 16) if head == 0 else (tail_lane >= 16)
        peak = jnp.maximum(
            jnp.max(scores, axis=1, keepdims=True),
            jnp.max(jnp.where(side, tail, -1e30), axis=1, keepdims=True),
        )
        expo = jnp.exp(scores - peak).astype(jnp.bfloat16)
        one = jnp.ones_like(value_rows[:main])
        values = jnp.where(left if head == 0 else ~left, value_rows[:main], one)
        parts.append(dot_nn(expo, values))
        peaks.append(peak)
    tail = jnp.exp(tail - jnp.where(tail_lane < 16, peaks[0], peaks[1])).astype(jnp.bfloat16)
    both = dot_nn(tail, jnp.concatenate([values_both, ones_both], axis=1))
    value_sum = jnp.where(left, parts[0], parts[1]) + both[:, : 2 * DH]
    total = jnp.where(left, parts[1], parts[0]) + both[:, 2 * DH :]
    return (value_sum / pltpu.roll(total, DH, 1)).astype(jnp.bfloat16)


def attend_kernel(valid, q_ref, k_ref, v_ref, out_ref):
    out_ref[...] = attend_pair(q_ref[...], k_ref[...], v_ref[...], valid)


def attend(query, key_rows, value_rows, valid):
    block = pl.BlockSpec((query.shape[0], 2 * DH), lambda i: (0, i))
    return pl.pallas_call(
        functools.partial(attend_kernel, valid),
        grid=(D // (2 * DH),),
        out_shape=jax.ShapeDtypeStruct(query.shape, jnp.bfloat16),
        in_specs=[block] * 3,
        out_specs=block,
        compiler_params=pltpu.CompilerParams(vmem_limit_bytes=32 << 20),
        name="attend",
    )(query, key_rows, value_rows)


def attend_back_pair(query, key_rows, value_rows, grads, valid):
    live = query.shape[0]
    left = lax.broadcasted_iota(jnp.int32, (1, 2 * DH), 1) < DH
    zero = jnp.zeros_like(query)
    query = query * DH ** (-0.5)
    picked = jnp.concatenate([jnp.where(left, query, zero), jnp.where(left, zero, query)], axis=0)
    up = jnp.concatenate([jnp.where(left, grads, zero), jnp.where(left, zero, grads)], axis=0)
    scores = dot_nt(key_rows, picked)
    scores = jnp.where(lax.broadcasted_iota(jnp.int32, scores.shape, 0) < valid, scores, -1e30)
    expo = jnp.exp(scores - jnp.max(scores, axis=0, keepdims=True))
    probs = expo * (1.0 / jnp.sum(expo, axis=0, keepdims=True))
    grad_probs = dot_nt(value_rows, up)
    weighted = jnp.sum(probs * grad_probs, axis=0, keepdims=True)
    grad_scores = (probs * (grad_probs - weighted)).astype(jnp.bfloat16)
    grad_query = dot_tn(grad_scores, key_rows)
    grad_query = jnp.where(left, grad_query[:live], grad_query[live:]) * DH ** (-0.5)
    grad_key = dot_nn(grad_scores, picked)
    grad_value = dot_nn(probs.astype(jnp.bfloat16), up)
    return tuple(grad.astype(jnp.bfloat16) for grad in (grad_query, grad_key, grad_value))


def attend_back_kernel(valid, q_ref, k_ref, v_ref, g_ref, dq_ref, dk_ref, dv_ref):
    dq_ref[...], dk_ref[...], dv_ref[...] = attend_back_pair(
        q_ref[...], k_ref[...], v_ref[...], g_ref[...], valid
    )


def attend_back(query, key_rows, value_rows, grad_context, valid):
    live = grad_context.shape[0]
    short = pl.BlockSpec((live, 2 * DH), lambda i: (0, i))
    tall = pl.BlockSpec((key_rows.shape[0], 2 * DH), lambda i: (0, i))
    low = jnp.bfloat16
    return pl.pallas_call(
        functools.partial(attend_back_kernel, valid),
        grid=(D // (2 * DH),),
        out_shape=[jax.ShapeDtypeStruct((live, D), low)] + [jax.ShapeDtypeStruct(key_rows.shape, low)] * 2,
        in_specs=[short, tall, tall, short],
        out_specs=[short, tall, tall],
        compiler_params=pltpu.CompilerParams(vmem_limit_bytes=32 << 20),
        name="attend_back",
    )(query, key_rows, value_rows, grad_context)


PACK_BIASES, PACK_OUT, PACK_GAINS, PACK_SHIFTS, PACK_INNER = 16, 18, 20, 22, 24


def gather_kernel(
    mem_rows, valid, toks, cots, pack, sq, so, si, sl, move, live_move,
    packs, fq, fk, fv, fo, fi, fl, stacked_a, moved_b, ups, query, key_rows, value_rows,
    context_live, normed_one, rstd_one, middle_live, before_live, hidden_live, normed_two, rstd_two, low_out,
    x_v, c_v, vq, vo, vi, vl, held, context, middle, middle_low, branch,
    send, recv, local, loads, extra,
):
    core, bits, peers = here()
    width = pack.shape[1]
    live = ups.shape[1]
    shards = (vq, vq, vq, vo, vi, vl)
    fulls = (fq, fk, fv, fo, fi, fl)
    mine = pl.ds(pl.multiple_of(core * width, width), width)
    shard_in = [
        pltpu.make_async_copy(src, dst, extra.at[n])
        for n, (src, dst) in enumerate(((sq, vq), (so, vo), (si, vi), (sl, vl)))
    ]
    rows_own = [
        pltpu.make_async_copy(toks.at[core], x_v.at[:, :, mine], extra.at[4]),
        pltpu.make_async_copy(cots.at[core], c_v.at[:, :, mine], extra.at[5]),
        pltpu.make_async_copy(pack, packs.at[core], extra.at[6]),
    ]
    for copy in shard_in + rows_own:
        copy.start()
    own = []
    for p, (array, part) in enumerate(GATHER_PIECES):
        own.append(pltpu.make_async_copy(
            shard_block(shards, (array, part), width),
            fulls[array].at[block_index(bits, ()) + (slice(None), columns(array, part, core, width))],
            local.at[p],
        ))
    greet(peers)
    for copy in shard_in:
        copy.wait()
    for copy in own:
        copy.start()

    def remote(src, dst, slot, peer):
        return pltpu.make_async_remote_copy(
            src_ref=src, dst_ref=dst, send_sem=send.at[slot], recv_sem=recv.at[slot],
            device_id=peer, device_id_type=MESH)

    def stage(p, s):
        array, part = GATHER_PIECES[p]
        order = GATHER_HOPS[p]
        cols = columns(array, part, core, width)
        dst = fulls[array].at[block_index(bits, order[:s]) + (slice(None), cols)]
        if s == 0:
            src = shard_block(shards, (array, part), width)
        else:
            src = dst
        peer = peers[order[s]] if s < 4 else peers[4]
        return remote(src, dst, p * 5 + s, peer)

    swaps = [
        remote(toks.at[1 - core], x_v.at[:, :, mine], 60, peers[4]),
        remote(cots.at[1 - core], c_v.at[:, :, mine], 61, peers[4]),
        remote(pack, packs.at[core], 62, peers[4]),
    ]
    started, loading = {}, {}

    def load(p):
        array, part = GATHER_PIECES[p]
        blocks = 4 if array > 3 else 1
        every = (slice(None),) * 5
        loading[p] = [
            pltpu.make_async_copy(
                fulls[array].at[every + (pl.ds((half * blocks + part) * width, width),)],
                held.at[(p % 6,) + every + (pl.ds(half * width, width),)],
                loads.at[2 * p + half],
            )
            for half in range(2)
        ]
        for copy in loading[p]:
            copy.start()

    def loaded(p):
        for copy in loading.pop(p):
            copy.wait()

    def weight(p, cols):
        block = held[p % 6, :, :, :, :, :, cols]
        return block.reshape(2 * width, block.shape[-1])

    def wide(row):
        return jnp.concatenate([packs[0, row : row + 1], packs[1, row : row + 1]], axis=1).astype(jnp.float32)

    def norm(resid, gain, shift):
        center = jnp.mean(resid, axis=1, keepdims=True)
        spread = jnp.mean(resid * resid, axis=1, keepdims=True) - center * center
        rstd = lax.rsqrt(spread + eps_norm)
        normed = (resid - center) * rstd
        return normed * gain + shift, normed, rstd

    def compute(task):
        if task == 0:
            for copy in rows_own:
                copy.wait()
            for swap in swaps:
                swap.wait_recv()
            memory = jnp.concatenate([packs[0, :16], packs[1, :16]], axis=1)
            is_memory = lax.broadcasted_iota(jnp.int32, memory.shape, 0) < mem_rows
            stacked_a[...] = dot_nn(move[0], x_v[0]).astype(jnp.bfloat16)
            stacked_a[:16] = jnp.where(is_memory, memory, stacked_a[:16])
            moved_b[...] = dot_nn(move[1], x_v[1]).astype(jnp.bfloat16)
            for n in range(2):
                ups[n] = dot_nn(live_move[n], c_v[n]).astype(jnp.bfloat16)
        elif task < 4:
            n = task - 1
            loaded(n)
            target = (query, key_rows, value_rows)[n]
            for half in range(2):
                cols = pl.ds(half * width, width)
                got = dot_nn(stacked_a[...], weight(n, cols))
                if n != 1:
                    row = PACK_BIASES + n // 2
                    got = got + packs[half, row : row + 1].astype(jnp.float32)
                target[:, cols] = got.astype(jnp.bfloat16)
        elif task < 8:

            def pair(n, carry):
                cols = pl.ds(pl.multiple_of((2 * (task - 4) + n) * 2 * DH, 2 * DH), 2 * DH)
                context[:, cols] = attend_pair(query[:, cols], key_rows[:, cols], value_rows[:, cols], valid)
                return carry

            lax.fori_loop(0, 2, pair, 0)
        elif task == 8:
            loaded(3)
            attended = dot_nt(context[...], weight(3, slice(None)))
            resid = stacked_a[...].astype(jnp.float32) + attended + wide(PACK_OUT)
            value, normed, rstd = norm(resid, wide(PACK_GAINS), wide(PACK_SHIFTS))
            middle[...] = value
            middle_low[...] = value.astype(jnp.bfloat16)
            middle_live[...] = value[:live].astype(jnp.bfloat16)
            context_live[...] = context[:live]
            normed_one[...] = normed[:live]
            rstd_one[...] = jnp.broadcast_to(rstd[:live], rstd_one.shape)
        elif task < 13:
            j = task - 9
            loaded(4 + 2 * j)
            loaded(5 + 2 * j)

            def hidden_block(half, carry):
                cols = pl.ds(pl.multiple_of(half * width, width), width)
                place = pl.ds(pl.multiple_of((half * 4 + j) * width, width), width)
                bias = packs[half, PACK_INNER + j : PACK_INNER + j + 1].astype(jnp.float32)
                before = dot_nn(middle_low[...], weight(4 + 2 * j, cols)) + bias
                before_live[:, place] = before[:live]
                hidden = gelu_value(before).astype(jnp.bfloat16)
                hidden_live[:, place] = hidden[:live]
                branch[...] = branch[...] + dot_nt(hidden, weight(5 + 2 * j, cols))
                return carry

            if j == 0:
                branch[...] = middle[...] + wide(PACK_OUT + 1)
            lax.fori_loop(0, 2, hidden_block, 0)
        else:
            value, normed, rstd = norm(branch[...], wide(PACK_GAINS + 1), wide(PACK_SHIFTS + 1))
            low_out[...] = value.astype(jnp.bfloat16)
            normed_two[...] = normed[:live]
            rstd_two[...] = jnp.broadcast_to(rstd[:live], rstd_two.shape)

    for tick, step in enumerate(GATHER_STEPS):
        if step >= 100:
            compute(step - 100)
            continue
        p, s = step // 8, step % 8
        if s > 0:
            started[p, s - 1].wait_recv()
        if s == 1:
            own[p].wait()
        if s == 5:
            load(p)
        else:
            started[p, s] = stage(p, s)
            started[p, s].start()
        if tick == 2:
            for swap in swaps:
                swap.start()
    for copy in started.values():
        copy.wait_send()
    for swap in swaps:
        swap.wait_send()


def gather_all(mem_rows, valid, toks, cots, pack, sq, so, si, sl, move, live_move):
    width = pack.shape[1]
    rows = sq.shape[1]
    low, full = jnp.bfloat16, jnp.float32
    total, live = move.shape[1], live_move.shape[1]
    hidden = 2 * si.shape[1]
    out = [((2,) + pack.shape, low)]
    for size in (2 * width, 2 * width, 2 * width, 2 * width, hidden, hidden):
        out.append(((2, 2, 2, 2, rows, size), low))
    out += [((total, 2 * width), low)] * 2 + [((2, live, 2 * width), low)]
    out += [((total, 2 * width), low)] * 3 + [((live, 2 * width), low)]
    out += [((live, 2 * width), full), ((live, 2 * width), full), ((live, 2 * width), low)]
    out += [((live, hidden), full), ((live, hidden), low)]
    out += [((live, 2 * width), full), ((live, 2 * width), full), ((total, 2 * width), low)]
    block = (2, 2, 2, 2, rows, 2 * width)
    got = pl.pallas_call(
        functools.partial(gather_kernel, mem_rows, valid),
        out_shape=[jax.ShapeDtypeStruct(*one) for one in out],
        in_specs=[HBM, HBM, VMEM] + [HBM] * 4 + [VMEM] * 2,
        out_specs=[VMEM] + [HBM] * 6 + [VMEM] * (len(out) - 7),
        scratch_shapes=[
            pltpu.VMEM(toks.shape[1:3] + (2 * width,), low),
            pltpu.VMEM(toks.shape[1:3] + (2 * width,), low),
            pltpu.VMEM(sq.shape, low),
            pltpu.VMEM(so.shape, low),
            pltpu.VMEM(si.shape, low),
            pltpu.VMEM(sl.shape, low),
            pltpu.VMEM((6,) + block, low),
            pltpu.VMEM((total, 2 * width), low),
            pltpu.VMEM((total, 2 * width), full),
            pltpu.VMEM((total, 2 * width), low),
            pltpu.VMEM((total, 2 * width), full),
            pltpu.SemaphoreType.DMA((63,)),
            pltpu.SemaphoreType.DMA((63,)),
            pltpu.SemaphoreType.DMA((12,)),
            pltpu.SemaphoreType.DMA((24,)),
            pltpu.SemaphoreType.DMA((7,)),
        ],
        compiler_params=pltpu.CompilerParams(collective_id=0, has_side_effects=True, vmem_limit_bytes=62 << 20),
        name="gather_all",
    )(toks, cots, pack, sq, so, si, sl, move, live_move)
    wide = [array.reshape(16 * rows, array.shape[-1]) for array in got[1:7]]
    return got[0], wide, got[7:]


def scatter_kernel(mem_rows, valid, *refs):
    (rows_a, out_a, context_a, middle_a, before_a, branch_a, hidden_a) = refs[0:7]
    second_rows = refs[7:17]
    query, keys_in, values_in, up, grad_one, wq, wk, wv, move, small, outs_a, outs_b, grads_b = refs[17:30]
    oq, oo, oi, ol, osmall, out_item, grad_item = refs[30:37]
    (acc, first, second, third, fourth, slots, wide_x, wide_s, held, grad_query, key_rows, value_rows,
     source, result, total_rows, small_v, small_in, small_recv, send, recv, extra, sent) = refs[37:]
    first_rows = (rows_a, grad_query, key_rows, value_rows, out_a, context_a, middle_a, before_a, branch_a, hidden_a)
    core, bits, peers = here()
    width = osmall.shape[1]
    live = grad_query.shape[0]
    bufs = (first, second, third, fourth)
    lefts = (0, 0, 0, 4, 6, 8)
    rights = (1, 2, 3, 5, 7, 9)
    turned = set()
    mine = pl.ds(pl.multiple_of(core * width, width), width)
    other = pl.ds(pl.multiple_of((1 - core) * width, width), width)
    stage_in = [
        pltpu.make_async_copy(keys_in, key_rows, extra.at[0]),
        pltpu.make_async_copy(values_in, value_rows, extra.at[1]),
    ]
    for copy in stage_in:
        copy.start()
    greet(peers)

    def bring(src, dst, sem):
        copy = pltpu.make_async_copy(src, dst, extra.at[sem])
        copy.start()
        return copy

    def remote(src, dst, slot, peer):
        return pltpu.make_async_remote_copy(
            src_ref=src, dst_ref=dst, send_sem=send.at[slot], recv_sem=recv.at[slot],
            device_id=peer, device_id_type=MESH)

    def turn(array):
        left = lefts[array]
        if left in turned:
            return
        turned.add(left)
        for n, rows in enumerate((first_rows, second_rows)):
            if left == 0:
                bring(rows[0], source, 2).wait()
                wide_x[n] = source[...].T
            else:
                wide_s[left // 2 - 2, n] = rows[left][...].T

    def multiply(array, offset, size):
        total = None
        for n, rows in enumerate((first_rows, second_rows)):
            right = rows[rights[array]][:, pl.ds(offset, size)]
            if array in (1, 2):
                left = wide_x[n]
            elif array == 0:
                left = wide_x[n, :, :live]
            else:
                left = wide_s[lefts[array] // 2 - 2, n]
            term = jnp.dot(left, right, preferred_element_type=jnp.float32)
            total = term if total is None else total + term
        return total

    tile = width // 2

    def produce(p, slot):
        array, part = SCATTER_PIECES[p]
        turn(array)
        blocks = 4 if array > 3 else 1
        base = ((1 - core) * blocks + part) * width

        def body(n, carry):
            offset = pl.multiple_of(base + n * tile, tile)
            got = multiply(array, offset, tile).astype(jnp.bfloat16)
            slots[slot, :, :, :, :, :, pl.ds(pl.multiple_of(n * tile, tile), tile)] = got.reshape(
                slots.shape[1:6] + (tile,)
            )
            return carry

        lax.fori_loop(0, 2, body, 0)

    def combine(p):
        array, part = SCATTER_PIECES[p]
        blocks = 4 if array > 3 else 1
        base = (core * blocks + part) * width

        def body(n, carry):
            offset = pl.multiple_of(base + n * tile, tile)
            cols = pl.ds(pl.multiple_of(n * tile, tile), tile)
            got = multiply(array, offset, tile).reshape(slots.shape[1:6] + (tile,))
            acc[p, :, :, :, :, :, cols] = (
                got + acc[p, :, :, :, :, :, cols].astype(jnp.float32)
            ).astype(jnp.bfloat16)
            return carry

        lax.fori_loop(0, 2, body, 0)

    def stage(p, s):
        if s == 0:
            return remote(slots.at[p % SLOTS], acc.at[p], p * 5, peers[4])
        order = SCATTER_HOPS[p]
        src = acc.at[(p,) + block_index(bits, order[s:], flip=order[s - 1])]
        return remote(src, bufs[s - 1].at[p], p * 5 + s, peers[order[s - 1]])

    def fold(p, s):
        array, part = SCATTER_PIECES[p]
        order = SCATTER_HOPS[p]
        free = [b for b in (3, 2, 1, 0) if b in order[s:]]
        for n in range(1 << len(free)):
            at = {b: (n >> i) % 2 for i, b in enumerate(reversed(free))}
            where = tuple(at.get(b, bits[b]) for b in (3, 2, 1, 0))
            got = bufs[s - 1][(p,) + tuple(at[b] for b in free)]
            if s < 4:
                acc[(p,) + where] = acc[(p,) + where] + got
            else:
                total = acc[(p,) + where].astype(jnp.float32) + got.astype(jnp.float32)
                if array < 3:
                    oq[array] = total
                elif array == 4:
                    oi[:, pl.ds(part * width, width)] = total
                elif array == 3:
                    oo[...] = total
                else:
                    ol[:, pl.ds(part * width, width)] = total

    small_started = {}

    def small_stage(s):
        peer = peers[4] if s == 0 else peers[s - 1]
        src = small_v.at[:, other] if s == 0 else small_in.at[s]
        return remote(src, small_recv.at[s], 60 + s, peer)

    def small_step(n):
        if n == 0:
            small_in[0] = small_v[:, mine]
        else:
            small_started[n - 1].wait_recv()
            total = small_in[n - 1] + small_recv[n - 1]
            if n < 5:
                small_in[n] = total
            else:
                osmall[...] = total
        if n < 5:
            small_started[n] = small_stage(n)
            small_started[n].start()

    swaps, places = [], []

    def unpermute(n, values, target, segment):
        if n > 1:
            swaps[n - 2].wait_send()
            places[n - 2].wait()
        result[n % 2] = dot_tn(move[segment], values).astype(jnp.bfloat16)
        places.append(
            pltpu.make_async_copy(result.at[n % 2, :, mine], target.at[core, segment], sent.at[n])
        )
        swaps.append(remote(result.at[n % 2, :, other], target.at[core, segment], 65 + n, peers[4]))
        places[n].start()
        swaps[n].start()

    weights = (wk, wv, wq)
    fetched = {}

    def compute(task):
        if task < 4:
            if task == 0:
                for copy in stage_in:
                    copy.wait()
                fetched[0] = bring(weights[0], held, 3)

            def pair(n, carry):
                cols = pl.ds(pl.multiple_of((2 * task + n) * 2 * DH, 2 * DH), 2 * DH)
                grad_query[:, cols], key_rows[:, cols], value_rows[:, cols] = attend_back_pair(
                    query[:, cols], key_rows[:, cols], value_rows[:, cols], up[:, cols], valid
                )
                return carry

            lax.fori_loop(0, 2, pair, 0)
        elif task < 7:
            n = task - 4
            fetched[n].wait()
            if n == 0:
                total_rows[...] = dot_nt(key_rows[...], held[...])
            elif n == 1:
                total_rows[...] = total_rows[...] + dot_nt(value_rows[...], held[...])
            else:
                total_rows[:live] = total_rows[:live] + grad_one[...] + dot_nt(grad_query[...], held[...])
                row = lax.broadcasted_iota(jnp.int32, (16, 2 * width), 0)
                small_v[...] = small[...]
                small_v[:16] = jnp.where(row < mem_rows, total_rows[:16], 0.0)
                query_sum = jnp.sum(grad_query[...].astype(jnp.float32), axis=0, keepdims=True)
                value_sum = jnp.sum(value_rows[...].astype(jnp.float32), axis=0, keepdims=True)
                small_v[16:24] = small[16:24] + jnp.where(
                    row[:8] == 0, query_sum, jnp.where(row[:8] == 1, value_sum, 0.0)
                )
            if n < 2:
                fetched[n + 1] = bring(weights[n + 1], held, 3)
        elif task == 7:
            unpermute(0, total_rows[...].astype(jnp.bfloat16), grad_item, 0)
        else:
            values, target, segment = (
                (outs_a, out_item, 0),
                (outs_b, out_item, 1),
                (grads_b, grad_item, 1),
            )[task - 8]
            bring(values, source, 2).wait()
            unpermute(task - 7, source[...], target, segment)

    started = {}
    ready = None
    for step in SCATTER_STEPS:
        if step >= 100:
            compute(step - 100)
            if step == 106:
                ready = 0
            continue
        p, s = step // 8, step % 8
        if s == 0:
            if p >= SLOTS:
                started[p - SLOTS, 0].wait_send()
            produce(p, p % SLOTS)
        else:
            started[p, s - 1].wait_recv()
            if s == 1:
                combine(p)
            else:
                fold(p, s - 1)
        if s < 5:
            started[p, s] = stage(p, s)
            started[p, s].start()
        if ready is not None:
            ready += 1
            if ready % 3 == 0 and ready <= 18:
                small_step(ready // 3 - 1)
    for (p, s), copy in started.items():
        if s > 0 or p >= len(SCATTER_PIECES) - SLOTS:
            copy.wait_send()
    for s in range(5):
        small_started[s].wait_send()
    for n in range(4):
        if n > 1:
            swaps[n].wait_send()
            places[n].wait()
        swaps[n].wait_recv()


def scatter_all(mem_rows, valid, first_rows, second_rows, tail, small, outs, grads):
    width = small.shape[1] // 2
    rows = 2 * width // 16
    low, full = jnp.bfloat16, jnp.float32
    count = len(SCATTER_PIECES)
    long, live = second_rows[0].shape[0], second_rows[1].shape[0]
    move = tail[-1]
    tokens = move.shape[2]
    item = (2, 2, tokens, width)
    return pl.pallas_call(
        functools.partial(scatter_kernel, mem_rows, valid),
        out_shape=[
            jax.ShapeDtypeStruct((3, rows, width), full),
            jax.ShapeDtypeStruct((rows, width), full),
            jax.ShapeDtypeStruct((rows, 4 * width), full),
            jax.ShapeDtypeStruct((rows, 4 * width), full),
            jax.ShapeDtypeStruct((small.shape[0], width), full),
            jax.ShapeDtypeStruct(item, low),
            jax.ShapeDtypeStruct(item, low),
        ],
        in_specs=[HBM] + [VMEM] * 6 + [HBM] + [VMEM] * 9
        + [VMEM, HBM, HBM, VMEM, VMEM, HBM, HBM, HBM, VMEM, VMEM, HBM, HBM, HBM],
        out_specs=[VMEM] * 5 + [HBM] * 2,
        scratch_shapes=[
            pltpu.VMEM((count, 2, 2, 2, 2, rows, width), low),
            pltpu.VMEM((count, 2, 2, 2, rows, width), low),
            pltpu.VMEM((count, 2, 2, rows, width), low),
            pltpu.VMEM((count, 2, rows, width), low),
            pltpu.VMEM((count, rows, width), low),
            pltpu.VMEM((SLOTS, 2, 2, 2, 2, rows, width), low),
            pltpu.VMEM((2, 2 * width, long), low),
            pltpu.VMEM((3, 2, 2 * width, live), low),
            pltpu.VMEM((2 * width, 2 * width), low),
            pltpu.VMEM((live, 2 * width), low),
            pltpu.VMEM((long, 2 * width), low),
            pltpu.VMEM((long, 2 * width), low),
            pltpu.VMEM((long, 2 * width), low),
            pltpu.VMEM((2, tokens, 2 * width), low),
            pltpu.VMEM((long, 2 * width), full),
            pltpu.VMEM(small.shape, full),
            pltpu.VMEM((5, small.shape[0], width), full),
            pltpu.VMEM((5, small.shape[0], width), full),
            pltpu.SemaphoreType.DMA((69,)),
            pltpu.SemaphoreType.DMA((69,)),
            pltpu.SemaphoreType.DMA((4,)),
            pltpu.SemaphoreType.DMA((4,)),
        ],
        compiler_params=pltpu.CompilerParams(collective_id=1, has_side_effects=True, vmem_limit_bytes=67_000_000),
        name="scatter_all",
    )(*first_rows, *second_rows, *tail[:-1], move, small, *outs, *grads)


def item_shards(
    tokens,
    memory,
    w_qkv,
    b_qv,
    w_out,
    out_biases,
    norm_gains,
    norm_shifts,
    w_in,
    b_in,
    w_down,
    cotangent,
    mlm_mask,
):
    core = lax.axis_index("tensor")
    segments, count = tokens.shape[1], tokens.shape[2]
    mem_rows = memory.shape[0]
    valid = mem_rows + count
    half = memory.shape[1]

    mask = lax.dynamic_index_in_dim(mlm_mask, core, 0, keepdims=False)
    lower_tri = (
        lax.broadcasted_iota(jnp.int32, (count, count), 0)
        <= lax.broadcasted_iota(jnp.int32, (count, count), 1)
    ).astype(jnp.bfloat16)
    ones = mask.astype(jnp.bfloat16)
    upto = dot_nn(ones, lower_tri).astype(jnp.int32)
    total = upto[:, -1:]
    index = lax.broadcasted_iota(jnp.int32, mask.shape, 1)
    place = mem_rows + jnp.where(mask > 0, upto - 1, total + index - upto)
    move = (
        lax.broadcasted_iota(jnp.int32, (segments, ROWS, count), 1) == place[:, None, :]
    ).astype(jnp.bfloat16)
    live_move = move[:, :LIVE] * ones[:, None, :]

    packed = jnp.concatenate(
        [
            jnp.pad(memory, ((0, PACK_BIASES - mem_rows), (0, 0))),
            b_qv,
            out_biases,
            norm_gains,
            norm_shifts,
            b_in.reshape(-1, half),
        ],
        axis=0,
    )
    packed = jnp.pad(packed, ((0, -packed.shape[0] % 16), (0, 0)))
    both, (wq, wk, wv, outer, inner, lower), first = gather_all(
        mem_rows,
        valid,
        tokens,
        cotangent,
        packed,
        w_qkv.transpose(1, 0, 2),
        w_out.T,
        w_in,
        w_down.T,
        move,
        live_move,
    )
    (
        stacked,
        moved,
        ups,
        query,
        key_rows,
        value_rows,
        context,
        normed_one,
        rstd_one,
        middle_low,
        before,
        hidden,
        normed_two,
        rstd_two,
        low_out,
    ) = first
    wide = jnp.concatenate([both[0], both[1]], axis=1).astype(jnp.float32)
    qv_bias, out_bias, gains, shifts = (
        wide[n : n + 2] for n in (PACK_BIASES, PACK_OUT, PACK_GAINS, PACK_SHIFTS)
    )
    inner_rows = b_in.shape[0] // half
    inner_bias = both[:, PACK_INNER : PACK_INNER + inner_rows].reshape(-1).astype(jnp.float32)
    stored = [
        (
            stacked,
            query,
            key_rows,
            value_rows,
            context,
            normed_one,
            rstd_one,
            middle_low,
            before,
            hidden,
            normed_two,
            rstd_two,
        )
    ]
    outs = [low_out]
    stacked = jnp.concatenate([low_out[:mem_rows], moved[mem_rows:]], axis=0)
    query = (dot_nn(stacked, wq) + qv_bias[0]).astype(jnp.bfloat16)
    key_rows = dot_nn(stacked, wk).astype(jnp.bfloat16)
    value_rows = (dot_nn(stacked, wv) + qv_bias[1]).astype(jnp.bfloat16)
    context = attend(query, key_rows, value_rows, valid)
    attended = dot_nt(context, outer)
    middle, normed_one, rstd_one = norm_rows(
        stacked.astype(jnp.float32) + attended + out_bias[0], gains[0], shifts[0]
    )
    middle_low = middle.astype(jnp.bfloat16)
    before = dot_nn(middle_low, inner) + inner_bias
    hidden = gelu_value(before).astype(jnp.bfloat16)
    branch = dot_nt(hidden, lower)
    layer_out, normed_two, rstd_two = norm_rows(
        middle + branch + out_bias[1], gains[1], shifts[1]
    )
    low_out = layer_out.astype(jnp.bfloat16)
    outs.append(low_out)
    stored.append(
        (
            stacked,
            query,
            key_rows,
            value_rows,
            context[:LIVE],
            normed_one[:LIVE],
            rstd_one[:LIVE],
            middle_low[:LIVE],
            before[:LIVE],
            hidden[:LIVE],
            normed_two[:LIVE],
            rstd_two[:LIVE],
        )
    )

    returning = jnp.zeros((mem_rows, D), jnp.float32)
    token_grads = []
    pieces = [None] * segments
    smalls = None
    for seg in reversed(range(segments)):
        (
            stacked,
            query,
            key_rows,
            value_rows,
            context,
            normed_one,
            rstd_one,
            middle_low,
            before,
            hidden,
            normed_two,
            rstd_two,
        ) = stored[seg]
        upstream = ups[seg].astype(jnp.float32)
        upstream = upstream + jnp.pad(returning, ((0, LIVE - mem_rows), (0, 0)))
        grad_two, gain_two, shift_two = norm_rows_back(upstream, normed_two, rstd_two, gains[1])
        grad_branch = grad_two.astype(jnp.bfloat16)
        grad_hidden = dot_nn(grad_branch, lower)
        grad_before = (grad_hidden * gelu_slope(before)).astype(jnp.bfloat16)
        grad_middle = grad_two + dot_nt(grad_before, inner)
        grad_one, gain_one, shift_one = norm_rows_back(
            grad_middle, normed_one, rstd_one, gains[0]
        )
        grad_attended = grad_one.astype(jnp.bfloat16)
        grad_context = dot_nn(grad_attended, outer).astype(jnp.bfloat16)
        sums = [jnp.zeros((D,), jnp.float32)] * 2
        if seg > 0:
            grad_query, grad_key, grad_value = attend_back(
                query, key_rows, value_rows, grad_context, valid
            )
            grad_stacked = dot_nt(grad_key, wk) + dot_nt(grad_value, wv)
            live_part = grad_one + dot_nt(grad_query, wq)
            grad_stacked = grad_stacked + jnp.pad(live_part, ((0, ROWS - LIVE), (0, 0)))
            returning = grad_stacked[:mem_rows]
            token_grads.append(grad_stacked.astype(jnp.bfloat16))
            attention_grads = [grad_query, grad_key, grad_value]
            sums = [jnp.sum(grad.astype(jnp.float32), axis=0) for grad in (grad_query, grad_value)]
        else:
            attention_grads = []
            tail = [query[:LIVE], key_rows, value_rows, grad_context, grad_one, wq, wk, wv, move]
        pieces[seg] = (
            stacked,
            *attention_grads,
            grad_attended,
            context,
            middle_low,
            grad_before,
            grad_branch,
            hidden,
        )
        sums = jnp.concatenate(
            [
                jnp.stack(
                    [
                        *sums,
                        jnp.sum(grad_one, axis=0),
                        jnp.sum(grad_two, axis=0),
                        gain_one,
                        gain_two,
                        shift_one,
                        shift_two,
                    ]
                ),
                jnp.sum(grad_before.astype(jnp.float32), axis=0).reshape(-1, D),
            ],
            axis=0,
        )
        smalls = sums if smalls is None else smalls + sums

    inner_sums = smalls[8:].reshape(2, inner_rows, half).transpose(1, 0, 2).reshape(inner_rows, D)
    small = jnp.concatenate([jnp.zeros((16, D), jnp.float32), smalls[:8], inner_sums], axis=0)
    small = jnp.pad(small, ((0, -small.shape[0] % 8), (0, 0)))
    grad_proj, grad_outer, grad_inner, grad_lower, mine, outputs, input_grad = scatter_all(
        mem_rows, valid, pieces[0], pieces[1], tail, small, outs, token_grads
    )
    return (
        outputs,
        input_grad.astype(jnp.float32),
        mine[:mem_rows],
        grad_proj.transpose(1, 0, 2),
        mine[16:18],
        grad_outer.T,
        mine[18:20],
        mine[20:22],
        mine[22:24],
        grad_inner,
        mine[24 : 24 + inner_rows].reshape(-1),
        grad_lower.T,
    )


def solution(mesh):
    def body(*arrays):
        if mesh.shape["dp"] == 16 and mesh.shape["tensor"] == arrays[0].shape[0] == arrays[0].shape[1] == 2:
            return item_shards(*arrays)
        return shards(*arrays)

    placed = (
        P("dp", None, None, "tensor"),
        P(None, "tensor"),
        P("dp", None, "tensor"),
        P(None, "tensor"),
        P("tensor", "dp"),
        P(None, "tensor"),
        P(None, "tensor"),
        P(None, "tensor"),
        P("dp", "tensor"),
        P("tensor"),
        P("tensor", "dp"),
        P("dp", None, None, "tensor"),
        P("dp", None, None),
    )
    return jax.shard_map(
        body,
        mesh=mesh,
        in_specs=placed,
        out_specs=(
            P("dp", None, None, "tensor"),
            P("dp", None, None, "tensor"),
            P(None, "tensor"),
            P("dp", None, "tensor"),
            P(None, "tensor"),
            P("tensor", "dp"),
            P(None, "tensor"),
            P(None, "tensor"),
            P(None, "tensor"),
            P("dp", "tensor"),
            P("tensor"),
            P("tensor", "dp"),
        ),
        check_vma=False,
    )
```

```python
import functools

import jax
import jax.numpy as jnp
from jax import lax
from jax.experimental import pallas as pl
from jax.experimental.pallas import tpu as pltpu
from jax.sharding import PartitionSpec as P

D = 1024
DH = 64
MICRO = 2


eps_norm = 1e-05
root_half = 0.7071067811865476
inv_root_two_pi = 0.3989422804014327


def gelu_value(before):
    return 0.5 * before * (1.0 + lax.erf(before * root_half))


def gelu_slope(before):
    return 0.5 * (1.0 + lax.erf(before * root_half)) + before * inv_root_two_pi * jnp.exp(
        -0.5 * before * before
    )


def fetch_weights(w_qkv, w_in, w_out, w_down):
    return (
        lax.all_gather(w_qkv, "dp", axis=0, tiled=True),
        lax.all_gather(w_in, "dp", axis=0, tiled=True),
        lax.all_gather(w_out, "dp", axis=1, tiled=True),
        lax.all_gather(w_down, "dp", axis=1, tiled=True),
    )


def reduce_weights(grad_proj, grad_inner, grad_outer, grad_lower):
    return (
        lax.psum_scatter(
            grad_proj.astype(jnp.bfloat16), "dp", scatter_dimension=0, tiled=True
        ).astype(jnp.float32),
        lax.psum_scatter(
            grad_inner.astype(jnp.bfloat16), "dp", scatter_dimension=0, tiled=True
        ).astype(jnp.float32),
        lax.psum_scatter(
            grad_outer.astype(jnp.bfloat16), "dp", scatter_dimension=1, tiled=True
        ).astype(jnp.float32),
        lax.psum_scatter(
            grad_lower.astype(jnp.bfloat16), "dp", scatter_dimension=1, tiled=True
        ).astype(jnp.float32),
    )


def gather_rows(block):
    return lax.all_gather(block, "tensor", axis=2, tiled=True)


def branch_sum(partial_value):
    return lax.psum_scatter(partial_value, "tensor", scatter_dimension=2, tiled=True)


def gather_grads(block):
    return lax.all_gather(block, "tensor", axis=2, tiled=True)


def input_sum(partial_value):
    return lax.psum_scatter(
        partial_value.astype(jnp.bfloat16), "tensor", scatter_dimension=2, tiled=True
    ).astype(jnp.float32)


def norm_forward(resid, gain, shift):
    totals = jnp.sum(resid, axis=-1)
    squares = jnp.sum(resid * resid, axis=-1)
    totals, squares = lax.psum((totals, squares), "tensor")
    center = totals / D
    spread = squares / D - center * center
    rstd = lax.rsqrt(spread + eps_norm)
    normed = (resid - center[..., None]) * rstd[..., None]
    return (normed * gain + shift, normed, rstd)


def norm_backward(upstream, normed, rstd, gain):
    scaled = upstream * gain
    first = jnp.sum(scaled, axis=-1)
    second = jnp.sum(scaled * normed, axis=-1)
    first, second = lax.psum((first, second), "tensor")
    result = rstd[..., None] * (scaled - first[..., None] / D - normed * (second[..., None] / D))
    return (result, jnp.sum(upstream * normed, axis=(0, 1)), jnp.sum(upstream, axis=(0, 1)))


def attention_scores(query, key_rows):
    return jnp.einsum(
        "bqhe,bkhe->bhqk", query, key_rows, preferred_element_type=jnp.float32
    ) * DH ** (-0.5)


def segment_forward(weights, smalls, memory_rows, token_rows):
    proj_weight, inner_weight, outer_weight, lower_weight = weights
    qv_bias, out_bias, gains, shifts, inner_bias = smalls
    batch = token_rows.shape[0]
    stacked = jnp.concatenate([memory_rows, token_rows], axis=1)
    length = stacked.shape[1]
    local = proj_weight.shape[2]
    heads = local // DH
    wide_rows = gather_rows(stacked)
    bias_three = jnp.stack([qv_bias[0], jnp.zeros_like(qv_bias[0]), qv_bias[1]])
    projected = (
        jnp.einsum("bld,dcf->blcf", wide_rows, proj_weight, preferred_element_type=jnp.float32)
        + bias_three
    ).astype(jnp.bfloat16)
    split = projected.reshape(batch, length, 3, heads, DH)
    scores = attention_scores(split[:, :, 0], split[:, :, 1])
    peak = jnp.max(scores, axis=-1, keepdims=True)
    expo = jnp.exp(scores - peak)
    totals = jnp.sum(expo, axis=-1, keepdims=True)
    probs = expo / totals
    logsum = peak[..., 0] + jnp.log(totals[..., 0])
    context = jnp.einsum(
        "bhqk,bkhe->bqhe",
        probs.astype(jnp.bfloat16),
        split[:, :, 2],
        preferred_element_type=jnp.float32,
    )
    context = context.astype(jnp.bfloat16).reshape(batch, length, local)
    attended = branch_sum(
        jnp.einsum("bld,df->blf", context, outer_weight, preferred_element_type=jnp.float32)
    )
    middle, normed_one, rstd_one = norm_forward(
        stacked.astype(jnp.float32) + attended + out_bias[0], gains[0], shifts[0]
    )
    middle_wide = gather_rows(middle.astype(jnp.bfloat16))
    before = (
        jnp.einsum("bld,df->blf", middle_wide, inner_weight, preferred_element_type=jnp.float32)
        + inner_bias
    )
    hidden = gelu_value(before).astype(jnp.bfloat16)
    branch = branch_sum(
        jnp.einsum("blf,fd->bld", hidden, lower_weight, preferred_element_type=jnp.float32)
    )
    layer_out, normed_two, rstd_two = norm_forward(
        middle + branch + out_bias[1], gains[1], shifts[1]
    )
    stored = (
        wide_rows,
        projected,
        logsum,
        context,
        normed_one,
        rstd_one,
        middle_wide,
        before,
        hidden,
        normed_two,
        rstd_two,
    )
    return (layer_out, stored)


def segment_backward(weights, smalls, upstream, stored):
    proj_weight, inner_weight, outer_weight, lower_weight = weights
    qv_bias, out_bias, gains, shifts, inner_bias = smalls
    (
        wide_rows,
        projected,
        logsum,
        context,
        normed_one,
        rstd_one,
        middle_wide,
        before,
        hidden,
        normed_two,
        rstd_two,
    ) = stored
    batch, length, local = context.shape
    heads = local // DH
    grad_two, gain_two, shift_two = norm_backward(upstream, normed_two, rstd_two, gains[1])
    grad_branch = gather_grads(grad_two.astype(jnp.bfloat16))
    grad_lower = jnp.einsum("blf,bld->fd", hidden, grad_branch, preferred_element_type=jnp.float32)
    grad_hidden = jnp.einsum(
        "bld,fd->blf", grad_branch, lower_weight, preferred_element_type=jnp.float32
    )
    grad_before = (grad_hidden * gelu_slope(before)).astype(jnp.bfloat16)
    grad_inner = jnp.einsum(
        "bld,blf->df", middle_wide, grad_before, preferred_element_type=jnp.float32
    )
    grad_inner_bias = jnp.sum(grad_before.astype(jnp.float32), axis=(0, 1))
    grad_middle = grad_two + lax.psum_scatter(
        jnp.einsum(
            "blf,df->bld", grad_before, inner_weight, preferred_element_type=jnp.float32
        ).astype(jnp.bfloat16),
        "tensor",
        scatter_dimension=2,
        tiled=True,
    ).astype(jnp.float32)
    grad_one, gain_one, shift_one = norm_backward(grad_middle, normed_one, rstd_one, gains[0])
    grad_attended = gather_grads(grad_one.astype(jnp.bfloat16))
    grad_outer = jnp.einsum(
        "bld,blf->df", context, grad_attended, preferred_element_type=jnp.float32
    )
    grad_context = jnp.einsum(
        "blf,df->bld", grad_attended, outer_weight, preferred_element_type=jnp.float32
    )
    grad_context = grad_context.astype(jnp.bfloat16)
    grad_context = grad_context.reshape(batch, length, heads, DH)
    split = projected.reshape(batch, length, 3, heads, DH)
    query, key_rows, value_rows = (split[:, :, 0], split[:, :, 1], split[:, :, 2])
    probs = jnp.exp(attention_scores(query, key_rows) - logsum[..., None])
    grad_probs = jnp.einsum(
        "bqhe,bkhe->bhqk", grad_context, value_rows, preferred_element_type=jnp.float32
    )
    weighted_sum = jnp.sum(probs * grad_probs, axis=-1, keepdims=True)
    grad_scores = (probs * (grad_probs - weighted_sum)).astype(jnp.bfloat16)
    grad_query = jnp.einsum(
        "bhqk,bkhe->bqhe", grad_scores, key_rows, preferred_element_type=jnp.float32
    ) * DH ** (-0.5)
    grad_key = jnp.einsum(
        "bhqk,bqhe->bkhe", grad_scores, query, preferred_element_type=jnp.float32
    ) * DH ** (-0.5)
    grad_value = jnp.einsum(
        "bhqk,bqhe->bkhe",
        probs.astype(jnp.bfloat16),
        grad_context,
        preferred_element_type=jnp.float32,
    )
    grad_projected = (
        jnp.stack([grad_query, grad_key, grad_value], axis=2)
        .reshape(batch, length, 3, local)
        .astype(jnp.bfloat16)
    )
    grad_proj = jnp.einsum(
        "bld,blcf->dcf", wide_rows, grad_projected, preferred_element_type=jnp.float32
    )
    column_sums = jnp.sum(grad_projected.astype(jnp.float32), axis=(0, 1))
    grad_qv = jnp.stack([column_sums[0], column_sums[2]])
    grad_stacked = grad_one + input_sum(
        jnp.einsum("blcf,dcf->bld", grad_projected, proj_weight, preferred_element_type=jnp.float32)
    )
    grad_biases = jnp.stack([jnp.sum(grad_one, axis=(0, 1)), jnp.sum(grad_two, axis=(0, 1))])
    large_grads = (grad_proj, grad_inner, grad_outer, grad_lower)
    small_grads = (
        grad_qv,
        grad_biases,
        jnp.stack([gain_one, gain_two]),
        jnp.stack([shift_one, shift_two]),
        grad_inner_bias,
    )
    return (grad_stacked, large_grads, small_grads)


def add_tuples(first, second):
    return tuple((left + right for left, right in zip(first, second)))


def shards(
    tokens,
    memory,
    w_qkv,
    b_qv,
    w_out,
    out_biases,
    norm_gains,
    norm_shifts,
    w_in,
    b_in,
    w_down,
    cotangent,
    mlm_mask,
):
    smalls = (
        b_qv.astype(jnp.float32),
        out_biases.astype(jnp.float32),
        norm_gains.astype(jnp.float32),
        norm_shifts.astype(jnp.float32),
        b_in.astype(jnp.float32),
    )
    per_batch = tokens.shape[0] // MICRO
    segments = tokens.shape[1]
    mem_rows = memory.shape[0]
    local = w_qkv.shape[2]
    inner_local = w_in.shape[1]
    empty_large = (
        jnp.zeros((D, 3, local), jnp.float32),
        jnp.zeros((D, inner_local), jnp.float32),
        jnp.zeros((local, D), jnp.float32),
        jnp.zeros((inner_local, D), jnp.float32),
    )
    full_grads = empty_large
    shard_grads = (
        jnp.zeros(w_qkv.shape, jnp.float32),
        jnp.zeros(w_in.shape, jnp.float32),
        jnp.zeros(w_out.shape, jnp.float32),
        jnp.zeros(w_down.shape, jnp.float32),
    )
    small_total = (
        jnp.zeros((2, local), jnp.float32),
        jnp.zeros((2, local), jnp.float32),
        jnp.zeros((2, local), jnp.float32),
        jnp.zeros((2, local), jnp.float32),
        jnp.zeros((inner_local,), jnp.float32),
    )
    memory_total = jnp.zeros((mem_rows, local), jnp.float32)
    out_blocks = []
    grad_blocks = []
    for batch_index in range(MICRO):
        offset = batch_index * per_batch
        batch_tokens = tokens[offset : offset + per_batch]
        batch_mask = mlm_mask[offset : offset + per_batch]
        batch_cot = cotangent[offset : offset + per_batch].astype(jnp.float32) * batch_mask[
            ..., None
        ].astype(jnp.float32)
        weights = fetch_weights(w_qkv, w_in, w_out, w_down)
        carried = memory[None]
        stored_all = []
        token_outs = []
        for seg_index in range(segments):
            layer_out, stored = segment_forward(
                weights, smalls, carried, batch_tokens[:, seg_index]
            )
            carried = layer_out[:, :mem_rows].astype(jnp.bfloat16)
            token_outs.append(layer_out[:, mem_rows:].astype(jnp.bfloat16))
            stored_all.append(stored)
        returning = jnp.zeros((per_batch, mem_rows, local), jnp.float32)
        token_grads = [None] * segments
        for seg_index in reversed(range(segments)):
            upstream = jnp.concatenate([returning, batch_cot[:, seg_index]], axis=1)
            grad_stacked, large_grads, small_grads = segment_backward(
                weights, smalls, upstream, stored_all[seg_index]
            )
            returning = grad_stacked[:, :mem_rows]
            token_grads[seg_index] = grad_stacked[:, mem_rows:]
            full_grads = add_tuples(full_grads, large_grads)
            small_total = add_tuples(small_total, small_grads)
        memory_total = memory_total + jnp.sum(returning, axis=0)
        reduced = reduce_weights(full_grads[0], full_grads[1], full_grads[2], full_grads[3])
        shard_grads = add_tuples(shard_grads, reduced)
        full_grads = empty_large
        out_blocks.append(jnp.stack(token_outs, axis=1))
        grad_blocks.append(jnp.stack(token_grads, axis=1))
    grad_qv, grad_biases, grad_gains, grad_shifts, grad_inner_bias, memory_grad = lax.psum(
        (
            small_total[0],
            small_total[1],
            small_total[2],
            small_total[3],
            small_total[4],
            memory_total,
        ),
        "dp",
    )
    outputs = jnp.concatenate(out_blocks, axis=0)
    input_grad = jnp.concatenate(grad_blocks, axis=0)
    return (
        outputs,
        input_grad,
        memory_grad,
        shard_grads[0],
        grad_qv,
        shard_grads[2],
        grad_biases,
        grad_gains,
        grad_shifts,
        shard_grads[1],
        grad_inner_bias,
        shard_grads[3],
    )


ROWS = 528
LIVE = 176


def dot_nn(left, right):
    return jnp.dot(left, right, preferred_element_type=jnp.float32)


def dot_nt(left, right):
    return lax.dot_general(
        left, right, (((1,), (1,)), ((), ())), preferred_element_type=jnp.float32
    )


def dot_tn(left, right):
    return lax.dot_general(
        left, right, (((0,), (0,)), ((), ())), preferred_element_type=jnp.float32
    )


def norm_rows(resid, gain, shift):
    center = jnp.mean(resid, axis=-1, keepdims=True)
    spread = jnp.mean(resid * resid, axis=-1, keepdims=True) - center * center
    rstd = lax.rsqrt(spread + eps_norm)
    normed = (resid - center) * rstd
    return (normed * gain + shift, normed, rstd)


def norm_rows_back(upstream, normed, rstd, gain):
    scaled = upstream * gain
    first = jnp.mean(scaled, axis=-1, keepdims=True)
    second = jnp.mean(scaled * normed, axis=-1, keepdims=True)
    result = rstd * (scaled - first - normed * second)
    return (result, jnp.sum(upstream * normed, axis=0), jnp.sum(upstream, axis=0))


MESH = pl.DeviceIdType.MESH
HBM = pl.BlockSpec(memory_space=pl.ANY)
VMEM = pl.BlockSpec(memory_space=pltpu.VMEM)
GATHER_PIECES = ((0, 0), (1, 0), (2, 0), (3, 0), (4, 0), (5, 0), (4, 1), (5, 1), (4, 2), (5, 2), (4, 3), (5, 3))
SCATTER_PIECES = ((5, 0), (5, 1), (5, 2), (5, 3), (4, 0), (4, 1), (4, 2), (4, 3), (3, 0), (0, 0), (1, 0), (2, 0))
GATHER_HOPS = (
    (3, 2, 1, 0), (3, 2, 0, 1), (3, 2, 1, 0), (3, 0, 1, 2), (3, 2, 1, 0), (3, 1, 0, 2),
    (3, 2, 0, 1), (3, 2, 1, 0), (3, 0, 1, 2), (3, 2, 0, 1), (3, 2, 1, 0), (3, 0, 1, 2),
)
SCATTER_HOPS = (
    (2, 1, 0, 3), (0, 1, 2, 3), (1, 0, 2, 3), (2, 1, 0, 3), (0, 1, 2, 3), (2, 0, 3, 1),
    (0, 1, 2, 3), (1, 2, 0, 3), (0, 2, 1, 3), (0, 1, 2, 3), (1, 0, 2, 3), (1, 0, 2, 3),
)
GATHER_STEPS = (
    0, 8, 1, 100, 16, 9, 24, 2, 17, 32, 10, 40, 3, 25, 48, 18, 11, 56, 33, 64,
    41, 19, 49, 72, 57, 80, 4, 34, 26, 88, 5, 65, 101, 12, 50, 42, 73, 13, 102, 58,
    35, 20, 81, 66, 21, 89, 103, 27, 74, 104, 51, 82, 105, 59, 106, 43, 107, 67, 28, 29,
    36, 108, 52, 90, 37, 44, 53, 75, 83, 45, 109, 91, 68, 60, 69, 61, 76, 110, 77, 92,
    84, 111, 93, 85, 112, 113,
)
SCATTER_STEPS = (
    0, 8, 16, 1, 9, 17, 24, 32, 100, 25, 33, 2, 40, 10, 48, 18, 101, 41, 3, 49,
    26, 56, 34, 64, 11, 102, 19, 57, 27, 65, 4, 42, 103, 12, 35, 72, 20, 80, 5, 73,
    50, 88, 13, 28, 36, 81, 21, 58, 89, 29, 51, 104, 37, 105, 66, 106, 59, 107, 43, 108,
    52, 82, 109, 110, 67, 74, 44, 90, 60, 53, 68, 61, 83, 69, 75, 45, 84, 91, 76, 85,
    92, 77, 93,
)
SLOTS = 2


def here():
    me = lax.axis_index("dp")
    core = lax.axis_index("tensor")
    bits = tuple((me // (1 << b)) % 2 for b in range(4))
    peers = tuple({"dp": me + (1 - 2 * bits[b]) * (1 << b)} for b in range(4))
    return core, bits, peers + ({"tensor": 1 - core},)


def greet(peers):
    barrier = pltpu.get_barrier_semaphore()
    for peer in peers:
        pl.semaphore_signal(barrier, inc=1, device_id=peer, device_id_type=MESH)
    pl.semaphore_wait(barrier, len(peers))


def block_index(bits, free, flip=None):
    index = []
    for b in (3, 2, 1, 0):
        if b == flip:
            index.append(1 - bits[b])
        elif b in free:
            index.append(slice(None))
        else:
            index.append(bits[b])
    return tuple(index)


def columns(array, part, core, width):
    blocks = 4 if array > 3 else 1
    return pl.ds(pl.multiple_of((core * blocks + part) * width, width), width)


def shard_block(shards, piece, width):
    array, part = piece
    if array < 3:
        return shards[array].at[array]
    return shards[array].at[:, pl.ds(part * width, width)]


def attend_pair(query, key_rows, value_rows, valid):
    main = key_rows.shape[0] - 16
    lane = lax.broadcasted_iota(jnp.int32, (1, 2 * DH), 1)
    left = lane < DH
    query = query * DH ** (-0.5)
    zero = jnp.zeros_like(query)
    tail_lane = lax.broadcasted_iota(jnp.int32, (1, 32), 1)
    tail_zero = jnp.zeros((16, 2 * DH), query.dtype)
    key_tail, value_tail = key_rows[main:], value_rows[main:]
    keys_both = jnp.concatenate(
        [jnp.where(left, key_tail, tail_zero), jnp.where(left, tail_zero, key_tail)], axis=0
    )
    values_both = jnp.concatenate(
        [jnp.where(left, value_tail, tail_zero), jnp.where(left, tail_zero, value_tail)], axis=0
    )
    ones_both = jnp.concatenate(
        [jnp.where(left, tail_zero, tail_zero + 1), jnp.where(left, tail_zero + 1, tail_zero)], axis=0
    )
    tail = dot_nt(query, keys_both)
    tail = jnp.where(tail_lane % 16 < valid - main, tail, -1e30)
    peaks, parts = [], []
    for head in range(2):
        picked = jnp.where(left if head == 0 else ~left, query, zero)
        scores = dot_nt(picked, key_rows[:main])
        side = (tail_lane < 16) if head == 0 else (tail_lane >= 16)
        peak = jnp.maximum(
            jnp.max(scores, axis=1, keepdims=True),
            jnp.max(jnp.where(side, tail, -1e30), axis=1, keepdims=True),
        )
        expo = jnp.exp(scores - peak).astype(jnp.bfloat16)
        one = jnp.ones_like(value_rows[:main])
        values = jnp.where(left if head == 0 else ~left, value_rows[:main], one)
        parts.append(dot_nn(expo, values))
        peaks.append(peak)
    tail = jnp.exp(tail - jnp.where(tail_lane < 16, peaks[0], peaks[1])).astype(jnp.bfloat16)
    both = dot_nn(tail, jnp.concatenate([values_both, ones_both], axis=1))
    value_sum = jnp.where(left, parts[0], parts[1]) + both[:, : 2 * DH]
    total = jnp.where(left, parts[1], parts[0]) + both[:, 2 * DH :]
    return (value_sum / pltpu.roll(total, DH, 1)).astype(jnp.bfloat16)


def attend_kernel(valid, q_ref, k_ref, v_ref, out_ref):
    out_ref[...] = attend_pair(q_ref[...], k_ref[...], v_ref[...], valid)


def attend(query, key_rows, value_rows, valid):
    block = pl.BlockSpec((query.shape[0], 2 * DH), lambda i: (0, i))
    return pl.pallas_call(
        functools.partial(attend_kernel, valid),
        grid=(D // (2 * DH),),
        out_shape=jax.ShapeDtypeStruct(query.shape, jnp.bfloat16),
        in_specs=[block] * 3,
        out_specs=block,
        compiler_params=pltpu.CompilerParams(vmem_limit_bytes=32 << 20),
        name="attend",
    )(query, key_rows, value_rows)


def attend_back_pair(query, key_rows, value_rows, grads, valid):
    live = query.shape[0]
    left = lax.broadcasted_iota(jnp.int32, (1, 2 * DH), 1) < DH
    zero = jnp.zeros_like(query)
    query = query * DH ** (-0.5)
    picked = jnp.concatenate([jnp.where(left, query, zero), jnp.where(left, zero, query)], axis=0)
    up = jnp.concatenate([jnp.where(left, grads, zero), jnp.where(left, zero, grads)], axis=0)
    scores = dot_nt(key_rows, picked)
    scores = jnp.where(lax.broadcasted_iota(jnp.int32, scores.shape, 0) < valid, scores, -1e30)
    expo = jnp.exp(scores - jnp.max(scores, axis=0, keepdims=True))
    probs = expo * (1.0 / jnp.sum(expo, axis=0, keepdims=True))
    grad_probs = dot_nt(value_rows, up)
    weighted = jnp.sum(probs * grad_probs, axis=0, keepdims=True)
    grad_scores = (probs * (grad_probs - weighted)).astype(jnp.bfloat16)
    grad_query = dot_tn(grad_scores, key_rows)
    grad_query = jnp.where(left, grad_query[:live], grad_query[live:]) * DH ** (-0.5)
    grad_key = dot_nn(grad_scores, picked)
    grad_value = dot_nn(probs.astype(jnp.bfloat16), up)
    return tuple(grad.astype(jnp.bfloat16) for grad in (grad_query, grad_key, grad_value))


def attend_back_kernel(valid, q_ref, k_ref, v_ref, g_ref, dq_ref, dk_ref, dv_ref):
    dq_ref[...], dk_ref[...], dv_ref[...] = attend_back_pair(
        q_ref[...], k_ref[...], v_ref[...], g_ref[...], valid
    )


def attend_back(query, key_rows, value_rows, grad_context, valid):
    live = grad_context.shape[0]
    short = pl.BlockSpec((live, 2 * DH), lambda i: (0, i))
    tall = pl.BlockSpec((key_rows.shape[0], 2 * DH), lambda i: (0, i))
    low = jnp.bfloat16
    return pl.pallas_call(
        functools.partial(attend_back_kernel, valid),
        grid=(D // (2 * DH),),
        out_shape=[jax.ShapeDtypeStruct((live, D), low)] + [jax.ShapeDtypeStruct(key_rows.shape, low)] * 2,
        in_specs=[short, tall, tall, short],
        out_specs=[short, tall, tall],
        compiler_params=pltpu.CompilerParams(vmem_limit_bytes=32 << 20),
        name="attend_back",
    )(query, key_rows, value_rows, grad_context)


PACK_BIASES, PACK_OUT, PACK_GAINS, PACK_SHIFTS, PACK_INNER = 16, 18, 20, 22, 24


def gather_kernel(
    mem_rows, valid, toks, cots, pack, sq, so, si, sl, move, live_move,
    packs, fq, fk, fv, fo, fi, fl, stacked_a, stacked_b, ups, query, key_rows, value_rows,
    query_live, context_live, normed_one, rstd_one, middle_live, before_live, hidden_live, normed_two, rstd_two, low_out,
    x_v, c_v, vq, vo, vi, vl, held, context, middle, middle_low, branch,
    send, recv, local, loads, extra,
):
    core, bits, peers = here()
    width = pack.shape[1]
    live = ups.shape[1]
    shards = (vq, vq, vq, vo, vi, vl)
    fulls = (fq, fk, fv, fo, fi, fl)
    mine = pl.ds(pl.multiple_of(core * width, width), width)
    shard_in = [
        pltpu.make_async_copy(src, dst, extra.at[n])
        for n, (src, dst) in enumerate(((sq, vq), (so, vo), (si, vi), (sl, vl)))
    ]
    rows_own = [
        pltpu.make_async_copy(toks.at[core], x_v.at[:, :, mine], extra.at[4]),
        pltpu.make_async_copy(cots.at[core], c_v.at[:, :, mine], extra.at[5]),
        pltpu.make_async_copy(pack, packs.at[core], extra.at[6]),
    ]
    for copy in shard_in + rows_own:
        copy.start()
    own = []
    for p, (array, part) in enumerate(GATHER_PIECES):
        own.append(pltpu.make_async_copy(
            shard_block(shards, (array, part), width),
            fulls[array].at[block_index(bits, ()) + (slice(None), columns(array, part, core, width))],
            local.at[p],
        ))
    greet(peers)
    for copy in shard_in:
        copy.wait()
    for copy in own:
        copy.start()

    def remote(src, dst, slot, peer):
        return pltpu.make_async_remote_copy(
            src_ref=src, dst_ref=dst, send_sem=send.at[slot], recv_sem=recv.at[slot],
            device_id=peer, device_id_type=MESH)

    def stage(p, s):
        array, part = GATHER_PIECES[p]
        order = GATHER_HOPS[p]
        cols = columns(array, part, core, width)
        dst = fulls[array].at[block_index(bits, order[:s]) + (slice(None), cols)]
        if s == 0:
            src = shard_block(shards, (array, part), width)
        else:
            src = dst
        peer = peers[order[s]] if s < 4 else peers[4]
        return remote(src, dst, p * 5 + s, peer)

    swaps = [
        remote(toks.at[1 - core], x_v.at[:, :, mine], 60, peers[4]),
        remote(cots.at[1 - core], c_v.at[:, :, mine], 61, peers[4]),
        remote(pack, packs.at[core], 62, peers[4]),
    ]
    started, loading = {}, {}

    def load(p):
        array, part = GATHER_PIECES[p]
        blocks = 4 if array > 3 else 1
        every = (slice(None),) * 5
        loading[p] = [
            pltpu.make_async_copy(
                fulls[array].at[every + (pl.ds((half * blocks + part) * width, width),)],
                held.at[(p % 6,) + every + (pl.ds(half * width, width),)],
                loads.at[2 * p + half],
            )
            for half in range(2)
        ]
        for copy in loading[p]:
            copy.start()

    def loaded(p):
        for copy in loading.pop(p):
            copy.wait()

    def weight(p, cols):
        block = held[p % 6, :, :, :, :, :, cols]
        return block.reshape(2 * width, block.shape[-1])

    def wide(row):
        return jnp.concatenate([packs[0, row : row + 1], packs[1, row : row + 1]], axis=1).astype(jnp.float32)

    def norm(resid, gain, shift):
        center = jnp.mean(resid, axis=1, keepdims=True)
        spread = jnp.mean(resid * resid, axis=1, keepdims=True) - center * center
        rstd = lax.rsqrt(spread + eps_norm)
        normed = (resid - center) * rstd
        return normed * gain + shift, normed, rstd

    def compute(task):
        if task == 0:
            for copy in rows_own:
                copy.wait()
            for swap in swaps:
                swap.wait_recv()
            memory = jnp.concatenate([packs[0, :16], packs[1, :16]], axis=1)
            is_memory = lax.broadcasted_iota(jnp.int32, memory.shape, 0) < mem_rows
            stacked_a[...] = dot_nn(move[0], x_v[0]).astype(jnp.bfloat16)
            stacked_a[:16] = jnp.where(is_memory, memory, stacked_a[:16])
            stacked_b[...] = dot_nn(move[1], x_v[1]).astype(jnp.bfloat16)
            for n in range(2):
                ups[n] = dot_nn(live_move[n], c_v[n]).astype(jnp.bfloat16)
        elif task < 4:
            n = task - 1
            loaded(n)
            target = (query, key_rows, value_rows)[n]
            for half in range(2):
                cols = pl.ds(half * width, width)
                got = dot_nn(stacked_a[...], weight(n, cols))
                if n != 1:
                    row = PACK_BIASES + n // 2
                    got = got + packs[half, row : row + 1].astype(jnp.float32)
                target[:, cols] = got.astype(jnp.bfloat16)
                if n == 0:
                    query_live[:, cols] = got[:live].astype(jnp.bfloat16)
        elif task < 8:

            def pair(n, carry):
                cols = pl.ds(pl.multiple_of((2 * (task - 4) + n) * 2 * DH, 2 * DH), 2 * DH)
                context[:, cols] = attend_pair(query[:, cols], key_rows[:, cols], value_rows[:, cols], valid)
                return carry

            lax.fori_loop(0, 2, pair, 0)
        elif task == 8:
            loaded(3)
            attended = dot_nt(context[...], weight(3, slice(None)))
            resid = stacked_a[...].astype(jnp.float32) + attended + wide(PACK_OUT)
            value, normed, rstd = norm(resid, wide(PACK_GAINS), wide(PACK_SHIFTS))
            middle[...] = value
            middle_low[...] = value.astype(jnp.bfloat16)
            middle_live[...] = value[:live].astype(jnp.bfloat16)
            context_live[...] = context[:live]
            normed_one[...] = normed[:live]
            rstd_one[...] = jnp.broadcast_to(rstd[:live], rstd_one.shape)
        elif task < 13:
            j = task - 9
            loaded(4 + 2 * j)
            loaded(5 + 2 * j)

            def hidden_block(half, carry):
                cols = pl.ds(pl.multiple_of(half * width, width), width)
                place = pl.ds(pl.multiple_of((half * 4 + j) * width, width), width)
                bias = packs[half, PACK_INNER + j : PACK_INNER + j + 1].astype(jnp.float32)
                before = dot_nn(middle_low[...], weight(4 + 2 * j, cols)) + bias
                before_live[:, place] = before[:live]
                hidden = gelu_value(before).astype(jnp.bfloat16)
                hidden_live[:, place] = hidden[:live]
                branch[...] = branch[...] + dot_nt(hidden, weight(5 + 2 * j, cols))
                return carry

            if j == 0:
                branch[...] = middle[...] + wide(PACK_OUT + 1)
            lax.fori_loop(0, 2, hidden_block, 0)
        else:
            value, normed, rstd = norm(branch[...], wide(PACK_GAINS + 1), wide(PACK_SHIFTS + 1))
            low_out[...] = value.astype(jnp.bfloat16)
            is_memory = lax.broadcasted_iota(jnp.int32, (16, 2 * width), 0) < mem_rows
            stacked_b[:16] = jnp.where(is_memory, low_out[:16], stacked_b[:16])
            normed_two[...] = normed[:live]
            rstd_two[...] = jnp.broadcast_to(rstd[:live], rstd_two.shape)

    for tick, step in enumerate(GATHER_STEPS):
        if step >= 100:
            compute(step - 100)
            continue
        p, s = step // 8, step % 8
        if s > 0:
            started[p, s - 1].wait_recv()
        if s == 1:
            own[p].wait()
        if s == 5:
            load(p)
        else:
            started[p, s] = stage(p, s)
            started[p, s].start()
        if tick == 2:
            for swap in swaps:
                swap.start()
    for copy in started.values():
        copy.wait_send()
    for swap in swaps:
        swap.wait_send()


def gather_all(mem_rows, valid, toks, cots, pack, sq, so, si, sl, move, live_move):
    width = pack.shape[1]
    rows = sq.shape[1]
    low, full = jnp.bfloat16, jnp.float32
    total, live = move.shape[1], live_move.shape[1]
    hidden = 2 * si.shape[1]
    out = [((2,) + pack.shape, low)]
    for size in (2 * width, 2 * width, 2 * width, 2 * width, hidden, hidden):
        out.append(((2, 2, 2, 2, rows, size), low))
    out += [((total, 2 * width), low)] * 2 + [((2, live, 2 * width), low)]
    out += [((total, 2 * width), low)] * 3 + [((live, 2 * width), low)] * 2
    out += [((live, 2 * width), full), ((live, 2 * width), full), ((live, 2 * width), low)]
    out += [((live, hidden), full), ((live, hidden), low)]
    out += [((live, 2 * width), full), ((live, 2 * width), full), ((total, 2 * width), low)]
    block = (2, 2, 2, 2, rows, 2 * width)
    got = pl.pallas_call(
        functools.partial(gather_kernel, mem_rows, valid),
        out_shape=[jax.ShapeDtypeStruct(*one) for one in out],
        in_specs=[HBM, HBM, VMEM] + [HBM] * 4 + [VMEM] * 2,
        out_specs=[VMEM] + [HBM] * 6 + [VMEM] * (len(out) - 7),
        scratch_shapes=[
            pltpu.VMEM(toks.shape[1:3] + (2 * width,), low),
            pltpu.VMEM(toks.shape[1:3] + (2 * width,), low),
            pltpu.VMEM(sq.shape, low),
            pltpu.VMEM(so.shape, low),
            pltpu.VMEM(si.shape, low),
            pltpu.VMEM(sl.shape, low),
            pltpu.VMEM((6,) + block, low),
            pltpu.VMEM((total, 2 * width), low),
            pltpu.VMEM((total, 2 * width), full),
            pltpu.VMEM((total, 2 * width), low),
            pltpu.VMEM((total, 2 * width), full),
            pltpu.SemaphoreType.DMA((63,)),
            pltpu.SemaphoreType.DMA((63,)),
            pltpu.SemaphoreType.DMA((12,)),
            pltpu.SemaphoreType.DMA((24,)),
            pltpu.SemaphoreType.DMA((7,)),
        ],
        compiler_params=pltpu.CompilerParams(collective_id=0, has_side_effects=True, vmem_limit_bytes=62 << 20),
        name="gather_all",
    )(toks, cots, pack, sq, so, si, sl, move, live_move)
    wide = [array.reshape(16 * rows, array.shape[-1]) for array in got[1:7]]
    return got[0], wide, got[7:]


def scatter_kernel(mem_rows, valid, *refs):
    (rows_a, out_a, context_a, middle_a, before_a, branch_a, hidden_a) = refs[0:7]
    second_rows = refs[7:17]
    query, keys_in, values_in, up, grad_one, wq, wk, wv, move, small_a, small_b, outs_a, outs_b, grads_b = refs[17:31]
    oq, oo, oi, ol, osmall, out_item, grad_item = refs[31:38]
    (acc, first, second, third, fourth, slots, wide_x, wide_s, held, grad_query, key_rows, value_rows,
     source, result, total_rows, small_v, small_in, small_recv, send, recv, extra, sent) = refs[38:]
    first_rows = (rows_a, grad_query, key_rows, value_rows, out_a, context_a, middle_a, before_a, branch_a, hidden_a)
    core, bits, peers = here()
    width = osmall.shape[1]
    live = grad_query.shape[0]
    bufs = (first, second, third, fourth)
    lefts = (0, 0, 0, 4, 6, 8)
    rights = (1, 2, 3, 5, 7, 9)
    turned = set()
    mine = pl.ds(pl.multiple_of(core * width, width), width)
    other = pl.ds(pl.multiple_of((1 - core) * width, width), width)
    stage_in = [
        pltpu.make_async_copy(keys_in, key_rows, extra.at[0]),
        pltpu.make_async_copy(values_in, value_rows, extra.at[1]),
    ]
    for copy in stage_in:
        copy.start()
    greet(peers)

    def bring(src, dst, sem):
        copy = pltpu.make_async_copy(src, dst, extra.at[sem])
        copy.start()
        return copy

    def remote(src, dst, slot, peer):
        return pltpu.make_async_remote_copy(
            src_ref=src, dst_ref=dst, send_sem=send.at[slot], recv_sem=recv.at[slot],
            device_id=peer, device_id_type=MESH)

    def turn(array):
        left = lefts[array]
        if left in turned:
            return
        turned.add(left)
        for n, rows in enumerate((first_rows, second_rows)):
            if left == 0:
                bring(rows[0], source, 2).wait()
                wide_x[n] = source[...].T
            else:
                wide_s[left // 2 - 2, n] = rows[left][...].T

    def multiply(array, offset, size):
        total = None
        for n, rows in enumerate((first_rows, second_rows)):
            right = rows[rights[array]][:, pl.ds(offset, size)]
            if array in (1, 2):
                left = wide_x[n]
            elif array == 0:
                left = wide_x[n, :, :live]
            else:
                left = wide_s[lefts[array] // 2 - 2, n]
            term = jnp.dot(left, right, preferred_element_type=jnp.float32)
            total = term if total is None else total + term
        return total

    tile = width // 2

    def produce(p, slot):
        array, part = SCATTER_PIECES[p]
        turn(array)
        blocks = 4 if array > 3 else 1
        base = ((1 - core) * blocks + part) * width

        def body(n, carry):
            offset = pl.multiple_of(base + n * tile, tile)
            got = multiply(array, offset, tile).astype(jnp.bfloat16)
            slots[slot, :, :, :, :, :, pl.ds(pl.multiple_of(n * tile, tile), tile)] = got.reshape(
                slots.shape[1:6] + (tile,)
            )
            return carry

        lax.fori_loop(0, 2, body, 0)

    def combine(p):
        array, part = SCATTER_PIECES[p]
        blocks = 4 if array > 3 else 1
        base = (core * blocks + part) * width

        def body(n, carry):
            offset = pl.multiple_of(base + n * tile, tile)
            cols = pl.ds(pl.multiple_of(n * tile, tile), tile)
            got = multiply(array, offset, tile).reshape(slots.shape[1:6] + (tile,))
            acc[p, :, :, :, :, :, cols] = (
                got + acc[p, :, :, :, :, :, cols].astype(jnp.float32)
            ).astype(jnp.bfloat16)
            return carry

        lax.fori_loop(0, 2, body, 0)

    def stage(p, s):
        if s == 0:
            return remote(slots.at[p % SLOTS], acc.at[p], p * 5, peers[4])
        order = SCATTER_HOPS[p]
        src = acc.at[(p,) + block_index(bits, order[s:], flip=order[s - 1])]
        return remote(src, bufs[s - 1].at[p], p * 5 + s, peers[order[s - 1]])

    def fold(p, s):
        array, part = SCATTER_PIECES[p]
        order = SCATTER_HOPS[p]
        free = [b for b in (3, 2, 1, 0) if b in order[s:]]
        for n in range(1 << len(free)):
            at = {b: (n >> i) % 2 for i, b in enumerate(reversed(free))}
            where = tuple(at.get(b, bits[b]) for b in (3, 2, 1, 0))
            got = bufs[s - 1][(p,) + tuple(at[b] for b in free)]
            if s < 4:
                acc[(p,) + where] = acc[(p,) + where] + got
            else:
                total = acc[(p,) + where].astype(jnp.float32) + got.astype(jnp.float32)
                if array < 3:
                    oq[array] = total
                elif array == 4:
                    oi[:, pl.ds(part * width, width)] = total
                elif array == 3:
                    oo[...] = total
                else:
                    ol[:, pl.ds(part * width, width)] = total

    small_started = {}

    def small_stage(s):
        peer = peers[4] if s == 0 else peers[s - 1]
        src = small_v.at[:, other] if s == 0 else small_in.at[s]
        return remote(src, small_recv.at[s], 60 + s, peer)

    def small_step(n):
        if n == 0:
            small_in[0] = small_v[:, mine]
        else:
            small_started[n - 1].wait_recv()
            total = small_in[n - 1] + small_recv[n - 1]
            if n < 5:
                small_in[n] = total
            else:
                osmall[...] = total
        if n < 5:
            small_started[n] = small_stage(n)
            small_started[n].start()

    swaps, places = [], []

    def unpermute(n, values, target, segment):
        if n > 1:
            swaps[n - 2].wait_send()
            places[n - 2].wait()
        result[n % 2] = dot_tn(move[segment], values).astype(jnp.bfloat16)
        places.append(
            pltpu.make_async_copy(result.at[n % 2, :, mine], target.at[core, segment], sent.at[n])
        )
        swaps.append(remote(result.at[n % 2, :, other], target.at[core, segment], 65 + n, peers[4]))
        places[n].start()
        swaps[n].start()

    weights = (wk, wv, wq)
    fetched = {}

    def compute(task):
        if task < 4:
            if task == 0:
                for copy in stage_in:
                    copy.wait()
                fetched[0] = bring(weights[0], held, 3)

            def pair(n, carry):
                cols = pl.ds(pl.multiple_of((2 * task + n) * 2 * DH, 2 * DH), 2 * DH)
                grad_query[:, cols], key_rows[:, cols], value_rows[:, cols] = attend_back_pair(
                    query[:, cols], key_rows[:, cols], value_rows[:, cols], up[:, cols], valid
                )
                return carry

            lax.fori_loop(0, 2, pair, 0)
        elif task < 7:
            n = task - 4
            fetched[n].wait()
            if n == 0:
                total_rows[...] = dot_nt(key_rows[...], held[...])
            elif n == 1:
                total_rows[...] = total_rows[...] + dot_nt(value_rows[...], held[...])
            else:
                total_rows[:live] = total_rows[:live] + grad_one[...] + dot_nt(grad_query[...], held[...])
                row = lax.broadcasted_iota(jnp.int32, (16, 2 * width), 0)
                small_v[:16] = jnp.where(row < mem_rows, total_rows[:16], 0.0)
                query_sum = jnp.sum(grad_query[...].astype(jnp.float32), axis=0, keepdims=True)
                value_sum = jnp.sum(value_rows[...].astype(jnp.float32), axis=0, keepdims=True)
                small_v[16:24] = small_a[...] + small_b[...] + jnp.where(
                    row[:8] == 0, query_sum, jnp.where(row[:8] == 1, value_sum, 0.0)
                )
                inner = [
                    jnp.sum(before[...].astype(jnp.float32), axis=0, keepdims=True)
                    for before in (before_a, second_rows[7])
                ]
                inner = inner[0] + inner[1]
                blocks = inner.shape[1] // (2 * width)
                small_v[24:] = jnp.concatenate(
                    [
                        jnp.concatenate(
                            [inner[:, (h * blocks + n) * width : (h * blocks + n + 1) * width] for h in range(2)],
                            axis=1,
                        )
                        for n in range(blocks)
                    ]
                    + [jnp.zeros((small_v.shape[0] - 24 - blocks, 2 * width), jnp.float32)],
                    axis=0,
                )
            if n < 2:
                fetched[n + 1] = bring(weights[n + 1], held, 3)
        elif task == 7:
            unpermute(0, total_rows[...].astype(jnp.bfloat16), grad_item, 0)
        else:
            values, target, segment = (
                (outs_a, out_item, 0),
                (outs_b, out_item, 1),
                (grads_b, grad_item, 1),
            )[task - 8]
            bring(values, source, 2).wait()
            unpermute(task - 7, source[...], target, segment)

    started = {}
    ready = None
    for step in SCATTER_STEPS:
        if step >= 100:
            compute(step - 100)
            if step == 106:
                ready = 0
            continue
        p, s = step // 8, step % 8
        if s == 0:
            if p >= SLOTS:
                started[p - SLOTS, 0].wait_send()
            produce(p, p % SLOTS)
        else:
            started[p, s - 1].wait_recv()
            if s == 1:
                combine(p)
            else:
                fold(p, s - 1)
        if s < 5:
            started[p, s] = stage(p, s)
            started[p, s].start()
        if ready is not None:
            ready += 1
            if ready % 3 == 0 and ready <= 18:
                small_step(ready // 3 - 1)
    for (p, s), copy in started.items():
        if s > 0 or p >= len(SCATTER_PIECES) - SLOTS:
            copy.wait_send()
    for s in range(5):
        small_started[s].wait_send()
    for n in range(4):
        if n > 1:
            swaps[n].wait_send()
            places[n].wait()
        swaps[n].wait_recv()


def scatter_all(mem_rows, valid, first_rows, second_rows, tail, smalls, outs, grads):
    width = smalls[0].shape[1] // 2
    small_rows = 32
    rows = 2 * width // 16
    low, full = jnp.bfloat16, jnp.float32
    count = len(SCATTER_PIECES)
    long, live = second_rows[0].shape[0], second_rows[1].shape[0]
    move = tail[-1]
    tokens = move.shape[2]
    item = (2, 2, tokens, width)
    return pl.pallas_call(
        functools.partial(scatter_kernel, mem_rows, valid),
        out_shape=[
            jax.ShapeDtypeStruct((3, rows, width), full),
            jax.ShapeDtypeStruct((rows, width), full),
            jax.ShapeDtypeStruct((rows, 4 * width), full),
            jax.ShapeDtypeStruct((rows, 4 * width), full),
            jax.ShapeDtypeStruct((small_rows, width), full),
            jax.ShapeDtypeStruct(item, low),
            jax.ShapeDtypeStruct(item, low),
        ],
        in_specs=[HBM] + [VMEM] * 6 + [HBM] + [VMEM] * 9
        + [VMEM, HBM, HBM, VMEM, VMEM, HBM, HBM, HBM, VMEM, VMEM, VMEM, HBM, HBM, HBM],
        out_specs=[VMEM] * 5 + [HBM] * 2,
        scratch_shapes=[
            pltpu.VMEM((count, 2, 2, 2, 2, rows, width), low),
            pltpu.VMEM((count, 2, 2, 2, rows, width), low),
            pltpu.VMEM((count, 2, 2, rows, width), low),
            pltpu.VMEM((count, 2, rows, width), low),
            pltpu.VMEM((count, rows, width), low),
            pltpu.VMEM((SLOTS, 2, 2, 2, 2, rows, width), low),
            pltpu.VMEM((2, 2 * width, long), low),
            pltpu.VMEM((3, 2, 2 * width, live), low),
            pltpu.VMEM((2 * width, 2 * width), low),
            pltpu.VMEM((live, 2 * width), low),
            pltpu.VMEM((long, 2 * width), low),
            pltpu.VMEM((long, 2 * width), low),
            pltpu.VMEM((long, 2 * width), low),
            pltpu.VMEM((2, tokens, 2 * width), low),
            pltpu.VMEM((long, 2 * width), full),
            pltpu.VMEM((small_rows, 2 * width), full),
            pltpu.VMEM((5, small_rows, width), full),
            pltpu.VMEM((5, small_rows, width), full),
            pltpu.SemaphoreType.DMA((69,)),
            pltpu.SemaphoreType.DMA((69,)),
            pltpu.SemaphoreType.DMA((4,)),
            pltpu.SemaphoreType.DMA((4,)),
        ],
        compiler_params=pltpu.CompilerParams(collective_id=1, has_side_effects=True, vmem_limit_bytes=67_000_000),
        name="scatter_all",
    )(*first_rows, *second_rows, *tail[:-1], move, *smalls, *outs, *grads)


def item_shards(
    tokens,
    memory,
    w_qkv,
    b_qv,
    w_out,
    out_biases,
    norm_gains,
    norm_shifts,
    w_in,
    b_in,
    w_down,
    cotangent,
    mlm_mask,
):
    core = lax.axis_index("tensor")
    segments, count = tokens.shape[1], tokens.shape[2]
    mem_rows = memory.shape[0]
    valid = mem_rows + count
    half = memory.shape[1]

    mask = lax.dynamic_index_in_dim(mlm_mask, core, 0, keepdims=False)
    lower_tri = (
        lax.broadcasted_iota(jnp.int32, (count, count), 0)
        <= lax.broadcasted_iota(jnp.int32, (count, count), 1)
    ).astype(jnp.bfloat16)
    ones = mask.astype(jnp.bfloat16)
    upto = dot_nn(ones, lower_tri).astype(jnp.int32)
    total = upto[:, -1:]
    index = lax.broadcasted_iota(jnp.int32, mask.shape, 1)
    place = mem_rows + jnp.where(mask > 0, upto - 1, total + index - upto)
    move = (
        lax.broadcasted_iota(jnp.int32, (segments, ROWS, count), 1) == place[:, None, :]
    ).astype(jnp.bfloat16)
    live_move = move[:, :LIVE] * ones[:, None, :]

    packed = jnp.concatenate(
        [
            jnp.pad(memory, ((0, PACK_BIASES - mem_rows), (0, 0))),
            b_qv,
            out_biases,
            norm_gains,
            norm_shifts,
            b_in.reshape(-1, half),
        ],
        axis=0,
    )
    packed = jnp.pad(packed, ((0, -packed.shape[0] % 16), (0, 0)))
    both, (wq, wk, wv, outer, inner, lower), first = gather_all(
        mem_rows,
        valid,
        tokens,
        cotangent,
        packed,
        w_qkv.transpose(1, 0, 2),
        w_out.T,
        w_in,
        w_down.T,
        move,
        live_move,
    )
    (
        stacked,
        stacked_next,
        ups,
        query,
        key_rows,
        value_rows,
        query_live,
        context,
        normed_one,
        rstd_one,
        middle_low,
        before,
        hidden,
        normed_two,
        rstd_two,
        low_out,
    ) = first
    wide = jnp.concatenate([both[0], both[1]], axis=1).astype(jnp.float32)
    qv_bias, out_bias, gains, shifts = (
        wide[n : n + 2] for n in (PACK_BIASES, PACK_OUT, PACK_GAINS, PACK_SHIFTS)
    )
    inner_rows = b_in.shape[0] // half
    inner_bias = both[:, PACK_INNER : PACK_INNER + inner_rows].reshape(-1).astype(jnp.float32)
    stored = [
        (
            stacked,
            query,
            key_rows,
            value_rows,
            context,
            normed_one,
            rstd_one,
            middle_low,
            before,
            hidden,
            normed_two,
            rstd_two,
        )
    ]
    outs = [low_out]
    stacked = stacked_next
    query = (dot_nn(stacked, wq) + qv_bias[0]).astype(jnp.bfloat16)
    key_rows = dot_nn(stacked, wk).astype(jnp.bfloat16)
    value_rows = (dot_nn(stacked, wv) + qv_bias[1]).astype(jnp.bfloat16)
    context = attend(query, key_rows, value_rows, valid)
    attended = dot_nt(context, outer)
    middle, normed_one, rstd_one = norm_rows(
        stacked.astype(jnp.float32) + attended + out_bias[0], gains[0], shifts[0]
    )
    middle_low = middle.astype(jnp.bfloat16)
    before = dot_nn(middle_low, inner) + inner_bias
    hidden = gelu_value(before).astype(jnp.bfloat16)
    branch = dot_nt(hidden, lower)
    layer_out, normed_two, rstd_two = norm_rows(
        middle + branch + out_bias[1], gains[1], shifts[1]
    )
    low_out = layer_out.astype(jnp.bfloat16)
    outs.append(low_out)
    stored.append(
        (
            stacked,
            query,
            key_rows,
            value_rows,
            context[:LIVE],
            normed_one[:LIVE],
            rstd_one[:LIVE],
            middle_low[:LIVE],
            before[:LIVE],
            hidden[:LIVE],
            normed_two[:LIVE],
            rstd_two[:LIVE],
        )
    )

    returning = jnp.zeros((mem_rows, D), jnp.float32)
    token_grads = []
    pieces = [None] * segments
    smalls = []
    for seg in reversed(range(segments)):
        (
            stacked,
            query,
            key_rows,
            value_rows,
            context,
            normed_one,
            rstd_one,
            middle_low,
            before,
            hidden,
            normed_two,
            rstd_two,
        ) = stored[seg]
        upstream = ups[seg].astype(jnp.float32)
        upstream = upstream + jnp.pad(returning, ((0, LIVE - mem_rows), (0, 0)))
        grad_two, gain_two, shift_two = norm_rows_back(upstream, normed_two, rstd_two, gains[1])
        grad_branch = grad_two.astype(jnp.bfloat16)
        grad_hidden = dot_nn(grad_branch, lower)
        grad_before = (grad_hidden * gelu_slope(before)).astype(jnp.bfloat16)
        grad_middle = grad_two + dot_nt(grad_before, inner)
        grad_one, gain_one, shift_one = norm_rows_back(
            grad_middle, normed_one, rstd_one, gains[0]
        )
        grad_attended = grad_one.astype(jnp.bfloat16)
        grad_context = dot_nn(grad_attended, outer).astype(jnp.bfloat16)
        sums = [jnp.zeros((D,), jnp.float32)] * 2
        if seg > 0:
            grad_query, grad_key, grad_value = attend_back(
                query, key_rows, value_rows, grad_context, valid
            )
            grad_stacked = dot_nt(grad_key, wk) + dot_nt(grad_value, wv)
            live_part = grad_one + dot_nt(grad_query, wq)
            grad_stacked = grad_stacked + jnp.pad(live_part, ((0, ROWS - LIVE), (0, 0)))
            returning = grad_stacked[:mem_rows]
            token_grads.append(grad_stacked.astype(jnp.bfloat16))
            attention_grads = [grad_query, grad_key, grad_value]
            sums = [jnp.sum(grad.astype(jnp.float32), axis=0) for grad in (grad_query, grad_value)]
        else:
            attention_grads = []
            tail = [query_live, key_rows, value_rows, grad_context, grad_one, wq, wk, wv, move]
        pieces[seg] = (
            stacked,
            *attention_grads,
            grad_attended,
            context,
            middle_low,
            grad_before,
            grad_branch,
            hidden,
        )
        smalls.append(
            jnp.stack(
                [
                    *sums,
                    jnp.sum(grad_one, axis=0),
                    jnp.sum(grad_two, axis=0),
                    gain_one,
                    gain_two,
                    shift_one,
                    shift_two,
                ]
            )
        )

    grad_proj, grad_outer, grad_inner, grad_lower, mine, outputs, input_grad = scatter_all(
        mem_rows, valid, pieces[0], pieces[1], tail, smalls, outs, token_grads
    )
    return (
        outputs,
        input_grad.astype(jnp.float32),
        mine[:mem_rows],
        grad_proj.transpose(1, 0, 2),
        mine[16:18],
        grad_outer.T,
        mine[18:20],
        mine[20:22],
        mine[22:24],
        grad_inner,
        mine[24 : 24 + inner_rows].reshape(-1),
        grad_lower.T,
    )


def solution(mesh):
    def body(*arrays):
        if mesh.shape["dp"] == 16 and mesh.shape["tensor"] == arrays[0].shape[0] == arrays[0].shape[1] == 2:
            return item_shards(*arrays)
        return shards(*arrays)

    placed = (
        P("dp", None, None, "tensor"),
        P(None, "tensor"),
        P("dp", None, "tensor"),
        P(None, "tensor"),
        P("tensor", "dp"),
        P(None, "tensor"),
        P(None, "tensor"),
        P(None, "tensor"),
        P("dp", "tensor"),
        P("tensor"),
        P("tensor", "dp"),
        P("dp", None, None, "tensor"),
        P("dp", None, None),
    )
    return jax.shard_map(
        body,
        mesh=mesh,
        in_specs=placed,
        out_specs=(
            P("dp", None, None, "tensor"),
            P("dp", None, None, "tensor"),
            P(None, "tensor"),
            P("dp", None, "tensor"),
            P(None, "tensor"),
            P("tensor", "dp"),
            P(None, "tensor"),
            P(None, "tensor"),
            P(None, "tensor"),
            P("dp", "tensor"),
            P("tensor"),
            P("tensor", "dp"),
        ),
        check_vma=False,
    )
```

```python
import functools

import jax
import jax.numpy as jnp
from jax import lax
from jax.experimental import pallas as pl
from jax.experimental.pallas import tpu as pltpu
from jax.sharding import PartitionSpec as P

D = 1024
DH = 64
MICRO = 2


eps_norm = 1e-05
root_half = 0.7071067811865476
inv_root_two_pi = 0.3989422804014327


def gelu_value(before):
    return 0.5 * before * (1.0 + lax.erf(before * root_half))


def gelu_slope(before):
    return 0.5 * (1.0 + lax.erf(before * root_half)) + before * inv_root_two_pi * jnp.exp(
        -0.5 * before * before
    )


def fetch_weights(w_qkv, w_in, w_out, w_down):
    return (
        lax.all_gather(w_qkv, "dp", axis=0, tiled=True),
        lax.all_gather(w_in, "dp", axis=0, tiled=True),
        lax.all_gather(w_out, "dp", axis=1, tiled=True),
        lax.all_gather(w_down, "dp", axis=1, tiled=True),
    )


def reduce_weights(grad_proj, grad_inner, grad_outer, grad_lower):
    return (
        lax.psum_scatter(
            grad_proj.astype(jnp.bfloat16), "dp", scatter_dimension=0, tiled=True
        ).astype(jnp.float32),
        lax.psum_scatter(
            grad_inner.astype(jnp.bfloat16), "dp", scatter_dimension=0, tiled=True
        ).astype(jnp.float32),
        lax.psum_scatter(
            grad_outer.astype(jnp.bfloat16), "dp", scatter_dimension=1, tiled=True
        ).astype(jnp.float32),
        lax.psum_scatter(
            grad_lower.astype(jnp.bfloat16), "dp", scatter_dimension=1, tiled=True
        ).astype(jnp.float32),
    )


def gather_rows(block):
    return lax.all_gather(block, "tensor", axis=2, tiled=True)


def branch_sum(partial_value):
    return lax.psum_scatter(partial_value, "tensor", scatter_dimension=2, tiled=True)


def gather_grads(block):
    return lax.all_gather(block, "tensor", axis=2, tiled=True)


def input_sum(partial_value):
    return lax.psum_scatter(
        partial_value.astype(jnp.bfloat16), "tensor", scatter_dimension=2, tiled=True
    ).astype(jnp.float32)


def norm_forward(resid, gain, shift):
    totals = jnp.sum(resid, axis=-1)
    squares = jnp.sum(resid * resid, axis=-1)
    totals, squares = lax.psum((totals, squares), "tensor")
    center = totals / D
    spread = squares / D - center * center
    rstd = lax.rsqrt(spread + eps_norm)
    normed = (resid - center[..., None]) * rstd[..., None]
    return (normed * gain + shift, normed, rstd)


def norm_backward(upstream, normed, rstd, gain):
    scaled = upstream * gain
    first = jnp.sum(scaled, axis=-1)
    second = jnp.sum(scaled * normed, axis=-1)
    first, second = lax.psum((first, second), "tensor")
    result = rstd[..., None] * (scaled - first[..., None] / D - normed * (second[..., None] / D))
    return (result, jnp.sum(upstream * normed, axis=(0, 1)), jnp.sum(upstream, axis=(0, 1)))


def attention_scores(query, key_rows):
    return jnp.einsum(
        "bqhe,bkhe->bhqk", query, key_rows, preferred_element_type=jnp.float32
    ) * DH ** (-0.5)


def segment_forward(weights, smalls, memory_rows, token_rows):
    proj_weight, inner_weight, outer_weight, lower_weight = weights
    qv_bias, out_bias, gains, shifts, inner_bias = smalls
    batch = token_rows.shape[0]
    stacked = jnp.concatenate([memory_rows, token_rows], axis=1)
    length = stacked.shape[1]
    local = proj_weight.shape[2]
    heads = local // DH
    wide_rows = gather_rows(stacked)
    bias_three = jnp.stack([qv_bias[0], jnp.zeros_like(qv_bias[0]), qv_bias[1]])
    projected = (
        jnp.einsum("bld,dcf->blcf", wide_rows, proj_weight, preferred_element_type=jnp.float32)
        + bias_three
    ).astype(jnp.bfloat16)
    split = projected.reshape(batch, length, 3, heads, DH)
    scores = attention_scores(split[:, :, 0], split[:, :, 1])
    peak = jnp.max(scores, axis=-1, keepdims=True)
    expo = jnp.exp(scores - peak)
    totals = jnp.sum(expo, axis=-1, keepdims=True)
    probs = expo / totals
    logsum = peak[..., 0] + jnp.log(totals[..., 0])
    context = jnp.einsum(
        "bhqk,bkhe->bqhe",
        probs.astype(jnp.bfloat16),
        split[:, :, 2],
        preferred_element_type=jnp.float32,
    )
    context = context.astype(jnp.bfloat16).reshape(batch, length, local)
    attended = branch_sum(
        jnp.einsum("bld,df->blf", context, outer_weight, preferred_element_type=jnp.float32)
    )
    middle, normed_one, rstd_one = norm_forward(
        stacked.astype(jnp.float32) + attended + out_bias[0], gains[0], shifts[0]
    )
    middle_wide = gather_rows(middle.astype(jnp.bfloat16))
    before = (
        jnp.einsum("bld,df->blf", middle_wide, inner_weight, preferred_element_type=jnp.float32)
        + inner_bias
    )
    hidden = gelu_value(before).astype(jnp.bfloat16)
    branch = branch_sum(
        jnp.einsum("blf,fd->bld", hidden, lower_weight, preferred_element_type=jnp.float32)
    )
    layer_out, normed_two, rstd_two = norm_forward(
        middle + branch + out_bias[1], gains[1], shifts[1]
    )
    stored = (
        wide_rows,
        projected,
        logsum,
        context,
        normed_one,
        rstd_one,
        middle_wide,
        before,
        hidden,
        normed_two,
        rstd_two,
    )
    return (layer_out, stored)


def segment_backward(weights, smalls, upstream, stored):
    proj_weight, inner_weight, outer_weight, lower_weight = weights
    qv_bias, out_bias, gains, shifts, inner_bias = smalls
    (
        wide_rows,
        projected,
        logsum,
        context,
        normed_one,
        rstd_one,
        middle_wide,
        before,
        hidden,
        normed_two,
        rstd_two,
    ) = stored
    batch, length, local = context.shape
    heads = local // DH
    grad_two, gain_two, shift_two = norm_backward(upstream, normed_two, rstd_two, gains[1])
    grad_branch = gather_grads(grad_two.astype(jnp.bfloat16))
    grad_lower = jnp.einsum("blf,bld->fd", hidden, grad_branch, preferred_element_type=jnp.float32)
    grad_hidden = jnp.einsum(
        "bld,fd->blf", grad_branch, lower_weight, preferred_element_type=jnp.float32
    )
    grad_before = (grad_hidden * gelu_slope(before)).astype(jnp.bfloat16)
    grad_inner = jnp.einsum(
        "bld,blf->df", middle_wide, grad_before, preferred_element_type=jnp.float32
    )
    grad_inner_bias = jnp.sum(grad_before.astype(jnp.float32), axis=(0, 1))
    grad_middle = grad_two + lax.psum_scatter(
        jnp.einsum(
            "blf,df->bld", grad_before, inner_weight, preferred_element_type=jnp.float32
        ).astype(jnp.bfloat16),
        "tensor",
        scatter_dimension=2,
        tiled=True,
    ).astype(jnp.float32)
    grad_one, gain_one, shift_one = norm_backward(grad_middle, normed_one, rstd_one, gains[0])
    grad_attended = gather_grads(grad_one.astype(jnp.bfloat16))
    grad_outer = jnp.einsum(
        "bld,blf->df", context, grad_attended, preferred_element_type=jnp.float32
    )
    grad_context = jnp.einsum(
        "blf,df->bld", grad_attended, outer_weight, preferred_element_type=jnp.float32
    )
    grad_context = grad_context.astype(jnp.bfloat16)
    grad_context = grad_context.reshape(batch, length, heads, DH)
    split = projected.reshape(batch, length, 3, heads, DH)
    query, key_rows, value_rows = (split[:, :, 0], split[:, :, 1], split[:, :, 2])
    probs = jnp.exp(attention_scores(query, key_rows) - logsum[..., None])
    grad_probs = jnp.einsum(
        "bqhe,bkhe->bhqk", grad_context, value_rows, preferred_element_type=jnp.float32
    )
    weighted_sum = jnp.sum(probs * grad_probs, axis=-1, keepdims=True)
    grad_scores = (probs * (grad_probs - weighted_sum)).astype(jnp.bfloat16)
    grad_query = jnp.einsum(
        "bhqk,bkhe->bqhe", grad_scores, key_rows, preferred_element_type=jnp.float32
    ) * DH ** (-0.5)
    grad_key = jnp.einsum(
        "bhqk,bqhe->bkhe", grad_scores, query, preferred_element_type=jnp.float32
    ) * DH ** (-0.5)
    grad_value = jnp.einsum(
        "bhqk,bqhe->bkhe",
        probs.astype(jnp.bfloat16),
        grad_context,
        preferred_element_type=jnp.float32,
    )
    grad_projected = (
        jnp.stack([grad_query, grad_key, grad_value], axis=2)
        .reshape(batch, length, 3, local)
        .astype(jnp.bfloat16)
    )
    grad_proj = jnp.einsum(
        "bld,blcf->dcf", wide_rows, grad_projected, preferred_element_type=jnp.float32
    )
    column_sums = jnp.sum(grad_projected.astype(jnp.float32), axis=(0, 1))
    grad_qv = jnp.stack([column_sums[0], column_sums[2]])
    grad_stacked = grad_one + input_sum(
        jnp.einsum("blcf,dcf->bld", grad_projected, proj_weight, preferred_element_type=jnp.float32)
    )
    grad_biases = jnp.stack([jnp.sum(grad_one, axis=(0, 1)), jnp.sum(grad_two, axis=(0, 1))])
    large_grads = (grad_proj, grad_inner, grad_outer, grad_lower)
    small_grads = (
        grad_qv,
        grad_biases,
        jnp.stack([gain_one, gain_two]),
        jnp.stack([shift_one, shift_two]),
        grad_inner_bias,
    )
    return (grad_stacked, large_grads, small_grads)


def add_tuples(first, second):
    return tuple((left + right for left, right in zip(first, second)))


def shards(
    tokens,
    memory,
    w_qkv,
    b_qv,
    w_out,
    out_biases,
    norm_gains,
    norm_shifts,
    w_in,
    b_in,
    w_down,
    cotangent,
    mlm_mask,
):
    smalls = (
        b_qv.astype(jnp.float32),
        out_biases.astype(jnp.float32),
        norm_gains.astype(jnp.float32),
        norm_shifts.astype(jnp.float32),
        b_in.astype(jnp.float32),
    )
    per_batch = tokens.shape[0] // MICRO
    segments = tokens.shape[1]
    mem_rows = memory.shape[0]
    local = w_qkv.shape[2]
    inner_local = w_in.shape[1]
    empty_large = (
        jnp.zeros((D, 3, local), jnp.float32),
        jnp.zeros((D, inner_local), jnp.float32),
        jnp.zeros((local, D), jnp.float32),
        jnp.zeros((inner_local, D), jnp.float32),
    )
    full_grads = empty_large
    shard_grads = (
        jnp.zeros(w_qkv.shape, jnp.float32),
        jnp.zeros(w_in.shape, jnp.float32),
        jnp.zeros(w_out.shape, jnp.float32),
        jnp.zeros(w_down.shape, jnp.float32),
    )
    small_total = (
        jnp.zeros((2, local), jnp.float32),
        jnp.zeros((2, local), jnp.float32),
        jnp.zeros((2, local), jnp.float32),
        jnp.zeros((2, local), jnp.float32),
        jnp.zeros((inner_local,), jnp.float32),
    )
    memory_total = jnp.zeros((mem_rows, local), jnp.float32)
    out_blocks = []
    grad_blocks = []
    for batch_index in range(MICRO):
        offset = batch_index * per_batch
        batch_tokens = tokens[offset : offset + per_batch]
        batch_mask = mlm_mask[offset : offset + per_batch]
        batch_cot = cotangent[offset : offset + per_batch].astype(jnp.float32) * batch_mask[
            ..., None
        ].astype(jnp.float32)
        weights = fetch_weights(w_qkv, w_in, w_out, w_down)
        carried = memory[None]
        stored_all = []
        token_outs = []
        for seg_index in range(segments):
            layer_out, stored = segment_forward(
                weights, smalls, carried, batch_tokens[:, seg_index]
            )
            carried = layer_out[:, :mem_rows].astype(jnp.bfloat16)
            token_outs.append(layer_out[:, mem_rows:].astype(jnp.bfloat16))
            stored_all.append(stored)
        returning = jnp.zeros((per_batch, mem_rows, local), jnp.float32)
        token_grads = [None] * segments
        for seg_index in reversed(range(segments)):
            upstream = jnp.concatenate([returning, batch_cot[:, seg_index]], axis=1)
            grad_stacked, large_grads, small_grads = segment_backward(
                weights, smalls, upstream, stored_all[seg_index]
            )
            returning = grad_stacked[:, :mem_rows]
            token_grads[seg_index] = grad_stacked[:, mem_rows:]
            full_grads = add_tuples(full_grads, large_grads)
            small_total = add_tuples(small_total, small_grads)
        memory_total = memory_total + jnp.sum(returning, axis=0)
        reduced = reduce_weights(full_grads[0], full_grads[1], full_grads[2], full_grads[3])
        shard_grads = add_tuples(shard_grads, reduced)
        full_grads = empty_large
        out_blocks.append(jnp.stack(token_outs, axis=1))
        grad_blocks.append(jnp.stack(token_grads, axis=1))
    grad_qv, grad_biases, grad_gains, grad_shifts, grad_inner_bias, memory_grad = lax.psum(
        (
            small_total[0],
            small_total[1],
            small_total[2],
            small_total[3],
            small_total[4],
            memory_total,
        ),
        "dp",
    )
    outputs = jnp.concatenate(out_blocks, axis=0)
    input_grad = jnp.concatenate(grad_blocks, axis=0)
    return (
        outputs,
        input_grad,
        memory_grad,
        shard_grads[0],
        grad_qv,
        shard_grads[2],
        grad_biases,
        grad_gains,
        grad_shifts,
        shard_grads[1],
        grad_inner_bias,
        shard_grads[3],
    )


ROWS = 528
LIVE = 176


def dot_nn(left, right):
    return jnp.dot(left, right, preferred_element_type=jnp.float32)


def dot_nt(left, right):
    return lax.dot_general(
        left, right, (((1,), (1,)), ((), ())), preferred_element_type=jnp.float32
    )


def dot_tn(left, right):
    return lax.dot_general(
        left, right, (((0,), (0,)), ((), ())), preferred_element_type=jnp.float32
    )


def norm_rows(resid, gain, shift):
    center = jnp.mean(resid, axis=-1, keepdims=True)
    spread = jnp.mean(resid * resid, axis=-1, keepdims=True) - center * center
    rstd = lax.rsqrt(spread + eps_norm)
    normed = (resid - center) * rstd
    return (normed * gain + shift, normed, rstd)


def norm_rows_back(upstream, normed, rstd, gain):
    scaled = upstream * gain
    first = jnp.mean(scaled, axis=-1, keepdims=True)
    second = jnp.mean(scaled * normed, axis=-1, keepdims=True)
    result = rstd * (scaled - first - normed * second)
    return (result, jnp.sum(upstream * normed, axis=0), jnp.sum(upstream, axis=0))


MESH = pl.DeviceIdType.MESH
HBM = pl.BlockSpec(memory_space=pl.ANY)
VMEM = pl.BlockSpec(memory_space=pltpu.VMEM)
GATHER_PIECES = ((0, 0), (1, 0), (2, 0), (3, 0), (4, 0), (5, 0), (4, 1), (5, 1), (4, 2), (5, 2), (4, 3), (5, 3))
SCATTER_PIECES = ((5, 0), (5, 1), (5, 2), (5, 3), (4, 0), (4, 1), (4, 2), (4, 3), (3, 0), (0, 0), (1, 0), (2, 0))
GATHER_HOPS = (
    (3, 2, 1, 0), (3, 2, 0, 1), (3, 2, 1, 0), (3, 0, 1, 2), (3, 2, 1, 0), (3, 1, 0, 2),
    (3, 2, 0, 1), (3, 2, 1, 0), (3, 0, 1, 2), (3, 2, 0, 1), (3, 2, 1, 0), (3, 0, 1, 2),
)
SCATTER_HOPS = (
    (2, 1, 0, 3), (0, 1, 2, 3), (1, 0, 2, 3), (2, 1, 0, 3), (0, 1, 2, 3), (2, 0, 3, 1),
    (0, 1, 2, 3), (1, 2, 0, 3), (0, 2, 1, 3), (0, 1, 2, 3), (1, 0, 2, 3), (1, 0, 2, 3),
)
GATHER_STEPS = (
    0, 8, 1, 100, 16, 9, 24, 2, 17, 32, 10, 40, 3, 25, 48, 18, 11, 56, 33, 64,
    41, 19, 49, 72, 57, 80, 4, 34, 26, 88, 5, 65, 101, 12, 50, 42, 73, 13, 102, 58,
    35, 20, 81, 66, 21, 89, 103, 27, 74, 104, 51, 82, 105, 59, 106, 43, 107, 67, 28, 29,
    36, 108, 52, 90, 37, 44, 53, 75, 83, 45, 109, 91, 68, 60, 69, 61, 76, 110, 77, 92,
    84, 111, 93, 85, 112, 113,
)
SCATTER_STEPS = (
    0, 8, 16, 1, 9, 17, 24, 32, 100, 25, 33, 2, 40, 10, 48, 18, 101, 41, 3, 49,
    26, 56, 34, 64, 11, 102, 19, 57, 27, 65, 4, 42, 103, 12, 35, 72, 20, 80, 5, 73,
    50, 88, 13, 28, 36, 81, 21, 58, 89, 29, 51, 104, 37, 105, 66, 106, 59, 107, 43, 108,
    52, 82, 109, 110, 67, 74, 44, 90, 60, 53, 68, 61, 83, 69, 75, 45, 84, 91, 76, 85,
    92, 77, 93,
)
SLOTS = 2


def here():
    me = lax.axis_index("dp")
    core = lax.axis_index("tensor")
    bits = tuple((me // (1 << b)) % 2 for b in range(4))
    peers = tuple({"dp": me + (1 - 2 * bits[b]) * (1 << b)} for b in range(4))
    return core, bits, peers + ({"tensor": 1 - core},)


def greet(peers):
    barrier = pltpu.get_barrier_semaphore()
    for peer in peers:
        pl.semaphore_signal(barrier, inc=1, device_id=peer, device_id_type=MESH)
    pl.semaphore_wait(barrier, len(peers))


def block_index(bits, free, flip=None):
    index = []
    for b in (3, 2, 1, 0):
        if b == flip:
            index.append(1 - bits[b])
        elif b in free:
            index.append(slice(None))
        else:
            index.append(bits[b])
    return tuple(index)


def columns(array, part, core, width):
    blocks = 4 if array > 3 else 1
    return pl.ds(pl.multiple_of((core * blocks + part) * width, width), width)


def shard_block(shards, piece, width):
    array, part = piece
    if array < 3:
        return shards[array].at[array]
    return shards[array].at[:, pl.ds(part * width, width)]


def attend_pair(query, key_rows, value_rows, valid):
    main = key_rows.shape[0] - 16
    lane = lax.broadcasted_iota(jnp.int32, (1, 2 * DH), 1)
    left = lane < DH
    query = query * DH ** (-0.5)
    zero = jnp.zeros_like(query)
    tail_lane = lax.broadcasted_iota(jnp.int32, (1, 32), 1)
    tail_zero = jnp.zeros((16, 2 * DH), query.dtype)
    key_tail, value_tail = key_rows[main:], value_rows[main:]
    keys_both = jnp.concatenate(
        [jnp.where(left, key_tail, tail_zero), jnp.where(left, tail_zero, key_tail)], axis=0
    )
    values_both = jnp.concatenate(
        [jnp.where(left, value_tail, tail_zero), jnp.where(left, tail_zero, value_tail)], axis=0
    )
    ones_both = jnp.concatenate(
        [jnp.where(left, tail_zero, tail_zero + 1), jnp.where(left, tail_zero + 1, tail_zero)], axis=0
    )
    tail = dot_nt(query, keys_both)
    tail = jnp.where(tail_lane % 16 < valid - main, tail, -1e30)
    peaks, parts = [], []
    for head in range(2):
        picked = jnp.where(left if head == 0 else ~left, query, zero)
        scores = dot_nt(picked, key_rows[:main])
        side = (tail_lane < 16) if head == 0 else (tail_lane >= 16)
        peak = jnp.maximum(
            jnp.max(scores, axis=1, keepdims=True),
            jnp.max(jnp.where(side, tail, -1e30), axis=1, keepdims=True),
        )
        expo = jnp.exp(scores - peak).astype(jnp.bfloat16)
        one = jnp.ones_like(value_rows[:main])
        values = jnp.where(left if head == 0 else ~left, value_rows[:main], one)
        parts.append(dot_nn(expo, values))
        peaks.append(peak)
    tail = jnp.exp(tail - jnp.where(tail_lane < 16, peaks[0], peaks[1])).astype(jnp.bfloat16)
    both = dot_nn(tail, jnp.concatenate([values_both, ones_both], axis=1))
    value_sum = jnp.where(left, parts[0], parts[1]) + both[:, : 2 * DH]
    total = jnp.where(left, parts[1], parts[0]) + both[:, 2 * DH :]
    return (value_sum / pltpu.roll(total, DH, 1)).astype(jnp.bfloat16)


def attend_kernel(valid, q_ref, k_ref, v_ref, out_ref):
    out_ref[...] = attend_pair(q_ref[...], k_ref[...], v_ref[...], valid)


def attend(query, key_rows, value_rows, valid):
    block = pl.BlockSpec((query.shape[0], 2 * DH), lambda i: (0, i))
    return pl.pallas_call(
        functools.partial(attend_kernel, valid),
        grid=(D // (2 * DH),),
        out_shape=jax.ShapeDtypeStruct(query.shape, jnp.bfloat16),
        in_specs=[block] * 3,
        out_specs=block,
        compiler_params=pltpu.CompilerParams(vmem_limit_bytes=32 << 20),
        name="attend",
    )(query, key_rows, value_rows)


def attend_back_pair(query, key_rows, value_rows, grads, valid):
    live = query.shape[0]
    left = lax.broadcasted_iota(jnp.int32, (1, 2 * DH), 1) < DH
    zero = jnp.zeros_like(query)
    query = query * DH ** (-0.5)
    picked = jnp.concatenate([jnp.where(left, query, zero), jnp.where(left, zero, query)], axis=0)
    up = jnp.concatenate([jnp.where(left, grads, zero), jnp.where(left, zero, grads)], axis=0)
    scores = dot_nt(key_rows, picked)
    scores = jnp.where(lax.broadcasted_iota(jnp.int32, scores.shape, 0) < valid, scores, -1e30)
    expo = jnp.exp(scores - jnp.max(scores, axis=0, keepdims=True))
    probs = expo * (1.0 / jnp.sum(expo, axis=0, keepdims=True))
    grad_probs = dot_nt(value_rows, up)
    weighted = jnp.sum(probs * grad_probs, axis=0, keepdims=True)
    grad_scores = (probs * (grad_probs - weighted)).astype(jnp.bfloat16)
    grad_query = dot_tn(grad_scores, key_rows)
    grad_query = jnp.where(left, grad_query[:live], grad_query[live:]) * DH ** (-0.5)
    grad_key = dot_nn(grad_scores, picked)
    grad_value = dot_nn(probs.astype(jnp.bfloat16), up)
    return tuple(grad.astype(jnp.bfloat16) for grad in (grad_query, grad_key, grad_value))


def attend_back_kernel(valid, q_ref, k_ref, v_ref, g_ref, dq_ref, dk_ref, dv_ref):
    dq_ref[...], dk_ref[...], dv_ref[...] = attend_back_pair(
        q_ref[...], k_ref[...], v_ref[...], g_ref[...], valid
    )


def attend_back(query, key_rows, value_rows, grad_context, valid):
    live = grad_context.shape[0]
    short = pl.BlockSpec((live, 2 * DH), lambda i: (0, i))
    tall = pl.BlockSpec((key_rows.shape[0], 2 * DH), lambda i: (0, i))
    low = jnp.bfloat16
    return pl.pallas_call(
        functools.partial(attend_back_kernel, valid),
        grid=(D // (2 * DH),),
        out_shape=[jax.ShapeDtypeStruct((live, D), low)] + [jax.ShapeDtypeStruct(key_rows.shape, low)] * 2,
        in_specs=[short, tall, tall, short],
        out_specs=[short, tall, tall],
        compiler_params=pltpu.CompilerParams(vmem_limit_bytes=32 << 20),
        name="attend_back",
    )(query, key_rows, value_rows, grad_context)


PACK_BIASES, PACK_OUT, PACK_GAINS, PACK_SHIFTS, PACK_INNER = 16, 18, 20, 22, 24


def gather_kernel(
    mem_rows, valid, toks, cots, pack, sq, so, si, sl, move, live_move,
    packs, fq, fk, fv, fo, fi, fl, stacked_a, stacked_b, ups, query, key_rows, value_rows,
    query_live, context_live, normed_one, rstd_one, middle_live, before_live, hidden_live, normed_two, rstd_two, low_out,
    x_v, c_v, vq, vo, vi, vl, held, context, middle, middle_low, branch,
    send, recv, local, loads, extra,
):
    core, bits, peers = here()
    width = pack.shape[1]
    live = ups.shape[1]
    shards = (vq, vq, vq, vo, vi, vl)
    fulls = (fq, fk, fv, fo, fi, fl)
    mine = pl.ds(pl.multiple_of(core * width, width), width)
    shard_in = [
        pltpu.make_async_copy(src, dst, extra.at[n])
        for n, (src, dst) in enumerate(((sq, vq), (so, vo), (si, vi), (sl, vl)))
    ]
    rows_own = [
        pltpu.make_async_copy(toks.at[core], x_v.at[:, :, mine], extra.at[4]),
        pltpu.make_async_copy(cots.at[core], c_v.at[:, :, mine], extra.at[5]),
        pltpu.make_async_copy(pack, packs.at[core], extra.at[6]),
    ]
    for copy in shard_in + rows_own:
        copy.start()
    own = []
    for p, (array, part) in enumerate(GATHER_PIECES):
        own.append(pltpu.make_async_copy(
            shard_block(shards, (array, part), width),
            fulls[array].at[block_index(bits, ()) + (slice(None), columns(array, part, core, width))],
            local.at[p],
        ))
    greet(peers)
    for copy in shard_in:
        copy.wait()
    for copy in own:
        copy.start()

    def remote(src, dst, slot, peer):
        return pltpu.make_async_remote_copy(
            src_ref=src, dst_ref=dst, send_sem=send.at[slot], recv_sem=recv.at[slot],
            device_id=peer, device_id_type=MESH)

    def stage(p, s):
        array, part = GATHER_PIECES[p]
        order = GATHER_HOPS[p]
        cols = columns(array, part, core, width)
        dst = fulls[array].at[block_index(bits, order[:s]) + (slice(None), cols)]
        if s == 0:
            src = shard_block(shards, (array, part), width)
        else:
            src = dst
        peer = peers[order[s]] if s < 4 else peers[4]
        return remote(src, dst, p * 5 + s, peer)

    swaps = [
        remote(toks.at[1 - core], x_v.at[:, :, mine], 60, peers[4]),
        remote(cots.at[1 - core], c_v.at[:, :, mine], 61, peers[4]),
        remote(pack, packs.at[core], 62, peers[4]),
    ]
    started, loading = {}, {}

    def load(p):
        array, part = GATHER_PIECES[p]
        blocks = 4 if array > 3 else 1
        every = (slice(None),) * 5
        loading[p] = [
            pltpu.make_async_copy(
                fulls[array].at[every + (pl.ds((half * blocks + part) * width, width),)],
                held.at[(p % 6,) + every + (pl.ds(half * width, width),)],
                loads.at[2 * p + half],
            )
            for half in range(2)
        ]
        for copy in loading[p]:
            copy.start()

    def loaded(p):
        for copy in loading.pop(p):
            copy.wait()

    def weight(p, cols):
        block = held[p % 6, :, :, :, :, :, cols]
        return block.reshape(2 * width, block.shape[-1])

    def wide(row):
        return jnp.concatenate([packs[0, row : row + 1], packs[1, row : row + 1]], axis=1).astype(jnp.float32)

    def norm(resid, gain, shift):
        center = jnp.mean(resid, axis=1, keepdims=True)
        spread = jnp.mean(resid * resid, axis=1, keepdims=True) - center * center
        rstd = lax.rsqrt(spread + eps_norm)
        normed = (resid - center) * rstd
        return normed * gain + shift, normed, rstd

    def compute(task):
        if task == 0:
            for copy in rows_own:
                copy.wait()
            for swap in swaps:
                swap.wait_recv()
            memory = jnp.concatenate([packs[0, :16], packs[1, :16]], axis=1)
            is_memory = lax.broadcasted_iota(jnp.int32, memory.shape, 0) < mem_rows
            stacked_a[...] = dot_nn(move[0], x_v[0]).astype(jnp.bfloat16)
            stacked_a[:16] = jnp.where(is_memory, memory, stacked_a[:16])
            stacked_b[...] = dot_nn(move[1], x_v[1]).astype(jnp.bfloat16)
            for n in range(2):
                ups[n] = dot_nn(live_move[n], c_v[n]).astype(jnp.bfloat16)
        elif task < 4:
            n = task - 1
            loaded(n)
            target = (query, key_rows, value_rows)[n]
            for half in range(2):
                cols = pl.ds(half * width, width)
                got = dot_nn(stacked_a[...], weight(n, cols))
                if n != 1:
                    row = PACK_BIASES + n // 2
                    got = got + packs[half, row : row + 1].astype(jnp.float32)
                target[:, cols] = got.astype(jnp.bfloat16)
                if n == 0:
                    query_live[:, cols] = got[:live].astype(jnp.bfloat16)
        elif task < 8:

            def pair(n, carry):
                cols = pl.ds(pl.multiple_of((2 * (task - 4) + n) * 2 * DH, 2 * DH), 2 * DH)
                context[:, cols] = attend_pair(query[:, cols], key_rows[:, cols], value_rows[:, cols], valid)
                return carry

            lax.fori_loop(0, 2, pair, 0)
        elif task == 8:
            loaded(3)
            attended = dot_nt(context[...], weight(3, slice(None)))
            resid = stacked_a[...].astype(jnp.float32) + attended + wide(PACK_OUT)
            value, normed, rstd = norm(resid, wide(PACK_GAINS), wide(PACK_SHIFTS))
            middle[...] = value
            middle_low[...] = value.astype(jnp.bfloat16)
            middle_live[...] = value[:live].astype(jnp.bfloat16)
            context_live[...] = context[:live]
            normed_one[...] = normed[:live]
            rstd_one[...] = jnp.broadcast_to(rstd[:live], rstd_one.shape)
        elif task < 13:
            j = task - 9
            loaded(4 + 2 * j)
            loaded(5 + 2 * j)

            def hidden_block(half, carry):
                cols = pl.ds(pl.multiple_of(half * width, width), width)
                place = pl.ds(pl.multiple_of((half * 4 + j) * width, width), width)
                bias = packs[half, PACK_INNER + j : PACK_INNER + j + 1].astype(jnp.float32)
                before = dot_nn(middle_low[...], weight(4 + 2 * j, cols)) + bias
                before_live[:, place] = before[:live]
                hidden = gelu_value(before).astype(jnp.bfloat16)
                hidden_live[:, place] = hidden[:live]
                branch[...] = branch[...] + dot_nt(hidden, weight(5 + 2 * j, cols))
                return carry

            if j == 0:
                branch[...] = middle[...] + wide(PACK_OUT + 1)
            lax.fori_loop(0, 2, hidden_block, 0)
        else:
            value, normed, rstd = norm(branch[...], wide(PACK_GAINS + 1), wide(PACK_SHIFTS + 1))
            low_out[...] = value.astype(jnp.bfloat16)
            is_memory = lax.broadcasted_iota(jnp.int32, (16, 2 * width), 0) < mem_rows
            stacked_b[:16] = jnp.where(is_memory, low_out[:16], stacked_b[:16])
            normed_two[...] = normed[:live]
            rstd_two[...] = jnp.broadcast_to(rstd[:live], rstd_two.shape)

    for tick, step in enumerate(GATHER_STEPS):
        if step >= 100:
            compute(step - 100)
            continue
        p, s = step // 8, step % 8
        if s > 0:
            started[p, s - 1].wait_recv()
        if s == 1:
            own[p].wait()
        if s == 5:
            load(p)
        else:
            started[p, s] = stage(p, s)
            started[p, s].start()
        if tick == 2:
            for swap in swaps:
                swap.start()
    for copy in started.values():
        copy.wait_send()
    for swap in swaps:
        swap.wait_send()


def gather_all(mem_rows, valid, toks, cots, pack, sq, so, si, sl, move, live_move):
    width = pack.shape[1]
    rows = sq.shape[1]
    low, full = jnp.bfloat16, jnp.float32
    total, live = move.shape[1], live_move.shape[1]
    hidden = 2 * si.shape[1]
    out = [((2,) + pack.shape, low)]
    for size in (2 * width, 2 * width, 2 * width, 2 * width, hidden, hidden):
        out.append(((2, 2, 2, 2, rows, size), low))
    out += [((total, 2 * width), low)] * 2 + [((2, live, 2 * width), low)]
    out += [((total, 2 * width), low)] * 3 + [((live, 2 * width), low)] * 2
    out += [((live, 2 * width), full), ((live, 2 * width), full), ((live, 2 * width), low)]
    out += [((live, hidden), full), ((live, hidden), low)]
    out += [((live, 2 * width), full), ((live, 2 * width), full), ((total, 2 * width), low)]
    block = (2, 2, 2, 2, rows, 2 * width)
    got = pl.pallas_call(
        functools.partial(gather_kernel, mem_rows, valid),
        out_shape=[jax.ShapeDtypeStruct(*one) for one in out],
        in_specs=[HBM, HBM, VMEM] + [HBM] * 4 + [VMEM] * 2,
        out_specs=[VMEM] + [HBM] * 6 + [VMEM] * (len(out) - 7),
        scratch_shapes=[
            pltpu.VMEM(toks.shape[1:3] + (2 * width,), low),
            pltpu.VMEM(toks.shape[1:3] + (2 * width,), low),
            pltpu.VMEM(sq.shape, low),
            pltpu.VMEM(so.shape, low),
            pltpu.VMEM(si.shape, low),
            pltpu.VMEM(sl.shape, low),
            pltpu.VMEM((6,) + block, low),
            pltpu.VMEM((total, 2 * width), low),
            pltpu.VMEM((total, 2 * width), full),
            pltpu.VMEM((total, 2 * width), low),
            pltpu.VMEM((total, 2 * width), full),
            pltpu.SemaphoreType.DMA((63,)),
            pltpu.SemaphoreType.DMA((63,)),
            pltpu.SemaphoreType.DMA((12,)),
            pltpu.SemaphoreType.DMA((24,)),
            pltpu.SemaphoreType.DMA((7,)),
        ],
        compiler_params=pltpu.CompilerParams(collective_id=0, has_side_effects=True, vmem_limit_bytes=62 << 20),
        name="gather_all",
    )(toks, cots, pack, sq, so, si, sl, move, live_move)
    wide = [array.reshape(16 * rows, array.shape[-1]) for array in got[1:7]]
    return got[0], wide, got[7:]


def scatter_kernel(mem_rows, valid, *refs):
    (rows_a, out_a, context_a, middle_a, before_a, branch_a, hidden_a) = refs[0:7]
    second_rows = refs[7:17]
    query, keys_in, values_in, up, grad_one, wq, wk, wv, move, small_a, small_b, outs_a, outs_b, grads_b = refs[17:31]
    oq, oo, oi, ol, osmall, out_item, grad_item = refs[31:38]
    (acc, first, second, third, fourth, slots, wide_x, wide_s, held, grad_query, key_rows, value_rows,
     source, result, total_rows, small_v, small_in, small_recv, send, recv, extra, sent) = refs[38:]
    first_rows = (rows_a, grad_query, key_rows, value_rows, out_a, context_a, middle_a, before_a, branch_a, hidden_a)
    both_rows = (first_rows, second_rows)
    core, bits, peers = here()
    width = osmall.shape[1]
    live = grad_query.shape[0]
    bufs = (first, second, third, fourth)
    lefts = (0, 0, 0, 4, 6, 8)
    rights = (1, 2, 3, 5, 7, 9)
    turned = set()
    mine = pl.ds(pl.multiple_of(core * width, width), width)
    other = pl.ds(pl.multiple_of((1 - core) * width, width), width)
    stage_in = [
        pltpu.make_async_copy(keys_in, key_rows, extra.at[0]),
        pltpu.make_async_copy(values_in, value_rows, extra.at[1]),
    ]
    for copy in stage_in:
        copy.start()
    greet(peers)

    def bring(src, dst, sem):
        copy = pltpu.make_async_copy(src, dst, extra.at[sem])
        copy.start()
        return copy

    def remote(src, dst, slot, peer):
        return pltpu.make_async_remote_copy(
            src_ref=src, dst_ref=dst, send_sem=send.at[slot], recv_sem=recv.at[slot],
            device_id=peer, device_id_type=MESH)

    def turn(array):
        left = lefts[array]
        if left in turned:
            return
        turned.add(left)
        for n, rows in enumerate((first_rows, second_rows)):
            if left == 0:
                bring(rows[0], source, 2).wait()
                wide_x[n] = source[...].T
            else:
                wide_s[left // 2 - 2, n] = rows[left][...].T

    def multiply(array, offset, size):
        total = None
        for n, rows in enumerate((first_rows, second_rows)):
            right = rows[rights[array]][:, pl.ds(offset, size)]
            if array in (1, 2):
                left = wide_x[n]
            elif array == 0:
                left = wide_x[n, :, :live]
            else:
                left = wide_s[lefts[array] // 2 - 2, n]
            term = jnp.dot(left, right, preferred_element_type=jnp.float32)
            total = term if total is None else total + term
        return total

    tile = width // 2

    def produce(p, slot):
        array, part = SCATTER_PIECES[p]
        turn(array)
        blocks = 4 if array > 3 else 1
        base = ((1 - core) * blocks + part) * width

        def body(n, carry):
            offset = pl.multiple_of(base + n * tile, tile)
            got = multiply(array, offset, tile).astype(jnp.bfloat16)
            slots[slot, :, :, :, :, :, pl.ds(pl.multiple_of(n * tile, tile), tile)] = got.reshape(
                slots.shape[1:6] + (tile,)
            )
            return carry

        lax.fori_loop(0, 2, body, 0)

    def combine(p):
        array, part = SCATTER_PIECES[p]
        blocks = 4 if array > 3 else 1
        base = (core * blocks + part) * width

        def body(n, carry):
            offset = pl.multiple_of(base + n * tile, tile)
            cols = pl.ds(pl.multiple_of(n * tile, tile), tile)
            got = multiply(array, offset, tile).reshape(slots.shape[1:6] + (tile,))
            acc[p, :, :, :, :, :, cols] = (
                got + acc[p, :, :, :, :, :, cols].astype(jnp.float32)
            ).astype(jnp.bfloat16)
            return carry

        lax.fori_loop(0, 2, body, 0)

    def stage(p, s):
        if s == 0:
            return remote(slots.at[p % SLOTS], acc.at[p], p * 5, peers[4])
        order = SCATTER_HOPS[p]
        src = acc.at[(p,) + block_index(bits, order[s:], flip=order[s - 1])]
        return remote(src, bufs[s - 1].at[p], p * 5 + s, peers[order[s - 1]])

    def fold(p, s):
        array, part = SCATTER_PIECES[p]
        order = SCATTER_HOPS[p]
        free = [b for b in (3, 2, 1, 0) if b in order[s:]]
        for n in range(1 << len(free)):
            at = {b: (n >> i) % 2 for i, b in enumerate(reversed(free))}
            where = tuple(at.get(b, bits[b]) for b in (3, 2, 1, 0))
            got = bufs[s - 1][(p,) + tuple(at[b] for b in free)]
            if s < 4:
                acc[(p,) + where] = acc[(p,) + where] + got
            else:
                total = acc[(p,) + where].astype(jnp.float32) + got.astype(jnp.float32)
                if array < 3:
                    oq[array] = total
                elif array == 4:
                    oi[:, pl.ds(part * width, width)] = total
                elif array == 3:
                    oo[...] = total
                else:
                    ol[:, pl.ds(part * width, width)] = total

    small_started = {}

    def small_stage(s):
        peer = peers[4] if s == 0 else peers[s - 1]
        src = small_v.at[:, other] if s == 0 else small_in.at[s]
        return remote(src, small_recv.at[s], 60 + s, peer)

    def small_step(n):
        if n == 0:
            small_in[0] = small_v[:, mine]
        else:
            small_started[n - 1].wait_recv()
            total = small_in[n - 1] + small_recv[n - 1]
            if n < 5:
                small_in[n] = total
            else:
                osmall[...] = total
        if n < 5:
            small_started[n] = small_stage(n)
            small_started[n].start()

    swaps, places = [], []

    def unpermute(n, values, target, segment):
        if n > 1:
            swaps[n - 2].wait_send()
            places[n - 2].wait()
        result[n % 2] = dot_tn(move[segment], values).astype(jnp.bfloat16)
        places.append(
            pltpu.make_async_copy(result.at[n % 2, :, mine], target.at[core, segment], sent.at[n])
        )
        swaps.append(remote(result.at[n % 2, :, other], target.at[core, segment], 65 + n, peers[4]))
        places[n].start()
        swaps[n].start()

    weights = (wk, wv, wq)
    fetched = {}

    def compute(task):
        if task < 4:
            if task == 0:
                for copy in stage_in:
                    copy.wait()
                fetched[0] = bring(weights[0], held, 3)

            def pair(n, carry):
                cols = pl.ds(pl.multiple_of((2 * task + n) * 2 * DH, 2 * DH), 2 * DH)
                grad_query[:, cols], key_rows[:, cols], value_rows[:, cols] = attend_back_pair(
                    query[:, cols], key_rows[:, cols], value_rows[:, cols], up[:, cols], valid
                )
                return carry

            lax.fori_loop(0, 2, pair, 0)
        elif task < 7:
            n = task - 4
            fetched[n].wait()
            if n == 0:
                total_rows[...] = dot_nt(key_rows[...], held[...])
            elif n == 1:
                total_rows[...] = total_rows[...] + dot_nt(value_rows[...], held[...])
            else:
                total_rows[:live] = total_rows[:live] + grad_one[...] + dot_nt(grad_query[...], held[...])
                row = lax.broadcasted_iota(jnp.int32, (16, 2 * width), 0)
                small_v[:16] = jnp.where(row < mem_rows, total_rows[:16], 0.0)
                query_sum, value_sum = (
                    sum(jnp.sum(rows[n][...].astype(jnp.float32), axis=0, keepdims=True) for rows in both_rows)
                    for n in (1, 3)
                )
                small_v[16:24] = small_a[...] + small_b[...] + jnp.where(
                    row[:8] == 0, query_sum, jnp.where(row[:8] == 1, value_sum, 0.0)
                )
                inner = [
                    jnp.sum(before[...].astype(jnp.float32), axis=0, keepdims=True)
                    for before in (before_a, second_rows[7])
                ]
                inner = inner[0] + inner[1]
                blocks = inner.shape[1] // (2 * width)
                small_v[24:] = jnp.concatenate(
                    [
                        jnp.concatenate(
                            [inner[:, (h * blocks + n) * width : (h * blocks + n + 1) * width] for h in range(2)],
                            axis=1,
                        )
                        for n in range(blocks)
                    ]
                    + [jnp.zeros((small_v.shape[0] - 24 - blocks, 2 * width), jnp.float32)],
                    axis=0,
                )
            if n < 2:
                fetched[n + 1] = bring(weights[n + 1], held, 3)
        elif task == 7:
            unpermute(0, total_rows[...].astype(jnp.bfloat16), grad_item, 0)
        else:
            values, target, segment = (
                (outs_a, out_item, 0),
                (outs_b, out_item, 1),
                (grads_b, grad_item, 1),
            )[task - 8]
            bring(values, source, 2).wait()
            unpermute(task - 7, source[...], target, segment)

    started = {}
    ready = None
    for step in SCATTER_STEPS:
        if step >= 100:
            compute(step - 100)
            if step == 106:
                ready = 0
            continue
        p, s = step // 8, step % 8
        if s == 0:
            if p >= SLOTS:
                started[p - SLOTS, 0].wait_send()
            produce(p, p % SLOTS)
        else:
            started[p, s - 1].wait_recv()
            if s == 1:
                combine(p)
            else:
                fold(p, s - 1)
        if s < 5:
            started[p, s] = stage(p, s)
            started[p, s].start()
        if ready is not None:
            ready += 1
            if ready % 3 == 0 and ready <= 18:
                small_step(ready // 3 - 1)
    for (p, s), copy in started.items():
        if s > 0 or p >= len(SCATTER_PIECES) - SLOTS:
            copy.wait_send()
    for s in range(5):
        small_started[s].wait_send()
    for n in range(4):
        if n > 1:
            swaps[n].wait_send()
            places[n].wait()
        swaps[n].wait_recv()


def scatter_all(mem_rows, valid, first_rows, second_rows, tail, smalls, outs, grads):
    width = smalls[0].shape[1] // 2
    small_rows = 32
    rows = 2 * width // 16
    low, full = jnp.bfloat16, jnp.float32
    count = len(SCATTER_PIECES)
    long, live = second_rows[0].shape[0], second_rows[1].shape[0]
    move = tail[-1]
    tokens = move.shape[2]
    item = (2, 2, tokens, width)
    return pl.pallas_call(
        functools.partial(scatter_kernel, mem_rows, valid),
        out_shape=[
            jax.ShapeDtypeStruct((3, rows, width), full),
            jax.ShapeDtypeStruct((rows, width), full),
            jax.ShapeDtypeStruct((rows, 4 * width), full),
            jax.ShapeDtypeStruct((rows, 4 * width), full),
            jax.ShapeDtypeStruct((small_rows, width), full),
            jax.ShapeDtypeStruct(item, low),
            jax.ShapeDtypeStruct(item, low),
        ],
        in_specs=[HBM] + [VMEM] * 6 + [HBM] + [VMEM] * 9
        + [VMEM, HBM, HBM, VMEM, VMEM, HBM, HBM, HBM, VMEM, VMEM, VMEM, HBM, HBM, HBM],
        out_specs=[VMEM] * 5 + [HBM] * 2,
        scratch_shapes=[
            pltpu.VMEM((count, 2, 2, 2, 2, rows, width), low),
            pltpu.VMEM((count, 2, 2, 2, rows, width), low),
            pltpu.VMEM((count, 2, 2, rows, width), low),
            pltpu.VMEM((count, 2, rows, width), low),
            pltpu.VMEM((count, rows, width), low),
            pltpu.VMEM((SLOTS, 2, 2, 2, 2, rows, width), low),
            pltpu.VMEM((2, 2 * width, long), low),
            pltpu.VMEM((3, 2, 2 * width, live), low),
            pltpu.VMEM((2 * width, 2 * width), low),
            pltpu.VMEM((live, 2 * width), low),
            pltpu.VMEM((long, 2 * width), low),
            pltpu.VMEM((long, 2 * width), low),
            pltpu.VMEM((long, 2 * width), low),
            pltpu.VMEM((2, tokens, 2 * width), low),
            pltpu.VMEM((long, 2 * width), full),
            pltpu.VMEM((small_rows, 2 * width), full),
            pltpu.VMEM((5, small_rows, width), full),
            pltpu.VMEM((5, small_rows, width), full),
            pltpu.SemaphoreType.DMA((69,)),
            pltpu.SemaphoreType.DMA((69,)),
            pltpu.SemaphoreType.DMA((4,)),
            pltpu.SemaphoreType.DMA((4,)),
        ],
        compiler_params=pltpu.CompilerParams(collective_id=1, has_side_effects=True, vmem_limit_bytes=67_000_000),
        name="scatter_all",
    )(*first_rows, *second_rows, *tail[:-1], move, *smalls, *outs, *grads)


def normalize(resid, gain, shift):
    center = jnp.mean(resid, axis=1, keepdims=True)
    spread = jnp.mean(resid * resid, axis=1, keepdims=True) - center * center
    rstd = lax.rsqrt(spread + eps_norm)
    normed = (resid - center) * rstd
    return normed * gain + shift, normed, rstd


def tail_kernel(
    context, stacked, outer, wide, inner, lower, bias,
    context_live, normed_one, rstd_one, middle_live, before_live, hidden_live, normed_two, rstd_two, low_out,
    middle_low, branch,
):
    step = pl.program_id(0)
    live = context_live.shape[0]

    @pl.when(step == 0)
    def _():
        resid = stacked[...].astype(jnp.float32) + dot_nt(context[...], outer[...])
        resid = resid + wide[PACK_OUT : PACK_OUT + 1]
        middle, normed, rstd = normalize(
            resid, wide[PACK_GAINS : PACK_GAINS + 1], wide[PACK_SHIFTS : PACK_SHIFTS + 1]
        )
        branch[...] = middle + wide[PACK_OUT + 1 : PACK_OUT + 2]
        middle_low[...] = middle.astype(jnp.bfloat16)
        middle_live[...] = middle[:live].astype(jnp.bfloat16)
        context_live[...] = context[:live]
        normed_one[...] = normed[:live]
        rstd_one[...] = jnp.broadcast_to(rstd[:live], rstd_one.shape)

    before = dot_nn(middle_low[...], inner[...]) + bias[...]
    before_live[...] = before[:live]
    hidden = gelu_value(before).astype(jnp.bfloat16)
    hidden_live[...] = hidden[:live]
    branch[...] = branch[...] + dot_nt(hidden, lower[...])

    @pl.when(step == pl.num_programs(0) - 1)
    def _():
        value, normed, rstd = normalize(
            branch[...], wide[PACK_GAINS + 1 : PACK_GAINS + 2], wide[PACK_SHIFTS + 1 : PACK_SHIFTS + 2]
        )
        low_out[...] = value.astype(jnp.bfloat16)
        normed_two[...] = normed[:live]
        rstd_two[...] = jnp.broadcast_to(rstd[:live], rstd_two.shape)


def whole_block(*shape):
    return pl.BlockSpec(shape, lambda j: (0,) * len(shape))


def layer_tail(context, stacked, outer, wide, inner, lower, bias, live):
    total, hidden, size = context.shape[0], inner.shape[1], 512
    low, full = jnp.bfloat16, jnp.float32
    step = lambda rows: pl.BlockSpec((rows, size), lambda j: (0, j))
    row = lambda dtype: (jax.ShapeDtypeStruct((live, D), dtype), whole_block(live, D))
    out = [
        row(low), row(full), row(full), row(low),
        (jax.ShapeDtypeStruct((live, hidden), full), step(live)),
        (jax.ShapeDtypeStruct((live, hidden), low), step(live)),
        row(full), row(full),
        (jax.ShapeDtypeStruct((total, D), low), whole_block(total, D)),
    ]
    return pl.pallas_call(
        tail_kernel,
        grid=(hidden // size,),
        out_shape=[one[0] for one in out],
        in_specs=[
            whole_block(total, D), whole_block(total, D), whole_block(D, D), whole_block(*wide.shape),
            step(D), step(D), step(1),
        ],
        out_specs=[one[1] for one in out],
        scratch_shapes=[pltpu.VMEM((total, D), low), pltpu.VMEM((total, D), full)],
        compiler_params=pltpu.CompilerParams(vmem_limit_bytes=56 << 20),
        name="layer_tail",
    )(context, stacked, outer, wide, inner, lower, bias)


def back_norm(upstream, normed, rstd, gain):
    scaled = upstream * gain
    first = jnp.mean(scaled, axis=1, keepdims=True)
    second = jnp.mean(scaled * normed, axis=1, keepdims=True)
    result = rstd * (scaled - first - normed * second)
    return result, jnp.sum(upstream * normed, axis=0, keepdims=True), jnp.sum(upstream, axis=0, keepdims=True)


def tail_back_kernel(
    upstream, normed_two, rstd_two, before, lower, inner, normed_one, rstd_one, outer, wide,
    grad_branch, grad_before, grad_one, grad_attended, grad_context, sums,
    grad_middle,
):
    step = pl.program_id(0)

    @pl.when(step == 0)
    def _():
        grad, gain, shift = back_norm(
            upstream[...], normed_two[...], rstd_two[...], wide[PACK_GAINS + 1 : PACK_GAINS + 2]
        )
        grad_middle[...] = grad
        grad_branch[...] = grad.astype(jnp.bfloat16)
        sums[...] = jnp.zeros_like(sums)
        sums[3:4] = jnp.sum(grad, axis=0, keepdims=True)
        sums[5:6] = gain
        sums[7:8] = shift

    grad_hidden = dot_nn(grad_branch[...], lower[...])
    low = (grad_hidden * gelu_slope(before[...])).astype(jnp.bfloat16)
    grad_before[...] = low
    grad_middle[...] = grad_middle[...] + dot_nt(low, inner[...])

    @pl.when(step == pl.num_programs(0) - 1)
    def _():
        grad, gain, shift = back_norm(
            grad_middle[...], normed_one[...], rstd_one[...], wide[PACK_GAINS : PACK_GAINS + 1]
        )
        grad_one[...] = grad
        attended = grad.astype(jnp.bfloat16)
        grad_attended[...] = attended
        grad_context[...] = dot_nn(attended, outer[...]).astype(jnp.bfloat16)
        sums[2:3] = jnp.sum(grad, axis=0, keepdims=True)
        sums[4:5] = gain
        sums[6:7] = shift


def tail_back(upstream, normed_two, rstd_two, before, lower, inner, normed_one, rstd_one, outer, wide):
    live, hidden, size = upstream.shape[0], inner.shape[1], 512
    low, full = jnp.bfloat16, jnp.float32
    step = lambda rows: pl.BlockSpec((rows, size), lambda j: (0, j))
    rows = whole_block(live, D)
    out = [
        (jax.ShapeDtypeStruct((live, D), low), rows),
        (jax.ShapeDtypeStruct((live, hidden), low), step(live)),
        (jax.ShapeDtypeStruct((live, D), full), rows),
        (jax.ShapeDtypeStruct((live, D), low), rows),
        (jax.ShapeDtypeStruct((live, D), low), rows),
        (jax.ShapeDtypeStruct((8, D), full), whole_block(8, D)),
    ]
    return pl.pallas_call(
        tail_back_kernel,
        grid=(hidden // size,),
        out_shape=[one[0] for one in out],
        in_specs=[
            rows, rows, rows, step(live), step(D), step(D), rows, rows, whole_block(D, D), whole_block(*wide.shape),
        ],
        out_specs=[one[1] for one in out],
        scratch_shapes=[pltpu.VMEM((live, D), full)],
        compiler_params=pltpu.CompilerParams(vmem_limit_bytes=40 << 20),
        name="tail_back",
    )(upstream, normed_two, rstd_two, before, lower, inner, normed_one, rstd_one, outer, wide)


def item_shards(
    tokens,
    memory,
    w_qkv,
    b_qv,
    w_out,
    out_biases,
    norm_gains,
    norm_shifts,
    w_in,
    b_in,
    w_down,
    cotangent,
    mlm_mask,
):
    core = lax.axis_index("tensor")
    segments, count = tokens.shape[1], tokens.shape[2]
    mem_rows = memory.shape[0]
    valid = mem_rows + count
    half = memory.shape[1]

    mask = lax.dynamic_index_in_dim(mlm_mask, core, 0, keepdims=False)
    lower_tri = (
        lax.broadcasted_iota(jnp.int32, (count, count), 0)
        <= lax.broadcasted_iota(jnp.int32, (count, count), 1)
    ).astype(jnp.bfloat16)
    ones = mask.astype(jnp.bfloat16)
    upto = dot_nn(ones, lower_tri).astype(jnp.int32)
    total = upto[:, -1:]
    index = lax.broadcasted_iota(jnp.int32, mask.shape, 1)
    place = mem_rows + jnp.where(mask > 0, upto - 1, total + index - upto)
    move = (
        lax.broadcasted_iota(jnp.int32, (segments, ROWS, count), 1) == place[:, None, :]
    ).astype(jnp.bfloat16)
    live_move = move[:, :LIVE] * ones[:, None, :]

    packed = jnp.concatenate(
        [
            jnp.pad(memory, ((0, PACK_BIASES - mem_rows), (0, 0))),
            b_qv,
            out_biases,
            norm_gains,
            norm_shifts,
            b_in.reshape(-1, half),
        ],
        axis=0,
    )
    packed = jnp.pad(packed, ((0, -packed.shape[0] % 16), (0, 0)))
    both, (wq, wk, wv, outer, inner, lower), first = gather_all(
        mem_rows,
        valid,
        tokens,
        cotangent,
        packed,
        w_qkv.transpose(1, 0, 2),
        w_out.T,
        w_in,
        w_down.T,
        move,
        live_move,
    )
    (
        stacked,
        stacked_next,
        ups,
        query,
        key_rows,
        value_rows,
        query_live,
        context,
        normed_one,
        rstd_one,
        middle_low,
        before,
        hidden,
        normed_two,
        rstd_two,
        low_out,
    ) = first
    wide = jnp.concatenate([both[0], both[1]], axis=1).astype(jnp.float32)
    qv_bias, out_bias, gains, shifts = (
        wide[n : n + 2] for n in (PACK_BIASES, PACK_OUT, PACK_GAINS, PACK_SHIFTS)
    )
    inner_rows = b_in.shape[0] // half
    inner_bias = both[:, PACK_INNER : PACK_INNER + inner_rows].reshape(-1).astype(jnp.float32)
    stored = [
        (
            stacked,
            query,
            key_rows,
            value_rows,
            context,
            normed_one,
            rstd_one,
            middle_low,
            before,
            hidden,
            normed_two,
            rstd_two,
        )
    ]
    outs = [low_out]
    stacked = stacked_next
    query = (dot_nn(stacked, wq) + qv_bias[0]).astype(jnp.bfloat16)
    key_rows = dot_nn(stacked, wk).astype(jnp.bfloat16)
    value_rows = (dot_nn(stacked, wv) + qv_bias[1]).astype(jnp.bfloat16)
    context = attend(query, key_rows, value_rows, valid)
    tail_values = layer_tail(context, stacked, outer, wide, inner, lower, inner_bias.reshape(1, -1), LIVE)
    (
        context,
        normed_one,
        rstd_one,
        middle_low,
        before,
        hidden,
        normed_two,
        rstd_two,
        low_out,
    ) = tail_values
    outs.append(low_out)
    stored.append(
        (
            stacked,
            query,
            key_rows,
            value_rows,
            context,
            normed_one,
            rstd_one,
            middle_low,
            before,
            hidden,
            normed_two,
            rstd_two,
        )
    )

    returning = jnp.zeros((mem_rows, D), jnp.float32)
    token_grads = []
    pieces = [None] * segments
    smalls = []
    for seg in reversed(range(segments)):
        (
            stacked,
            query,
            key_rows,
            value_rows,
            context,
            normed_one,
            rstd_one,
            middle_low,
            before,
            hidden,
            normed_two,
            rstd_two,
        ) = stored[seg]
        upstream = ups[seg].astype(jnp.float32)
        upstream = upstream + jnp.pad(returning, ((0, LIVE - mem_rows), (0, 0)))
        grad_branch, grad_before, grad_one, grad_attended, grad_context, sums = tail_back(
            upstream, normed_two, rstd_two, before, lower, inner, normed_one, rstd_one, outer, wide
        )
        smalls.append(sums)
        if seg > 0:
            grad_query, grad_key, grad_value = attend_back(
                query, key_rows, value_rows, grad_context, valid
            )
            grad_stacked = dot_nt(grad_key, wk) + dot_nt(grad_value, wv)
            live_part = grad_one + dot_nt(grad_query, wq)
            grad_stacked = grad_stacked + jnp.pad(live_part, ((0, ROWS - LIVE), (0, 0)))
            returning = grad_stacked[:mem_rows]
            token_grads.append(grad_stacked.astype(jnp.bfloat16))
            attention_grads = [grad_query, grad_key, grad_value]
        else:
            attention_grads = []
            tail = [query_live, key_rows, value_rows, grad_context, grad_one, wq, wk, wv, move]
        pieces[seg] = (
            stacked,
            *attention_grads,
            grad_attended,
            context,
            middle_low,
            grad_before,
            grad_branch,
            hidden,
        )

    grad_proj, grad_outer, grad_inner, grad_lower, mine, outputs, input_grad = scatter_all(
        mem_rows, valid, pieces[0], pieces[1], tail, smalls, outs, token_grads
    )
    return (
        outputs,
        input_grad.astype(jnp.float32),
        mine[:mem_rows],
        grad_proj.transpose(1, 0, 2),
        mine[16:18],
        grad_outer.T,
        mine[18:20],
        mine[20:22],
        mine[22:24],
        grad_inner,
        mine[24 : 24 + inner_rows].reshape(-1),
        grad_lower.T,
    )


def solution(mesh):
    def body(*arrays):
        if mesh.shape["dp"] == 16 and mesh.shape["tensor"] == arrays[0].shape[0] == arrays[0].shape[1] == 2:
            return item_shards(*arrays)
        return shards(*arrays)

    placed = (
        P("dp", None, None, "tensor"),
        P(None, "tensor"),
        P("dp", None, "tensor"),
        P(None, "tensor"),
        P("tensor", "dp"),
        P(None, "tensor"),
        P(None, "tensor"),
        P(None, "tensor"),
        P("dp", "tensor"),
        P("tensor"),
        P("tensor", "dp"),
        P("dp", None, None, "tensor"),
        P("dp", None, None),
    )
    return jax.shard_map(
        body,
        mesh=mesh,
        in_specs=placed,
        out_specs=(
            P("dp", None, None, "tensor"),
            P("dp", None, None, "tensor"),
            P(None, "tensor"),
            P("dp", None, "tensor"),
            P(None, "tensor"),
            P("tensor", "dp"),
            P(None, "tensor"),
            P(None, "tensor"),
            P(None, "tensor"),
            P("dp", "tensor"),
            P("tensor"),
            P("tensor", "dp"),
        ),
        check_vma=False,
    )
```

```python
import functools

import jax
import jax.numpy as jnp
from jax import lax
from jax.experimental import pallas as pl
from jax.experimental.pallas import tpu as pltpu
from jax.sharding import PartitionSpec as P

D = 1024
DH = 64
MICRO = 2


eps_norm = 1e-05
root_half = 0.7071067811865476
inv_root_two_pi = 0.3989422804014327


def gelu_value(before):
    return 0.5 * before * (1.0 + lax.erf(before * root_half))


def gelu_slope(before):
    return 0.5 * (1.0 + lax.erf(before * root_half)) + before * inv_root_two_pi * jnp.exp(
        -0.5 * before * before
    )


def fetch_weights(w_qkv, w_in, w_out, w_down):
    return (
        lax.all_gather(w_qkv, "dp", axis=0, tiled=True),
        lax.all_gather(w_in, "dp", axis=0, tiled=True),
        lax.all_gather(w_out, "dp", axis=1, tiled=True),
        lax.all_gather(w_down, "dp", axis=1, tiled=True),
    )


def reduce_weights(grad_proj, grad_inner, grad_outer, grad_lower):
    return (
        lax.psum_scatter(
            grad_proj.astype(jnp.bfloat16), "dp", scatter_dimension=0, tiled=True
        ).astype(jnp.float32),
        lax.psum_scatter(
            grad_inner.astype(jnp.bfloat16), "dp", scatter_dimension=0, tiled=True
        ).astype(jnp.float32),
        lax.psum_scatter(
            grad_outer.astype(jnp.bfloat16), "dp", scatter_dimension=1, tiled=True
        ).astype(jnp.float32),
        lax.psum_scatter(
            grad_lower.astype(jnp.bfloat16), "dp", scatter_dimension=1, tiled=True
        ).astype(jnp.float32),
    )


def gather_rows(block):
    return lax.all_gather(block, "tensor", axis=2, tiled=True)


def branch_sum(partial_value):
    return lax.psum_scatter(partial_value, "tensor", scatter_dimension=2, tiled=True)


def gather_grads(block):
    return lax.all_gather(block, "tensor", axis=2, tiled=True)


def input_sum(partial_value):
    return lax.psum_scatter(
        partial_value.astype(jnp.bfloat16), "tensor", scatter_dimension=2, tiled=True
    ).astype(jnp.float32)


def norm_forward(resid, gain, shift):
    totals = jnp.sum(resid, axis=-1)
    squares = jnp.sum(resid * resid, axis=-1)
    totals, squares = lax.psum((totals, squares), "tensor")
    center = totals / D
    spread = squares / D - center * center
    rstd = lax.rsqrt(spread + eps_norm)
    normed = (resid - center[..., None]) * rstd[..., None]
    return (normed * gain + shift, normed, rstd)


def norm_backward(upstream, normed, rstd, gain):
    scaled = upstream * gain
    first = jnp.sum(scaled, axis=-1)
    second = jnp.sum(scaled * normed, axis=-1)
    first, second = lax.psum((first, second), "tensor")
    result = rstd[..., None] * (scaled - first[..., None] / D - normed * (second[..., None] / D))
    return (result, jnp.sum(upstream * normed, axis=(0, 1)), jnp.sum(upstream, axis=(0, 1)))


def attention_scores(query, key_rows):
    return jnp.einsum(
        "bqhe,bkhe->bhqk", query, key_rows, preferred_element_type=jnp.float32
    ) * DH ** (-0.5)


def segment_forward(weights, smalls, memory_rows, token_rows):
    proj_weight, inner_weight, outer_weight, lower_weight = weights
    qv_bias, out_bias, gains, shifts, inner_bias = smalls
    batch = token_rows.shape[0]
    stacked = jnp.concatenate([memory_rows, token_rows], axis=1)
    length = stacked.shape[1]
    local = proj_weight.shape[2]
    heads = local // DH
    wide_rows = gather_rows(stacked)
    bias_three = jnp.stack([qv_bias[0], jnp.zeros_like(qv_bias[0]), qv_bias[1]])
    projected = (
        jnp.einsum("bld,dcf->blcf", wide_rows, proj_weight, preferred_element_type=jnp.float32)
        + bias_three
    ).astype(jnp.bfloat16)
    split = projected.reshape(batch, length, 3, heads, DH)
    scores = attention_scores(split[:, :, 0], split[:, :, 1])
    peak = jnp.max(scores, axis=-1, keepdims=True)
    expo = jnp.exp(scores - peak)
    totals = jnp.sum(expo, axis=-1, keepdims=True)
    probs = expo / totals
    logsum = peak[..., 0] + jnp.log(totals[..., 0])
    context = jnp.einsum(
        "bhqk,bkhe->bqhe",
        probs.astype(jnp.bfloat16),
        split[:, :, 2],
        preferred_element_type=jnp.float32,
    )
    context = context.astype(jnp.bfloat16).reshape(batch, length, local)
    attended = branch_sum(
        jnp.einsum("bld,df->blf", context, outer_weight, preferred_element_type=jnp.float32)
    )
    middle, normed_one, rstd_one = norm_forward(
        stacked.astype(jnp.float32) + attended + out_bias[0], gains[0], shifts[0]
    )
    middle_wide = gather_rows(middle.astype(jnp.bfloat16))
    before = (
        jnp.einsum("bld,df->blf", middle_wide, inner_weight, preferred_element_type=jnp.float32)
        + inner_bias
    )
    hidden = gelu_value(before).astype(jnp.bfloat16)
    branch = branch_sum(
        jnp.einsum("blf,fd->bld", hidden, lower_weight, preferred_element_type=jnp.float32)
    )
    layer_out, normed_two, rstd_two = norm_forward(
        middle + branch + out_bias[1], gains[1], shifts[1]
    )
    stored = (
        wide_rows,
        projected,
        logsum,
        context,
        normed_one,
        rstd_one,
        middle_wide,
        before,
        hidden,
        normed_two,
        rstd_two,
    )
    return (layer_out, stored)


def segment_backward(weights, smalls, upstream, stored):
    proj_weight, inner_weight, outer_weight, lower_weight = weights
    qv_bias, out_bias, gains, shifts, inner_bias = smalls
    (
        wide_rows,
        projected,
        logsum,
        context,
        normed_one,
        rstd_one,
        middle_wide,
        before,
        hidden,
        normed_two,
        rstd_two,
    ) = stored
    batch, length, local = context.shape
    heads = local // DH
    grad_two, gain_two, shift_two = norm_backward(upstream, normed_two, rstd_two, gains[1])
    grad_branch = gather_grads(grad_two.astype(jnp.bfloat16))
    grad_lower = jnp.einsum("blf,bld->fd", hidden, grad_branch, preferred_element_type=jnp.float32)
    grad_hidden = jnp.einsum(
        "bld,fd->blf", grad_branch, lower_weight, preferred_element_type=jnp.float32
    )
    grad_before = (grad_hidden * gelu_slope(before)).astype(jnp.bfloat16)
    grad_inner = jnp.einsum(
        "bld,blf->df", middle_wide, grad_before, preferred_element_type=jnp.float32
    )
    grad_inner_bias = jnp.sum(grad_before.astype(jnp.float32), axis=(0, 1))
    grad_middle = grad_two + lax.psum_scatter(
        jnp.einsum(
            "blf,df->bld", grad_before, inner_weight, preferred_element_type=jnp.float32
        ).astype(jnp.bfloat16),
        "tensor",
        scatter_dimension=2,
        tiled=True,
    ).astype(jnp.float32)
    grad_one, gain_one, shift_one = norm_backward(grad_middle, normed_one, rstd_one, gains[0])
    grad_attended = gather_grads(grad_one.astype(jnp.bfloat16))
    grad_outer = jnp.einsum(
        "bld,blf->df", context, grad_attended, preferred_element_type=jnp.float32
    )
    grad_context = jnp.einsum(
        "blf,df->bld", grad_attended, outer_weight, preferred_element_type=jnp.float32
    )
    grad_context = grad_context.astype(jnp.bfloat16)
    grad_context = grad_context.reshape(batch, length, heads, DH)
    split = projected.reshape(batch, length, 3, heads, DH)
    query, key_rows, value_rows = (split[:, :, 0], split[:, :, 1], split[:, :, 2])
    probs = jnp.exp(attention_scores(query, key_rows) - logsum[..., None])
    grad_probs = jnp.einsum(
        "bqhe,bkhe->bhqk", grad_context, value_rows, preferred_element_type=jnp.float32
    )
    weighted_sum = jnp.sum(probs * grad_probs, axis=-1, keepdims=True)
    grad_scores = (probs * (grad_probs - weighted_sum)).astype(jnp.bfloat16)
    grad_query = jnp.einsum(
        "bhqk,bkhe->bqhe", grad_scores, key_rows, preferred_element_type=jnp.float32
    ) * DH ** (-0.5)
    grad_key = jnp.einsum(
        "bhqk,bqhe->bkhe", grad_scores, query, preferred_element_type=jnp.float32
    ) * DH ** (-0.5)
    grad_value = jnp.einsum(
        "bhqk,bqhe->bkhe",
        probs.astype(jnp.bfloat16),
        grad_context,
        preferred_element_type=jnp.float32,
    )
    grad_projected = (
        jnp.stack([grad_query, grad_key, grad_value], axis=2)
        .reshape(batch, length, 3, local)
        .astype(jnp.bfloat16)
    )
    grad_proj = jnp.einsum(
        "bld,blcf->dcf", wide_rows, grad_projected, preferred_element_type=jnp.float32
    )
    column_sums = jnp.sum(grad_projected.astype(jnp.float32), axis=(0, 1))
    grad_qv = jnp.stack([column_sums[0], column_sums[2]])
    grad_stacked = grad_one + input_sum(
        jnp.einsum("blcf,dcf->bld", grad_projected, proj_weight, preferred_element_type=jnp.float32)
    )
    grad_biases = jnp.stack([jnp.sum(grad_one, axis=(0, 1)), jnp.sum(grad_two, axis=(0, 1))])
    large_grads = (grad_proj, grad_inner, grad_outer, grad_lower)
    small_grads = (
        grad_qv,
        grad_biases,
        jnp.stack([gain_one, gain_two]),
        jnp.stack([shift_one, shift_two]),
        grad_inner_bias,
    )
    return (grad_stacked, large_grads, small_grads)


def add_tuples(first, second):
    return tuple((left + right for left, right in zip(first, second)))


def shards(
    tokens,
    memory,
    w_qkv,
    b_qv,
    w_out,
    out_biases,
    norm_gains,
    norm_shifts,
    w_in,
    b_in,
    w_down,
    cotangent,
    mlm_mask,
):
    smalls = (
        b_qv.astype(jnp.float32),
        out_biases.astype(jnp.float32),
        norm_gains.astype(jnp.float32),
        norm_shifts.astype(jnp.float32),
        b_in.astype(jnp.float32),
    )
    per_batch = tokens.shape[0] // MICRO
    segments = tokens.shape[1]
    mem_rows = memory.shape[0]
    local = w_qkv.shape[2]
    inner_local = w_in.shape[1]
    empty_large = (
        jnp.zeros((D, 3, local), jnp.float32),
        jnp.zeros((D, inner_local), jnp.float32),
        jnp.zeros((local, D), jnp.float32),
        jnp.zeros((inner_local, D), jnp.float32),
    )
    full_grads = empty_large
    shard_grads = (
        jnp.zeros(w_qkv.shape, jnp.float32),
        jnp.zeros(w_in.shape, jnp.float32),
        jnp.zeros(w_out.shape, jnp.float32),
        jnp.zeros(w_down.shape, jnp.float32),
    )
    small_total = (
        jnp.zeros((2, local), jnp.float32),
        jnp.zeros((2, local), jnp.float32),
        jnp.zeros((2, local), jnp.float32),
        jnp.zeros((2, local), jnp.float32),
        jnp.zeros((inner_local,), jnp.float32),
    )
    memory_total = jnp.zeros((mem_rows, local), jnp.float32)
    out_blocks = []
    grad_blocks = []
    for batch_index in range(MICRO):
        offset = batch_index * per_batch
        batch_tokens = tokens[offset : offset + per_batch]
        batch_mask = mlm_mask[offset : offset + per_batch]
        batch_cot = cotangent[offset : offset + per_batch].astype(jnp.float32) * batch_mask[
            ..., None
        ].astype(jnp.float32)
        weights = fetch_weights(w_qkv, w_in, w_out, w_down)
        carried = memory[None]
        stored_all = []
        token_outs = []
        for seg_index in range(segments):
            layer_out, stored = segment_forward(
                weights, smalls, carried, batch_tokens[:, seg_index]
            )
            carried = layer_out[:, :mem_rows].astype(jnp.bfloat16)
            token_outs.append(layer_out[:, mem_rows:].astype(jnp.bfloat16))
            stored_all.append(stored)
        returning = jnp.zeros((per_batch, mem_rows, local), jnp.float32)
        token_grads = [None] * segments
        for seg_index in reversed(range(segments)):
            upstream = jnp.concatenate([returning, batch_cot[:, seg_index]], axis=1)
            grad_stacked, large_grads, small_grads = segment_backward(
                weights, smalls, upstream, stored_all[seg_index]
            )
            returning = grad_stacked[:, :mem_rows]
            token_grads[seg_index] = grad_stacked[:, mem_rows:]
            full_grads = add_tuples(full_grads, large_grads)
            small_total = add_tuples(small_total, small_grads)
        memory_total = memory_total + jnp.sum(returning, axis=0)
        reduced = reduce_weights(full_grads[0], full_grads[1], full_grads[2], full_grads[3])
        shard_grads = add_tuples(shard_grads, reduced)
        full_grads = empty_large
        out_blocks.append(jnp.stack(token_outs, axis=1))
        grad_blocks.append(jnp.stack(token_grads, axis=1))
    grad_qv, grad_biases, grad_gains, grad_shifts, grad_inner_bias, memory_grad = lax.psum(
        (
            small_total[0],
            small_total[1],
            small_total[2],
            small_total[3],
            small_total[4],
            memory_total,
        ),
        "dp",
    )
    outputs = jnp.concatenate(out_blocks, axis=0)
    input_grad = jnp.concatenate(grad_blocks, axis=0)
    return (
        outputs,
        input_grad,
        memory_grad,
        shard_grads[0],
        grad_qv,
        shard_grads[2],
        grad_biases,
        grad_gains,
        grad_shifts,
        shard_grads[1],
        grad_inner_bias,
        shard_grads[3],
    )


ROWS = 528
LIVE = 176


def dot_nn(left, right):
    return jnp.dot(left, right, preferred_element_type=jnp.float32)


def dot_nt(left, right):
    return lax.dot_general(
        left, right, (((1,), (1,)), ((), ())), preferred_element_type=jnp.float32
    )


def dot_tn(left, right):
    return lax.dot_general(
        left, right, (((0,), (0,)), ((), ())), preferred_element_type=jnp.float32
    )


def norm_rows(resid, gain, shift):
    center = jnp.mean(resid, axis=-1, keepdims=True)
    spread = jnp.mean(resid * resid, axis=-1, keepdims=True) - center * center
    rstd = lax.rsqrt(spread + eps_norm)
    normed = (resid - center) * rstd
    return (normed * gain + shift, normed, rstd)


def norm_rows_back(upstream, normed, rstd, gain):
    scaled = upstream * gain
    first = jnp.mean(scaled, axis=-1, keepdims=True)
    second = jnp.mean(scaled * normed, axis=-1, keepdims=True)
    result = rstd * (scaled - first - normed * second)
    return (result, jnp.sum(upstream * normed, axis=0), jnp.sum(upstream, axis=0))


MESH = pl.DeviceIdType.MESH
HBM = pl.BlockSpec(memory_space=pl.ANY)
VMEM = pl.BlockSpec(memory_space=pltpu.VMEM)
GATHER_PIECES = ((0, 0), (1, 0), (2, 0), (3, 0), (4, 0), (5, 0), (4, 1), (5, 1), (4, 2), (5, 2), (4, 3), (5, 3))
SCATTER_PIECES = ((5, 0), (5, 1), (5, 2), (5, 3), (4, 0), (4, 1), (4, 2), (4, 3), (3, 0), (0, 0), (1, 0), (2, 0))
GATHER_HOPS = (
    (3, 2, 1, 0), (3, 2, 0, 1), (3, 2, 1, 0), (3, 0, 1, 2), (3, 2, 1, 0), (3, 1, 0, 2),
    (3, 2, 0, 1), (3, 2, 1, 0), (3, 0, 1, 2), (3, 2, 0, 1), (3, 2, 1, 0), (3, 0, 1, 2),
)
SCATTER_HOPS = (
    (2, 1, 0, 3), (0, 1, 2, 3), (1, 0, 2, 3), (2, 1, 0, 3), (0, 1, 2, 3), (2, 0, 3, 1),
    (0, 1, 2, 3), (1, 2, 0, 3), (0, 2, 1, 3), (0, 1, 2, 3), (1, 0, 2, 3), (1, 0, 2, 3),
)
GATHER_STEPS = (
    0, 8, 1, 100, 16, 9, 24, 2, 17, 32, 10, 40, 3, 25, 48, 18, 11, 56, 33, 64,
    41, 19, 49, 72, 57, 80, 4, 34, 26, 88, 5, 65, 101, 12, 50, 42, 73, 13, 102, 58,
    35, 20, 81, 66, 21, 89, 103, 27, 74, 104, 51, 82, 105, 59, 106, 43, 107, 67, 28, 29,
    36, 108, 52, 90, 37, 44, 53, 75, 83, 45, 109, 91, 68, 60, 69, 61, 76, 110, 77, 92,
    84, 111, 93, 85, 112, 113,
)
SCATTER_STEPS = (
    0, 8, 16, 1, 9, 17, 24, 32, 100, 25, 33, 2, 40, 10, 48, 18, 101, 41, 3, 49,
    26, 56, 34, 64, 11, 102, 19, 57, 27, 65, 4, 42, 103, 12, 35, 72, 20, 80, 5, 73,
    50, 88, 13, 28, 36, 81, 21, 58, 89, 29, 51, 104, 37, 105, 66, 106, 59, 107, 43, 108,
    52, 82, 109, 110, 67, 74, 44, 90, 60, 53, 68, 61, 83, 69, 75, 45, 84, 91, 76, 85,
    92, 77, 93,
)
SLOTS = 2


def here():
    me = lax.axis_index("dp")
    core = lax.axis_index("tensor")
    bits = tuple((me // (1 << b)) % 2 for b in range(4))
    peers = tuple({"dp": me + (1 - 2 * bits[b]) * (1 << b)} for b in range(4))
    return core, bits, peers + ({"tensor": 1 - core},)


def greet(peers):
    barrier = pltpu.get_barrier_semaphore()
    for peer in peers:
        pl.semaphore_signal(barrier, inc=1, device_id=peer, device_id_type=MESH)
    pl.semaphore_wait(barrier, len(peers))


def block_index(bits, free, flip=None):
    index = []
    for b in (3, 2, 1, 0):
        if b == flip:
            index.append(1 - bits[b])
        elif b in free:
            index.append(slice(None))
        else:
            index.append(bits[b])
    return tuple(index)


def columns(array, part, core, width):
    blocks = 4 if array > 3 else 1
    return pl.ds(pl.multiple_of((core * blocks + part) * width, width), width)


def shard_block(shards, piece, width):
    array, part = piece
    if array < 3:
        return shards[array].at[array]
    return shards[array].at[:, pl.ds(part * width, width)]


def attend_pair(query, key_rows, value_rows, valid):
    main = key_rows.shape[0] - 16
    lane = lax.broadcasted_iota(jnp.int32, (1, 2 * DH), 1)
    left = lane < DH
    query = query * DH ** (-0.5)
    zero = jnp.zeros_like(query)
    tail_lane = lax.broadcasted_iota(jnp.int32, (1, 32), 1)
    tail_zero = jnp.zeros((16, 2 * DH), query.dtype)
    key_tail, value_tail = key_rows[main:], value_rows[main:]
    keys_both = jnp.concatenate(
        [jnp.where(left, key_tail, tail_zero), jnp.where(left, tail_zero, key_tail)], axis=0
    )
    values_both = jnp.concatenate(
        [jnp.where(left, value_tail, tail_zero), jnp.where(left, tail_zero, value_tail)], axis=0
    )
    ones_both = jnp.concatenate(
        [jnp.where(left, tail_zero, tail_zero + 1), jnp.where(left, tail_zero + 1, tail_zero)], axis=0
    )
    tail = dot_nt(query, keys_both)
    tail = jnp.where(tail_lane % 16 < valid - main, tail, -1e30)
    peaks, parts = [], []
    for head in range(2):
        picked = jnp.where(left if head == 0 else ~left, query, zero)
        scores = dot_nt(picked, key_rows[:main])
        side = (tail_lane < 16) if head == 0 else (tail_lane >= 16)
        peak = jnp.maximum(
            jnp.max(scores, axis=1, keepdims=True),
            jnp.max(jnp.where(side, tail, -1e30), axis=1, keepdims=True),
        )
        expo = jnp.exp(scores - peak).astype(jnp.bfloat16)
        one = jnp.ones_like(value_rows[:main])
        values = jnp.where(left if head == 0 else ~left, value_rows[:main], one)
        parts.append(dot_nn(expo, values))
        peaks.append(peak)
    tail = jnp.exp(tail - jnp.where(tail_lane < 16, peaks[0], peaks[1])).astype(jnp.bfloat16)
    both = dot_nn(tail, jnp.concatenate([values_both, ones_both], axis=1))
    value_sum = jnp.where(left, parts[0], parts[1]) + both[:, : 2 * DH]
    total = jnp.where(left, parts[1], parts[0]) + both[:, 2 * DH :]
    return (value_sum / pltpu.roll(total, DH, 1)).astype(jnp.bfloat16)


def attend_kernel(valid, q_ref, k_ref, v_ref, out_ref):
    out_ref[...] = attend_pair(q_ref[...], k_ref[...], v_ref[...], valid)


def attend(query, key_rows, value_rows, valid):
    block = pl.BlockSpec((query.shape[0], 2 * DH), lambda i: (0, i))
    return pl.pallas_call(
        functools.partial(attend_kernel, valid),
        grid=(D // (2 * DH),),
        out_shape=jax.ShapeDtypeStruct(query.shape, jnp.bfloat16),
        in_specs=[block] * 3,
        out_specs=block,
        compiler_params=pltpu.CompilerParams(vmem_limit_bytes=12 << 20),
        name="attend",
    )(query, key_rows, value_rows)


def attend_back_pair(query, key_rows, value_rows, grads, valid):
    live = query.shape[0]
    left = lax.broadcasted_iota(jnp.int32, (1, 2 * DH), 1) < DH
    zero = jnp.zeros_like(query)
    query = query * DH ** (-0.5)
    picked = jnp.concatenate([jnp.where(left, query, zero), jnp.where(left, zero, query)], axis=0)
    up = jnp.concatenate([jnp.where(left, grads, zero), jnp.where(left, zero, grads)], axis=0)
    scores = dot_nt(key_rows, picked)
    scores = jnp.where(lax.broadcasted_iota(jnp.int32, scores.shape, 0) < valid, scores, -1e30)
    expo = jnp.exp(scores - jnp.max(scores, axis=0, keepdims=True))
    probs = expo * (1.0 / jnp.sum(expo, axis=0, keepdims=True))
    grad_probs = dot_nt(value_rows, up)
    weighted = jnp.sum(probs * grad_probs, axis=0, keepdims=True)
    grad_scores = (probs * (grad_probs - weighted)).astype(jnp.bfloat16)
    grad_query = dot_tn(grad_scores, key_rows)
    grad_query = jnp.where(left, grad_query[:live], grad_query[live:]) * DH ** (-0.5)
    grad_key = dot_nn(grad_scores, picked)
    grad_value = dot_nn(probs.astype(jnp.bfloat16), up)
    return tuple(grad.astype(jnp.bfloat16) for grad in (grad_query, grad_key, grad_value))


def attend_back_kernel(valid, q_ref, k_ref, v_ref, g_ref, dq_ref, dk_ref, dv_ref):
    dq_ref[...], dk_ref[...], dv_ref[...] = attend_back_pair(
        q_ref[...], k_ref[...], v_ref[...], g_ref[...], valid
    )


def attend_back(query, key_rows, value_rows, grad_context, valid):
    live = grad_context.shape[0]
    short = pl.BlockSpec((live, 2 * DH), lambda i: (0, i))
    tall = pl.BlockSpec((key_rows.shape[0], 2 * DH), lambda i: (0, i))
    low = jnp.bfloat16
    return pl.pallas_call(
        functools.partial(attend_back_kernel, valid),
        grid=(D // (2 * DH),),
        out_shape=[jax.ShapeDtypeStruct((live, D), low)] + [jax.ShapeDtypeStruct(key_rows.shape, low)] * 2,
        in_specs=[short, tall, tall, short],
        out_specs=[short, tall, tall],
        compiler_params=pltpu.CompilerParams(vmem_limit_bytes=12 << 20),
        name="attend_back",
    )(query, key_rows, value_rows, grad_context)


PACK_BIASES, PACK_OUT, PACK_GAINS, PACK_SHIFTS, PACK_INNER = 16, 18, 20, 22, 24


def gather_kernel(
    mem_rows, valid, toks, cots, pack, sq, so, si, sl, move, live_move,
    packs, fq, fk, fv, fo, fi, fl, stacked_a, stacked_b, ups, query, key_rows, value_rows,
    query_live, context_live, normed_one, rstd_one, middle_live, before_live, hidden_live, normed_two, rstd_two, low_out,
    x_v, c_v, vq, vo, vi, vl, held, context, middle, middle_low, branch,
    send, recv, local, loads, extra,
):
    core, bits, peers = here()
    width = pack.shape[1]
    live = ups.shape[1]
    shards = (vq, vq, vq, vo, vi, vl)
    fulls = (fq, fk, fv, fo, fi, fl)
    mine = pl.ds(pl.multiple_of(core * width, width), width)
    shard_in = [
        pltpu.make_async_copy(src, dst, extra.at[n])
        for n, (src, dst) in enumerate(((sq, vq), (so, vo), (si, vi), (sl, vl)))
    ]
    rows_own = [
        pltpu.make_async_copy(toks.at[core], x_v.at[:, :, mine], extra.at[4]),
        pltpu.make_async_copy(cots.at[core], c_v.at[:, :, mine], extra.at[5]),
        pltpu.make_async_copy(pack, packs.at[core], extra.at[6]),
    ]
    for copy in shard_in + rows_own:
        copy.start()
    own = []
    for p, (array, part) in enumerate(GATHER_PIECES):
        own.append(pltpu.make_async_copy(
            shard_block(shards, (array, part), width),
            fulls[array].at[block_index(bits, ()) + (slice(None), columns(array, part, core, width))],
            local.at[p],
        ))
    greet(peers)
    for copy in shard_in:
        copy.wait()
    for copy in own:
        copy.start()

    def remote(src, dst, slot, peer):
        return pltpu.make_async_remote_copy(
            src_ref=src, dst_ref=dst, send_sem=send.at[slot], recv_sem=recv.at[slot],
            device_id=peer, device_id_type=MESH)

    def stage(p, s):
        array, part = GATHER_PIECES[p]
        order = GATHER_HOPS[p]
        cols = columns(array, part, core, width)
        dst = fulls[array].at[block_index(bits, order[:s]) + (slice(None), cols)]
        if s == 0:
            src = shard_block(shards, (array, part), width)
        else:
            src = dst
        peer = peers[order[s]] if s < 4 else peers[4]
        return remote(src, dst, p * 5 + s, peer)

    swaps = [
        remote(toks.at[1 - core], x_v.at[:, :, mine], 60, peers[4]),
        remote(cots.at[1 - core], c_v.at[:, :, mine], 61, peers[4]),
        remote(pack, packs.at[core], 62, peers[4]),
    ]
    started, loading = {}, {}

    def load(p):
        array, part = GATHER_PIECES[p]
        blocks = 4 if array > 3 else 1
        every = (slice(None),) * 5
        loading[p] = [
            pltpu.make_async_copy(
                fulls[array].at[every + (pl.ds((half * blocks + part) * width, width),)],
                held.at[(p % 6,) + every + (pl.ds(half * width, width),)],
                loads.at[2 * p + half],
            )
            for half in range(2)
        ]
        for copy in loading[p]:
            copy.start()

    def loaded(p):
        for copy in loading.pop(p):
            copy.wait()

    def weight(p, cols):
        block = held[p % 6, :, :, :, :, :, cols]
        return block.reshape(2 * width, block.shape[-1])

    def wide(row):
        return jnp.concatenate([packs[0, row : row + 1], packs[1, row : row + 1]], axis=1).astype(jnp.float32)

    def norm(resid, gain, shift):
        center = jnp.mean(resid, axis=1, keepdims=True)
        spread = jnp.mean(resid * resid, axis=1, keepdims=True) - center * center
        rstd = lax.rsqrt(spread + eps_norm)
        normed = (resid - center) * rstd
        return normed * gain + shift, normed, rstd

    def compute(task):
        if task == 0:
            for copy in rows_own:
                copy.wait()
            for swap in swaps:
                swap.wait_recv()
            memory = jnp.concatenate([packs[0, :16], packs[1, :16]], axis=1)
            is_memory = lax.broadcasted_iota(jnp.int32, memory.shape, 0) < mem_rows
            stacked_a[...] = dot_nn(move[0], x_v[0]).astype(jnp.bfloat16)
            stacked_a[:16] = jnp.where(is_memory, memory, stacked_a[:16])
            stacked_b[...] = dot_nn(move[1], x_v[1]).astype(jnp.bfloat16)
            for n in range(2):
                ups[n] = dot_nn(live_move[n], c_v[n]).astype(jnp.bfloat16)
        elif task < 4:
            n = task - 1
            loaded(n)
            target = (query, key_rows, value_rows)[n]
            for half in range(2):
                cols = pl.ds(half * width, width)
                got = dot_nn(stacked_a[...], weight(n, cols))
                if n != 1:
                    row = PACK_BIASES + n // 2
                    got = got + packs[half, row : row + 1].astype(jnp.float32)
                target[:, cols] = got.astype(jnp.bfloat16)
                if n == 0:
                    query_live[:, cols] = got[:live].astype(jnp.bfloat16)
        elif task < 8:

            def pair(n, carry):
                cols = pl.ds(pl.multiple_of((2 * (task - 4) + n) * 2 * DH, 2 * DH), 2 * DH)
                context[:, cols] = attend_pair(query[:, cols], key_rows[:, cols], value_rows[:, cols], valid)
                return carry

            lax.fori_loop(0, 2, pair, 0)
        elif task == 8:
            loaded(3)
            attended = dot_nt(context[...], weight(3, slice(None)))
            resid = stacked_a[...].astype(jnp.float32) + attended + wide(PACK_OUT)
            value, normed, rstd = norm(resid, wide(PACK_GAINS), wide(PACK_SHIFTS))
            middle[...] = value
            middle_low[...] = value.astype(jnp.bfloat16)
            middle_live[...] = value[:live].astype(jnp.bfloat16)
            context_live[...] = context[:live]
            normed_one[...] = normed[:live]
            rstd_one[...] = jnp.broadcast_to(rstd[:live], rstd_one.shape)
        elif task < 13:
            j = task - 9
            loaded(4 + 2 * j)
            loaded(5 + 2 * j)

            def hidden_block(half, carry):
                cols = pl.ds(pl.multiple_of(half * width, width), width)
                place = pl.ds(pl.multiple_of((half * 4 + j) * width, width), width)
                bias = packs[half, PACK_INNER + j : PACK_INNER + j + 1].astype(jnp.float32)
                before = dot_nn(middle_low[...], weight(4 + 2 * j, cols)) + bias
                before_live[:, place] = before[:live]
                hidden = gelu_value(before).astype(jnp.bfloat16)
                hidden_live[:, place] = hidden[:live]
                branch[...] = branch[...] + dot_nt(hidden, weight(5 + 2 * j, cols))
                return carry

            if j == 0:
                branch[...] = middle[...] + wide(PACK_OUT + 1)
            lax.fori_loop(0, 2, hidden_block, 0)
        else:
            value, normed, rstd = norm(branch[...], wide(PACK_GAINS + 1), wide(PACK_SHIFTS + 1))
            low_out[...] = value.astype(jnp.bfloat16)
            is_memory = lax.broadcasted_iota(jnp.int32, (16, 2 * width), 0) < mem_rows
            stacked_b[:16] = jnp.where(is_memory, low_out[:16], stacked_b[:16])
            normed_two[...] = normed[:live]
            rstd_two[...] = jnp.broadcast_to(rstd[:live], rstd_two.shape)

    for tick, step in enumerate(GATHER_STEPS):
        if step >= 100:
            compute(step - 100)
            continue
        p, s = step // 8, step % 8
        if s > 0:
            started[p, s - 1].wait_recv()
        if s == 1:
            own[p].wait()
        if s == 5:
            load(p)
        else:
            started[p, s] = stage(p, s)
            started[p, s].start()
        if tick == 2:
            for swap in swaps:
                swap.start()
    for copy in started.values():
        copy.wait_send()
    for swap in swaps:
        swap.wait_send()


def gather_all(mem_rows, valid, toks, cots, pack, sq, so, si, sl, move, live_move):
    width = pack.shape[1]
    rows = sq.shape[1]
    low, full = jnp.bfloat16, jnp.float32
    total, live = move.shape[1], live_move.shape[1]
    hidden = 2 * si.shape[1]
    out = [((2,) + pack.shape, low)]
    for size in (2 * width, 2 * width, 2 * width, 2 * width, hidden, hidden):
        out.append(((2, 2, 2, 2, rows, size), low))
    out += [((total, 2 * width), low)] * 2 + [((2, live, 2 * width), low)]
    out += [((total, 2 * width), low)] * 3 + [((live, 2 * width), low)] * 2
    out += [((live, 2 * width), full), ((live, 2 * width), full), ((live, 2 * width), low)]
    out += [((live, hidden), full), ((live, hidden), low)]
    out += [((live, 2 * width), full), ((live, 2 * width), full), ((total, 2 * width), low)]
    block = (2, 2, 2, 2, rows, 2 * width)
    got = pl.pallas_call(
        functools.partial(gather_kernel, mem_rows, valid),
        out_shape=[jax.ShapeDtypeStruct(*one) for one in out],
        in_specs=[HBM, HBM, VMEM] + [HBM] * 4 + [VMEM] * 2,
        out_specs=[VMEM] + [HBM] * 6 + [VMEM] * (len(out) - 7),
        scratch_shapes=[
            pltpu.VMEM(toks.shape[1:3] + (2 * width,), low),
            pltpu.VMEM(toks.shape[1:3] + (2 * width,), low),
            pltpu.VMEM(sq.shape, low),
            pltpu.VMEM(so.shape, low),
            pltpu.VMEM(si.shape, low),
            pltpu.VMEM(sl.shape, low),
            pltpu.VMEM((6,) + block, low),
            pltpu.VMEM((total, 2 * width), low),
            pltpu.VMEM((total, 2 * width), full),
            pltpu.VMEM((total, 2 * width), low),
            pltpu.VMEM((total, 2 * width), full),
            pltpu.SemaphoreType.DMA((63,)),
            pltpu.SemaphoreType.DMA((63,)),
            pltpu.SemaphoreType.DMA((12,)),
            pltpu.SemaphoreType.DMA((24,)),
            pltpu.SemaphoreType.DMA((7,)),
        ],
        compiler_params=pltpu.CompilerParams(collective_id=0, has_side_effects=True, vmem_limit_bytes=62 << 20),
        name="gather_all",
    )(toks, cots, pack, sq, so, si, sl, move, live_move)
    wide = [array.reshape(16 * rows, array.shape[-1]) for array in got[1:7]]
    return got[0], wide, got[7:]


def scatter_kernel(mem_rows, valid, *refs):
    (rows_a, out_a, context_a, middle_a, before_a, branch_a, hidden_a) = refs[0:7]
    second_rows = refs[7:17]
    query, keys_in, values_in, up, grad_one, wq, wk, wv, move, small, outs_a, outs_b, grads_b = refs[17:30]
    oq, oo, oi, ol, osmall, out_item, grad_item = refs[30:37]
    (acc, first, second, third, fourth, slots, wide_x, wide_s, held, grad_query, key_rows, value_rows,
     source, result, total_rows, small_v, small_in, small_recv, send, recv, extra, sent) = refs[37:]
    first_rows = (rows_a, grad_query, key_rows, value_rows, out_a, context_a, middle_a, before_a, branch_a, hidden_a)
    core, bits, peers = here()
    width = osmall.shape[1]
    live = grad_query.shape[0]
    bufs = (first, second, third, fourth)
    lefts = (0, 0, 0, 4, 6, 8)
    rights = (1, 2, 3, 5, 7, 9)
    turned = set()
    mine = pl.ds(pl.multiple_of(core * width, width), width)
    other = pl.ds(pl.multiple_of((1 - core) * width, width), width)
    stage_in = [
        pltpu.make_async_copy(keys_in, key_rows, extra.at[0]),
        pltpu.make_async_copy(values_in, value_rows, extra.at[1]),
    ]
    for copy in stage_in:
        copy.start()
    greet(peers)

    def bring(src, dst, sem):
        copy = pltpu.make_async_copy(src, dst, extra.at[sem])
        copy.start()
        return copy

    def remote(src, dst, slot, peer):
        return pltpu.make_async_remote_copy(
            src_ref=src, dst_ref=dst, send_sem=send.at[slot], recv_sem=recv.at[slot],
            device_id=peer, device_id_type=MESH)

    def turn(array):
        left = lefts[array]
        if left in turned:
            return
        turned.add(left)
        for n, rows in enumerate((first_rows, second_rows)):
            if left == 0:
                bring(rows[0], source, 2).wait()
                wide_x[n] = source[...].T
            else:
                wide_s[left // 2 - 2, n] = rows[left][...].T

    def multiply(array, offset, size):
        total = None
        for n, rows in enumerate((first_rows, second_rows)):
            right = rows[rights[array]][:, pl.ds(offset, size)]
            if array in (1, 2):
                left = wide_x[n]
            elif array == 0:
                left = wide_x[n, :, :live]
            else:
                left = wide_s[lefts[array] // 2 - 2, n]
            term = jnp.dot(left, right, preferred_element_type=jnp.float32)
            total = term if total is None else total + term
        return total

    tile = width // 2

    def produce(p, slot):
        array, part = SCATTER_PIECES[p]
        turn(array)
        blocks = 4 if array > 3 else 1
        base = ((1 - core) * blocks + part) * width

        def body(n, carry):
            offset = pl.multiple_of(base + n * tile, tile)
            got = multiply(array, offset, tile).astype(jnp.bfloat16)
            slots[slot, :, :, :, :, :, pl.ds(pl.multiple_of(n * tile, tile), tile)] = got.reshape(
                slots.shape[1:6] + (tile,)
            )
            return carry

        lax.fori_loop(0, 2, body, 0)

    def combine(p):
        array, part = SCATTER_PIECES[p]
        blocks = 4 if array > 3 else 1
        base = (core * blocks + part) * width

        def body(n, carry):
            offset = pl.multiple_of(base + n * tile, tile)
            cols = pl.ds(pl.multiple_of(n * tile, tile), tile)
            got = multiply(array, offset, tile).reshape(slots.shape[1:6] + (tile,))
            acc[p, :, :, :, :, :, cols] = (
                got + acc[p, :, :, :, :, :, cols].astype(jnp.float32)
            ).astype(jnp.bfloat16)
            return carry

        lax.fori_loop(0, 2, body, 0)

    def stage(p, s):
        if s == 0:
            return remote(slots.at[p % SLOTS], acc.at[p], p * 5, peers[4])
        order = SCATTER_HOPS[p]
        src = acc.at[(p,) + block_index(bits, order[s:], flip=order[s - 1])]
        return remote(src, bufs[s - 1].at[p], p * 5 + s, peers[order[s - 1]])

    def fold(p, s):
        array, part = SCATTER_PIECES[p]
        order = SCATTER_HOPS[p]
        free = [b for b in (3, 2, 1, 0) if b in order[s:]]
        for n in range(1 << len(free)):
            at = {b: (n >> i) % 2 for i, b in enumerate(reversed(free))}
            where = tuple(at.get(b, bits[b]) for b in (3, 2, 1, 0))
            got = bufs[s - 1][(p,) + tuple(at[b] for b in free)]
            if s < 4:
                acc[(p,) + where] = acc[(p,) + where] + got
            else:
                total = acc[(p,) + where].astype(jnp.float32) + got.astype(jnp.float32)
                if array < 3:
                    oq[array] = total
                elif array == 4:
                    oi[:, pl.ds(part * width, width)] = total
                elif array == 3:
                    oo[...] = total
                else:
                    ol[:, pl.ds(part * width, width)] = total

    small_started = {}

    def small_stage(s):
        peer = peers[4] if s == 0 else peers[s - 1]
        src = small_v.at[:, other] if s == 0 else small_in.at[s]
        return remote(src, small_recv.at[s], 60 + s, peer)

    def small_step(n):
        if n == 0:
            small_in[0] = small_v[:, mine]
        else:
            small_started[n - 1].wait_recv()
            total = small_in[n - 1] + small_recv[n - 1]
            if n < 5:
                small_in[n] = total
            else:
                osmall[...] = total
        if n < 5:
            small_started[n] = small_stage(n)
            small_started[n].start()

    swaps, places = [], []

    def unpermute(n, values, target, segment):
        if n > 1:
            swaps[n - 2].wait_send()
            places[n - 2].wait()
        result[n % 2] = dot_tn(move[segment], values).astype(jnp.bfloat16)
        places.append(
            pltpu.make_async_copy(result.at[n % 2, :, mine], target.at[core, segment], sent.at[n])
        )
        swaps.append(remote(result.at[n % 2, :, other], target.at[core, segment], 65 + n, peers[4]))
        places[n].start()
        swaps[n].start()

    weights = (wk, wv, wq)
    fetched = {}

    def compute(task):
        if task < 4:
            if task == 0:
                for copy in stage_in:
                    copy.wait()
                fetched[0] = bring(weights[0], held, 3)

            def pair(n, carry):
                cols = pl.ds(pl.multiple_of((2 * task + n) * 2 * DH, 2 * DH), 2 * DH)
                grad_query[:, cols], key_rows[:, cols], value_rows[:, cols] = attend_back_pair(
                    query[:, cols], key_rows[:, cols], value_rows[:, cols], up[:, cols], valid
                )
                return carry

            lax.fori_loop(0, 2, pair, 0)
        elif task < 7:
            n = task - 4
            fetched[n].wait()
            if n == 0:
                total_rows[...] = dot_nt(key_rows[...], held[...])
            elif n == 1:
                total_rows[...] = total_rows[...] + dot_nt(value_rows[...], held[...])
            else:
                total_rows[:live] = total_rows[:live] + grad_one[...] + dot_nt(grad_query[...], held[...])
                row = lax.broadcasted_iota(jnp.int32, (16, 2 * width), 0)
                small_v[...] = small[...]
                small_v[:16] = jnp.where(row < mem_rows, total_rows[:16], 0.0)
                query_sum = jnp.sum(grad_query[...].astype(jnp.float32), axis=0, keepdims=True)
                value_sum = jnp.sum(value_rows[...].astype(jnp.float32), axis=0, keepdims=True)
                small_v[16:24] = small[16:24] + jnp.where(
                    row[:8] == 0, query_sum, jnp.where(row[:8] == 1, value_sum, 0.0)
                )
            if n < 2:
                fetched[n + 1] = bring(weights[n + 1], held, 3)
        elif task == 7:
            unpermute(0, total_rows[...].astype(jnp.bfloat16), grad_item, 0)
        else:
            values, target, segment = (
                (outs_a, out_item, 0),
                (outs_b, out_item, 1),
                (grads_b, grad_item, 1),
            )[task - 8]
            bring(values, source, 2).wait()
            unpermute(task - 7, source[...], target, segment)

    started = {}
    ready = None
    for step in SCATTER_STEPS:
        if step >= 100:
            compute(step - 100)
            if step == 106:
                ready = 0
            continue
        p, s = step // 8, step % 8
        if s == 0:
            if p >= SLOTS:
                started[p - SLOTS, 0].wait_send()
            produce(p, p % SLOTS)
        else:
            started[p, s - 1].wait_recv()
            if s == 1:
                combine(p)
            else:
                fold(p, s - 1)
        if s < 5:
            started[p, s] = stage(p, s)
            started[p, s].start()
        if ready is not None:
            ready += 1
            if ready % 3 == 0 and ready <= 18:
                small_step(ready // 3 - 1)
    for (p, s), copy in started.items():
        if s > 0 or p >= len(SCATTER_PIECES) - SLOTS:
            copy.wait_send()
    for s in range(5):
        small_started[s].wait_send()
    for n in range(4):
        if n > 1:
            swaps[n].wait_send()
            places[n].wait()
        swaps[n].wait_recv()


def scatter_all(mem_rows, valid, first_rows, second_rows, tail, small, outs, grads):
    width = small.shape[1] // 2
    rows = 2 * width // 16
    low, full = jnp.bfloat16, jnp.float32
    count = len(SCATTER_PIECES)
    long, live = second_rows[0].shape[0], second_rows[1].shape[0]
    move = tail[-1]
    tokens = move.shape[2]
    item = (2, 2, tokens, width)
    return pl.pallas_call(
        functools.partial(scatter_kernel, mem_rows, valid),
        out_shape=[
            jax.ShapeDtypeStruct((3, rows, width), full),
            jax.ShapeDtypeStruct((rows, width), full),
            jax.ShapeDtypeStruct((rows, 4 * width), full),
            jax.ShapeDtypeStruct((rows, 4 * width), full),
            jax.ShapeDtypeStruct((small.shape[0], width), full),
            jax.ShapeDtypeStruct(item, low),
            jax.ShapeDtypeStruct(item, low),
        ],
        in_specs=[HBM] + [VMEM] * 6 + [HBM] + [VMEM] * 9
        + [VMEM, HBM, HBM, VMEM, VMEM, HBM, HBM, HBM, VMEM, VMEM, HBM, HBM, HBM],
        out_specs=[VMEM] * 5 + [HBM] * 2,
        scratch_shapes=[
            pltpu.VMEM((count, 2, 2, 2, 2, rows, width), low),
            pltpu.VMEM((count, 2, 2, 2, rows, width), low),
            pltpu.VMEM((count, 2, 2, rows, width), low),
            pltpu.VMEM((count, 2, rows, width), low),
            pltpu.VMEM((count, rows, width), low),
            pltpu.VMEM((SLOTS, 2, 2, 2, 2, rows, width), low),
            pltpu.VMEM((2, 2 * width, long), low),
            pltpu.VMEM((3, 2, 2 * width, live), low),
            pltpu.VMEM((2 * width, 2 * width), low),
            pltpu.VMEM((live, 2 * width), low),
            pltpu.VMEM((long, 2 * width), low),
            pltpu.VMEM((long, 2 * width), low),
            pltpu.VMEM((long, 2 * width), low),
            pltpu.VMEM((2, tokens, 2 * width), low),
            pltpu.VMEM((long, 2 * width), full),
            pltpu.VMEM(small.shape, full),
            pltpu.VMEM((5, small.shape[0], width), full),
            pltpu.VMEM((5, small.shape[0], width), full),
            pltpu.SemaphoreType.DMA((69,)),
            pltpu.SemaphoreType.DMA((69,)),
            pltpu.SemaphoreType.DMA((4,)),
            pltpu.SemaphoreType.DMA((4,)),
        ],
        compiler_params=pltpu.CompilerParams(collective_id=1, has_side_effects=True, vmem_limit_bytes=67_000_000),
        name="scatter_all",
    )(*first_rows, *second_rows, *tail[:-1], move, small, *outs, *grads)


def item_shards(
    tokens,
    memory,
    w_qkv,
    b_qv,
    w_out,
    out_biases,
    norm_gains,
    norm_shifts,
    w_in,
    b_in,
    w_down,
    cotangent,
    mlm_mask,
):
    core = lax.axis_index("tensor")
    segments, count = tokens.shape[1], tokens.shape[2]
    mem_rows = memory.shape[0]
    valid = mem_rows + count
    half = memory.shape[1]

    mask = lax.dynamic_index_in_dim(mlm_mask, core, 0, keepdims=False)
    lower_tri = (
        lax.broadcasted_iota(jnp.int32, (count, count), 0)
        <= lax.broadcasted_iota(jnp.int32, (count, count), 1)
    ).astype(jnp.bfloat16)
    ones = mask.astype(jnp.bfloat16)
    upto = dot_nn(ones, lower_tri).astype(jnp.int32)
    total = upto[:, -1:]
    index = lax.broadcasted_iota(jnp.int32, mask.shape, 1)
    place = mem_rows + jnp.where(mask > 0, upto - 1, total + index - upto)
    move = (
        lax.broadcasted_iota(jnp.int32, (segments, ROWS, count), 1) == place[:, None, :]
    ).astype(jnp.bfloat16)
    live_move = move[:, :LIVE] * ones[:, None, :]

    packed = jnp.concatenate(
        [
            jnp.pad(memory, ((0, PACK_BIASES - mem_rows), (0, 0))),
            b_qv,
            out_biases,
            norm_gains,
            norm_shifts,
            b_in.reshape(-1, half),
        ],
        axis=0,
    )
    packed = jnp.pad(packed, ((0, -packed.shape[0] % 16), (0, 0)))
    both, (wq, wk, wv, outer, inner, lower), first = gather_all(
        mem_rows,
        valid,
        tokens,
        cotangent,
        packed,
        w_qkv.transpose(1, 0, 2),
        w_out.T,
        w_in,
        w_down.T,
        move,
        live_move,
    )
    (
        stacked,
        stacked_next,
        ups,
        query,
        key_rows,
        value_rows,
        query_live,
        context,
        normed_one,
        rstd_one,
        middle_low,
        before,
        hidden,
        normed_two,
        rstd_two,
        low_out,
    ) = first
    wide = jnp.concatenate([both[0], both[1]], axis=1).astype(jnp.float32)
    qv_bias, out_bias, gains, shifts = (
        wide[n : n + 2] for n in (PACK_BIASES, PACK_OUT, PACK_GAINS, PACK_SHIFTS)
    )
    inner_rows = b_in.shape[0] // half
    inner_bias = both[:, PACK_INNER : PACK_INNER + inner_rows].reshape(-1).astype(jnp.float32)
    stored = [
        (
            stacked,
            query,
            key_rows,
            value_rows,
            context,
            normed_one,
            rstd_one,
            middle_low,
            before,
            hidden,
            normed_two,
            rstd_two,
        )
    ]
    outs = [low_out]
    stacked = stacked_next
    query = (dot_nn(stacked, wq) + qv_bias[0]).astype(jnp.bfloat16)
    key_rows = dot_nn(stacked, wk).astype(jnp.bfloat16)
    value_rows = (dot_nn(stacked, wv) + qv_bias[1]).astype(jnp.bfloat16)
    context = attend(query, key_rows, value_rows, valid)
    attended = dot_nt(context, outer)
    middle, normed_one, rstd_one = norm_rows(
        stacked.astype(jnp.float32) + attended + out_bias[0], gains[0], shifts[0]
    )
    middle_low = middle.astype(jnp.bfloat16)
    before = dot_nn(middle_low, inner) + inner_bias
    hidden = gelu_value(before).astype(jnp.bfloat16)
    branch = dot_nt(hidden, lower)
    layer_out, normed_two, rstd_two = norm_rows(
        middle + branch + out_bias[1], gains[1], shifts[1]
    )
    low_out = layer_out.astype(jnp.bfloat16)
    outs.append(low_out)
    stored.append(
        (
            stacked,
            query,
            key_rows,
            value_rows,
            context[:LIVE],
            normed_one[:LIVE],
            rstd_one[:LIVE],
            middle_low[:LIVE],
            before[:LIVE].astype(jnp.bfloat16).astype(jnp.float32),
            hidden[:LIVE],
            normed_two[:LIVE],
            rstd_two[:LIVE],
        )
    )

    returning = jnp.zeros((mem_rows, D), jnp.float32)
    token_grads = []
    pieces = [None] * segments
    smalls = None
    for seg in reversed(range(segments)):
        (
            stacked,
            query,
            key_rows,
            value_rows,
            context,
            normed_one,
            rstd_one,
            middle_low,
            before,
            hidden,
            normed_two,
            rstd_two,
        ) = stored[seg]
        upstream = ups[seg].astype(jnp.float32)
        upstream = upstream + jnp.pad(returning, ((0, LIVE - mem_rows), (0, 0)))
        grad_two, gain_two, shift_two = norm_rows_back(upstream, normed_two, rstd_two, gains[1])
        grad_branch = grad_two.astype(jnp.bfloat16)
        grad_hidden = dot_nn(grad_branch, lower)
        grad_before = (grad_hidden * gelu_slope(before)).astype(jnp.bfloat16)
        grad_middle = grad_two + dot_nt(grad_before, inner)
        grad_one, gain_one, shift_one = norm_rows_back(
            grad_middle, normed_one, rstd_one, gains[0]
        )
        grad_attended = grad_one.astype(jnp.bfloat16)
        grad_context = dot_nn(grad_attended, outer).astype(jnp.bfloat16)
        sums = [jnp.zeros((D,), jnp.float32)] * 2
        if seg > 0:
            grad_query, grad_key, grad_value = attend_back(
                query, key_rows, value_rows, grad_context, valid
            )
            grad_stacked = dot_nt(grad_key, wk) + dot_nt(grad_value, wv)
            live_part = grad_one + dot_nt(grad_query, wq)
            grad_stacked = grad_stacked + jnp.pad(live_part, ((0, ROWS - LIVE), (0, 0)))
            returning = grad_stacked[:mem_rows]
            token_grads.append(grad_stacked.astype(jnp.bfloat16))
            attention_grads = [grad_query, grad_key, grad_value]
            sums = [jnp.sum(grad.astype(jnp.float32), axis=0) for grad in (grad_query, grad_value)]
        else:
            attention_grads = []
            tail = [query_live, key_rows, value_rows, grad_context, grad_one, wq, wk, wv, move]
        pieces[seg] = (
            stacked,
            *attention_grads,
            grad_attended,
            context,
            middle_low,
            grad_before,
            grad_branch,
            hidden,
        )
        sums = jnp.concatenate(
            [
                jnp.stack(
                    [
                        *sums,
                        jnp.sum(grad_one, axis=0),
                        jnp.sum(grad_two, axis=0),
                        gain_one,
                        gain_two,
                        shift_one,
                        shift_two,
                    ]
                ),
                jnp.sum(grad_before.astype(jnp.float32), axis=0).reshape(-1, D),
            ],
            axis=0,
        )
        smalls = sums if smalls is None else smalls + sums

    inner_sums = smalls[8:].reshape(2, inner_rows, half).transpose(1, 0, 2).reshape(inner_rows, D)
    small = jnp.concatenate([jnp.zeros((16, D), jnp.float32), smalls[:8], inner_sums], axis=0)
    small = jnp.pad(small, ((0, -small.shape[0] % 8), (0, 0)))
    grad_proj, grad_outer, grad_inner, grad_lower, mine, outputs, input_grad = scatter_all(
        mem_rows, valid, pieces[0], pieces[1], tail, small, outs, token_grads
    )
    return (
        outputs,
        input_grad.astype(jnp.float32),
        mine[:mem_rows],
        grad_proj.transpose(1, 0, 2),
        mine[16:18],
        grad_outer.T,
        mine[18:20],
        mine[20:22],
        mine[22:24],
        grad_inner,
        mine[24 : 24 + inner_rows].reshape(-1),
        grad_lower.T,
    )


def solution(mesh):
    def body(*arrays):
        if mesh.shape["dp"] == 16 and mesh.shape["tensor"] == arrays[0].shape[0] == arrays[0].shape[1] == 2:
            return item_shards(*arrays)
        return shards(*arrays)

    placed = (
        P("dp", None, None, "tensor"),
        P(None, "tensor"),
        P("dp", None, "tensor"),
        P(None, "tensor"),
        P("tensor", "dp"),
        P(None, "tensor"),
        P(None, "tensor"),
        P(None, "tensor"),
        P("dp", "tensor"),
        P("tensor"),
        P("tensor", "dp"),
        P("dp", None, None, "tensor"),
        P("dp", None, None),
    )
    return jax.shard_map(
        body,
        mesh=mesh,
        in_specs=placed,
        out_specs=(
            P("dp", None, None, "tensor"),
            P("dp", None, None, "tensor"),
            P(None, "tensor"),
            P("dp", None, "tensor"),
            P(None, "tensor"),
            P("tensor", "dp"),
            P(None, "tensor"),
            P(None, "tensor"),
            P(None, "tensor"),
            P("dp", "tensor"),
            P("tensor"),
            P("tensor", "dp"),
        ),
        check_vma=False,
    )
```

```python
import functools

import jax
import jax.numpy as jnp
from jax import lax
from jax.experimental import pallas as pl
from jax.experimental.pallas import tpu as pltpu
from jax.sharding import PartitionSpec as P

D = 1024
DH = 64
MICRO = 2


eps_norm = 1e-05
root_half = 0.7071067811865476
inv_root_two_pi = 0.3989422804014327


def gelu_value(before):
    return 0.5 * before * (1.0 + lax.erf(before * root_half))


def gelu_slope(before):
    return 0.5 * (1.0 + lax.erf(before * root_half)) + before * inv_root_two_pi * jnp.exp(
        -0.5 * before * before
    )


def fetch_weights(w_qkv, w_in, w_out, w_down):
    return (
        lax.all_gather(w_qkv, "dp", axis=0, tiled=True),
        lax.all_gather(w_in, "dp", axis=0, tiled=True),
        lax.all_gather(w_out, "dp", axis=1, tiled=True),
        lax.all_gather(w_down, "dp", axis=1, tiled=True),
    )


def reduce_weights(grad_proj, grad_inner, grad_outer, grad_lower):
    return (
        lax.psum_scatter(
            grad_proj.astype(jnp.bfloat16), "dp", scatter_dimension=0, tiled=True
        ).astype(jnp.float32),
        lax.psum_scatter(
            grad_inner.astype(jnp.bfloat16), "dp", scatter_dimension=0, tiled=True
        ).astype(jnp.float32),
        lax.psum_scatter(
            grad_outer.astype(jnp.bfloat16), "dp", scatter_dimension=1, tiled=True
        ).astype(jnp.float32),
        lax.psum_scatter(
            grad_lower.astype(jnp.bfloat16), "dp", scatter_dimension=1, tiled=True
        ).astype(jnp.float32),
    )


def gather_rows(block):
    return lax.all_gather(block, "tensor", axis=2, tiled=True)


def branch_sum(partial_value):
    return lax.psum_scatter(partial_value, "tensor", scatter_dimension=2, tiled=True)


def gather_grads(block):
    return lax.all_gather(block, "tensor", axis=2, tiled=True)


def input_sum(partial_value):
    return lax.psum_scatter(
        partial_value.astype(jnp.bfloat16), "tensor", scatter_dimension=2, tiled=True
    ).astype(jnp.float32)


def norm_forward(resid, gain, shift):
    totals = jnp.sum(resid, axis=-1)
    squares = jnp.sum(resid * resid, axis=-1)
    totals, squares = lax.psum((totals, squares), "tensor")
    center = totals / D
    spread = squares / D - center * center
    rstd = lax.rsqrt(spread + eps_norm)
    normed = (resid - center[..., None]) * rstd[..., None]
    return (normed * gain + shift, normed, rstd)


def norm_backward(upstream, normed, rstd, gain):
    scaled = upstream * gain
    first = jnp.sum(scaled, axis=-1)
    second = jnp.sum(scaled * normed, axis=-1)
    first, second = lax.psum((first, second), "tensor")
    result = rstd[..., None] * (scaled - first[..., None] / D - normed * (second[..., None] / D))
    return (result, jnp.sum(upstream * normed, axis=(0, 1)), jnp.sum(upstream, axis=(0, 1)))


def attention_scores(query, key_rows):
    return jnp.einsum(
        "bqhe,bkhe->bhqk", query, key_rows, preferred_element_type=jnp.float32
    ) * DH ** (-0.5)


def segment_forward(weights, smalls, memory_rows, token_rows):
    proj_weight, inner_weight, outer_weight, lower_weight = weights
    qv_bias, out_bias, gains, shifts, inner_bias = smalls
    batch = token_rows.shape[0]
    stacked = jnp.concatenate([memory_rows, token_rows], axis=1)
    length = stacked.shape[1]
    local = proj_weight.shape[2]
    heads = local // DH
    wide_rows = gather_rows(stacked)
    bias_three = jnp.stack([qv_bias[0], jnp.zeros_like(qv_bias[0]), qv_bias[1]])
    projected = (
        jnp.einsum("bld,dcf->blcf", wide_rows, proj_weight, preferred_element_type=jnp.float32)
        + bias_three
    ).astype(jnp.bfloat16)
    split = projected.reshape(batch, length, 3, heads, DH)
    scores = attention_scores(split[:, :, 0], split[:, :, 1])
    peak = jnp.max(scores, axis=-1, keepdims=True)
    expo = jnp.exp(scores - peak)
    totals = jnp.sum(expo, axis=-1, keepdims=True)
    probs = expo / totals
    logsum = peak[..., 0] + jnp.log(totals[..., 0])
    context = jnp.einsum(
        "bhqk,bkhe->bqhe",
        probs.astype(jnp.bfloat16),
        split[:, :, 2],
        preferred_element_type=jnp.float32,
    )
    context = context.astype(jnp.bfloat16).reshape(batch, length, local)
    attended = branch_sum(
        jnp.einsum("bld,df->blf", context, outer_weight, preferred_element_type=jnp.float32)
    )
    middle, normed_one, rstd_one = norm_forward(
        stacked.astype(jnp.float32) + attended + out_bias[0], gains[0], shifts[0]
    )
    middle_wide = gather_rows(middle.astype(jnp.bfloat16))
    before = (
        jnp.einsum("bld,df->blf", middle_wide, inner_weight, preferred_element_type=jnp.float32)
        + inner_bias
    )
    hidden = gelu_value(before).astype(jnp.bfloat16)
    branch = branch_sum(
        jnp.einsum("blf,fd->bld", hidden, lower_weight, preferred_element_type=jnp.float32)
    )
    layer_out, normed_two, rstd_two = norm_forward(
        middle + branch + out_bias[1], gains[1], shifts[1]
    )
    stored = (
        wide_rows,
        projected,
        logsum,
        context,
        normed_one,
        rstd_one,
        middle_wide,
        before,
        hidden,
        normed_two,
        rstd_two,
    )
    return (layer_out, stored)


def segment_backward(weights, smalls, upstream, stored):
    proj_weight, inner_weight, outer_weight, lower_weight = weights
    qv_bias, out_bias, gains, shifts, inner_bias = smalls
    (
        wide_rows,
        projected,
        logsum,
        context,
        normed_one,
        rstd_one,
        middle_wide,
        before,
        hidden,
        normed_two,
        rstd_two,
    ) = stored
    batch, length, local = context.shape
    heads = local // DH
    grad_two, gain_two, shift_two = norm_backward(upstream, normed_two, rstd_two, gains[1])
    grad_branch = gather_grads(grad_two.astype(jnp.bfloat16))
    grad_lower = jnp.einsum("blf,bld->fd", hidden, grad_branch, preferred_element_type=jnp.float32)
    grad_hidden = jnp.einsum(
        "bld,fd->blf", grad_branch, lower_weight, preferred_element_type=jnp.float32
    )
    grad_before = (grad_hidden * gelu_slope(before)).astype(jnp.bfloat16)
    grad_inner = jnp.einsum(
        "bld,blf->df", middle_wide, grad_before, preferred_element_type=jnp.float32
    )
    grad_inner_bias = jnp.sum(grad_before.astype(jnp.float32), axis=(0, 1))
    grad_middle = grad_two + lax.psum_scatter(
        jnp.einsum(
            "blf,df->bld", grad_before, inner_weight, preferred_element_type=jnp.float32
        ).astype(jnp.bfloat16),
        "tensor",
        scatter_dimension=2,
        tiled=True,
    ).astype(jnp.float32)
    grad_one, gain_one, shift_one = norm_backward(grad_middle, normed_one, rstd_one, gains[0])
    grad_attended = gather_grads(grad_one.astype(jnp.bfloat16))
    grad_outer = jnp.einsum(
        "bld,blf->df", context, grad_attended, preferred_element_type=jnp.float32
    )
    grad_context = jnp.einsum(
        "blf,df->bld", grad_attended, outer_weight, preferred_element_type=jnp.float32
    )
    grad_context = grad_context.astype(jnp.bfloat16)
    grad_context = grad_context.reshape(batch, length, heads, DH)
    split = projected.reshape(batch, length, 3, heads, DH)
    query, key_rows, value_rows = (split[:, :, 0], split[:, :, 1], split[:, :, 2])
    probs = jnp.exp(attention_scores(query, key_rows) - logsum[..., None])
    grad_probs = jnp.einsum(
        "bqhe,bkhe->bhqk", grad_context, value_rows, preferred_element_type=jnp.float32
    )
    weighted_sum = jnp.sum(probs * grad_probs, axis=-1, keepdims=True)
    grad_scores = (probs * (grad_probs - weighted_sum)).astype(jnp.bfloat16)
    grad_query = jnp.einsum(
        "bhqk,bkhe->bqhe", grad_scores, key_rows, preferred_element_type=jnp.float32
    ) * DH ** (-0.5)
    grad_key = jnp.einsum(
        "bhqk,bqhe->bkhe", grad_scores, query, preferred_element_type=jnp.float32
    ) * DH ** (-0.5)
    grad_value = jnp.einsum(
        "bhqk,bqhe->bkhe",
        probs.astype(jnp.bfloat16),
        grad_context,
        preferred_element_type=jnp.float32,
    )
    grad_projected = (
        jnp.stack([grad_query, grad_key, grad_value], axis=2)
        .reshape(batch, length, 3, local)
        .astype(jnp.bfloat16)
    )
    grad_proj = jnp.einsum(
        "bld,blcf->dcf", wide_rows, grad_projected, preferred_element_type=jnp.float32
    )
    column_sums = jnp.sum(grad_projected.astype(jnp.float32), axis=(0, 1))
    grad_qv = jnp.stack([column_sums[0], column_sums[2]])
    grad_stacked = grad_one + input_sum(
        jnp.einsum("blcf,dcf->bld", grad_projected, proj_weight, preferred_element_type=jnp.float32)
    )
    grad_biases = jnp.stack([jnp.sum(grad_one, axis=(0, 1)), jnp.sum(grad_two, axis=(0, 1))])
    large_grads = (grad_proj, grad_inner, grad_outer, grad_lower)
    small_grads = (
        grad_qv,
        grad_biases,
        jnp.stack([gain_one, gain_two]),
        jnp.stack([shift_one, shift_two]),
        grad_inner_bias,
    )
    return (grad_stacked, large_grads, small_grads)


def add_tuples(first, second):
    return tuple((left + right for left, right in zip(first, second)))


def shards(
    tokens,
    memory,
    w_qkv,
    b_qv,
    w_out,
    out_biases,
    norm_gains,
    norm_shifts,
    w_in,
    b_in,
    w_down,
    cotangent,
    mlm_mask,
):
    smalls = (
        b_qv.astype(jnp.float32),
        out_biases.astype(jnp.float32),
        norm_gains.astype(jnp.float32),
        norm_shifts.astype(jnp.float32),
        b_in.astype(jnp.float32),
    )
    per_batch = tokens.shape[0] // MICRO
    segments = tokens.shape[1]
    mem_rows = memory.shape[0]
    local = w_qkv.shape[2]
    inner_local = w_in.shape[1]
    empty_large = (
        jnp.zeros((D, 3, local), jnp.float32),
        jnp.zeros((D, inner_local), jnp.float32),
        jnp.zeros((local, D), jnp.float32),
        jnp.zeros((inner_local, D), jnp.float32),
    )
    full_grads = empty_large
    shard_grads = (
        jnp.zeros(w_qkv.shape, jnp.float32),
        jnp.zeros(w_in.shape, jnp.float32),
        jnp.zeros(w_out.shape, jnp.float32),
        jnp.zeros(w_down.shape, jnp.float32),
    )
    small_total = (
        jnp.zeros((2, local), jnp.float32),
        jnp.zeros((2, local), jnp.float32),
        jnp.zeros((2, local), jnp.float32),
        jnp.zeros((2, local), jnp.float32),
        jnp.zeros((inner_local,), jnp.float32),
    )
    memory_total = jnp.zeros((mem_rows, local), jnp.float32)
    out_blocks = []
    grad_blocks = []
    for batch_index in range(MICRO):
        offset = batch_index * per_batch
        batch_tokens = tokens[offset : offset + per_batch]
        batch_mask = mlm_mask[offset : offset + per_batch]
        batch_cot = cotangent[offset : offset + per_batch].astype(jnp.float32) * batch_mask[
            ..., None
        ].astype(jnp.float32)
        weights = fetch_weights(w_qkv, w_in, w_out, w_down)
        carried = memory[None]
        stored_all = []
        token_outs = []
        for seg_index in range(segments):
            layer_out, stored = segment_forward(
                weights, smalls, carried, batch_tokens[:, seg_index]
            )
            carried = layer_out[:, :mem_rows].astype(jnp.bfloat16)
            token_outs.append(layer_out[:, mem_rows:].astype(jnp.bfloat16))
            stored_all.append(stored)
        returning = jnp.zeros((per_batch, mem_rows, local), jnp.float32)
        token_grads = [None] * segments
        for seg_index in reversed(range(segments)):
            upstream = jnp.concatenate([returning, batch_cot[:, seg_index]], axis=1)
            grad_stacked, large_grads, small_grads = segment_backward(
                weights, smalls, upstream, stored_all[seg_index]
            )
            returning = grad_stacked[:, :mem_rows]
            token_grads[seg_index] = grad_stacked[:, mem_rows:]
            full_grads = add_tuples(full_grads, large_grads)
            small_total = add_tuples(small_total, small_grads)
        memory_total = memory_total + jnp.sum(returning, axis=0)
        reduced = reduce_weights(full_grads[0], full_grads[1], full_grads[2], full_grads[3])
        shard_grads = add_tuples(shard_grads, reduced)
        full_grads = empty_large
        out_blocks.append(jnp.stack(token_outs, axis=1))
        grad_blocks.append(jnp.stack(token_grads, axis=1))
    grad_qv, grad_biases, grad_gains, grad_shifts, grad_inner_bias, memory_grad = lax.psum(
        (
            small_total[0],
            small_total[1],
            small_total[2],
            small_total[3],
            small_total[4],
            memory_total,
        ),
        "dp",
    )
    outputs = jnp.concatenate(out_blocks, axis=0)
    input_grad = jnp.concatenate(grad_blocks, axis=0)
    return (
        outputs,
        input_grad,
        memory_grad,
        shard_grads[0],
        grad_qv,
        shard_grads[2],
        grad_biases,
        grad_gains,
        grad_shifts,
        shard_grads[1],
        grad_inner_bias,
        shard_grads[3],
    )


ROWS = 528
LIVE = 176


def dot_nn(left, right):
    return jnp.dot(left, right, preferred_element_type=jnp.float32)


def dot_nt(left, right):
    return lax.dot_general(
        left, right, (((1,), (1,)), ((), ())), preferred_element_type=jnp.float32
    )


def dot_tn(left, right):
    return lax.dot_general(
        left, right, (((0,), (0,)), ((), ())), preferred_element_type=jnp.float32
    )


def norm_rows(resid, gain, shift):
    center = jnp.mean(resid, axis=-1, keepdims=True)
    spread = jnp.mean(resid * resid, axis=-1, keepdims=True) - center * center
    rstd = lax.rsqrt(spread + eps_norm)
    normed = (resid - center) * rstd
    return (normed * gain + shift, normed, rstd)


def norm_rows_back(upstream, normed, rstd, gain):
    scaled = upstream * gain
    first = jnp.mean(scaled, axis=-1, keepdims=True)
    second = jnp.mean(scaled * normed, axis=-1, keepdims=True)
    result = rstd * (scaled - first - normed * second)
    return (result, jnp.sum(upstream * normed, axis=0), jnp.sum(upstream, axis=0))


MESH = pl.DeviceIdType.MESH
HBM = pl.BlockSpec(memory_space=pl.ANY)
VMEM = pl.BlockSpec(memory_space=pltpu.VMEM)
GATHER_PIECES = ((0, 0), (1, 0), (2, 0), (3, 0), (4, 0), (5, 0), (4, 1), (5, 1), (4, 2), (5, 2), (4, 3), (5, 3))
SCATTER_PIECES = ((5, 0), (5, 1), (5, 2), (5, 3), (4, 0), (4, 1), (4, 2), (4, 3), (3, 0), (0, 0), (1, 0), (2, 0))
GATHER_HOPS = (
    (3, 2, 1, 0), (3, 2, 0, 1), (3, 2, 1, 0), (3, 0, 1, 2), (3, 2, 1, 0), (3, 1, 0, 2),
    (3, 2, 0, 1), (3, 2, 1, 0), (3, 0, 1, 2), (3, 2, 0, 1), (3, 2, 1, 0), (3, 0, 1, 2),
)
SCATTER_HOPS = (
    (2, 1, 0, 3), (0, 1, 2, 3), (1, 0, 2, 3), (2, 1, 0, 3), (0, 1, 2, 3), (2, 0, 3, 1),
    (0, 1, 2, 3), (1, 2, 0, 3), (0, 2, 1, 3), (0, 1, 2, 3), (1, 0, 2, 3), (1, 0, 2, 3),
)
GATHER_STEPS = (
    0, 8, 1, 100, 16, 9, 24, 2, 17, 32, 10, 40, 3, 25, 48, 18, 11, 56, 33, 64,
    41, 19, 49, 72, 57, 80, 4, 34, 26, 88, 5, 65, 101, 12, 50, 42, 73, 13, 102, 58,
    35, 20, 81, 66, 21, 89, 103, 27, 74, 104, 51, 82, 105, 59, 106, 43, 107, 67, 28, 29,
    36, 108, 52, 90, 37, 44, 53, 75, 83, 45, 109, 91, 68, 60, 69, 61, 76, 110, 77, 92,
    84, 111, 93, 85, 112, 113,
)
SCATTER_STEPS = (
    0, 8, 16, 1, 9, 17, 24, 32, 100, 25, 33, 2, 40, 10, 48, 18, 101, 41, 3, 49,
    26, 56, 34, 64, 11, 102, 19, 57, 27, 65, 4, 42, 103, 12, 35, 72, 20, 80, 5, 73,
    50, 88, 13, 28, 36, 81, 21, 58, 89, 29, 51, 104, 37, 105, 66, 106, 59, 107, 43, 108,
    52, 82, 109, 110, 67, 74, 44, 90, 60, 53, 68, 61, 83, 69, 75, 45, 84, 91, 76, 85,
    92, 77, 93,
)
SLOTS = 2


def here():
    me = lax.axis_index("dp")
    core = lax.axis_index("tensor")
    bits = tuple((me // (1 << b)) % 2 for b in range(4))
    peers = tuple({"dp": me + (1 - 2 * bits[b]) * (1 << b)} for b in range(4))
    return core, bits, peers + ({"tensor": 1 - core},)


def greet(peers):
    barrier = pltpu.get_barrier_semaphore()
    for peer in peers:
        pl.semaphore_signal(barrier, inc=1, device_id=peer, device_id_type=MESH)
    pl.semaphore_wait(barrier, len(peers))


def block_index(bits, free, flip=None):
    index = []
    for b in (3, 2, 1, 0):
        if b == flip:
            index.append(1 - bits[b])
        elif b in free:
            index.append(slice(None))
        else:
            index.append(bits[b])
    return tuple(index)


def columns(array, part, core, width):
    blocks = 4 if array > 3 else 1
    return pl.ds(pl.multiple_of((core * blocks + part) * width, width), width)


def shard_block(shards, piece, width):
    array, part = piece
    if array < 3:
        return shards[array].at[array]
    return shards[array].at[:, pl.ds(part * width, width)]


def attend_pair(query, key_rows, value_rows, valid):
    main = key_rows.shape[0] - 16
    lane = lax.broadcasted_iota(jnp.int32, (1, 2 * DH), 1)
    left = lane < DH
    query = query * DH ** (-0.5)
    zero = jnp.zeros_like(query)
    tail_lane = lax.broadcasted_iota(jnp.int32, (1, 32), 1)
    tail_zero = jnp.zeros((16, 2 * DH), query.dtype)
    key_tail, value_tail = key_rows[main:], value_rows[main:]
    keys_both = jnp.concatenate(
        [jnp.where(left, key_tail, tail_zero), jnp.where(left, tail_zero, key_tail)], axis=0
    )
    values_both = jnp.concatenate(
        [jnp.where(left, value_tail, tail_zero), jnp.where(left, tail_zero, value_tail)], axis=0
    )
    ones_both = jnp.concatenate(
        [jnp.where(left, tail_zero, tail_zero + 1), jnp.where(left, tail_zero + 1, tail_zero)], axis=0
    )
    tail = dot_nt(query, keys_both)
    tail = jnp.where(tail_lane % 16 < valid - main, tail, -1e30)
    peaks, parts = [], []
    for head in range(2):
        picked = jnp.where(left if head == 0 else ~left, query, zero)
        scores = dot_nt(picked, key_rows[:main])
        side = (tail_lane < 16) if head == 0 else (tail_lane >= 16)
        peak = jnp.maximum(
            jnp.max(scores, axis=1, keepdims=True),
            jnp.max(jnp.where(side, tail, -1e30), axis=1, keepdims=True),
        )
        expo = jnp.exp(scores - peak).astype(jnp.bfloat16)
        one = jnp.ones_like(value_rows[:main])
        values = jnp.where(left if head == 0 else ~left, value_rows[:main], one)
        parts.append(dot_nn(expo, values))
        peaks.append(peak)
    tail = jnp.exp(tail - jnp.where(tail_lane < 16, peaks[0], peaks[1])).astype(jnp.bfloat16)
    both = dot_nn(tail, jnp.concatenate([values_both, ones_both], axis=1))
    value_sum = jnp.where(left, parts[0], parts[1]) + both[:, : 2 * DH]
    total = jnp.where(left, parts[1], parts[0]) + both[:, 2 * DH :]
    return (value_sum / pltpu.roll(total, DH, 1)).astype(jnp.bfloat16)


def attend_kernel(valid, q_ref, k_ref, v_ref, out_ref):
    out_ref[...] = attend_pair(q_ref[...], k_ref[...], v_ref[...], valid)


def attend(query, key_rows, value_rows, valid):
    block = pl.BlockSpec((query.shape[0], 2 * DH), lambda i: (0, i))
    return pl.pallas_call(
        functools.partial(attend_kernel, valid),
        grid=(D // (2 * DH),),
        out_shape=jax.ShapeDtypeStruct(query.shape, jnp.bfloat16),
        in_specs=[block] * 3,
        out_specs=block,
        compiler_params=pltpu.CompilerParams(vmem_limit_bytes=12 << 20),
        name="attend",
    )(query, key_rows, value_rows)


def attend_back_pair(query, key_rows, value_rows, grads, valid):
    live = query.shape[0]
    left = lax.broadcasted_iota(jnp.int32, (1, 2 * DH), 1) < DH
    zero = jnp.zeros_like(query)
    query = query * DH ** (-0.5)
    picked = jnp.concatenate([jnp.where(left, query, zero), jnp.where(left, zero, query)], axis=0)
    up = jnp.concatenate([jnp.where(left, grads, zero), jnp.where(left, zero, grads)], axis=0)
    scores = dot_nt(key_rows, picked)
    scores = jnp.where(lax.broadcasted_iota(jnp.int32, scores.shape, 0) < valid, scores, -1e30)
    expo = jnp.exp(scores - jnp.max(scores, axis=0, keepdims=True))
    probs = expo * (1.0 / jnp.sum(expo, axis=0, keepdims=True))
    grad_probs = dot_nt(value_rows, up)
    weighted = jnp.sum(probs * grad_probs, axis=0, keepdims=True)
    grad_scores = (probs * (grad_probs - weighted)).astype(jnp.bfloat16)
    grad_query = dot_tn(grad_scores, key_rows)
    grad_query = jnp.where(left, grad_query[:live], grad_query[live:]) * DH ** (-0.5)
    grad_key = dot_nn(grad_scores, picked)
    grad_value = dot_nn(probs.astype(jnp.bfloat16), up)
    return tuple(grad.astype(jnp.bfloat16) for grad in (grad_query, grad_key, grad_value))


def attend_back_kernel(valid, q_ref, k_ref, v_ref, g_ref, dq_ref, dk_ref, dv_ref):
    dq_ref[...], dk_ref[...], dv_ref[...] = attend_back_pair(
        q_ref[...], k_ref[...], v_ref[...], g_ref[...], valid
    )


def attend_back(query, key_rows, value_rows, grad_context, valid):
    live = grad_context.shape[0]
    short = pl.BlockSpec((live, 2 * DH), lambda i: (0, i))
    tall = pl.BlockSpec((key_rows.shape[0], 2 * DH), lambda i: (0, i))
    low = jnp.bfloat16
    return pl.pallas_call(
        functools.partial(attend_back_kernel, valid),
        grid=(D // (2 * DH),),
        out_shape=[jax.ShapeDtypeStruct((live, D), low)] + [jax.ShapeDtypeStruct(key_rows.shape, low)] * 2,
        in_specs=[short, tall, tall, short],
        out_specs=[short, tall, tall],
        compiler_params=pltpu.CompilerParams(vmem_limit_bytes=12 << 20),
        name="attend_back",
    )(query, key_rows, value_rows, grad_context)


PACK_BIASES, PACK_OUT, PACK_GAINS, PACK_SHIFTS, PACK_INNER = 16, 18, 20, 22, 24


def gather_kernel(
    mem_rows, valid, toks, cots, pack, sq, so, si, sl, move, live_move,
    packs, fq, fk, fv, fo, fi, fl, stacked_a, stacked_b, ups, query, key_rows, value_rows,
    query_live, context_live, normed_one, rstd_one, middle_live, before_live, hidden_live, normed_two, rstd_two, low_out,
    x_v, c_v, vq, vo, vi, vl, held, context, middle, middle_low, branch,
    send, recv, local, loads, extra,
):
    core, bits, peers = here()
    width = pack.shape[1]
    live = ups.shape[1]
    shards = (vq, vq, vq, vo, vi, vl)
    fulls = (fq, fk, fv, fo, fi, fl)
    mine = pl.ds(pl.multiple_of(core * width, width), width)
    shard_in = [
        pltpu.make_async_copy(src, dst, extra.at[n])
        for n, (src, dst) in enumerate(((sq, vq), (so, vo), (si, vi), (sl, vl)))
    ]
    rows_own = [
        pltpu.make_async_copy(toks.at[core], x_v.at[:, :, mine], extra.at[4]),
        pltpu.make_async_copy(cots.at[core], c_v.at[:, :, mine], extra.at[5]),
        pltpu.make_async_copy(pack, packs.at[core], extra.at[6]),
    ]
    for copy in shard_in + rows_own:
        copy.start()
    own = []
    for p, (array, part) in enumerate(GATHER_PIECES):
        own.append(pltpu.make_async_copy(
            shard_block(shards, (array, part), width),
            fulls[array].at[block_index(bits, ()) + (slice(None), columns(array, part, core, width))],
            local.at[p],
        ))
    greet(peers)
    for copy in shard_in:
        copy.wait()
    for copy in own:
        copy.start()

    def remote(src, dst, slot, peer):
        return pltpu.make_async_remote_copy(
            src_ref=src, dst_ref=dst, send_sem=send.at[slot], recv_sem=recv.at[slot],
            device_id=peer, device_id_type=MESH)

    def stage(p, s):
        array, part = GATHER_PIECES[p]
        order = GATHER_HOPS[p]
        cols = columns(array, part, core, width)
        dst = fulls[array].at[block_index(bits, order[:s]) + (slice(None), cols)]
        if s == 0:
            src = shard_block(shards, (array, part), width)
        else:
            src = dst
        peer = peers[order[s]] if s < 4 else peers[4]
        return remote(src, dst, p * 5 + s, peer)

    swaps = [
        remote(toks.at[1 - core], x_v.at[:, :, mine], 60, peers[4]),
        remote(cots.at[1 - core], c_v.at[:, :, mine], 61, peers[4]),
        remote(pack, packs.at[core], 62, peers[4]),
    ]
    started, loading = {}, {}

    def load(p):
        array, part = GATHER_PIECES[p]
        blocks = 4 if array > 3 else 1
        every = (slice(None),) * 5
        loading[p] = [
            pltpu.make_async_copy(
                fulls[array].at[every + (pl.ds((half * blocks + part) * width, width),)],
                held.at[(p % 6,) + every + (pl.ds(half * width, width),)],
                loads.at[2 * p + half],
            )
            for half in range(2)
        ]
        for copy in loading[p]:
            copy.start()

    def loaded(p):
        for copy in loading.pop(p):
            copy.wait()

    def weight(p, cols):
        block = held[p % 6, :, :, :, :, :, cols]
        return block.reshape(2 * width, block.shape[-1])

    def wide(row):
        return jnp.concatenate([packs[0, row : row + 1], packs[1, row : row + 1]], axis=1).astype(jnp.float32)

    def norm(resid, gain, shift):
        center = jnp.mean(resid, axis=1, keepdims=True)
        spread = jnp.mean(resid * resid, axis=1, keepdims=True) - center * center
        rstd = lax.rsqrt(spread + eps_norm)
        normed = (resid - center) * rstd
        return normed * gain + shift, normed, rstd

    def compute(task):
        if task == 0:
            for copy in rows_own:
                copy.wait()
            for swap in swaps:
                swap.wait_recv()
            memory = jnp.concatenate([packs[0, :16], packs[1, :16]], axis=1)
            is_memory = lax.broadcasted_iota(jnp.int32, memory.shape, 0) < mem_rows
            stacked_a[...] = dot_nn(move[0], x_v[0]).astype(jnp.bfloat16)
            stacked_a[:16] = jnp.where(is_memory, memory, stacked_a[:16])
            stacked_b[...] = dot_nn(move[1], x_v[1]).astype(jnp.bfloat16)
            for n in range(2):
                ups[n] = dot_nn(live_move[n], c_v[n]).astype(jnp.bfloat16)
        elif task < 4:
            n = task - 1
            loaded(n)
            target = (query, key_rows, value_rows)[n]
            for half in range(2):
                cols = pl.ds(half * width, width)
                got = dot_nn(stacked_a[...], weight(n, cols))
                if n != 1:
                    row = PACK_BIASES + n // 2
                    got = got + packs[half, row : row + 1].astype(jnp.float32)
                target[:, cols] = got.astype(jnp.bfloat16)
                if n == 0:
                    query_live[:, cols] = got[:live].astype(jnp.bfloat16)
        elif task < 8:

            def pair(n, carry):
                cols = pl.ds(pl.multiple_of((2 * (task - 4) + n) * 2 * DH, 2 * DH), 2 * DH)
                context[:, cols] = attend_pair(query[:, cols], key_rows[:, cols], value_rows[:, cols], valid)
                return carry

            lax.fori_loop(0, 2, pair, 0)
        elif task == 8:
            loaded(3)
            attended = dot_nt(context[...], weight(3, slice(None)))
            resid = stacked_a[...].astype(jnp.float32) + attended + wide(PACK_OUT)
            value, normed, rstd = norm(resid, wide(PACK_GAINS), wide(PACK_SHIFTS))
            middle[...] = value
            middle_low[...] = value.astype(jnp.bfloat16)
            middle_live[...] = value[:live].astype(jnp.bfloat16)
            context_live[...] = context[:live]
            normed_one[...] = normed[:live]
            rstd_one[...] = jnp.broadcast_to(rstd[:live], rstd_one.shape)
        elif task < 13:
            j = task - 9
            loaded(4 + 2 * j)
            loaded(5 + 2 * j)

            def hidden_block(half, carry):
                cols = pl.ds(pl.multiple_of(half * width, width), width)
                place = pl.ds(pl.multiple_of((half * 4 + j) * width, width), width)
                bias = packs[half, PACK_INNER + j : PACK_INNER + j + 1].astype(jnp.float32)
                before = dot_nn(middle_low[...], weight(4 + 2 * j, cols)) + bias
                before_live[:, place] = before[:live]
                hidden = gelu_value(before).astype(jnp.bfloat16)
                hidden_live[:, place] = hidden[:live]
                branch[...] = branch[...] + dot_nt(hidden, weight(5 + 2 * j, cols))
                return carry

            if j == 0:
                branch[...] = middle[...] + wide(PACK_OUT + 1)
            lax.fori_loop(0, 2, hidden_block, 0)
        else:
            value, normed, rstd = norm(branch[...], wide(PACK_GAINS + 1), wide(PACK_SHIFTS + 1))
            low_out[...] = value.astype(jnp.bfloat16)
            is_memory = lax.broadcasted_iota(jnp.int32, (16, 2 * width), 0) < mem_rows
            stacked_b[:16] = jnp.where(is_memory, low_out[:16], stacked_b[:16])
            normed_two[...] = normed[:live]
            rstd_two[...] = jnp.broadcast_to(rstd[:live], rstd_two.shape)

    for tick, step in enumerate(GATHER_STEPS):
        if step >= 100:
            compute(step - 100)
            continue
        p, s = step // 8, step % 8
        if s > 0:
            started[p, s - 1].wait_recv()
        if s == 1:
            own[p].wait()
        if s == 5:
            load(p)
        else:
            started[p, s] = stage(p, s)
            started[p, s].start()
        if tick == 2:
            for swap in swaps:
                swap.start()
    for copy in started.values():
        copy.wait_send()
    for swap in swaps:
        swap.wait_send()


def gather_all(mem_rows, valid, toks, cots, pack, sq, so, si, sl, move, live_move):
    width = pack.shape[1]
    rows = sq.shape[1]
    low, full = jnp.bfloat16, jnp.float32
    total, live = move.shape[1], live_move.shape[1]
    hidden = 2 * si.shape[1]
    out = [((2,) + pack.shape, low)]
    for size in (2 * width, 2 * width, 2 * width, 2 * width, hidden, hidden):
        out.append(((2, 2, 2, 2, rows, size), low))
    out += [((total, 2 * width), low)] * 2 + [((2, live, 2 * width), low)]
    out += [((total, 2 * width), low)] * 3 + [((live, 2 * width), low)] * 2
    out += [((live, 2 * width), full), ((live, 2 * width), full), ((live, 2 * width), low)]
    out += [((live, hidden), full), ((live, hidden), low)]
    out += [((live, 2 * width), full), ((live, 2 * width), full), ((total, 2 * width), low)]
    block = (2, 2, 2, 2, rows, 2 * width)
    got = pl.pallas_call(
        functools.partial(gather_kernel, mem_rows, valid),
        out_shape=[jax.ShapeDtypeStruct(*one) for one in out],
        in_specs=[HBM, HBM, VMEM] + [HBM] * 4 + [VMEM] * 2,
        out_specs=[VMEM] + [HBM] * 6 + [VMEM] * (len(out) - 7),
        scratch_shapes=[
            pltpu.VMEM(toks.shape[1:3] + (2 * width,), low),
            pltpu.VMEM(toks.shape[1:3] + (2 * width,), low),
            pltpu.VMEM(sq.shape, low),
            pltpu.VMEM(so.shape, low),
            pltpu.VMEM(si.shape, low),
            pltpu.VMEM(sl.shape, low),
            pltpu.VMEM((6,) + block, low),
            pltpu.VMEM((total, 2 * width), low),
            pltpu.VMEM((total, 2 * width), full),
            pltpu.VMEM((total, 2 * width), low),
            pltpu.VMEM((total, 2 * width), full),
            pltpu.SemaphoreType.DMA((63,)),
            pltpu.SemaphoreType.DMA((63,)),
            pltpu.SemaphoreType.DMA((12,)),
            pltpu.SemaphoreType.DMA((24,)),
            pltpu.SemaphoreType.DMA((7,)),
        ],
        compiler_params=pltpu.CompilerParams(collective_id=0, has_side_effects=True, vmem_limit_bytes=62 << 20),
        name="gather_all",
    )(toks, cots, pack, sq, so, si, sl, move, live_move)
    wide = [array.reshape(16 * rows, array.shape[-1]) for array in got[1:7]]
    return got[0], wide, got[7:]


def scatter_kernel(mem_rows, valid, *refs):
    (rows_a, out_a, context_a, middle_a, before_a, branch_a, hidden_a) = refs[0:7]
    second_in = refs[7:17]
    query, keys_in, values_in, up, grad_one, wq, wk, wv, move, small_a, small_b, outs_a, outs_b, grads_b = refs[17:31]
    oq, oo, oi, ol, osmall, out_item, grad_item = refs[31:38]
    (acc, first, second, third, fourth, slots, wide_x, wide_s, held, grad_query, key_rows, value_rows,
     source, result, total_rows, small_v, small_in, small_recv, context_b, middle_b, hidden_b,
     send, recv, extra, sent) = refs[38:]
    second_rows = second_in[:5] + (context_b, middle_b) + second_in[7:9] + (hidden_b,)
    first_rows = (rows_a, grad_query, key_rows, value_rows, out_a, context_a, middle_a, before_a, branch_a, hidden_a)
    core, bits, peers = here()
    width = osmall.shape[1]
    live = grad_query.shape[0]
    bufs = (first, second, third, fourth)
    lefts = (0, 0, 0, 4, 6, 8)
    rights = (1, 2, 3, 5, 7, 9)
    turned = set()
    mine = pl.ds(pl.multiple_of(core * width, width), width)
    other = pl.ds(pl.multiple_of((1 - core) * width, width), width)
    stage_in = [
        pltpu.make_async_copy(keys_in, key_rows, extra.at[0]),
        pltpu.make_async_copy(values_in, value_rows, extra.at[1]),
    ]
    live_in = [
        pltpu.make_async_copy(second_in[n].at[pl.ds(0, live)], second_rows[n], extra.at[4 + k])
        for k, n in enumerate((9, 6, 5))
    ]
    for copy in live_in + stage_in:
        copy.start()
    greet(peers)
    for copy in live_in:
        copy.wait()

    def bring(src, dst, sem):
        copy = pltpu.make_async_copy(src, dst, extra.at[sem])
        copy.start()
        return copy

    def remote(src, dst, slot, peer):
        return pltpu.make_async_remote_copy(
            src_ref=src, dst_ref=dst, send_sem=send.at[slot], recv_sem=recv.at[slot],
            device_id=peer, device_id_type=MESH)

    def turn(array):
        left = lefts[array]
        if left in turned:
            return
        turned.add(left)
        for n, rows in enumerate((first_rows, second_rows)):
            if left == 0:
                bring(rows[0], source, 2).wait()
                wide_x[n] = source[...].T
            else:
                wide_s[left // 2 - 2, n] = rows[left][...].T

    def multiply(array, offset, size):
        total = None
        for n, rows in enumerate((first_rows, second_rows)):
            right = rows[rights[array]][:, pl.ds(offset, size)]
            if array in (1, 2):
                left = wide_x[n]
            elif array == 0:
                left = wide_x[n, :, :live]
            else:
                left = wide_s[lefts[array] // 2 - 2, n]
            term = jnp.dot(left, right, preferred_element_type=jnp.float32)
            total = term if total is None else total + term
        return total

    tile = width // 2

    def produce(p, slot):
        array, part = SCATTER_PIECES[p]
        turn(array)
        blocks = 4 if array > 3 else 1
        base = ((1 - core) * blocks + part) * width

        def body(n, carry):
            offset = pl.multiple_of(base + n * tile, tile)
            got = multiply(array, offset, tile).astype(jnp.bfloat16)
            slots[slot, :, :, :, :, :, pl.ds(pl.multiple_of(n * tile, tile), tile)] = got.reshape(
                slots.shape[1:6] + (tile,)
            )
            return carry

        lax.fori_loop(0, 2, body, 0)

    def combine(p):
        array, part = SCATTER_PIECES[p]
        blocks = 4 if array > 3 else 1
        base = (core * blocks + part) * width

        def body(n, carry):
            offset = pl.multiple_of(base + n * tile, tile)
            cols = pl.ds(pl.multiple_of(n * tile, tile), tile)
            got = multiply(array, offset, tile).reshape(slots.shape[1:6] + (tile,))
            acc[p, :, :, :, :, :, cols] = (
                got + acc[p, :, :, :, :, :, cols].astype(jnp.float32)
            ).astype(jnp.bfloat16)
            return carry

        lax.fori_loop(0, 2, body, 0)

    def stage(p, s):
        if s == 0:
            return remote(slots.at[p % SLOTS], acc.at[p], p * 5, peers[4])
        order = SCATTER_HOPS[p]
        src = acc.at[(p,) + block_index(bits, order[s:], flip=order[s - 1])]
        return remote(src, bufs[s - 1].at[p], p * 5 + s, peers[order[s - 1]])

    def fold(p, s):
        array, part = SCATTER_PIECES[p]
        order = SCATTER_HOPS[p]
        free = [b for b in (3, 2, 1, 0) if b in order[s:]]
        for n in range(1 << len(free)):
            at = {b: (n >> i) % 2 for i, b in enumerate(reversed(free))}
            where = tuple(at.get(b, bits[b]) for b in (3, 2, 1, 0))
            got = bufs[s - 1][(p,) + tuple(at[b] for b in free)]
            if s < 4:
                acc[(p,) + where] = acc[(p,) + where] + got
            else:
                total = acc[(p,) + where].astype(jnp.float32) + got.astype(jnp.float32)
                if array < 3:
                    oq[array] = total
                elif array == 4:
                    oi[:, pl.ds(part * width, width)] = total
                elif array == 3:
                    oo[...] = total
                else:
                    ol[:, pl.ds(part * width, width)] = total

    small_started = {}

    def small_stage(s):
        peer = peers[4] if s == 0 else peers[s - 1]
        src = small_v.at[:, other] if s == 0 else small_in.at[s]
        return remote(src, small_recv.at[s], 60 + s, peer)

    def small_step(n):
        if n == 0:
            small_in[0] = small_v[:, mine]
        else:
            small_started[n - 1].wait_recv()
            total = small_in[n - 1] + small_recv[n - 1]
            if n < 5:
                small_in[n] = total
            else:
                osmall[...] = total
        if n < 5:
            small_started[n] = small_stage(n)
            small_started[n].start()

    swaps, places = [], []

    def unpermute(n, values, target, segment):
        if n > 1:
            swaps[n - 2].wait_send()
            places[n - 2].wait()
        result[n % 2] = dot_tn(move[segment], values).astype(jnp.bfloat16)
        places.append(
            pltpu.make_async_copy(result.at[n % 2, :, mine], target.at[core, segment], sent.at[n])
        )
        swaps.append(remote(result.at[n % 2, :, other], target.at[core, segment], 65 + n, peers[4]))
        places[n].start()
        swaps[n].start()

    weights = (wk, wv, wq)
    fetched = {}

    def compute(task):
        if task < 4:
            if task == 0:
                for copy in stage_in:
                    copy.wait()
                fetched[0] = bring(weights[0], held, 3)

            def pair(n, carry):
                cols = pl.ds(pl.multiple_of((2 * task + n) * 2 * DH, 2 * DH), 2 * DH)
                grad_query[:, cols], key_rows[:, cols], value_rows[:, cols] = attend_back_pair(
                    query[:, cols], key_rows[:, cols], value_rows[:, cols], up[:, cols], valid
                )
                return carry

            lax.fori_loop(0, 2, pair, 0)
        elif task < 7:
            n = task - 4
            fetched[n].wait()
            if n == 0:
                total_rows[...] = dot_nt(key_rows[...], held[...])
            elif n == 1:
                total_rows[...] = total_rows[...] + dot_nt(value_rows[...], held[...])
            else:
                total_rows[:live] = total_rows[:live] + grad_one[...] + dot_nt(grad_query[...], held[...])
                row = lax.broadcasted_iota(jnp.int32, (16, 2 * width), 0)
                small_v[:16] = jnp.where(row < mem_rows, total_rows[:16], 0.0)
                query_sum = jnp.sum(grad_query[...].astype(jnp.float32), axis=0, keepdims=True)
                value_sum = jnp.sum(value_rows[...].astype(jnp.float32), axis=0, keepdims=True)
                small_v[16:24] = small_a[...] + small_b[...] + jnp.where(
                    row[:8] == 0, query_sum, jnp.where(row[:8] == 1, value_sum, 0.0)
                )
                inner = [
                    jnp.sum(before[...].astype(jnp.float32), axis=0, keepdims=True)
                    for before in (before_a, second_rows[7])
                ]
                inner = inner[0] + inner[1]
                blocks = inner.shape[1] // (2 * width)
                small_v[24:] = jnp.concatenate(
                    [
                        jnp.concatenate(
                            [inner[:, (h * blocks + n) * width : (h * blocks + n + 1) * width] for h in range(2)],
                            axis=1,
                        )
                        for n in range(blocks)
                    ]
                    + [jnp.zeros((small_v.shape[0] - 24 - blocks, 2 * width), jnp.float32)],
                    axis=0,
                )
            if n < 2:
                fetched[n + 1] = bring(weights[n + 1], held, 3)
        elif task == 7:
            unpermute(0, total_rows[...].astype(jnp.bfloat16), grad_item, 0)
        else:
            values, target, segment = (
                (outs_a, out_item, 0),
                (outs_b, out_item, 1),
                (grads_b, grad_item, 1),
            )[task - 8]
            bring(values, source, 2).wait()
            unpermute(task - 7, source[...], target, segment)

    started = {}
    ready = None
    for step in SCATTER_STEPS:
        if step >= 100:
            compute(step - 100)
            if step == 106:
                ready = 0
            continue
        p, s = step // 8, step % 8
        if s == 0:
            if p >= SLOTS:
                started[p - SLOTS, 0].wait_send()
            produce(p, p % SLOTS)
        else:
            started[p, s - 1].wait_recv()
            if s == 1:
                combine(p)
            else:
                fold(p, s - 1)
        if s < 5:
            started[p, s] = stage(p, s)
            started[p, s].start()
        if ready is not None:
            ready += 1
            if ready % 3 == 0 and ready <= 18:
                small_step(ready // 3 - 1)
    for (p, s), copy in started.items():
        if s > 0 or p >= len(SCATTER_PIECES) - SLOTS:
            copy.wait_send()
    for s in range(5):
        small_started[s].wait_send()
    for n in range(4):
        if n > 1:
            swaps[n].wait_send()
            places[n].wait()
        swaps[n].wait_recv()


def scatter_all(mem_rows, valid, first_rows, second_rows, tail, smalls, outs, grads):
    width = smalls[0].shape[1] // 2
    small_rows = 32
    rows = 2 * width // 16
    low, full = jnp.bfloat16, jnp.float32
    count = len(SCATTER_PIECES)
    long, live = second_rows[0].shape[0], second_rows[1].shape[0]
    move = tail[-1]
    tokens = move.shape[2]
    item = (2, 2, tokens, width)
    return pl.pallas_call(
        functools.partial(scatter_kernel, mem_rows, valid),
        out_shape=[
            jax.ShapeDtypeStruct((3, rows, width), full),
            jax.ShapeDtypeStruct((rows, width), full),
            jax.ShapeDtypeStruct((rows, 4 * width), full),
            jax.ShapeDtypeStruct((rows, 4 * width), full),
            jax.ShapeDtypeStruct((small_rows, width), full),
            jax.ShapeDtypeStruct(item, low),
            jax.ShapeDtypeStruct(item, low),
        ],
        in_specs=[HBM] + [VMEM] * 6 + [HBM] + [VMEM] * 4 + [HBM] * 2 + [VMEM] * 2 + [HBM]
        + [VMEM, HBM, HBM, VMEM, VMEM, HBM, HBM, HBM, VMEM, VMEM, VMEM, HBM, HBM, HBM],
        out_specs=[VMEM] * 5 + [HBM] * 2,
        scratch_shapes=[
            pltpu.VMEM((count, 2, 2, 2, 2, rows, width), low),
            pltpu.VMEM((count, 2, 2, 2, rows, width), low),
            pltpu.VMEM((count, 2, 2, rows, width), low),
            pltpu.VMEM((count, 2, rows, width), low),
            pltpu.VMEM((count, rows, width), low),
            pltpu.VMEM((SLOTS, 2, 2, 2, 2, rows, width), low),
            pltpu.VMEM((2, 2 * width, long), low),
            pltpu.VMEM((3, 2, 2 * width, live), low),
            pltpu.VMEM((2 * width, 2 * width), low),
            pltpu.VMEM((live, 2 * width), low),
            pltpu.VMEM((long, 2 * width), low),
            pltpu.VMEM((long, 2 * width), low),
            pltpu.VMEM((long, 2 * width), low),
            pltpu.VMEM((2, tokens, 2 * width), low),
            pltpu.VMEM((long, 2 * width), full),
            pltpu.VMEM((small_rows, 2 * width), full),
            pltpu.VMEM((5, small_rows, width), full),
            pltpu.VMEM((5, small_rows, width), full),
            pltpu.VMEM((live, 2 * width), low),
            pltpu.VMEM((live, 2 * width), low),
            pltpu.VMEM((live, first_rows[6].shape[1]), low),
            pltpu.SemaphoreType.DMA((69,)),
            pltpu.SemaphoreType.DMA((69,)),
            pltpu.SemaphoreType.DMA((7,)),
            pltpu.SemaphoreType.DMA((4,)),
        ],
        compiler_params=pltpu.CompilerParams(collective_id=1, has_side_effects=True, vmem_limit_bytes=67_000_000),
        name="scatter_all",
    )(*first_rows, *second_rows, *tail[:-1], move, *smalls, *outs, *grads)


def item_shards(
    tokens,
    memory,
    w_qkv,
    b_qv,
    w_out,
    out_biases,
    norm_gains,
    norm_shifts,
    w_in,
    b_in,
    w_down,
    cotangent,
    mlm_mask,
):
    core = lax.axis_index("tensor")
    segments, count = tokens.shape[1], tokens.shape[2]
    mem_rows = memory.shape[0]
    valid = mem_rows + count
    half = memory.shape[1]

    mask = lax.dynamic_index_in_dim(mlm_mask, core, 0, keepdims=False)
    lower_tri = (
        lax.broadcasted_iota(jnp.int32, (count, count), 0)
        <= lax.broadcasted_iota(jnp.int32, (count, count), 1)
    ).astype(jnp.bfloat16)
    ones = mask.astype(jnp.bfloat16)
    upto = dot_nn(ones, lower_tri).astype(jnp.int32)
    total = upto[:, -1:]
    index = lax.broadcasted_iota(jnp.int32, mask.shape, 1)
    place = mem_rows + jnp.where(mask > 0, upto - 1, total + index - upto)
    move = (
        lax.broadcasted_iota(jnp.int32, (segments, ROWS, count), 1) == place[:, None, :]
    ).astype(jnp.bfloat16)
    live_move = move[:, :LIVE] * ones[:, None, :]

    packed = jnp.concatenate(
        [
            jnp.pad(memory, ((0, PACK_BIASES - mem_rows), (0, 0))),
            b_qv,
            out_biases,
            norm_gains,
            norm_shifts,
            b_in.reshape(-1, half),
        ],
        axis=0,
    )
    packed = jnp.pad(packed, ((0, -packed.shape[0] % 16), (0, 0)))
    both, (wq, wk, wv, outer, inner, lower), first = gather_all(
        mem_rows,
        valid,
        tokens,
        cotangent,
        packed,
        w_qkv.transpose(1, 0, 2),
        w_out.T,
        w_in,
        w_down.T,
        move,
        live_move,
    )
    (
        stacked,
        stacked_next,
        ups,
        query,
        key_rows,
        value_rows,
        query_live,
        context,
        normed_one,
        rstd_one,
        middle_low,
        before,
        hidden,
        normed_two,
        rstd_two,
        low_out,
    ) = first
    wide = jnp.concatenate([both[0], both[1]], axis=1).astype(jnp.float32)
    qv_bias, out_bias, gains, shifts = (
        wide[n : n + 2] for n in (PACK_BIASES, PACK_OUT, PACK_GAINS, PACK_SHIFTS)
    )
    inner_rows = b_in.shape[0] // half
    inner_bias = both[:, PACK_INNER : PACK_INNER + inner_rows].reshape(-1).astype(jnp.float32)
    stored = [
        (
            stacked,
            query,
            key_rows,
            value_rows,
            context,
            normed_one,
            rstd_one,
            middle_low,
            before,
            hidden,
            normed_two,
            rstd_two,
        )
    ]
    outs = [low_out]
    stacked = stacked_next
    query = (dot_nn(stacked, wq) + qv_bias[0]).astype(jnp.bfloat16)
    key_rows = dot_nn(stacked, wk).astype(jnp.bfloat16)
    value_rows = (dot_nn(stacked, wv) + qv_bias[1]).astype(jnp.bfloat16)
    context = attend(query, key_rows, value_rows, valid)
    attended = dot_nt(context, outer)
    middle, normed_one, rstd_one = norm_rows(
        stacked.astype(jnp.float32) + attended + out_bias[0], gains[0], shifts[0]
    )
    middle_low = middle.astype(jnp.bfloat16)
    before = dot_nn(middle_low, inner) + inner_bias
    hidden = gelu_value(before).astype(jnp.bfloat16)
    branch = dot_nt(hidden, lower)
    layer_out, normed_two, rstd_two = norm_rows(
        middle + branch + out_bias[1], gains[1], shifts[1]
    )
    low_out = layer_out.astype(jnp.bfloat16)
    outs.append(low_out)
    stored.append(
        (
            stacked,
            query,
            key_rows,
            value_rows,
            context,
            normed_one[:LIVE],
            rstd_one[:LIVE],
            middle_low,
            before[:LIVE].astype(jnp.bfloat16).astype(jnp.float32),
            hidden,
            normed_two[:LIVE],
            rstd_two[:LIVE],
        )
    )

    returning = jnp.zeros((mem_rows, D), jnp.float32)
    token_grads = []
    pieces = [None] * segments
    smalls = []
    for seg in reversed(range(segments)):
        (
            stacked,
            query,
            key_rows,
            value_rows,
            context,
            normed_one,
            rstd_one,
            middle_low,
            before,
            hidden,
            normed_two,
            rstd_two,
        ) = stored[seg]
        upstream = ups[seg].astype(jnp.float32)
        upstream = upstream + jnp.pad(returning, ((0, LIVE - mem_rows), (0, 0)))
        grad_two, gain_two, shift_two = norm_rows_back(upstream, normed_two, rstd_two, gains[1])
        grad_branch = grad_two.astype(jnp.bfloat16)
        grad_hidden = dot_nn(grad_branch, lower)
        grad_before = (grad_hidden * gelu_slope(before)).astype(jnp.bfloat16)
        grad_middle = grad_two + dot_nt(grad_before, inner)
        grad_one, gain_one, shift_one = norm_rows_back(
            grad_middle, normed_one, rstd_one, gains[0]
        )
        grad_attended = grad_one.astype(jnp.bfloat16)
        grad_context = dot_nn(grad_attended, outer).astype(jnp.bfloat16)
        sums = [jnp.zeros((D,), jnp.float32)] * 2
        if seg > 0:
            grad_query, grad_key, grad_value = attend_back(
                query, key_rows, value_rows, grad_context, valid
            )
            grad_stacked = dot_nt(grad_key, wk) + dot_nt(grad_value, wv)
            live_part = grad_one + dot_nt(grad_query, wq)
            grad_stacked = grad_stacked + jnp.pad(live_part, ((0, ROWS - LIVE), (0, 0)))
            returning = grad_stacked[:mem_rows]
            token_grads.append(grad_stacked.astype(jnp.bfloat16))
            attention_grads = [grad_query, grad_key, grad_value]
            sums = [jnp.sum(grad.astype(jnp.float32), axis=0) for grad in (grad_query, grad_value)]
        else:
            attention_grads = []
            tail = [query_live, key_rows, value_rows, grad_context, grad_one, wq, wk, wv, move]
        pieces[seg] = (
            stacked,
            *attention_grads,
            grad_attended,
            context,
            middle_low,
            grad_before,
            grad_branch,
            hidden,
        )
        smalls.append(
            jnp.stack(
                [
                    *sums,
                    jnp.sum(grad_one, axis=0),
                    jnp.sum(grad_two, axis=0),
                    gain_one,
                    gain_two,
                    shift_one,
                    shift_two,
                ]
            )
        )

    grad_proj, grad_outer, grad_inner, grad_lower, mine, outputs, input_grad = scatter_all(
        mem_rows, valid, pieces[0], pieces[1], tail, smalls, outs, token_grads
    )
    return (
        outputs,
        input_grad.astype(jnp.float32),
        mine[:mem_rows],
        grad_proj.transpose(1, 0, 2),
        mine[16:18],
        grad_outer.T,
        mine[18:20],
        mine[20:22],
        mine[22:24],
        grad_inner,
        mine[24 : 24 + inner_rows].reshape(-1),
        grad_lower.T,
    )


def solution(mesh):
    def body(*arrays):
        if mesh.shape["dp"] == 16 and mesh.shape["tensor"] == arrays[0].shape[0] == arrays[0].shape[1] == 2:
            return item_shards(*arrays)
        return shards(*arrays)

    placed = (
        P("dp", None, None, "tensor"),
        P(None, "tensor"),
        P("dp", None, "tensor"),
        P(None, "tensor"),
        P("tensor", "dp"),
        P(None, "tensor"),
        P(None, "tensor"),
        P(None, "tensor"),
        P("dp", "tensor"),
        P("tensor"),
        P("tensor", "dp"),
        P("dp", None, None, "tensor"),
        P("dp", None, None),
    )
    return jax.shard_map(
        body,
        mesh=mesh,
        in_specs=placed,
        out_specs=(
            P("dp", None, None, "tensor"),
            P("dp", None, None, "tensor"),
            P(None, "tensor"),
            P("dp", None, "tensor"),
            P(None, "tensor"),
            P("tensor", "dp"),
            P(None, "tensor"),
            P(None, "tensor"),
            P(None, "tensor"),
            P("dp", "tensor"),
            P("tensor"),
            P("tensor", "dp"),
        ),
        check_vma=False,
    )
```

```python
import functools

import jax
import jax.numpy as jnp
from jax import lax
from jax.experimental import pallas as pl
from jax.experimental.pallas import tpu as pltpu
from jax.sharding import PartitionSpec as P

D = 1024
DH = 64
MICRO = 2


eps_norm = 1e-05
root_half = 0.7071067811865476
inv_root_two_pi = 0.3989422804014327


def gelu_value(before):
    return 0.5 * before * (1.0 + lax.erf(before * root_half))


def gelu_slope(before):
    return 0.5 * (1.0 + lax.erf(before * root_half)) + before * inv_root_two_pi * jnp.exp(
        -0.5 * before * before
    )


def fetch_weights(w_qkv, w_in, w_out, w_down):
    return (
        lax.all_gather(w_qkv, "dp", axis=0, tiled=True),
        lax.all_gather(w_in, "dp", axis=0, tiled=True),
        lax.all_gather(w_out, "dp", axis=1, tiled=True),
        lax.all_gather(w_down, "dp", axis=1, tiled=True),
    )


def reduce_weights(grad_proj, grad_inner, grad_outer, grad_lower):
    return (
        lax.psum_scatter(
            grad_proj.astype(jnp.bfloat16), "dp", scatter_dimension=0, tiled=True
        ).astype(jnp.float32),
        lax.psum_scatter(
            grad_inner.astype(jnp.bfloat16), "dp", scatter_dimension=0, tiled=True
        ).astype(jnp.float32),
        lax.psum_scatter(
            grad_outer.astype(jnp.bfloat16), "dp", scatter_dimension=1, tiled=True
        ).astype(jnp.float32),
        lax.psum_scatter(
            grad_lower.astype(jnp.bfloat16), "dp", scatter_dimension=1, tiled=True
        ).astype(jnp.float32),
    )


def gather_rows(block):
    return lax.all_gather(block, "tensor", axis=2, tiled=True)


def branch_sum(partial_value):
    return lax.psum_scatter(partial_value, "tensor", scatter_dimension=2, tiled=True)


def gather_grads(block):
    return lax.all_gather(block, "tensor", axis=2, tiled=True)


def input_sum(partial_value):
    return lax.psum_scatter(
        partial_value.astype(jnp.bfloat16), "tensor", scatter_dimension=2, tiled=True
    ).astype(jnp.float32)


def norm_forward(resid, gain, shift):
    totals = jnp.sum(resid, axis=-1)
    squares = jnp.sum(resid * resid, axis=-1)
    totals, squares = lax.psum((totals, squares), "tensor")
    center = totals / D
    spread = squares / D - center * center
    rstd = lax.rsqrt(spread + eps_norm)
    normed = (resid - center[..., None]) * rstd[..., None]
    return (normed * gain + shift, normed, rstd)


def norm_backward(upstream, normed, rstd, gain):
    scaled = upstream * gain
    first = jnp.sum(scaled, axis=-1)
    second = jnp.sum(scaled * normed, axis=-1)
    first, second = lax.psum((first, second), "tensor")
    result = rstd[..., None] * (scaled - first[..., None] / D - normed * (second[..., None] / D))
    return (result, jnp.sum(upstream * normed, axis=(0, 1)), jnp.sum(upstream, axis=(0, 1)))


def attention_scores(query, key_rows):
    return jnp.einsum(
        "bqhe,bkhe->bhqk", query, key_rows, preferred_element_type=jnp.float32
    ) * DH ** (-0.5)


def segment_forward(weights, smalls, memory_rows, token_rows):
    proj_weight, inner_weight, outer_weight, lower_weight = weights
    qv_bias, out_bias, gains, shifts, inner_bias = smalls
    batch = token_rows.shape[0]
    stacked = jnp.concatenate([memory_rows, token_rows], axis=1)
    length = stacked.shape[1]
    local = proj_weight.shape[2]
    heads = local // DH
    wide_rows = gather_rows(stacked)
    bias_three = jnp.stack([qv_bias[0], jnp.zeros_like(qv_bias[0]), qv_bias[1]])
    projected = (
        jnp.einsum("bld,dcf->blcf", wide_rows, proj_weight, preferred_element_type=jnp.float32)
        + bias_three
    ).astype(jnp.bfloat16)
    split = projected.reshape(batch, length, 3, heads, DH)
    scores = attention_scores(split[:, :, 0], split[:, :, 1])
    peak = jnp.max(scores, axis=-1, keepdims=True)
    expo = jnp.exp(scores - peak)
    totals = jnp.sum(expo, axis=-1, keepdims=True)
    probs = expo / totals
    logsum = peak[..., 0] + jnp.log(totals[..., 0])
    context = jnp.einsum(
        "bhqk,bkhe->bqhe",
        probs.astype(jnp.bfloat16),
        split[:, :, 2],
        preferred_element_type=jnp.float32,
    )
    context = context.astype(jnp.bfloat16).reshape(batch, length, local)
    attended = branch_sum(
        jnp.einsum("bld,df->blf", context, outer_weight, preferred_element_type=jnp.float32)
    )
    middle, normed_one, rstd_one = norm_forward(
        stacked.astype(jnp.float32) + attended + out_bias[0], gains[0], shifts[0]
    )
    middle_wide = gather_rows(middle.astype(jnp.bfloat16))
    before = (
        jnp.einsum("bld,df->blf", middle_wide, inner_weight, preferred_element_type=jnp.float32)
        + inner_bias
    )
    hidden = gelu_value(before).astype(jnp.bfloat16)
    branch = branch_sum(
        jnp.einsum("blf,fd->bld", hidden, lower_weight, preferred_element_type=jnp.float32)
    )
    layer_out, normed_two, rstd_two = norm_forward(
        middle + branch + out_bias[1], gains[1], shifts[1]
    )
    stored = (
        wide_rows,
        projected,
        logsum,
        context,
        normed_one,
        rstd_one,
        middle_wide,
        before,
        hidden,
        normed_two,
        rstd_two,
    )
    return (layer_out, stored)


def segment_backward(weights, smalls, upstream, stored):
    proj_weight, inner_weight, outer_weight, lower_weight = weights
    qv_bias, out_bias, gains, shifts, inner_bias = smalls
    (
        wide_rows,
        projected,
        logsum,
        context,
        normed_one,
        rstd_one,
        middle_wide,
        before,
        hidden,
        normed_two,
        rstd_two,
    ) = stored
    batch, length, local = context.shape
    heads = local // DH
    grad_two, gain_two, shift_two = norm_backward(upstream, normed_two, rstd_two, gains[1])
    grad_branch = gather_grads(grad_two.astype(jnp.bfloat16))
    grad_lower = jnp.einsum("blf,bld->fd", hidden, grad_branch, preferred_element_type=jnp.float32)
    grad_hidden = jnp.einsum(
        "bld,fd->blf", grad_branch, lower_weight, preferred_element_type=jnp.float32
    )
    grad_before = (grad_hidden * gelu_slope(before)).astype(jnp.bfloat16)
    grad_inner = jnp.einsum(
        "bld,blf->df", middle_wide, grad_before, preferred_element_type=jnp.float32
    )
    grad_inner_bias = jnp.sum(grad_before.astype(jnp.float32), axis=(0, 1))
    grad_middle = grad_two + lax.psum_scatter(
        jnp.einsum(
            "blf,df->bld", grad_before, inner_weight, preferred_element_type=jnp.float32
        ).astype(jnp.bfloat16),
        "tensor",
        scatter_dimension=2,
        tiled=True,
    ).astype(jnp.float32)
    grad_one, gain_one, shift_one = norm_backward(grad_middle, normed_one, rstd_one, gains[0])
    grad_attended = gather_grads(grad_one.astype(jnp.bfloat16))
    grad_outer = jnp.einsum(
        "bld,blf->df", context, grad_attended, preferred_element_type=jnp.float32
    )
    grad_context = jnp.einsum(
        "blf,df->bld", grad_attended, outer_weight, preferred_element_type=jnp.float32
    )
    grad_context = grad_context.astype(jnp.bfloat16)
    grad_context = grad_context.reshape(batch, length, heads, DH)
    split = projected.reshape(batch, length, 3, heads, DH)
    query, key_rows, value_rows = (split[:, :, 0], split[:, :, 1], split[:, :, 2])
    probs = jnp.exp(attention_scores(query, key_rows) - logsum[..., None])
    grad_probs = jnp.einsum(
        "bqhe,bkhe->bhqk", grad_context, value_rows, preferred_element_type=jnp.float32
    )
    weighted_sum = jnp.sum(probs * grad_probs, axis=-1, keepdims=True)
    grad_scores = (probs * (grad_probs - weighted_sum)).astype(jnp.bfloat16)
    grad_query = jnp.einsum(
        "bhqk,bkhe->bqhe", grad_scores, key_rows, preferred_element_type=jnp.float32
    ) * DH ** (-0.5)
    grad_key = jnp.einsum(
        "bhqk,bqhe->bkhe", grad_scores, query, preferred_element_type=jnp.float32
    ) * DH ** (-0.5)
    grad_value = jnp.einsum(
        "bhqk,bqhe->bkhe",
        probs.astype(jnp.bfloat16),
        grad_context,
        preferred_element_type=jnp.float32,
    )
    grad_projected = (
        jnp.stack([grad_query, grad_key, grad_value], axis=2)
        .reshape(batch, length, 3, local)
        .astype(jnp.bfloat16)
    )
    grad_proj = jnp.einsum(
        "bld,blcf->dcf", wide_rows, grad_projected, preferred_element_type=jnp.float32
    )
    column_sums = jnp.sum(grad_projected.astype(jnp.float32), axis=(0, 1))
    grad_qv = jnp.stack([column_sums[0], column_sums[2]])
    grad_stacked = grad_one + input_sum(
        jnp.einsum("blcf,dcf->bld", grad_projected, proj_weight, preferred_element_type=jnp.float32)
    )
    grad_biases = jnp.stack([jnp.sum(grad_one, axis=(0, 1)), jnp.sum(grad_two, axis=(0, 1))])
    large_grads = (grad_proj, grad_inner, grad_outer, grad_lower)
    small_grads = (
        grad_qv,
        grad_biases,
        jnp.stack([gain_one, gain_two]),
        jnp.stack([shift_one, shift_two]),
        grad_inner_bias,
    )
    return (grad_stacked, large_grads, small_grads)


def add_tuples(first, second):
    return tuple((left + right for left, right in zip(first, second)))


def shards(
    tokens,
    memory,
    w_qkv,
    b_qv,
    w_out,
    out_biases,
    norm_gains,
    norm_shifts,
    w_in,
    b_in,
    w_down,
    cotangent,
    mlm_mask,
):
    smalls = (
        b_qv.astype(jnp.float32),
        out_biases.astype(jnp.float32),
        norm_gains.astype(jnp.float32),
        norm_shifts.astype(jnp.float32),
        b_in.astype(jnp.float32),
    )
    per_batch = tokens.shape[0] // MICRO
    segments = tokens.shape[1]
    mem_rows = memory.shape[0]
    local = w_qkv.shape[2]
    inner_local = w_in.shape[1]
    empty_large = (
        jnp.zeros((D, 3, local), jnp.float32),
        jnp.zeros((D, inner_local), jnp.float32),
        jnp.zeros((local, D), jnp.float32),
        jnp.zeros((inner_local, D), jnp.float32),
    )
    full_grads = empty_large
    shard_grads = (
        jnp.zeros(w_qkv.shape, jnp.float32),
        jnp.zeros(w_in.shape, jnp.float32),
        jnp.zeros(w_out.shape, jnp.float32),
        jnp.zeros(w_down.shape, jnp.float32),
    )
    small_total = (
        jnp.zeros((2, local), jnp.float32),
        jnp.zeros((2, local), jnp.float32),
        jnp.zeros((2, local), jnp.float32),
        jnp.zeros((2, local), jnp.float32),
        jnp.zeros((inner_local,), jnp.float32),
    )
    memory_total = jnp.zeros((mem_rows, local), jnp.float32)
    out_blocks = []
    grad_blocks = []
    for batch_index in range(MICRO):
        offset = batch_index * per_batch
        batch_tokens = tokens[offset : offset + per_batch]
        batch_mask = mlm_mask[offset : offset + per_batch]
        batch_cot = cotangent[offset : offset + per_batch].astype(jnp.float32) * batch_mask[
            ..., None
        ].astype(jnp.float32)
        weights = fetch_weights(w_qkv, w_in, w_out, w_down)
        carried = memory[None]
        stored_all = []
        token_outs = []
        for seg_index in range(segments):
            layer_out, stored = segment_forward(
                weights, smalls, carried, batch_tokens[:, seg_index]
            )
            carried = layer_out[:, :mem_rows].astype(jnp.bfloat16)
            token_outs.append(layer_out[:, mem_rows:].astype(jnp.bfloat16))
            stored_all.append(stored)
        returning = jnp.zeros((per_batch, mem_rows, local), jnp.float32)
        token_grads = [None] * segments
        for seg_index in reversed(range(segments)):
            upstream = jnp.concatenate([returning, batch_cot[:, seg_index]], axis=1)
            grad_stacked, large_grads, small_grads = segment_backward(
                weights, smalls, upstream, stored_all[seg_index]
            )
            returning = grad_stacked[:, :mem_rows]
            token_grads[seg_index] = grad_stacked[:, mem_rows:]
            full_grads = add_tuples(full_grads, large_grads)
            small_total = add_tuples(small_total, small_grads)
        memory_total = memory_total + jnp.sum(returning, axis=0)
        reduced = reduce_weights(full_grads[0], full_grads[1], full_grads[2], full_grads[3])
        shard_grads = add_tuples(shard_grads, reduced)
        full_grads = empty_large
        out_blocks.append(jnp.stack(token_outs, axis=1))
        grad_blocks.append(jnp.stack(token_grads, axis=1))
    grad_qv, grad_biases, grad_gains, grad_shifts, grad_inner_bias, memory_grad = lax.psum(
        (
            small_total[0],
            small_total[1],
            small_total[2],
            small_total[3],
            small_total[4],
            memory_total,
        ),
        "dp",
    )
    outputs = jnp.concatenate(out_blocks, axis=0)
    input_grad = jnp.concatenate(grad_blocks, axis=0)
    return (
        outputs,
        input_grad,
        memory_grad,
        shard_grads[0],
        grad_qv,
        shard_grads[2],
        grad_biases,
        grad_gains,
        grad_shifts,
        shard_grads[1],
        grad_inner_bias,
        shard_grads[3],
    )


ROWS = 528
LIVE = 176


def dot_nn(left, right):
    return jnp.dot(left, right, preferred_element_type=jnp.float32)


def dot_nt(left, right):
    return lax.dot_general(
        left, right, (((1,), (1,)), ((), ())), preferred_element_type=jnp.float32
    )


def dot_tn(left, right):
    return lax.dot_general(
        left, right, (((0,), (0,)), ((), ())), preferred_element_type=jnp.float32
    )


def norm_rows(resid, gain, shift):
    center = jnp.mean(resid, axis=-1, keepdims=True)
    spread = jnp.mean(resid * resid, axis=-1, keepdims=True) - center * center
    rstd = lax.rsqrt(spread + eps_norm)
    normed = (resid - center) * rstd
    return (normed * gain + shift, normed, rstd)


def norm_rows_back(upstream, normed, rstd, gain):
    scaled = upstream * gain
    first = jnp.mean(scaled, axis=-1, keepdims=True)
    second = jnp.mean(scaled * normed, axis=-1, keepdims=True)
    result = rstd * (scaled - first - normed * second)
    return (result, jnp.sum(upstream * normed, axis=0), jnp.sum(upstream, axis=0))


MESH = pl.DeviceIdType.MESH
HBM = pl.BlockSpec(memory_space=pl.ANY)
VMEM = pl.BlockSpec(memory_space=pltpu.VMEM)
GATHER_PIECES = ((0, 0), (1, 0), (2, 0), (3, 0), (4, 0), (5, 0), (4, 1), (5, 1), (4, 2), (5, 2), (4, 3), (5, 3))
SCATTER_PIECES = ((5, 0), (5, 1), (5, 2), (5, 3), (4, 0), (4, 1), (4, 2), (4, 3), (3, 0), (0, 0), (1, 0), (2, 0))
GATHER_HOPS = (
    (3, 2, 1, 0), (3, 2, 0, 1), (3, 2, 1, 0), (3, 0, 1, 2), (3, 2, 1, 0), (3, 1, 0, 2),
    (3, 2, 0, 1), (3, 2, 1, 0), (3, 0, 1, 2), (3, 2, 0, 1), (3, 2, 1, 0), (3, 0, 1, 2),
)
SCATTER_HOPS = (
    (2, 1, 0, 3), (0, 1, 2, 3), (1, 0, 2, 3), (2, 1, 0, 3), (0, 1, 2, 3), (2, 0, 3, 1),
    (0, 1, 2, 3), (1, 2, 0, 3), (0, 2, 1, 3), (0, 1, 2, 3), (1, 0, 2, 3), (1, 0, 2, 3),
)
GATHER_STEPS = (
    0, 8, 1, 100, 16, 9, 24, 2, 17, 32, 10, 40, 3, 25, 48, 18, 11, 56, 33, 64,
    41, 19, 49, 72, 57, 80, 4, 34, 26, 88, 5, 65, 101, 12, 50, 42, 73, 13, 102, 58,
    35, 20, 81, 66, 21, 89, 103, 27, 74, 104, 51, 82, 105, 59, 106, 43, 107, 67, 28, 29,
    36, 108, 52, 90, 37, 44, 53, 75, 83, 45, 109, 91, 68, 60, 69, 61, 76, 110, 77, 92,
    84, 111, 93, 85, 112, 113,
)
SCATTER_STEPS = (
    0, 8, 16, 1, 9, 17, 24, 32, 100, 25, 33, 2, 40, 10, 48, 18, 101, 41, 3, 49,
    26, 56, 34, 64, 11, 102, 19, 57, 27, 65, 4, 42, 103, 12, 35, 72, 20, 80, 5, 73,
    50, 88, 13, 28, 36, 81, 21, 58, 89, 29, 51, 104, 37, 105, 66, 106, 59, 107, 43, 108,
    52, 82, 109, 110, 67, 74, 44, 90, 60, 53, 68, 61, 83, 69, 75, 45, 84, 91, 76, 85,
    92, 77, 93,
)
SLOTS = 2


def here():
    me = lax.axis_index("dp")
    core = lax.axis_index("tensor")
    bits = tuple((me // (1 << b)) % 2 for b in range(4))
    peers = tuple({"dp": me + (1 - 2 * bits[b]) * (1 << b)} for b in range(4))
    return core, bits, peers + ({"tensor": 1 - core},)


def greet(peers):
    barrier = pltpu.get_barrier_semaphore()
    for peer in peers:
        pl.semaphore_signal(barrier, inc=1, device_id=peer, device_id_type=MESH)
    pl.semaphore_wait(barrier, len(peers))


def block_index(bits, free, flip=None):
    index = []
    for b in (3, 2, 1, 0):
        if b == flip:
            index.append(1 - bits[b])
        elif b in free:
            index.append(slice(None))
        else:
            index.append(bits[b])
    return tuple(index)


def columns(array, part, core, width):
    blocks = 4 if array > 3 else 1
    return pl.ds(pl.multiple_of((core * blocks + part) * width, width), width)


def shard_block(shards, piece, width):
    array, part = piece
    if array < 3:
        return shards[array].at[array]
    return shards[array].at[:, pl.ds(part * width, width)]


def attend_pair(query, key_rows, value_rows, valid):
    main = key_rows.shape[0] - 16
    lane = lax.broadcasted_iota(jnp.int32, (1, 2 * DH), 1)
    left = lane < DH
    query = query * DH ** (-0.5)
    zero = jnp.zeros_like(query)
    tail_lane = lax.broadcasted_iota(jnp.int32, (1, 32), 1)
    tail_zero = jnp.zeros((16, 2 * DH), query.dtype)
    key_tail, value_tail = key_rows[main:], value_rows[main:]
    keys_both = jnp.concatenate(
        [jnp.where(left, key_tail, tail_zero), jnp.where(left, tail_zero, key_tail)], axis=0
    )
    values_both = jnp.concatenate(
        [jnp.where(left, value_tail, tail_zero), jnp.where(left, tail_zero, value_tail)], axis=0
    )
    ones_both = jnp.concatenate(
        [jnp.where(left, tail_zero, tail_zero + 1), jnp.where(left, tail_zero + 1, tail_zero)], axis=0
    )
    tail = dot_nt(query, keys_both)
    tail = jnp.where(tail_lane % 16 < valid - main, tail, -1e30)
    peaks, parts = [], []
    for head in range(2):
        picked = jnp.where(left if head == 0 else ~left, query, zero)
        scores = dot_nt(picked, key_rows[:main])
        side = (tail_lane < 16) if head == 0 else (tail_lane >= 16)
        peak = jnp.maximum(
            jnp.max(scores, axis=1, keepdims=True),
            jnp.max(jnp.where(side, tail, -1e30), axis=1, keepdims=True),
        )
        expo = jnp.exp(scores - peak).astype(jnp.bfloat16)
        one = jnp.ones_like(value_rows[:main])
        values = jnp.where(left if head == 0 else ~left, value_rows[:main], one)
        parts.append(dot_nn(expo, values))
        peaks.append(peak)
    tail = jnp.exp(tail - jnp.where(tail_lane < 16, peaks[0], peaks[1])).astype(jnp.bfloat16)
    both = dot_nn(tail, jnp.concatenate([values_both, ones_both], axis=1))
    value_sum = jnp.where(left, parts[0], parts[1]) + both[:, : 2 * DH]
    total = jnp.where(left, parts[1], parts[0]) + both[:, 2 * DH :]
    return (value_sum / pltpu.roll(total, DH, 1)).astype(jnp.bfloat16)


def attend_kernel(valid, q_ref, k_ref, v_ref, out_ref):
    out_ref[...] = attend_pair(q_ref[...], k_ref[...], v_ref[...], valid)


def attend(query, key_rows, value_rows, valid):
    block = pl.BlockSpec((query.shape[0], 2 * DH), lambda i: (0, i))
    return pl.pallas_call(
        functools.partial(attend_kernel, valid),
        grid=(D // (2 * DH),),
        out_shape=jax.ShapeDtypeStruct(query.shape, jnp.bfloat16),
        in_specs=[block] * 3,
        out_specs=block,
        compiler_params=pltpu.CompilerParams(vmem_limit_bytes=12 << 20),
        name="attend",
    )(query, key_rows, value_rows)


def attend_back_pair(query, key_rows, value_rows, grads, valid):
    live = query.shape[0]
    left = lax.broadcasted_iota(jnp.int32, (1, 2 * DH), 1) < DH
    zero = jnp.zeros_like(query)
    query = query * DH ** (-0.5)
    picked = jnp.concatenate([jnp.where(left, query, zero), jnp.where(left, zero, query)], axis=0)
    up = jnp.concatenate([jnp.where(left, grads, zero), jnp.where(left, zero, grads)], axis=0)
    scores = dot_nt(key_rows, picked)
    scores = jnp.where(lax.broadcasted_iota(jnp.int32, scores.shape, 0) < valid, scores, -1e30)
    expo = jnp.exp(scores - jnp.max(scores, axis=0, keepdims=True))
    probs = expo * (1.0 / jnp.sum(expo, axis=0, keepdims=True))
    grad_probs = dot_nt(value_rows, up)
    weighted = jnp.sum(probs * grad_probs, axis=0, keepdims=True)
    grad_scores = (probs * (grad_probs - weighted)).astype(jnp.bfloat16)
    grad_query = dot_tn(grad_scores, key_rows)
    grad_query = jnp.where(left, grad_query[:live], grad_query[live:]) * DH ** (-0.5)
    grad_key = dot_nn(grad_scores, picked)
    grad_value = dot_nn(probs.astype(jnp.bfloat16), up)
    return tuple(grad.astype(jnp.bfloat16) for grad in (grad_query, grad_key, grad_value))


def attend_back_kernel(valid, q_ref, k_ref, v_ref, g_ref, dq_ref, dk_ref, dv_ref):
    dq_ref[...], dk_ref[...], dv_ref[...] = attend_back_pair(
        q_ref[...], k_ref[...], v_ref[...], g_ref[...], valid
    )


def attend_back(query, key_rows, value_rows, grad_context, valid):
    live = grad_context.shape[0]
    short = pl.BlockSpec((live, 2 * DH), lambda i: (0, i))
    tall = pl.BlockSpec((key_rows.shape[0], 2 * DH), lambda i: (0, i))
    low = jnp.bfloat16
    return pl.pallas_call(
        functools.partial(attend_back_kernel, valid),
        grid=(D // (2 * DH),),
        out_shape=[jax.ShapeDtypeStruct((live, D), low)] + [jax.ShapeDtypeStruct(key_rows.shape, low)] * 2,
        in_specs=[short, tall, tall, short],
        out_specs=[short, tall, tall],
        compiler_params=pltpu.CompilerParams(vmem_limit_bytes=12 << 20),
        name="attend_back",
    )(query, key_rows, value_rows, grad_context)


PACK_BIASES, PACK_OUT, PACK_GAINS, PACK_SHIFTS, PACK_INNER = 16, 18, 20, 22, 24


def gather_kernel(
    mem_rows, valid, toks, cots, pack, sq, so, si, sl, move, live_move,
    packs, fq, fk, fv, fo, fi, fl, stacked_a, stacked_b, ups, query, key_rows, value_rows,
    query_live, context_live, normed_one, rstd_one, middle_live, before_live, hidden_live, normed_two, rstd_two, low_out,
    x_v, c_v, vq, vo, vi, vl, held, context, middle, middle_low, branch,
    send, recv, local, loads, extra,
):
    core, bits, peers = here()
    width = pack.shape[1]
    live = ups.shape[1]
    shards = (vq, vq, vq, vo, vi, vl)
    fulls = (fq, fk, fv, fo, fi, fl)
    mine = pl.ds(pl.multiple_of(core * width, width), width)
    shard_in = [
        pltpu.make_async_copy(src, dst, extra.at[n])
        for n, (src, dst) in enumerate(((sq, vq), (so, vo), (si, vi), (sl, vl)))
    ]
    rows_own = [
        pltpu.make_async_copy(toks.at[core], x_v.at[:, :, mine], extra.at[4]),
        pltpu.make_async_copy(cots.at[core], c_v.at[:, :, mine], extra.at[5]),
        pltpu.make_async_copy(pack, packs.at[core], extra.at[6]),
    ]
    for copy in shard_in + rows_own:
        copy.start()
    own = []
    for p, (array, part) in enumerate(GATHER_PIECES):
        own.append(pltpu.make_async_copy(
            shard_block(shards, (array, part), width),
            fulls[array].at[block_index(bits, ()) + (slice(None), columns(array, part, core, width))],
            local.at[p],
        ))
    greet(peers)
    for copy in shard_in:
        copy.wait()
    for copy in own:
        copy.start()

    def remote(src, dst, slot, peer):
        return pltpu.make_async_remote_copy(
            src_ref=src, dst_ref=dst, send_sem=send.at[slot], recv_sem=recv.at[slot],
            device_id=peer, device_id_type=MESH)

    def stage(p, s):
        array, part = GATHER_PIECES[p]
        order = GATHER_HOPS[p]
        cols = columns(array, part, core, width)
        dst = fulls[array].at[block_index(bits, order[:s]) + (slice(None), cols)]
        if s == 0:
            src = shard_block(shards, (array, part), width)
        else:
            src = dst
        peer = peers[order[s]] if s < 4 else peers[4]
        return remote(src, dst, p * 5 + s, peer)

    swaps = [
        remote(toks.at[1 - core], x_v.at[:, :, mine], 60, peers[4]),
        remote(cots.at[1 - core], c_v.at[:, :, mine], 61, peers[4]),
        remote(pack, packs.at[core], 62, peers[4]),
    ]
    started, loading = {}, {}

    def load(p):
        array, part = GATHER_PIECES[p]
        blocks = 4 if array > 3 else 1
        every = (slice(None),) * 5
        loading[p] = [
            pltpu.make_async_copy(
                fulls[array].at[every + (pl.ds((half * blocks + part) * width, width),)],
                held.at[(p % 6,) + every + (pl.ds(half * width, width),)],
                loads.at[2 * p + half],
            )
            for half in range(2)
        ]
        for copy in loading[p]:
            copy.start()

    def loaded(p):
        for copy in loading.pop(p):
            copy.wait()

    def weight(p, cols):
        block = held[p % 6, :, :, :, :, :, cols]
        return block.reshape(2 * width, block.shape[-1])

    def wide(row):
        return jnp.concatenate([packs[0, row : row + 1], packs[1, row : row + 1]], axis=1).astype(jnp.float32)

    def norm(resid, gain, shift):
        center = jnp.mean(resid, axis=1, keepdims=True)
        spread = jnp.mean(resid * resid, axis=1, keepdims=True) - center * center
        rstd = lax.rsqrt(spread + eps_norm)
        normed = (resid - center) * rstd
        return normed * gain + shift, normed, rstd

    def compute(task):
        if task == 0:
            for copy in rows_own:
                copy.wait()
            for swap in swaps:
                swap.wait_recv()
            memory = jnp.concatenate([packs[0, :16], packs[1, :16]], axis=1)
            is_memory = lax.broadcasted_iota(jnp.int32, memory.shape, 0) < mem_rows
            stacked_a[...] = dot_nn(move[0], x_v[0]).astype(jnp.bfloat16)
            stacked_a[:16] = jnp.where(is_memory, memory, stacked_a[:16])
            stacked_b[...] = dot_nn(move[1], x_v[1]).astype(jnp.bfloat16)
            for n in range(2):
                ups[n] = dot_nn(live_move[n], c_v[n]).astype(jnp.bfloat16)
        elif task < 4:
            n = task - 1
            loaded(n)
            target = (query, key_rows, value_rows)[n]
            for half in range(2):
                cols = pl.ds(half * width, width)
                got = dot_nn(stacked_a[...], weight(n, cols))
                if n != 1:
                    row = PACK_BIASES + n // 2
                    got = got + packs[half, row : row + 1].astype(jnp.float32)
                target[:, cols] = got.astype(jnp.bfloat16)
                if n == 0:
                    query_live[:, cols] = got[:live].astype(jnp.bfloat16)
        elif task < 8:

            def pair(n, carry):
                cols = pl.ds(pl.multiple_of((2 * (task - 4) + n) * 2 * DH, 2 * DH), 2 * DH)
                context[:, cols] = attend_pair(query[:, cols], key_rows[:, cols], value_rows[:, cols], valid)
                return carry

            lax.fori_loop(0, 2, pair, 0)
        elif task == 8:
            loaded(3)
            attended = dot_nt(context[...], weight(3, slice(None)))
            resid = stacked_a[...].astype(jnp.float32) + attended + wide(PACK_OUT)
            value, normed, rstd = norm(resid, wide(PACK_GAINS), wide(PACK_SHIFTS))
            middle[...] = value
            middle_low[...] = value.astype(jnp.bfloat16)
            middle_live[...] = value[:live].astype(jnp.bfloat16)
            context_live[...] = context[:live]
            normed_one[...] = normed[:live]
            rstd_one[...] = jnp.broadcast_to(rstd[:live], rstd_one.shape)
        elif task < 13:
            j = task - 9
            loaded(4 + 2 * j)
            loaded(5 + 2 * j)

            def hidden_block(half, carry):
                cols = pl.ds(pl.multiple_of(half * width, width), width)
                place = pl.ds(pl.multiple_of((half * 4 + j) * width, width), width)
                bias = packs[half, PACK_INNER + j : PACK_INNER + j + 1].astype(jnp.float32)
                before = dot_nn(middle_low[...], weight(4 + 2 * j, cols)) + bias
                before_live[:, place] = before[:live]
                hidden = gelu_value(before).astype(jnp.bfloat16)
                hidden_live[:, place] = hidden[:live]
                branch[...] = branch[...] + dot_nt(hidden, weight(5 + 2 * j, cols))
                return carry

            if j == 0:
                branch[...] = middle[...] + wide(PACK_OUT + 1)
            lax.fori_loop(0, 2, hidden_block, 0)
        else:
            value, normed, rstd = norm(branch[...], wide(PACK_GAINS + 1), wide(PACK_SHIFTS + 1))
            low_out[...] = value.astype(jnp.bfloat16)
            is_memory = lax.broadcasted_iota(jnp.int32, (16, 2 * width), 0) < mem_rows
            stacked_b[:16] = jnp.where(is_memory, low_out[:16], stacked_b[:16])
            normed_two[...] = normed[:live]
            rstd_two[...] = jnp.broadcast_to(rstd[:live], rstd_two.shape)

    for tick, step in enumerate(GATHER_STEPS):
        if step >= 100:
            compute(step - 100)
            continue
        p, s = step // 8, step % 8
        if s > 0:
            started[p, s - 1].wait_recv()
        if s == 1:
            own[p].wait()
        if s == 5:
            load(p)
        else:
            started[p, s] = stage(p, s)
            started[p, s].start()
        if tick == 2:
            for swap in swaps:
                swap.start()
    for copy in started.values():
        copy.wait_send()
    for swap in swaps:
        swap.wait_send()


def gather_all(mem_rows, valid, toks, cots, pack, sq, so, si, sl, move, live_move):
    width = pack.shape[1]
    rows = sq.shape[1]
    low, full = jnp.bfloat16, jnp.float32
    total, live = move.shape[1], live_move.shape[1]
    hidden = 2 * si.shape[1]
    out = [((2,) + pack.shape, low)]
    for size in (2 * width, 2 * width, 2 * width, 2 * width, hidden, hidden):
        out.append(((2, 2, 2, 2, rows, size), low))
    out += [((total, 2 * width), low)] * 2 + [((2, live, 2 * width), low)]
    out += [((total, 2 * width), low)] * 3 + [((live, 2 * width), low)] * 2
    out += [((live, 2 * width), full), ((live, 2 * width), full), ((live, 2 * width), low)]
    out += [((live, hidden), full), ((live, hidden), low)]
    out += [((live, 2 * width), full), ((live, 2 * width), full), ((total, 2 * width), low)]
    block = (2, 2, 2, 2, rows, 2 * width)
    got = pl.pallas_call(
        functools.partial(gather_kernel, mem_rows, valid),
        out_shape=[jax.ShapeDtypeStruct(*one) for one in out],
        in_specs=[HBM, HBM, VMEM] + [HBM] * 4 + [VMEM] * 2,
        out_specs=[VMEM] + [HBM] * 6 + [VMEM] * (len(out) - 7),
        scratch_shapes=[
            pltpu.VMEM(toks.shape[1:3] + (2 * width,), low),
            pltpu.VMEM(toks.shape[1:3] + (2 * width,), low),
            pltpu.VMEM(sq.shape, low),
            pltpu.VMEM(so.shape, low),
            pltpu.VMEM(si.shape, low),
            pltpu.VMEM(sl.shape, low),
            pltpu.VMEM((6,) + block, low),
            pltpu.VMEM((total, 2 * width), low),
            pltpu.VMEM((total, 2 * width), full),
            pltpu.VMEM((total, 2 * width), low),
            pltpu.VMEM((total, 2 * width), full),
            pltpu.SemaphoreType.DMA((63,)),
            pltpu.SemaphoreType.DMA((63,)),
            pltpu.SemaphoreType.DMA((12,)),
            pltpu.SemaphoreType.DMA((24,)),
            pltpu.SemaphoreType.DMA((7,)),
        ],
        compiler_params=pltpu.CompilerParams(collective_id=0, has_side_effects=True, vmem_limit_bytes=62 << 20),
        name="gather_all",
    )(toks, cots, pack, sq, so, si, sl, move, live_move)
    wide = [array.reshape(16 * rows, array.shape[-1]) for array in got[1:7]]
    return got[0], wide, got[7:]


def scatter_kernel(mem_rows, valid, *refs):
    (rows_a, out_a, context_a, middle_a, before_a, branch_a, hidden_a) = refs[0:7]
    second_in = refs[7:17]
    query, keys_in, values_in, up, grad_one, wq, wk, wv, move, small_a, small_b, outs_a, outs_b, grads_b = refs[17:31]
    oq, oo, oi, ol, osmall, out_item, grad_item = refs[31:38]
    (acc, first, second, third, fourth, slots, wide_x, wide_s, held, grad_query, key_rows, value_rows,
     source, result, total_rows, small_v, small_in, small_recv, context_b, middle_b, hidden_b,
     send, recv, extra, sent) = refs[38:]
    second_rows = second_in[:5] + (context_b, middle_b) + second_in[7:9] + (hidden_b,)
    first_rows = (rows_a, grad_query, key_rows, value_rows, out_a, context_a, middle_a, before_a, branch_a, hidden_a)
    core, bits, peers = here()
    width = osmall.shape[1]
    live = grad_query.shape[0]
    bufs = (first, second, third, fourth)
    lefts = (0, 0, 0, 4, 6, 8)
    rights = (1, 2, 3, 5, 7, 9)
    turned = set()
    mine = pl.ds(pl.multiple_of(core * width, width), width)
    other = pl.ds(pl.multiple_of((1 - core) * width, width), width)
    stage_in = [
        pltpu.make_async_copy(keys_in, key_rows, extra.at[0]),
        pltpu.make_async_copy(values_in, value_rows, extra.at[1]),
    ]
    live_in = [
        pltpu.make_async_copy(second_in[n].at[pl.ds(0, live)], second_rows[n], extra.at[4 + k])
        for k, n in enumerate((9, 6, 5))
    ]
    for copy in live_in + stage_in:
        copy.start()
    greet(peers)
    for copy in live_in:
        copy.wait()

    def bring(src, dst, sem):
        copy = pltpu.make_async_copy(src, dst, extra.at[sem])
        copy.start()
        return copy

    def remote(src, dst, slot, peer):
        return pltpu.make_async_remote_copy(
            src_ref=src, dst_ref=dst, send_sem=send.at[slot], recv_sem=recv.at[slot],
            device_id=peer, device_id_type=MESH)

    def turn(array):
        left = lefts[array]
        if left in turned:
            return
        turned.add(left)
        for n, rows in enumerate((first_rows, second_rows)):
            if left == 0:
                bring(rows[0], source, 2).wait()
                wide_x[n] = source[...].T
            else:
                wide_s[left // 2 - 2, n] = rows[left][...].T

    def multiply(array, offset, size):
        total = None
        for n, rows in enumerate((first_rows, second_rows)):
            right = rows[rights[array]][:, pl.ds(offset, size)]
            if array in (1, 2):
                left = wide_x[n]
            elif array == 0:
                left = wide_x[n, :, :live]
            else:
                left = wide_s[lefts[array] // 2 - 2, n]
            term = jnp.dot(left, right, preferred_element_type=jnp.float32)
            total = term if total is None else total + term
        return total

    tile = width // 2

    def produce(p, slot):
        array, part = SCATTER_PIECES[p]
        turn(array)
        blocks = 4 if array > 3 else 1
        base = ((1 - core) * blocks + part) * width

        def body(n, carry):
            offset = pl.multiple_of(base + n * tile, tile)
            got = multiply(array, offset, tile).astype(jnp.bfloat16)
            slots[slot, :, :, :, :, :, pl.ds(pl.multiple_of(n * tile, tile), tile)] = got.reshape(
                slots.shape[1:6] + (tile,)
            )
            return carry

        lax.fori_loop(0, 2, body, 0)

    def combine(p):
        array, part = SCATTER_PIECES[p]
        blocks = 4 if array > 3 else 1
        base = (core * blocks + part) * width

        def body(n, carry):
            offset = pl.multiple_of(base + n * tile, tile)
            cols = pl.ds(pl.multiple_of(n * tile, tile), tile)
            got = multiply(array, offset, tile).reshape(slots.shape[1:6] + (tile,))
            acc[p, :, :, :, :, :, cols] = (
                got + acc[p, :, :, :, :, :, cols].astype(jnp.float32)
            ).astype(jnp.bfloat16)
            return carry

        lax.fori_loop(0, 2, body, 0)

    def stage(p, s):
        if s == 0:
            return remote(slots.at[p % SLOTS], acc.at[p], p * 5, peers[4])
        order = SCATTER_HOPS[p]
        src = acc.at[(p,) + block_index(bits, order[s:], flip=order[s - 1])]
        return remote(src, bufs[s - 1].at[p], p * 5 + s, peers[order[s - 1]])

    def fold(p, s):
        array, part = SCATTER_PIECES[p]
        order = SCATTER_HOPS[p]
        free = [b for b in (3, 2, 1, 0) if b in order[s:]]
        for n in range(1 << len(free)):
            at = {b: (n >> i) % 2 for i, b in enumerate(reversed(free))}
            where = tuple(at.get(b, bits[b]) for b in (3, 2, 1, 0))
            got = bufs[s - 1][(p,) + tuple(at[b] for b in free)]
            if s < 4:
                acc[(p,) + where] = acc[(p,) + where] + got
            else:
                total = acc[(p,) + where].astype(jnp.float32) + got.astype(jnp.float32)
                if array < 3:
                    oq[array] = total
                elif array == 4:
                    oi[:, pl.ds(part * width, width)] = total
                elif array == 3:
                    oo[...] = total
                else:
                    ol[:, pl.ds(part * width, width)] = total

    small_started = {}

    def small_stage(s):
        peer = peers[4] if s == 0 else peers[s - 1]
        src = small_v.at[:, other] if s == 0 else small_in.at[s]
        return remote(src, small_recv.at[s], 60 + s, peer)

    def small_step(n):
        if n == 0:
            small_in[0] = small_v[:, mine]
        else:
            small_started[n - 1].wait_recv()
            total = small_in[n - 1] + small_recv[n - 1]
            if n < 5:
                small_in[n] = total
            else:
                osmall[...] = total
        if n < 5:
            small_started[n] = small_stage(n)
            small_started[n].start()

    swaps, places = [], []

    def unpermute(n, values, target, segment):
        if n > 1:
            swaps[n - 2].wait_send()
            places[n - 2].wait()
        result[n % 2] = dot_tn(move[segment], values).astype(jnp.bfloat16)
        places.append(
            pltpu.make_async_copy(result.at[n % 2, :, mine], target.at[core, segment], sent.at[n])
        )
        swaps.append(remote(result.at[n % 2, :, other], target.at[core, segment], 65 + n, peers[4]))
        places[n].start()
        swaps[n].start()

    weights = (wk, wv, wq)
    fetched = {}

    def compute(task):
        if task < 4:
            if task == 0:
                for copy in stage_in:
                    copy.wait()
                fetched[0] = bring(weights[0], held, 3)

            def pair(n, carry):
                cols = pl.ds(pl.multiple_of((2 * task + n) * 2 * DH, 2 * DH), 2 * DH)
                grad_query[:, cols], key_rows[:, cols], value_rows[:, cols] = attend_back_pair(
                    query[:, cols], key_rows[:, cols], value_rows[:, cols], up[:, cols], valid
                )
                return carry

            lax.fori_loop(0, 2, pair, 0)
        elif task < 7:
            n = task - 4
            fetched[n].wait()
            if n == 0:
                total_rows[...] = dot_nt(key_rows[...], held[...])
            elif n == 1:
                total_rows[...] = total_rows[...] + dot_nt(value_rows[...], held[...])
            else:
                total_rows[:live] = total_rows[:live] + grad_one[...] + dot_nt(grad_query[...], held[...])
                row = lax.broadcasted_iota(jnp.int32, (16, 2 * width), 0)
                small_v[:16] = jnp.where(row < mem_rows, total_rows[:16], 0.0)
                query_sum = jnp.sum(grad_query[...].astype(jnp.float32), axis=0, keepdims=True)
                value_sum = jnp.sum(value_rows[...].astype(jnp.float32), axis=0, keepdims=True)
                small_v[16:24] = small_a[...] + small_b[...] + jnp.where(
                    row[:8] == 0, query_sum, jnp.where(row[:8] == 1, value_sum, 0.0)
                )
                inner = [
                    jnp.sum(before[...].astype(jnp.float32), axis=0, keepdims=True)
                    for before in (before_a, second_rows[7])
                ]
                inner = inner[0] + inner[1]
                blocks = inner.shape[1] // (2 * width)
                small_v[24:] = jnp.concatenate(
                    [
                        jnp.concatenate(
                            [inner[:, (h * blocks + n) * width : (h * blocks + n + 1) * width] for h in range(2)],
                            axis=1,
                        )
                        for n in range(blocks)
                    ]
                    + [jnp.zeros((small_v.shape[0] - 24 - blocks, 2 * width), jnp.float32)],
                    axis=0,
                )
            if n < 2:
                fetched[n + 1] = bring(weights[n + 1], held, 3)
        elif task == 7:
            unpermute(0, total_rows[...].astype(jnp.bfloat16), grad_item, 0)
        else:
            values, target, segment = (
                (outs_a, out_item, 0),
                (outs_b, out_item, 1),
                (grads_b, grad_item, 1),
            )[task - 8]
            bring(values, source, 2).wait()
            unpermute(task - 7, source[...], target, segment)

    started = {}
    ready = None
    for step in SCATTER_STEPS:
        if step >= 100:
            compute(step - 100)
            if step == 106:
                ready = 0
            continue
        p, s = step // 8, step % 8
        if s == 0:
            if p >= SLOTS:
                started[p - SLOTS, 0].wait_send()
            produce(p, p % SLOTS)
        else:
            started[p, s - 1].wait_recv()
            if s == 1:
                combine(p)
            else:
                fold(p, s - 1)
        if s < 5:
            started[p, s] = stage(p, s)
            started[p, s].start()
        if ready is not None:
            ready += 1
            if ready % 3 == 0 and ready <= 18:
                small_step(ready // 3 - 1)
    for (p, s), copy in started.items():
        if s > 0 or p >= len(SCATTER_PIECES) - SLOTS:
            copy.wait_send()
    for s in range(5):
        small_started[s].wait_send()
    for n in range(4):
        if n > 1:
            swaps[n].wait_send()
            places[n].wait()
        swaps[n].wait_recv()


def scatter_all(mem_rows, valid, first_rows, second_rows, tail, smalls, outs, grads):
    width = smalls[0].shape[1] // 2
    small_rows = 32
    rows = 2 * width // 16
    low, full = jnp.bfloat16, jnp.float32
    count = len(SCATTER_PIECES)
    long, live = second_rows[0].shape[0], second_rows[1].shape[0]
    move = tail[-1]
    tokens = move.shape[2]
    item = (2, 2, tokens, width)
    return pl.pallas_call(
        functools.partial(scatter_kernel, mem_rows, valid),
        out_shape=[
            jax.ShapeDtypeStruct((3, rows, width), full),
            jax.ShapeDtypeStruct((rows, width), full),
            jax.ShapeDtypeStruct((rows, 4 * width), full),
            jax.ShapeDtypeStruct((rows, 4 * width), full),
            jax.ShapeDtypeStruct((small_rows, width), full),
            jax.ShapeDtypeStruct(item, low),
            jax.ShapeDtypeStruct(item, low),
        ],
        in_specs=[HBM] + [VMEM] * 6 + [HBM] + [VMEM] * 4 + [HBM] * 2 + [VMEM] * 2 + [HBM]
        + [VMEM, HBM, HBM, VMEM, VMEM, HBM, HBM, HBM, VMEM, VMEM, VMEM, HBM, HBM, HBM],
        out_specs=[VMEM] * 5 + [HBM] * 2,
        scratch_shapes=[
            pltpu.VMEM((count, 2, 2, 2, 2, rows, width), low),
            pltpu.VMEM((count, 2, 2, 2, rows, width), low),
            pltpu.VMEM((count, 2, 2, rows, width), low),
            pltpu.VMEM((count, 2, rows, width), low),
            pltpu.VMEM((count, rows, width), low),
            pltpu.VMEM((SLOTS, 2, 2, 2, 2, rows, width), low),
            pltpu.VMEM((2, 2 * width, long), low),
            pltpu.VMEM((3, 2, 2 * width, live), low),
            pltpu.VMEM((2 * width, 2 * width), low),
            pltpu.VMEM((live, 2 * width), low),
            pltpu.VMEM((long, 2 * width), low),
            pltpu.VMEM((long, 2 * width), low),
            pltpu.VMEM((long, 2 * width), low),
            pltpu.VMEM((2, tokens, 2 * width), low),
            pltpu.VMEM((long, 2 * width), full),
            pltpu.VMEM((small_rows, 2 * width), full),
            pltpu.VMEM((5, small_rows, width), full),
            pltpu.VMEM((5, small_rows, width), full),
            pltpu.VMEM((live, 2 * width), low),
            pltpu.VMEM((live, 2 * width), low),
            pltpu.VMEM((live, first_rows[6].shape[1]), low),
            pltpu.SemaphoreType.DMA((69,)),
            pltpu.SemaphoreType.DMA((69,)),
            pltpu.SemaphoreType.DMA((7,)),
            pltpu.SemaphoreType.DMA((4,)),
        ],
        compiler_params=pltpu.CompilerParams(collective_id=1, has_side_effects=True, vmem_limit_bytes=67_000_000),
        name="scatter_all",
    )(*first_rows, *second_rows, *tail[:-1], move, *smalls, *outs, *grads)


def item_shards(
    tokens,
    memory,
    w_qkv,
    b_qv,
    w_out,
    out_biases,
    norm_gains,
    norm_shifts,
    w_in,
    b_in,
    w_down,
    cotangent,
    mlm_mask,
):
    core = lax.axis_index("tensor")
    segments, count = tokens.shape[1], tokens.shape[2]
    mem_rows = memory.shape[0]
    valid = mem_rows + count
    half = memory.shape[1]

    mask = lax.dynamic_index_in_dim(mlm_mask, core, 0, keepdims=False)
    lower_tri = (
        lax.broadcasted_iota(jnp.int32, (count, count), 0)
        <= lax.broadcasted_iota(jnp.int32, (count, count), 1)
    ).astype(jnp.bfloat16)
    ones = mask.astype(jnp.bfloat16)
    upto = dot_nn(ones, lower_tri).astype(jnp.int32)
    total = upto[:, -1:]
    index = lax.broadcasted_iota(jnp.int32, mask.shape, 1)
    place = mem_rows + jnp.where(mask > 0, upto - 1, total + index - upto)
    move = (
        lax.broadcasted_iota(jnp.int32, (segments, ROWS, count), 1) == place[:, None, :]
    ).astype(jnp.bfloat16)
    live_move = move[:, :LIVE] * ones[:, None, :]

    packed = jnp.concatenate(
        [
            jnp.pad(memory, ((0, PACK_BIASES - mem_rows), (0, 0))),
            b_qv,
            out_biases,
            norm_gains,
            norm_shifts,
            b_in.reshape(-1, half),
        ],
        axis=0,
    )
    packed = jnp.pad(packed, ((0, -packed.shape[0] % 16), (0, 0)))
    both, (wq, wk, wv, outer, inner, lower), first = gather_all(
        mem_rows,
        valid,
        tokens,
        cotangent,
        packed,
        w_qkv.transpose(1, 0, 2),
        w_out.T,
        w_in,
        w_down.T,
        move,
        live_move,
    )
    (
        stacked,
        stacked_next,
        ups,
        query,
        key_rows,
        value_rows,
        query_live,
        context,
        normed_one,
        rstd_one,
        middle_low,
        before,
        hidden,
        normed_two,
        rstd_two,
        low_out,
    ) = first
    wide = jnp.concatenate([both[0], both[1]], axis=1).astype(jnp.float32)
    qv_bias, out_bias, gains, shifts = (
        wide[n : n + 2] for n in (PACK_BIASES, PACK_OUT, PACK_GAINS, PACK_SHIFTS)
    )
    inner_rows = b_in.shape[0] // half
    inner_bias = both[:, PACK_INNER : PACK_INNER + inner_rows].reshape(-1).astype(jnp.float32)
    stored = [
        (
            stacked,
            query,
            key_rows,
            value_rows,
            context,
            normed_one,
            rstd_one,
            middle_low,
            before,
            hidden,
            normed_two,
            rstd_two,
        )
    ]
    outs = [low_out]
    stacked = stacked_next
    query = (dot_nn(stacked, wq) + qv_bias[0]).astype(jnp.bfloat16)
    key_rows = dot_nn(stacked, wk).astype(jnp.bfloat16)
    value_rows = (dot_nn(stacked, wv) + qv_bias[1]).astype(jnp.bfloat16)
    context = attend(query, key_rows, value_rows, valid)
    attended = dot_nt(context, outer)
    middle, normed_one, rstd_one = norm_rows(
        stacked.astype(jnp.float32) + attended + out_bias[0], gains[0], shifts[0]
    )
    middle_low = middle.astype(jnp.bfloat16)
    before = dot_nn(middle_low, inner) + inner_bias
    hidden = gelu_value(before).astype(jnp.bfloat16)
    middle_unit = hidden.shape[1] // 2
    branch = dot_nt(hidden[:, :middle_unit], lower[:, :middle_unit]) + dot_nt(
        hidden[:, middle_unit:], lower[:, middle_unit:]
    )
    layer_out, normed_two, rstd_two = norm_rows(
        middle + branch + out_bias[1], gains[1], shifts[1]
    )
    low_out = layer_out.astype(jnp.bfloat16)
    outs.append(low_out)
    stored.append(
        (
            stacked,
            query,
            key_rows,
            value_rows,
            context,
            normed_one[:LIVE],
            rstd_one[:LIVE],
            middle_low,
            before[:LIVE].astype(jnp.bfloat16).astype(jnp.float32),
            hidden,
            normed_two[:LIVE],
            rstd_two[:LIVE],
        )
    )

    returning = jnp.zeros((mem_rows, D), jnp.float32)
    token_grads = []
    pieces = [None] * segments
    smalls = []
    for seg in reversed(range(segments)):
        (
            stacked,
            query,
            key_rows,
            value_rows,
            context,
            normed_one,
            rstd_one,
            middle_low,
            before,
            hidden,
            normed_two,
            rstd_two,
        ) = stored[seg]
        upstream = ups[seg].astype(jnp.float32)
        upstream = upstream + jnp.pad(returning, ((0, LIVE - mem_rows), (0, 0)))
        grad_two, gain_two, shift_two = norm_rows_back(upstream, normed_two, rstd_two, gains[1])
        grad_branch = grad_two.astype(jnp.bfloat16)
        grad_hidden = dot_nn(grad_branch, lower)
        grad_before = (grad_hidden * gelu_slope(before)).astype(jnp.bfloat16)
        grad_middle = grad_two + dot_nt(grad_before, inner)
        grad_one, gain_one, shift_one = norm_rows_back(
            grad_middle, normed_one, rstd_one, gains[0]
        )
        grad_attended = grad_one.astype(jnp.bfloat16)
        grad_context = dot_nn(grad_attended, outer).astype(jnp.bfloat16)
        sums = [jnp.zeros((D,), jnp.float32)] * 2
        if seg > 0:
            grad_query, grad_key, grad_value = attend_back(
                query, key_rows, value_rows, grad_context, valid
            )
            grad_stacked = dot_nt(grad_key, wk) + dot_nt(grad_value, wv)
            live_part = grad_one + dot_nt(grad_query, wq)
            grad_stacked = grad_stacked + jnp.pad(live_part, ((0, ROWS - LIVE), (0, 0)))
            returning = grad_stacked[:mem_rows]
            token_grads.append(grad_stacked.astype(jnp.bfloat16))
            attention_grads = [grad_query, grad_key, grad_value]
            sums = [jnp.sum(grad.astype(jnp.float32), axis=0) for grad in (grad_query, grad_value)]
        else:
            attention_grads = []
            tail = [query_live, key_rows, value_rows, grad_context, grad_one, wq, wk, wv, move]
        pieces[seg] = (
            stacked,
            *attention_grads,
            grad_attended,
            context,
            middle_low,
            grad_before,
            grad_branch,
            hidden,
        )
        smalls.append(
            jnp.stack(
                [
                    *sums,
                    jnp.sum(grad_one, axis=0),
                    jnp.sum(grad_two, axis=0),
                    gain_one,
                    gain_two,
                    shift_one,
                    shift_two,
                ]
            )
        )

    grad_proj, grad_outer, grad_inner, grad_lower, mine, outputs, input_grad = scatter_all(
        mem_rows, valid, pieces[0], pieces[1], tail, smalls, outs, token_grads
    )
    return (
        outputs,
        input_grad.astype(jnp.float32),
        mine[:mem_rows],
        grad_proj.transpose(1, 0, 2),
        mine[16:18],
        grad_outer.T,
        mine[18:20],
        mine[20:22],
        mine[22:24],
        grad_inner,
        mine[24 : 24 + inner_rows].reshape(-1),
        grad_lower.T,
    )


def solution(mesh):
    def body(*arrays):
        if mesh.shape["dp"] == 16 and mesh.shape["tensor"] == arrays[0].shape[0] == arrays[0].shape[1] == 2:
            return item_shards(*arrays)
        return shards(*arrays)

    placed = (
        P("dp", None, None, "tensor"),
        P(None, "tensor"),
        P("dp", None, "tensor"),
        P(None, "tensor"),
        P("tensor", "dp"),
        P(None, "tensor"),
        P(None, "tensor"),
        P(None, "tensor"),
        P("dp", "tensor"),
        P("tensor"),
        P("tensor", "dp"),
        P("dp", None, None, "tensor"),
        P("dp", None, None),
    )
    return jax.shard_map(
        body,
        mesh=mesh,
        in_specs=placed,
        out_specs=(
            P("dp", None, None, "tensor"),
            P("dp", None, None, "tensor"),
            P(None, "tensor"),
            P("dp", None, "tensor"),
            P(None, "tensor"),
            P("tensor", "dp"),
            P(None, "tensor"),
            P(None, "tensor"),
            P(None, "tensor"),
            P("dp", "tensor"),
            P("tensor"),
            P("tensor", "dp"),
        ),
        check_vma=False,
    )
```
